32 devices in a mesh: dp: 8 (over z, x), tensor: 4 (over y, core).
Axes of the slice: x: 2, y: 2, z: 4, core: 2. Of those that a mesh axis runs over, the one named last changes fastest.
Arguments:
- tokens: bfloat16 [16, 512, 768], P('dp', 'tensor'), may hold values from -6 to 6
- characters: bfloat16 [16, 2048, 256], P('dp', 'tensor'), may hold values from -6 to 6
- doc_lengths: int32 [16, 8], P('dp'), may hold values from 1 to 256, 512 in all within a row
- token_chars: int32 [16, 512], P('dp'), may hold values from 1 to 8, 2048 in all within a row
- w_qkv: bfloat16 [768, 3, 768], P(None, None, 'tensor'), may hold values from -0.21875 to 0.21875
- w_out: bfloat16 [768, 768], P('tensor'), may hold values from -0.875 to 0.875
- w_in: bfloat16 [768, 3072], P(None, 'tensor'), may hold values from -0.21875 to 0.21875
- w_down: bfloat16 [3072, 768], P('tensor'), may hold values from -0.109375 to 0.109375
- w_gru: bfloat16 [256, 2, 2, 384], P(None, None, None, 'tensor'), may hold values from -0.375 to 0.375
- gate_bias: float32 [2, 384], P(None, 'tensor'), may hold values from -4 to 1
- w_conv: bfloat16 [3, 1536, 768], P(None, None, 'tensor'), may hold values from -0.09375 to 0.09375
- w_merge: bfloat16 [768, 2, 768], P('tensor'), may hold values from -0.21875 to 0.21875
- norm_gain: float32 [4, 768], replicated, may hold values from 0.5 to 1.5
- norm_bias: float32 [4, 768], replicated, may hold values from -1.75 to 1.75
- token_cot: float32 [16, 512, 768], P('dp', 'tensor'), may hold values from -6 to 6
- char_cot: float32 [16, 512, 768], P('dp', 'tensor'), may hold values from -6 to 6
Outputs:
- token_out: bfloat16 [16, 512, 768], P('dp', 'tensor')
- char_out: bfloat16 [16, 512, 768], P('dp', 'tensor')
- grad_tokens: float32 [16, 512, 768], P('dp', 'tensor')
- grad_characters: float32 [16, 2048, 256], P('dp', 'tensor')
- grad_qkv: float32 [768, 3, 768], P(None, None, 'tensor')
- grad_out: float32 [768, 768], P('tensor')
- grad_in: float32 [768, 3072], P(None, 'tensor')
- grad_down: float32 [3072, 768], P('tensor')
- grad_gru: float32 [256, 2, 2, 384], P(None, None, None, 'tensor')
- grad_gate_bias: float32 [2, 384], P(None, 'tensor')
- grad_conv: float32 [3, 1536, 768], P(None, None, 'tensor')
- grad_merge: float32 [768, 2, 768], P('tensor')
- grad_gain: float32 [4, 768], replicated
- grad_bias: float32 [4, 768], replicated
The draws below stay inside these ranges and needn't reach their ends.
Inputs may be any that keep to these rules, and one draw needn't show every extreme that they name: `doc_lengths`: A sequence's 8 entries are the token counts of its documents in order, summing to 512; in every sequence one document has exactly 256 tokens. `token_chars`: A sequence's 512 entries are the character counts of its tokens in order, summing to 2048; in every sequence some token has exactly 8 characters.
All inputs are finite; a program needn't handle non-finite values.
Results may differ from the reference program's by a relative error of at most 0.023.
Values may be sent and summed in bfloat16 or wider, within the bound.
A program may use at most 192 MiB of HBM per device.

```python
import math
import jax
import jax.numpy as jnp
import numpy as np
from jax import lax

D = 768
HEADS = 12
HD = 64
FF = 3072
DC = 256
GH = 384
FC = 768
LEN = 512
DOCS = 8
CPT = 4
SEQS = 16
NC = 2048


def steps_of(key, shape, split, low, largest):
    level = 1.0
    for dim, blocks in split:
        draws = jax.random.uniform(jax.random.fold_in(jax.random.fold_in(key, 6), dim), (blocks,), jnp.float32, low / len(split), largest / len(split))
        level = level * jnp.repeat(jnp.exp(draws), shape[dim] // blocks).reshape((-1,) + (1,) * (len(shape) - 1 - dim))
    return level


def profile(number_of, total, limit, skew):
    loads = [(1 << 20) // math.isqrt(standing ** skew) + 1 for standing in range(2, number_of + 1)]
    spare, given = total - limit - (number_of - 1), [1] * (number_of - 1)
    while spare > 0:
        candidates = [i for i in range(number_of - 1) if given[i] < limit]
        mass, budget = sum([loads[i] for i in candidates]), spare
        for i in candidates:
            more = min(limit - given[i], max(1, budget * loads[i] // mass), spare)
            given[i] = given[i] + more
            spare = spare - more
    return np.array([limit] + given)


def ragged_sizes(stream_key, amount, total, bound, skew):
    if amount == 2:
        one = jax.random.randint(stream_key, (), max(1, total - bound), min(bound, total - 1) + 1)
        return jnp.stack([one, total - one])
    lengths = jnp.asarray(profile(amount, total, bound, skew), jnp.int32)
    pairs = (amount - 1) // 2
    donor, taker = lengths[1:1 + 2 * pairs:2], lengths[2:2 + 2 * pairs:2]
    room = jnp.minimum(donor - 1, bound - taker)
    shifted = jax.random.randint(jax.random.fold_in(stream_key, 1), (pairs,), 0, 1 << 20) % (room + 1)
    lengths = lengths.at[1:1 + 2 * pairs:2].set(donor - shifted).at[2:2 + 2 * pairs:2].set(taker + shifted)
    return lengths[jax.random.permutation(jax.random.fold_in(stream_key, 2), amount)]


def bell_draw(key, shape, scale, limit, cuts=(), kind=jnp.bfloat16):
    result = jax.random.normal(key, shape, jnp.float32) * scale
    if len(cuts) > 0:
        result = steps_of(key, shape, cuts, -0.22, 0.18) * result
    return jnp.clip(result, min=-limit, max=limit).astype(kind)


def setup_inputs(seed: int = 0) -> dict:
    seeds = jax.random.split(jax.random.key(seed), 17)
    tokens = bell_draw(seeds[0], (SEQS, LEN, D), 1.0, 6.0, ((0, 8), (1, 4)))
    characters = bell_draw(seeds[1], (SEQS, NC, DC), 1.0, 6.0, ((0, 8), (1, 4)))
    doc_lengths = jax.vmap(lambda own: ragged_sizes(own, DOCS, LEN, LEN // 2, 2))(jax.random.split(seeds[2], SEQS)).reshape((SEQS, DOCS)).astype(jnp.int32)
    token_chars = jax.vmap(lambda own: ragged_sizes(own, LEN, NC, 2 * CPT, 1))(jax.random.split(seeds[3], SEQS)).reshape((SEQS, LEN)).astype(jnp.int32)
    w_qkv = bell_draw(seeds[4], (D, 3, D), D ** -0.5, 0.21875, ((2, 4),))
    w_out = bell_draw(seeds[5], (D, D), (D // 16) ** -0.5, 0.875, ((0, 4),))
    w_in = bell_draw(seeds[6], (D, FF), D ** -0.5, 0.21875, ((1, 4),))
    w_down = bell_draw(seeds[7], (FF, D), FF ** -0.5, 0.109375, ((0, 4),))
    w_gru = bell_draw(seeds[8], (DC, 2, 2, GH), DC ** -0.5, 0.375, ((3, 4),))
    gate_bias = jnp.clip(-4.0 + 5.0 * jax.random.uniform(seeds[9], (2, GH), jnp.float32) ** steps_of(seeds[9], (2, GH), ((1, 4),), -0.2, 0.2), -4.0, 1.0)
    w_conv = bell_draw(seeds[10], (3, 2 * D, FC), (6 * D) ** -0.5, 0.09375, ((2, 4),))
    w_merge = bell_draw(seeds[11], (FC, 2, D), FC ** -0.5, 0.21875, ((0, 4),))
    norm_gain = jnp.clip(1.0 + 0.1 * jax.random.normal(seeds[12], (4, D), jnp.float32), 0.5, 1.5)
    norm_bias = bell_draw(seeds[13], (4, D), 0.3, 1.75, (), jnp.float32)
    token_cot = bell_draw(seeds[14], (SEQS, LEN, D), 1.0, 6.0, ((0, 8), (1, 4)), jnp.float32)
    char_cot = bell_draw(seeds[15], (SEQS, LEN, D), 1.0, 6.0, ((0, 8), (1, 4)), jnp.float32)
    return dict(tokens=tokens, characters=characters, doc_lengths=doc_lengths, token_chars=token_chars, w_qkv=w_qkv, w_out=w_out, w_in=w_in, w_down=w_down, w_gru=w_gru, gate_bias=gate_bias, w_conv=w_conv, w_merge=w_merge, norm_gain=norm_gain, norm_bias=norm_bias, token_cot=token_cot, char_cot=char_cot)


@jax.custom_vjp
def low(v):
    return lax.optimization_barrier(v.astype(jnp.bfloat16)).astype(jnp.float32)

@jax.custom_vjp
def low_back(v):
    return v

def low_keep(v):
    return (low(v), None)

def low_pass(kept, grad):
    return (grad,)

def back_keep(v):
    return (v, None)

def back_low(kept, grad):
    return (low(grad),)
low.defvjp(low_keep, low_pass)
low_back.defvjp(back_keep, back_low)
NORM_EPSILON = 1e-06
MASK_VALUE = -1e+30
HIGH_PRECISION = lax.Precision.HIGHEST

def layer_norm(row_values, gain_row, shift_row):
    average = lax.optimization_barrier(jnp.mean(row_values, axis=-1, keepdims=True))
    centered = row_values - average
    spread = lax.optimization_barrier(jnp.mean(centered * centered, axis=-1, keepdims=True))
    return centered * lax.rsqrt(spread + NORM_EPSILON) * gain_row + shift_row

def gelu_exact(values):
    return jax.nn.gelu(values, approximate=False)

def layout(doc_sizes, char_counts, char_total):
    length = char_counts.shape[0]
    doc_ends = jnp.cumsum(doc_sizes, dtype=jnp.int32)
    positions = jnp.arange(length, dtype=jnp.int32)
    segment = lax.optimization_barrier(jnp.sum((positions[:, None] >= doc_ends[None, :]).astype(jnp.int32), axis=1, dtype=jnp.int32))
    token_ends = jnp.cumsum(char_counts, dtype=jnp.int32)
    char_positions = jnp.arange(char_total, dtype=jnp.int32)
    char_token = jnp.searchsorted(token_ends, char_positions, side='right').astype(jnp.int32)
    last_char = (token_ends - 1).astype(jnp.int32)
    first_char = (token_ends - char_counts).astype(jnp.int32)
    char_segment = jnp.take(segment, char_token)
    char_same = (char_segment[1:] == char_segment[:-1]).astype(jnp.float32)
    token_same = (segment[1:] == segment[:-1]).astype(jnp.float32)
    zero_one = jnp.zeros((1,), jnp.float32)
    keep_forward = jnp.concatenate([zero_one, char_same])
    keep_backward = jnp.concatenate([char_same, zero_one])
    prev_ok = jnp.concatenate([zero_one, token_same])
    next_ok = jnp.concatenate([token_same, zero_one])
    return (segment, first_char, last_char, keep_forward, keep_backward, prev_ok, next_ok)

def combine_linear(earlier, later):
    return (earlier[0] * later[0], later[0] * earlier[1] + later[1])

def gru_tokens(projected, gate_bias, keep_forward, keep_backward, first_char, last_char):
    gates = jax.nn.sigmoid(projected[:, :, 0, :] + gate_bias[None])
    drive = gates * projected[:, :, 1, :]
    decay = 1.0 - gates
    forward_states = lax.associative_scan(combine_linear, (decay[:, 0] * keep_forward[:, None], drive[:, 0]))[1]
    backward_states = lax.associative_scan(combine_linear, (decay[:, 1] * keep_backward[:, None], drive[:, 1]), reverse=True)[1]
    return jnp.stack([jnp.take(forward_states, last_char, axis=0), jnp.take(backward_states, first_char, axis=0)], axis=1)

def conv_inputs(joined, prev_ok, next_ok):
    zero_row = jnp.zeros((1, joined.shape[1]), joined.dtype)
    preceding = jnp.concatenate([zero_row, joined[:-1]], axis=0) * prev_ok[:, None].astype(joined.dtype)
    following = jnp.concatenate([joined[1:], zero_row], axis=0) * next_ok[:, None].astype(joined.dtype)
    return jnp.concatenate([preceding, joined, following], axis=1)

def attend_block(query_block, seg_block, key_low, value_low, segment):
    scores = low_back(jnp.einsum('qhd,khd->hqk', query_block, key_low, precision=HIGH_PRECISION))
    same_doc = (seg_block[:, None] == segment[None, :])[None]
    scores = jnp.where(same_doc, scores, MASK_VALUE)
    row_max = lax.optimization_barrier(jnp.max(scores, axis=-1, keepdims=True))
    log_total = row_max + jnp.log(lax.optimization_barrier(jnp.sum(jnp.exp(scores - row_max), axis=-1, keepdims=True)))
    prob_low = low(jnp.exp(scores - log_total))
    return jnp.einsum('hqk,khd->qhd', prob_low, value_low, precision=HIGH_PRECISION)

def forward(weights, token_rows, char_rows, structure):
    w_qkv, w_out, w_in, w_down, w_gru, gate_bias, w_conv, w_merge, norm_gain, norm_bias = weights
    segment, first_char, last_char, keep_forward, keep_backward, prev_ok, next_ok = structure
    length = token_rows.shape[0]
    char_total = char_rows.shape[0]
    qkv = jnp.dot(token_rows, w_qkv.reshape(D, 3 * HEADS * HD), precision=HIGH_PRECISION, preferred_element_type=jnp.float32).reshape(length, 3, HEADS, HD)
    queries = low(low_back(qkv[:, 0] * 0.125))
    key_low = low(low_back(qkv[:, 1]))
    value_low = low(low_back(qkv[:, 2]))
    block_rows = min(512, length)
    block_count = length // block_rows

    def one_block(pieces):
        return attend_block(pieces[0], pieces[1], key_low, value_low, segment)
    context = lax.map(jax.checkpoint(one_block), (queries.reshape(block_count, block_rows, HEADS, HD), segment.reshape(block_count, block_rows)))
    context = low(low_back(context.reshape(length, HEADS * HD)))
    attn = low_back(jnp.dot(context, w_out, precision=HIGH_PRECISION, preferred_element_type=jnp.float32))
    hidden = layer_norm(token_rows + attn, norm_gain[0], norm_bias[0])
    hidden_low = low(hidden)
    pre_act = low_back(jnp.dot(hidden_low, w_in, precision=HIGH_PRECISION, preferred_element_type=jnp.float32))
    activation = low(gelu_exact(pre_act))
    ffn = low_back(jnp.dot(activation, w_down, precision=HIGH_PRECISION, preferred_element_type=jnp.float32))
    token_mid = layer_norm(hidden + ffn, norm_gain[1], norm_bias[1])
    mid_low = low(token_mid)
    projected = low_back(jnp.dot(char_rows, w_gru.reshape(DC, 4 * GH), precision=HIGH_PRECISION, preferred_element_type=jnp.float32)).reshape(char_total, 2, 2, GH)
    char_tokens = low(gru_tokens(projected, gate_bias, keep_forward, keep_backward, first_char, last_char))
    char_flat = char_tokens.reshape(length, 2 * GH)
    joined = jnp.concatenate([mid_low, char_flat], axis=1)
    stacked = conv_inputs(joined, prev_ok, next_ok)
    pre_merge = low_back(jnp.dot(stacked, w_conv.reshape(3 * 2 * D, FC), precision=HIGH_PRECISION, preferred_element_type=jnp.float32))
    merged = low(gelu_exact(pre_merge))
    branch = low_back(jnp.dot(merged, w_merge.reshape(FC, 2 * D), precision=HIGH_PRECISION, preferred_element_type=jnp.float32))
    token_out = layer_norm(token_mid + branch[:, :D], norm_gain[2], norm_bias[2])
    char_out = layer_norm(char_flat + branch[:, D:], norm_gain[3], norm_bias[3])
    return (token_out, char_out)

def reference(tokens, characters, doc_lengths, token_chars, w_qkv, w_out, w_in, w_down, w_gru, gate_bias, w_conv, w_merge, norm_gain, norm_bias, token_cot, char_cot):
    weights = (w_qkv.astype(jnp.float32), w_out.astype(jnp.float32), w_in.astype(jnp.float32), w_down.astype(jnp.float32), w_gru.astype(jnp.float32), gate_bias.astype(jnp.float32), w_conv.astype(jnp.float32), w_merge.astype(jnp.float32), norm_gain.astype(jnp.float32), norm_bias.astype(jnp.float32))

    def per_sequence(totals, pieces):
        token_rows, char_rows, doc_sizes, char_counts, token_grad, char_grad = pieces
        structure = layout(doc_sizes, char_counts, char_rows.shape[0])

        def wrapped(weight_set, token_in, char_in):
            return forward(weight_set, token_in, char_in, structure)
        outputs, pullback = jax.vjp(wrapped, weights, token_rows.astype(jnp.float32), char_rows.astype(jnp.float32))
        weight_grads, token_back, char_back = pullback((token_grad, char_grad))
        totals = jax.tree.map(jnp.add, totals, weight_grads)
        return (totals, (outputs[0].astype(jnp.bfloat16), outputs[1].astype(jnp.bfloat16), token_back, char_back))
    start_totals = jax.tree.map(jnp.zeros_like, weights)
    totals, per_rows = lax.scan(per_sequence, start_totals, (tokens, characters, doc_lengths, token_chars, token_cot, char_cot))
    token_out, char_out, grad_tokens, grad_characters = per_rows
    grad_qkv, grad_out, grad_in, grad_down, grad_gru, grad_gate_bias, grad_conv, grad_merge, grad_gain, grad_bias = totals
    return (token_out, char_out, grad_tokens, grad_characters, grad_qkv, grad_out, grad_in, grad_down, grad_gru, grad_gate_bias, grad_conv, grad_merge, grad_gain, grad_bias)
```

```python
import jax
import jax.numpy as jnp
from jax import lax
from jax.experimental import pallas as pl
from jax.experimental.pallas import tpu as pltpu
from jax.sharding import PartitionSpec as P

HD = 64


NORM_EPSILON = 1e-06
MASK_VALUE = -1e30
HIGH_PRECISION = lax.Precision.HIGHEST


def layer_norm(row_values, gain_row, shift_row):
    average = jnp.mean(row_values, axis=-1, keepdims=True)
    centered = row_values - average
    spread = jnp.mean(centered * centered, axis=-1, keepdims=True)
    return centered * lax.rsqrt(spread + NORM_EPSILON) * gain_row + shift_row


def gelu_exact(values):
    return jax.nn.gelu(values, approximate=False)


def layout(doc_sizes, char_counts, char_total):
    length = char_counts.shape[0]
    docs = doc_sizes.shape[0]
    doc_ids = jnp.arange(docs, dtype=jnp.int32)
    doc_ends = jnp.sum(
        jnp.where(doc_ids[None, :] <= doc_ids[:, None], doc_sizes[None, :], 0), axis=1
    )
    positions = jnp.arange(length, dtype=jnp.int32)
    segment = jnp.sum(
        (positions[:, None] >= doc_ends[None, :]).astype(jnp.int32), axis=1, dtype=jnp.int32
    )
    token_ends = jnp.sum(
        jnp.where(positions[None, :] <= positions[:, None], char_counts[None, :], 0), axis=1
    )
    last_char = token_ends - 1
    first_char = token_ends - char_counts
    char_ends = jnp.sum(
        jnp.where(positions[None, :] < doc_ends[:, None], char_counts[None, :], 0), axis=1
    )
    char_positions = jnp.arange(char_total, dtype=jnp.int32)
    starts = char_ends - jnp.sum(
        jnp.where(
            (positions[None, :] < doc_ends[:, None])
            & (positions[None, :] >= (doc_ends - doc_sizes)[:, None]),
            char_counts[None, :],
            0,
        ),
        axis=1,
    )
    keep_forward = 1.0 - jnp.any(char_positions[:, None] == starts[None, :], axis=1).astype(
        jnp.float32
    )
    keep_backward = 1.0 - jnp.any(
        char_positions[:, None] == (char_ends - 1)[None, :], axis=1
    ).astype(jnp.float32)
    token_starts = doc_ends - doc_sizes
    prev_ok = 1.0 - jnp.any(positions[:, None] == token_starts[None, :], axis=1).astype(
        jnp.float32
    )
    next_ok = 1.0 - jnp.any(positions[:, None] == (doc_ends - 1)[None, :], axis=1).astype(
        jnp.float32
    )
    return (segment, first_char, last_char, keep_forward, keep_backward, prev_ok, next_ok)


LANE = 128
CHUNKS = 32
VMEM = pl.BlockSpec(memory_space=pltpu.VMEM)


def recur(first, second, decays, drives, outs, steps):
    ups = (first, second)

    def at(ref, tile, step):
        row = step if ups[tile] else steps - 1 - step
        return ref[tile, pl.ds(row, CHUNKS, stride=steps), :]

    def put(ref, tile, step, value):
        row = step if ups[tile] else steps - 1 - step
        ref[tile, pl.ds(row, CHUNKS, stride=steps), :] = value

    zero = jnp.zeros((CHUNKS, LANE), jnp.float32)
    one = jnp.ones((CHUNKS, LANE), jnp.float32)

    def summary(step, carry):
        new = []
        for tile in range(2):
            state, mult = carry[2 * tile], carry[2 * tile + 1]
            decay = at(decays, tile, step)
            new += [decay * state + at(drives, tile, step), decay * mult]
        return tuple(new)

    ends = lax.fori_loop(0, steps, summary, (zero, one, zero, one), unroll=4)
    starts = []
    for tile in range(2):
        final, mult = ends[2 * tile], ends[2 * tile + 1]
        order = range(CHUNKS) if ups[tile] else range(CHUNKS - 1, -1, -1)
        carry = jnp.zeros((1, LANE), jnp.float32)
        rows = [None] * CHUNKS
        for chunk in order:
            rows[chunk] = carry
            carry = mult[chunk : chunk + 1] * carry + final[chunk : chunk + 1]
        starts.append(jnp.concatenate(rows, axis=0))

    def write(step, carry):
        new = []
        for tile in range(2):
            state = at(decays, tile, step) * carry[tile] + at(drives, tile, step)
            put(outs, tile, step, state)
            new.append(state)
        return tuple(new)

    lax.fori_loop(0, steps, write, tuple(starts), unroll=4)


def gates_of(chars, w_ref, bias_ref, keep_ref, gate_ref, cand_ref, decay_ref, drive_ref):
    proj = jnp.dot(chars, w_ref[...], preferred_element_type=jnp.float32)
    for tile in range(2):
        cols = pl.ds(tile * LANE, LANE)
        logits = proj[:, tile * LANE : (tile + 1) * LANE] + bias_ref[:, cols]
        gate = jax.nn.sigmoid(logits)
        cand = proj[:, (2 + tile) * LANE : (3 + tile) * LANE]
        gate_ref[tile] = gate
        cand_ref[tile] = cand
        decay_ref[tile] = (1.0 - gate) * keep_ref[:, tile : tile + 1]
        drive_ref[tile] = gate * cand


def gru_fwd_kernel(chars_ref, w_ref, bias_ref, keep_ref, pick_ref, tok_ref, state_ref,
                   gate_ref, cand_ref, decay_ref, drive_ref):
    total = chars_ref.shape[0]
    steps = total // CHUNKS
    gates_of(chars_ref[...], w_ref, bias_ref, keep_ref, gate_ref, cand_ref, decay_ref, drive_ref)
    recur(True, False, decay_ref, drive_ref, state_ref, steps)
    length = pick_ref.shape[0]
    ids = lax.broadcasted_iota(jnp.int32, (length, total), 1)
    for tile in range(2):
        hot = (ids == pick_ref[:, tile : tile + 1]).astype(jnp.bfloat16)
        cols = pl.ds(tile * LANE, LANE)
        low = state_ref[tile].astype(jnp.bfloat16)
        tok_ref[:, cols] = jnp.dot(hot, low, preferred_element_type=jnp.float32).astype(
            jnp.bfloat16
        )


def gru_bwd_kernel(chars_ref, w_ref, bias_ref, keep_ref, pick_ref, state_ref, grad_ref,
                   proj_grad_ref, bias_grad_ref, gate_ref, cand_ref, decay_ref, drive_ref, flow_ref):
    total = chars_ref.shape[0]
    steps = total // CHUNKS
    gates_of(chars_ref[...], w_ref, bias_ref, keep_ref, gate_ref, cand_ref, decay_ref, drive_ref)
    length = pick_ref.shape[1]
    ids = lax.broadcasted_iota(jnp.int32, (total, length), 0)
    for tile in range(2):
        hot = (ids == pick_ref[tile : tile + 1, :]).astype(jnp.bfloat16)
        cols = pl.ds(tile * LANE, LANE)
        drive_ref[tile] = jnp.dot(hot, grad_ref[:, cols], preferred_element_type=jnp.float32)
    flow_ref[0, pl.ds(0, total - 1), :] = decay_ref[0, pl.ds(1, total - 1), :]
    flow_ref[0, pl.ds(total - 1, 1), :] = jnp.zeros((1, LANE), jnp.float32)
    flow_ref[1, pl.ds(1, total - 1), :] = decay_ref[1, pl.ds(0, total - 1), :]
    flow_ref[1, pl.ds(0, 1), :] = jnp.zeros((1, LANE), jnp.float32)
    recur(False, True, flow_ref, drive_ref, decay_ref, steps)
    for tile in range(2):
        flow = decay_ref[tile] * gate_ref[tile]
        logit_grad = flow * (cand_ref[tile] - state_ref[tile])
        proj_grad_ref[:, pl.ds(tile * LANE, LANE)] = logit_grad.astype(jnp.bfloat16)
        proj_grad_ref[:, pl.ds((2 + tile) * LANE, LANE)] = flow.astype(jnp.bfloat16)
        bias_grad_ref[:, pl.ds(tile * LANE, LANE)] = jnp.sum(logit_grad, axis=0, keepdims=True)


def gru_call(kernel, outs, scratch_count, total):
    return pl.pallas_call(
        kernel,
        out_shape=outs,
        scratch_shapes=[pltpu.VMEM((2, total, LANE), jnp.float32)] * scratch_count,
        compiler_params=pltpu.CompilerParams(vmem_limit_bytes=48 * 1024 * 1024),
    )


def gru_weights(w_gru, gate_bias):
    width, _, _, units = w_gru.shape
    matrix = jnp.pad(jnp.swapaxes(w_gru, 1, 2), ((0, 0), (0, 0), (0, 0), (0, LANE - units)))
    bias = jnp.pad(gate_bias, ((0, 0), (0, LANE - units)))
    return matrix.reshape(width, 4 * LANE), bias.reshape(1, 2 * LANE)


def conv_inputs(joined, prev_ok, next_ok):
    zero_row = jnp.zeros((1, joined.shape[1]), joined.dtype)
    preceding = jnp.concatenate([zero_row, joined[:-1]], axis=0) * prev_ok[:, None].astype(
        joined.dtype
    )
    following = jnp.concatenate([joined[1:], zero_row], axis=0) * next_ok[:, None].astype(
        joined.dtype
    )
    return jnp.concatenate([preceding, joined, following], axis=1)


def conv_back(grad_stacked, prev_ok, next_ok):
    column_count = grad_stacked.shape[1] // 3
    from_prev = grad_stacked[:, :column_count] * prev_ok[:, None]
    from_next = grad_stacked[:, 2 * column_count :] * next_ok[:, None]
    zero_row = jnp.zeros((1, column_count), jnp.float32)
    middle = grad_stacked[:, column_count : 2 * column_count]
    return (
        middle
        + jnp.concatenate([from_prev[1:], zero_row], axis=0)
        + jnp.concatenate([zero_row, from_next[:-1]], axis=0)
    )


def inner_rows(left_rows, right_rows):
    return lax.dot_general(
        left_rows, right_rows, (((0,), (0,)), ((), ())), preferred_element_type=jnp.float32
    )


def times_transposed(left_rows, right_matrix):
    return lax.dot_general(
        left_rows, right_matrix, (((1,), (1,)), ((), ())), preferred_element_type=jnp.float32
    )


def reduce_weights(grads):
    low = lax.psum(tuple(g.astype(jnp.bfloat16) for g in grads), "dp")
    return tuple(g.astype(jnp.float32) for g in low)


def local(
    tokens,
    characters,
    doc_lengths,
    token_chars,
    w_qkv,
    w_out,
    w_in,
    w_down,
    w_gru,
    gate_bias,
    w_conv,
    w_merge,
    norm_gain,
    norm_bias,
    token_cot,
    char_cot,
):
    micro_count = tokens.shape[0]
    shard_len = tokens.shape[1]
    model_width = tokens.shape[2]
    char_width = characters.shape[2]
    group_size = lax.axis_size("tensor")
    group_rank = lax.axis_index("tensor")
    length = shard_len * group_size
    char_total = characters.shape[1] * group_size
    head_cols = w_qkv.shape[2]
    heads_here = head_cols // HD
    units_here = w_gru.shape[3]
    merge_here = w_conv.shape[2]
    row_start = group_rank * shard_len
    qkv_matrix = w_qkv.reshape(model_width, 3 * head_cols)
    gru_matrix, gru_bias = gru_weights(w_gru, gate_bias)
    conv_matrix = w_conv.reshape(3 * 2 * model_width, merge_here)
    merge_matrix = w_merge.reshape(merge_here, 2 * model_width)
    token_outs = []
    char_outs = []
    token_grads = []
    char_grads = []
    weight_total = None
    gain_total = jnp.zeros((4, model_width), jnp.float32)
    bias_total = jnp.zeros((4, model_width), jnp.float32)
    for micro_index in range(micro_count):
        token_rows = tokens[micro_index]
        char_rows = characters[micro_index]
        segment, first_char, last_char, keep_forward, keep_backward, prev_ok, next_ok = layout(
            doc_lengths[micro_index], token_chars[micro_index], char_total
        )
        all_tokens, all_chars = (
            lax.all_gather(token_rows, "tensor", axis=0, tiled=True),
            lax.all_gather(char_rows, "tensor", axis=0, tiled=True),
        )
        qkv = jnp.dot(all_tokens, qkv_matrix, preferred_element_type=jnp.float32).reshape(
            length, 3, heads_here, HD
        )
        queries = (qkv[:, 0] * 0.125).astype(jnp.bfloat16)
        key_low = qkv[:, 1].astype(jnp.bfloat16)
        value_low = qkv[:, 2].astype(jnp.bfloat16)
        query_block = queries
        same_doc = (segment[:, None] == segment[None, :])[None]
        scores = jnp.einsum(
            "qhd,khd->hqk", query_block, key_low, preferred_element_type=jnp.float32
        )
        scores = jnp.where(same_doc, scores, MASK_VALUE)
        row_max = jnp.max(scores, axis=-1, keepdims=True)
        log_total = row_max + jnp.log(jnp.sum(jnp.exp(scores - row_max), axis=-1, keepdims=True))
        prob_low = jnp.exp(scores - log_total).astype(jnp.bfloat16)
        context_parts = jnp.einsum(
            "hqk,khd->qhd", prob_low, value_low, preferred_element_type=jnp.float32
        )
        context_low = context_parts.reshape(length, head_cols).astype(jnp.bfloat16)
        attn_share = lax.psum_scatter(
            jnp.dot(context_low, w_out, preferred_element_type=jnp.float32).astype(jnp.bfloat16),
            "tensor",
            scatter_dimension=0,
            tiled=True,
        ).astype(jnp.float32)
        residual_one = token_rows.astype(jnp.float32) + attn_share
        hidden = layer_norm(residual_one, norm_gain[0], norm_bias[0])
        hidden_all = lax.all_gather(hidden.astype(jnp.bfloat16), "tensor", axis=0, tiled=True)
        pre_act = jnp.dot(hidden_all, w_in, preferred_element_type=jnp.float32)
        activation = gelu_exact(pre_act).astype(jnp.bfloat16)
        ffn_share = lax.psum_scatter(
            jnp.dot(activation, w_down, preferred_element_type=jnp.float32).astype(jnp.bfloat16),
            "tensor",
            scatter_dimension=0,
            tiled=True,
        ).astype(jnp.float32)
        residual_two = hidden + ffn_share
        token_mid = layer_norm(residual_two, norm_gain[1], norm_bias[1])
        keep = jnp.stack([keep_forward, keep_backward], axis=1)
        picks = jnp.stack([last_char, first_char], axis=1)
        char_padded, char_states = gru_call(
            gru_fwd_kernel,
            (
                jax.ShapeDtypeStruct((length, 2 * LANE), jnp.bfloat16),
                jax.ShapeDtypeStruct((2, char_total, LANE), jnp.float32),
            ),
            4,
            char_total,
        )(all_chars, gru_matrix, gru_bias, keep, picks)
        char_tokens = char_padded.reshape(length, 2, LANE)[:, :, :units_here]
        mid_all, char_all = (
            lax.all_gather(token_mid.astype(jnp.bfloat16), "tensor", axis=0, tiled=True),
            lax.all_gather(char_tokens.astype(jnp.bfloat16), "tensor", axis=2, tiled=True),
        )
        char_flat = char_all.reshape(length, model_width)
        joined = jnp.concatenate([mid_all, char_flat], axis=1)
        stacked = conv_inputs(joined, prev_ok, next_ok)
        pre_merge = jnp.dot(stacked, conv_matrix, preferred_element_type=jnp.float32)
        merged_low = gelu_exact(pre_merge).astype(jnp.bfloat16)
        merge_share = lax.psum_scatter(
            jnp.dot(merged_low, merge_matrix, preferred_element_type=jnp.float32).astype(
                jnp.bfloat16
            ),
            "tensor",
            scatter_dimension=0,
            tiled=True,
        ).astype(jnp.float32)
        char_mine = lax.dynamic_slice_in_dim(char_flat, row_start, shard_len, 0).astype(jnp.float32)
        residual_three = token_mid + merge_share[:, :model_width]
        residual_four = char_mine + merge_share[:, model_width:]
        token_final, pull_three = jax.vjp(layer_norm, residual_three, norm_gain[2], norm_bias[2])
        char_final, pull_four = jax.vjp(layer_norm, residual_four, norm_gain[3], norm_bias[3])
        token_outs.append(token_final.astype(jnp.bfloat16))
        char_outs.append(char_final.astype(jnp.bfloat16))
        grad_res3, grad_g3, grad_b3 = pull_three(token_cot[micro_index])
        grad_res4, grad_g4, grad_b4 = pull_four(char_cot[micro_index])
        branch_grad = jnp.concatenate([grad_res3, grad_res4], axis=1).astype(jnp.bfloat16)
        branch_all = lax.all_gather(branch_grad, "tensor", axis=0, tiled=True)
        grad_merge_w = inner_rows(merged_low, branch_all)
        grad_merged = times_transposed(branch_all, merge_matrix)
        unused_merge, pull_merge = jax.vjp(gelu_exact, pre_merge)
        grad_pre_merge = pull_merge(grad_merged)[0].astype(jnp.bfloat16)
        grad_conv_w = inner_rows(stacked, grad_pre_merge)
        grad_joined = conv_back(times_transposed(grad_pre_merge, conv_matrix), prev_ok, next_ok)
        placed = lax.dynamic_update_slice_in_dim(
            jnp.zeros((length, model_width), jnp.float32), grad_res4, row_start, 0
        )
        grad_char_part = (grad_joined[:, model_width:] + placed).reshape(
            length, 2, units_here * group_size
        )
        grad_mid_conv, grad_char_tokens = (
            lax.psum_scatter(
                grad_joined[:, :model_width].astype(jnp.bfloat16),
                "tensor",
                scatter_dimension=0,
                tiled=True,
            ).astype(jnp.float32),
            lax.psum_scatter(
                grad_char_part.astype(jnp.bfloat16), "tensor", scatter_dimension=2, tiled=True
            ).astype(jnp.float32),
        )
        grad_mid = grad_res3 + grad_mid_conv
        unused_two, pull_two = jax.vjp(layer_norm, residual_two, norm_gain[1], norm_bias[1])
        grad_res2, grad_g2, grad_b2 = pull_two(grad_mid)
        ffn_grad_all = lax.all_gather(grad_res2.astype(jnp.bfloat16), "tensor", axis=0, tiled=True)
        grad_down_w = inner_rows(activation, ffn_grad_all)
        grad_activation = times_transposed(ffn_grad_all, w_down)
        unused_act, pull_act = jax.vjp(gelu_exact, pre_act)
        grad_pre = pull_act(grad_activation)[0].astype(jnp.bfloat16)
        grad_in_w = inner_rows(hidden_all, grad_pre)
        grad_hidden = grad_res2 + lax.psum_scatter(
            times_transposed(grad_pre, w_in).astype(jnp.bfloat16),
            "tensor",
            scatter_dimension=0,
            tiled=True,
        ).astype(jnp.float32)
        unused_one, pull_one = jax.vjp(layer_norm, residual_one, norm_gain[0], norm_bias[0])
        grad_res1, grad_g1, grad_b1 = pull_one(grad_hidden)
        attn_grad_all = lax.all_gather(grad_res1.astype(jnp.bfloat16), "tensor", axis=0, tiled=True)
        grad_out_w = inner_rows(context_low, attn_grad_all)
        grad_context = (
            times_transposed(attn_grad_all, w_out)
            .astype(jnp.bfloat16)
            .reshape(length, heads_here, HD)
        )
        query_block = queries
        same_doc = (segment[:, None] == segment[None, :])[None]
        scores = jnp.einsum(
            "qhd,khd->hqk", query_block, key_low, preferred_element_type=jnp.float32
        )
        scores = jnp.where(same_doc, scores, MASK_VALUE)
        prob_full = jnp.exp(scores - log_total)
        grad_probs = jnp.einsum(
            "qhd,khd->hqk", grad_context, value_low, preferred_element_type=jnp.float32
        )
        row_dot = jnp.sum(prob_full * grad_probs, axis=-1, keepdims=True)
        grad_scores = (prob_full * (grad_probs - row_dot)).astype(jnp.bfloat16)
        query_grads = jnp.einsum(
            "hqk,khd->qhd", grad_scores, key_low, preferred_element_type=jnp.float32
        )
        grad_keys = jnp.einsum(
            "hqk,qhd->khd", grad_scores, query_block, preferred_element_type=jnp.float32
        )
        grad_values = jnp.einsum(
            "hqk,qhd->khd",
            prob_full.astype(jnp.bfloat16),
            grad_context,
            preferred_element_type=jnp.float32,
        )
        query_grad = query_grads.astype(jnp.bfloat16) * 0.125
        grad_qkv_low = jnp.stack(
            [query_grad, grad_keys.astype(jnp.bfloat16), grad_values.astype(jnp.bfloat16)], axis=1
        ).reshape(length, 3 * head_cols)
        grad_qkv_w = inner_rows(all_tokens, grad_qkv_low)
        token_part = times_transposed(grad_qkv_low, qkv_matrix)
        grad_tok_pad = jnp.pad(
            grad_char_tokens.astype(jnp.bfloat16), ((0, 0), (0, 0), (0, LANE - units_here))
        ).reshape(length, 2 * LANE)
        grad_proj_low, grad_gate = gru_call(
            gru_bwd_kernel,
            (
                jax.ShapeDtypeStruct((char_total, 4 * LANE), jnp.bfloat16),
                jax.ShapeDtypeStruct((1, 2 * LANE), jnp.float32),
            ),
            5,
            char_total,
        )(all_chars, gru_matrix, gru_bias, keep, picks.T, char_states, grad_tok_pad)
        grad_gate = grad_gate.reshape(2, LANE)[:, :units_here]
        grad_gru_w = jnp.swapaxes(
            inner_rows(all_chars, grad_proj_low).reshape(char_width, 2, 2, LANE)[..., :units_here],
            1,
            2,
        )
        char_part = times_transposed(grad_proj_low, gru_matrix)
        token_back, char_back = (
            lax.psum_scatter(
                token_part.astype(jnp.bfloat16), "tensor", scatter_dimension=0, tiled=True
            ).astype(jnp.float32),
            lax.psum_scatter(
                char_part.astype(jnp.bfloat16), "tensor", scatter_dimension=0, tiled=True
            ).astype(jnp.float32),
        )
        token_grads.append(grad_res1 + token_back)
        char_grads.append(char_back)
        gain_total = gain_total + jnp.stack([grad_g1, grad_g2, grad_g3, grad_g4], axis=0)
        bias_total = bias_total + jnp.stack([grad_b1, grad_b2, grad_b3, grad_b4], axis=0)
        micro_grads = (
            grad_qkv_w.reshape(model_width, 3, head_cols),
            grad_out_w,
            grad_in_w,
            grad_down_w,
            grad_gru_w,
            grad_gate,
            grad_conv_w.reshape(3, 2 * model_width, merge_here),
            grad_merge_w.reshape(merge_here, 2, model_width),
        )
        if weight_total is None:
            weight_total = micro_grads
        else:
            weight_total = jax.tree.map(jnp.add, weight_total, micro_grads)
    weight_final = reduce_weights(weight_total)
    gain_grad, bias_grad = lax.psum((gain_total, bias_total), ("dp", "tensor"))
    return (
        jnp.stack(token_outs, axis=0),
        jnp.stack(char_outs, axis=0),
        jnp.stack(token_grads, axis=0),
        jnp.stack(char_grads, axis=0),
        weight_final[0],
        weight_final[1],
        weight_final[2],
        weight_final[3],
        weight_final[4],
        weight_final[5],
        weight_final[6],
        weight_final[7],
        gain_grad,
        bias_grad,
    )


def solution(mesh):
    return jax.shard_map(
        local,
        mesh=mesh,
        in_specs=(
            P("dp", "tensor", None),
            P("dp", "tensor", None),
            P("dp", None),
            P("dp", None),
            P(None, None, "tensor"),
            P("tensor", None),
            P(None, "tensor"),
            P("tensor", None),
            P(None, None, None, "tensor"),
            P(None, "tensor"),
            P(None, None, "tensor"),
            P("tensor", None, None),
            P(),
            P(),
            P("dp", "tensor", None),
            P("dp", "tensor", None),
        ),
        out_specs=(
            P("dp", "tensor", None),
            P("dp", "tensor", None),
            P("dp", "tensor", None),
            P("dp", "tensor", None),
            P(None, None, "tensor"),
            P("tensor", None),
            P(None, "tensor"),
            P("tensor", None),
            P(None, None, None, "tensor"),
            P(None, "tensor"),
            P(None, None, "tensor"),
            P("tensor", None, None),
            P(),
            P(),
        ),
        check_vma=False,
    )
```

```python
import functools

import jax
import jax.numpy as jnp
from jax import lax
from jax.experimental import pallas as pl
from jax.experimental.pallas import tpu as pltpu
from jax.sharding import PartitionSpec as P

HD = 64


NORM_EPSILON = 1e-06
MASK_VALUE = -1e30
HIGH_PRECISION = lax.Precision.HIGHEST


def layer_norm(row_values, gain_row, shift_row):
    average = jnp.mean(row_values, axis=-1, keepdims=True)
    centered = row_values - average
    spread = jnp.mean(centered * centered, axis=-1, keepdims=True)
    return centered * lax.rsqrt(spread + NORM_EPSILON) * gain_row + shift_row


def gelu_exact(values):
    return jax.nn.gelu(values, approximate=False)


def layout(doc_sizes, char_counts, char_total):
    length = char_counts.shape[0]
    docs = doc_sizes.shape[0]
    doc_ids = jnp.arange(docs, dtype=jnp.int32)
    doc_ends = jnp.sum(
        jnp.where(doc_ids[None, :] <= doc_ids[:, None], doc_sizes[None, :], 0), axis=1
    )
    positions = jnp.arange(length, dtype=jnp.int32)
    segment = jnp.sum(
        (positions[:, None] >= doc_ends[None, :]).astype(jnp.int32), axis=1, dtype=jnp.int32
    )
    token_ends = jnp.sum(
        jnp.where(positions[None, :] <= positions[:, None], char_counts[None, :], 0), axis=1
    )
    last_char = token_ends - 1
    first_char = token_ends - char_counts
    char_ends = jnp.sum(
        jnp.where(positions[None, :] < doc_ends[:, None], char_counts[None, :], 0), axis=1
    )
    char_positions = jnp.arange(char_total, dtype=jnp.int32)
    starts = char_ends - jnp.sum(
        jnp.where(
            (positions[None, :] < doc_ends[:, None])
            & (positions[None, :] >= (doc_ends - doc_sizes)[:, None]),
            char_counts[None, :],
            0,
        ),
        axis=1,
    )
    keep_forward = 1.0 - jnp.any(char_positions[:, None] == starts[None, :], axis=1).astype(
        jnp.float32
    )
    keep_backward = 1.0 - jnp.any(
        char_positions[:, None] == (char_ends - 1)[None, :], axis=1
    ).astype(jnp.float32)
    token_starts = doc_ends - doc_sizes
    prev_ok = 1.0 - jnp.any(positions[:, None] == token_starts[None, :], axis=1).astype(
        jnp.float32
    )
    next_ok = 1.0 - jnp.any(positions[:, None] == (doc_ends - 1)[None, :], axis=1).astype(
        jnp.float32
    )
    return (segment, first_char, last_char, keep_forward, keep_backward, prev_ok, next_ok)


F32 = jnp.float32
BF16 = jnp.bfloat16
LANE = 128
CHUNKS = 32
MIB = 1024 * 1024
VMEM = pl.BlockSpec(memory_space=pltpu.VMEM)


def recur(first, second, decays, drives, outs, steps):
    ups = (first, second)

    def at(ref, tile, step):
        row = step if ups[tile] else steps - 1 - step
        return ref[tile, pl.ds(row, CHUNKS, stride=steps), :]

    def put(ref, tile, step, value):
        row = step if ups[tile] else steps - 1 - step
        ref[tile, pl.ds(row, CHUNKS, stride=steps), :] = value

    zero = jnp.zeros((CHUNKS, LANE), jnp.float32)
    one = jnp.ones((CHUNKS, LANE), jnp.float32)

    def summary(step, carry):
        new = []
        for tile in range(2):
            state, mult = carry[2 * tile], carry[2 * tile + 1]
            decay = at(decays, tile, step)
            new += [decay * state + at(drives, tile, step), decay * mult]
        return tuple(new)

    ends = lax.fori_loop(0, steps, summary, (zero, one, zero, one), unroll=4)
    starts = []
    for tile in range(2):
        final, mult = ends[2 * tile], ends[2 * tile + 1]
        order = range(CHUNKS) if ups[tile] else range(CHUNKS - 1, -1, -1)
        carry = jnp.zeros((1, LANE), jnp.float32)
        rows = [None] * CHUNKS
        for chunk in order:
            rows[chunk] = carry
            carry = mult[chunk : chunk + 1] * carry + final[chunk : chunk + 1]
        starts.append(jnp.concatenate(rows, axis=0))

    def write(step, carry):
        new = []
        for tile in range(2):
            state = at(decays, tile, step) * carry[tile] + at(drives, tile, step)
            put(outs, tile, step, state)
            new.append(state)
        return tuple(new)

    lax.fori_loop(0, steps, write, tuple(starts), unroll=4)


def gates_of(chars, w_ref, bias_ref, keep_ref, gate_ref, cand_ref, decay_ref, drive_ref):
    proj = jnp.dot(chars, w_ref[...], preferred_element_type=jnp.float32)
    for tile in range(2):
        cols = pl.ds(tile * LANE, LANE)
        logits = proj[:, tile * LANE : (tile + 1) * LANE] + bias_ref[:, cols]
        gate = jax.nn.sigmoid(logits)
        cand = proj[:, (2 + tile) * LANE : (3 + tile) * LANE]
        gate_ref[tile] = gate
        cand_ref[tile] = cand
        decay_ref[tile] = (1.0 - gate) * keep_ref[:, tile : tile + 1]
        drive_ref[tile] = gate * cand


def gru_bwd_kernel(chars_ref, w_ref, bias_ref, keep_ref, pick_ref, state_ref, grad_ref,
                   proj_grad_ref, bias_grad_ref, gate_ref, cand_ref, decay_ref, drive_ref, flow_ref):
    total = chars_ref.shape[0]
    steps = total // CHUNKS
    gates_of(chars_ref[...], w_ref, bias_ref, keep_ref, gate_ref, cand_ref, decay_ref, drive_ref)
    length = pick_ref.shape[1]
    ids = lax.broadcasted_iota(jnp.int32, (total, length), 0)
    for tile in range(2):
        hot = (ids == pick_ref[tile : tile + 1, :]).astype(jnp.bfloat16)
        cols = pl.ds(tile * LANE, LANE)
        drive_ref[tile] = jnp.dot(hot, grad_ref[:, cols], preferred_element_type=jnp.float32)
    flow_ref[0, pl.ds(0, total - 1), :] = decay_ref[0, pl.ds(1, total - 1), :]
    flow_ref[0, pl.ds(total - 1, 1), :] = jnp.zeros((1, LANE), jnp.float32)
    flow_ref[1, pl.ds(1, total - 1), :] = decay_ref[1, pl.ds(0, total - 1), :]
    flow_ref[1, pl.ds(0, 1), :] = jnp.zeros((1, LANE), jnp.float32)
    recur(False, True, flow_ref, drive_ref, decay_ref, steps)
    for tile in range(2):
        flow = decay_ref[tile] * gate_ref[tile]
        logit_grad = flow * (cand_ref[tile] - state_ref[tile])
        proj_grad_ref[:, pl.ds(tile * LANE, LANE)] = logit_grad.astype(jnp.bfloat16)
        proj_grad_ref[:, pl.ds((2 + tile) * LANE, LANE)] = flow.astype(jnp.bfloat16)
        bias_grad_ref[:, pl.ds(tile * LANE, LANE)] = jnp.sum(logit_grad, axis=0, keepdims=True)


def gru_call(kernel, outs, scratch_count, total):
    return pl.pallas_call(
        kernel,
        out_shape=outs,
        scratch_shapes=[pltpu.VMEM((2, total, LANE), jnp.float32)] * scratch_count,
        compiler_params=pltpu.CompilerParams(vmem_limit_bytes=48 * 1024 * 1024),
    )


def gru_weights(w_gru, gate_bias):
    width, _, _, units = w_gru.shape
    matrix = jnp.pad(jnp.swapaxes(w_gru, 1, 2), ((0, 0), (0, 0), (0, 0), (0, LANE - units)))
    bias = jnp.pad(gate_bias, ((0, 0), (0, LANE - units)))
    return matrix.reshape(width, 4 * LANE), bias.reshape(1, 2 * LANE)


def conv_inputs(joined, prev_ok, next_ok):
    zero_row = jnp.zeros((1, joined.shape[1]), joined.dtype)
    preceding = jnp.concatenate([zero_row, joined[:-1]], axis=0) * prev_ok[:, None].astype(
        joined.dtype
    )
    following = jnp.concatenate([joined[1:], zero_row], axis=0) * next_ok[:, None].astype(
        joined.dtype
    )
    return jnp.concatenate([preceding, joined, following], axis=1)


def conv_back(grad_stacked, prev_ok, next_ok):
    column_count = grad_stacked.shape[1] // 3
    from_prev = grad_stacked[:, :column_count] * prev_ok[:, None]
    from_next = grad_stacked[:, 2 * column_count :] * next_ok[:, None]
    zero_row = jnp.zeros((1, column_count), jnp.float32)
    middle = grad_stacked[:, column_count : 2 * column_count]
    return (
        middle
        + jnp.concatenate([from_prev[1:], zero_row], axis=0)
        + jnp.concatenate([zero_row, from_next[:-1]], axis=0)
    )


def inner_rows(left_rows, right_rows):
    return lax.dot_general(
        left_rows, right_rows, (((0,), (0,)), ((), ())), preferred_element_type=jnp.float32
    )


def times_transposed(left_rows, right_matrix):
    return lax.dot_general(
        left_rows, right_matrix, (((1,), (1,)), ((), ())), preferred_element_type=jnp.float32
    )


def nn(left, right):
    return jnp.dot(left, right, preferred_element_type=F32)


def nt(left, right):
    return lax.dot_general(left, right, (((1,), (1,)), ((), ())), preferred_element_type=F32)


def tn(left, right):
    return lax.dot_general(left, right, (((0,), (0,)), ((), ())), preferred_element_type=F32)


def gelu_pair(values):
    cdf = 0.5 * (1.0 + lax.erf(values * 0.7071067811865476))
    density = 0.3989422804014327 * jnp.exp(-0.5 * values * values)
    return values * cdf, cdf + values * density


def normalize(rows):
    centered = rows - jnp.mean(rows, axis=-1, keepdims=True)
    scale = lax.rsqrt(jnp.mean(centered * centered, axis=-1, keepdims=True) + NORM_EPSILON)
    return centered * scale, scale


def normalize_back(unit, scale, grad_unit):
    return scale * (
        grad_unit
        - jnp.mean(grad_unit, axis=-1, keepdims=True)
        - unit * jnp.mean(grad_unit * unit, axis=-1, keepdims=True)
    )


class Group:
    def __init__(self, send, recv, seqs):
        self.me = lax.axis_index("tensor")
        self.low = self.me % 2
        self.high = self.me // 2
        self.pair = self.high * 2 + (1 - self.low)
        self.far = (1 - self.high) * 2 + self.low
        self.send, self.recv, self.seqs, self.used = send, recv, seqs, 0

    def block(self, turn):
        left = 3 - turn
        return ((self.high + left // 2) % 2) * 2 + (self.low + left % 2) % 2

    def slots(self, count):
        first = self.used
        self.used += count
        return [first + i for i in range(count)]

    def copy(self, slot, seq, source, target, peer):
        index = slot * self.seqs + seq
        return pltpu.make_async_remote_copy(
            src_ref=source,
            dst_ref=target,
            send_sem=self.send.at[index],
            recv_sem=self.recv.at[index],
            device_id={"tensor": peer},
            device_id_type=pl.DeviceIdType.MESH,
        )

    def greet(self):
        barrier = pltpu.get_barrier_semaphore()
        for peer in (self.pair, self.far):
            pl.semaphore_signal(
                barrier, inc=1, device_id={"tensor": peer}, device_id_type=pl.DeviceIdType.MESH
            )
        pl.semaphore_wait(barrier, 2)


class Gather:
    def __init__(self, group, buf, source=None):
        self.group, self.buf, self.source = group, buf, source
        self.near, self.over, self.fwd = group.slots(3)

    def own(self, seq):
        return self.buf.at[seq, self.group.me] if self.source is None else self.source.at[seq]

    def near_copy(self, seq):
        g = self.group
        return g.copy(self.near, seq, self.own(seq), self.buf.at[seq, g.me], g.pair)

    def over_copy(self, seq):
        g = self.group
        return g.copy(self.over, seq, self.own(seq), self.buf.at[seq, g.me], g.far)

    def fwd_copy(self, seq):
        g = self.group
        other = self.buf.at[seq, g.far]
        return g.copy(self.fwd, seq, other, other, g.pair)

    def start(self, seq):
        self.over_copy(seq).start()
        self.near_copy(seq).start()

    def forward(self, seq):
        self.over_copy(seq).wait_recv()
        self.fwd_copy(seq).start()

    def finish(self, seq):
        near = self.near_copy(seq)
        fwd = self.fwd_copy(seq)
        near.wait_recv()
        fwd.wait_recv()
        near.wait_send()
        self.over_copy(seq).wait_send()
        fwd.wait_send()


class Scatter:
    def __init__(self, group, stage, got, own, temp):
        self.group, self.stage, self.got, self.held, self.temp = group, stage, got, own, temp
        self.names = group.slots(3)

    def copies(self, seq):
        g = self.group
        peers = (g.pair, g.pair, g.far)
        return [
            g.copy(self.names[i], seq, self.stage(seq, i), self.got(seq, i), peers[i])
            for i in range(3)
        ]

    def start(self, seq, part):
        mine, other, over = self.copies(seq)

        def turn(step, carry):
            self.temp[...] = part(self.group.block(step))

            @pl.when(step == 0)
            def _():
                self.stage(seq, 1)[...] = self.temp[...].astype(BF16)
                other.start()

            @pl.when(step == 1)
            def _():
                other.wait_recv()
                self.stage(seq, 2)[...] = (self.temp[...] + self.got(seq, 1)[...]).astype(BF16)
                over.start()

            @pl.when(step == 2)
            def _():
                self.stage(seq, 0)[...] = self.temp[...].astype(BF16)
                mine.start()

            @pl.when(step == 3)
            def _():
                self.held(seq)[...] = self.temp[...]

            return carry

        lax.fori_loop(0, 4, turn, 0)

    def finish(self, seq):
        mine, other, over = self.copies(seq)
        mine.wait_recv()
        over.wait_recv()
        total = self.held(seq)[...] + self.got(seq, 0)[...] + self.got(seq, 2)[...]
        mine.wait_send()
        other.wait_send()
        over.wait_send()
        return total


def recur_plain(ups, decays, drives, outs, steps):
    def rows(tile, step):
        row = step if ups[tile] else steps - 1 - step
        return pl.ds(row, CHUNKS, stride=steps)

    zero = jnp.zeros((CHUNKS, LANE), F32)
    one = jnp.ones((CHUNKS, LANE), F32)

    def summary(step, carry):
        new = []
        for tile in range(2):
            state, mult = carry[2 * tile], carry[2 * tile + 1]
            decay = decays[tile, rows(tile, step), :]
            new += [decay * state + drives[tile, rows(tile, step), :], decay * mult]
        return tuple(new)

    ends = lax.fori_loop(0, steps, summary, (zero, one, zero, one), unroll=4)
    starts = []
    for tile in range(2):
        final, mult = ends[2 * tile], ends[2 * tile + 1]
        order = range(CHUNKS) if ups[tile] else range(CHUNKS - 1, -1, -1)
        carry = jnp.zeros((1, LANE), F32)
        heads = [None] * CHUNKS
        for chunk in order:
            heads[chunk] = carry
            carry = mult[chunk : chunk + 1] * carry + final[chunk : chunk + 1]
        starts.append(jnp.concatenate(heads, axis=0))

    def write(step, carry):
        new = []
        for tile in range(2):
            here = rows(tile, step)
            state = decays[tile, here, :] * carry[tile] + drives[tile, here, :]
            outs[tile, here, :] = state
            new.append(state)
        return tuple(new)

    lax.fori_loop(0, steps, write, tuple(starts), unroll=4)


def forward_kernel(
    units, tokens, chars, wq, wout, win, wdown, wg, gate_bias, wc, wm, gain, bias, cot_t, cot_c,
    segc, segr, pickc, keep, edges,
    token_out, char_out, o_x, o_c, o_qkv, o_p, o_ctx, o_h, o_act, o_dact, o_mid, o_st, o_mg,
    o_dmg, o_states, o_unit0, o_unit1, o_scale, o_res3, o_branch, norm_grads,
    x, c, qkv, p, ctx, h, act, dact, mid, st, mg, dmg, states, unit0, unit1, scale, res3, branch,
    hidden, middle, outs_t, outs_c, decay, drive, taps, perm,
    stage, got, held, temp, send, recv, local,
):
    seqs, length = tokens.shape[0], segr.shape[2]
    shard, width = tokens.shape[1], tokens.shape[2]
    block_chars = chars.shape[1]
    heads = p.shape[1]
    g = Group(send, recv, seqs)
    me = g.me
    saves = []

    def keep_out(seq, source, target):
        saves.append((source, target, len(saves)))

    def local_copy(number, seq, source, target):
        return pltpu.make_async_copy(source, target, local.at[number * seqs + seq])

    gx, gc = Gather(g, x, tokens), Gather(g, c, chars)
    gh, gm, gs = Gather(g, h), Gather(g, mid), Gather(g, st)
    narrow = lambda ref: (lambda s, i: ref.at[s, i, :, pl.ds(0, width)])
    wide = lambda ref: (lambda s, i: ref.at[s, i])
    own_n = lambda s: held.at[s, :, pl.ds(0, width)]
    own_w = lambda s: held.at[s]
    thin = temp.at[:, pl.ds(0, width)]
    s_attn = Scatter(g, narrow(stage), narrow(got), own_n, thin)
    s_ffn = Scatter(g, narrow(stage), narrow(got), own_n, thin)
    s_branch = Scatter(g, wide(stage), wide(got), own_w, temp)

    def own_x(seq):
        return local_copy(0, seq, tokens.at[seq], x.at[seq, me])

    def own_c(seq):
        return local_copy(1, seq, chars.at[seq], c.at[seq, me])

    plan = [
        (x, o_x), (c, o_c), (qkv, o_qkv), (p, o_p), (ctx, o_ctx), (h, o_h), (act, o_act),
        (dact, o_dact), (mid, o_mid), (st, o_st), (mg, o_mg), (dmg, o_dmg), (states, o_states),
        (unit0, o_unit0), (unit1, o_unit1), (scale, o_scale), (res3, o_res3), (branch, o_branch),
        (outs_t, token_out), (outs_c, char_out),
    ]

    def save(seq, *names):
        for name in names:
            for number, (source, target) in enumerate(plan):
                if source is name:
                    local_copy(2 + number, seq, source.at[seq], target.at[seq]).start()

    def each(body):
        def run(seq, carry):
            body(seq)
            return carry

        lax.fori_loop(0, seqs, run, 0)

    each(lambda s: (own_x(s).start(), own_c(s).start()))
    g.greet()
    each(gx.start)
    each(gc.start)

    for t in range(4):
        for d in range(2):
            row = lax.broadcasted_iota(jnp.int32, (LANE, width), 0)
            col = lax.broadcasted_iota(jnp.int32, (LANE, width), 1)
            first = d * 4 * units + t * units
            hit = (col - first == row) & (row < units)
            perm[pl.ds((2 * t + d) * LANE, LANE), :] = hit.astype(F32).astype(BF16)
    taps[...] = jnp.zeros_like(taps)
    norm_grads[...] = jnp.zeros_like(norm_grads)

    lane = lax.broadcasted_iota(jnp.int32, (shard, LANE), 1)
    left = lane < HD

    def attention(s):
        gx.forward(s)
        gx.finish(s)
        own_x(s).wait()
        save(s, x)

        def project(t, carry):
            rows = pl.ds(pl.multiple_of(t * shard, shard), shard)
            out = nn(x[s, t], wq[...])
            cols = qkv.shape[3]
            qkv[s, 0, rows, :] = (out[:, :cols] * 0.125).astype(BF16)
            qkv[s, 1, rows, :] = out[:, cols : 2 * cols].astype(BF16)
            qkv[s, 2, rows, :] = out[:, 2 * cols :].astype(BF16)
            return carry

        lax.fori_loop(0, 4, project, 0)
        save(s, qkv)

        def part(b):
            rows = pl.ds(pl.multiple_of(b * shard, shard), shard)
            same = segc[s, rows, :] == segr[s]
            for tile in range(qkv.shape[3] // LANE):
                cols = pl.ds(tile * LANE, LANE)
                result = None
                for half in range(2):
                    head = 2 * tile + half
                    if head >= heads:
                        continue
                    query = qkv[s, 0, rows, cols]
                    if 2 * tile + 1 < heads:
                        query = jnp.where(left if half == 0 else ~left, query, jnp.zeros_like(query))
                    scores = jnp.where(same, nt(query, qkv[s, 1, :, cols]), MASK_VALUE)
                    power = jnp.exp(scores - jnp.max(scores, axis=-1, keepdims=True))
                    probs = (power * (1.0 / jnp.sum(power, axis=-1, keepdims=True))).astype(BF16)
                    p[s, head, rows, :] = probs
                    mixed = nn(probs, qkv[s, 2, :, cols])
                    result = mixed if result is None else jnp.where(left, result, mixed)
                ctx[s, rows, cols] = result.astype(BF16)
            return nn(ctx[s, rows, :], wout[...])

        s_attn.start(s, part)
        save(s, p, ctx)

    each(attention)

    def first_norm(s):
        total = x[s, me].astype(F32) + s_attn.finish(s)
        unit, spread = normalize(total)
        unit0[s] = unit
        scale[s, 0] = jnp.broadcast_to(spread, (shard, LANE))
        hidden[s] = unit * gain[0:1] + bias[0:1]
        h[s, me] = hidden[s].astype(BF16)
        gh.start(s)
        save(s, unit0)

    def gru(s):
        gc.forward(s)
        gc.finish(s)
        own_c(s).wait()
        save(s, c)

        def gates(t, carry):
            rows = pl.ds(pl.multiple_of(t * LANE, LANE), LANE)
            per = block_chars // LANE
            inner = pl.ds(pl.multiple_of((t % per) * LANE, LANE), LANE)
            proj = nn(c[s, t // per, inner, :], wg[...])
            for tile in range(2):
                cols = slice(tile * LANE, (tile + 1) * LANE)
                gate = jax.nn.sigmoid(proj[:, cols] + gate_bias_pad(tile))
                cand = proj[:, (2 + tile) * LANE : (3 + tile) * LANE]
                decay[tile, rows, :] = (1.0 - gate) * keep[s, rows, tile : tile + 1]
                drive[tile, rows, :] = gate * cand
            return carry

        def gate_bias_pad(tile):
            return gate_bias[:, tile * LANE : (tile + 1) * LANE]

        total = 4 * block_chars
        lax.fori_loop(0, total // LANE, gates, 0)
        recur_plain((True, False), decay, drive, states.at[s], total // CHUNKS)

        def pick(t, carry):
            rows = pl.ds(pl.multiple_of(t * shard, shard), shard)
            for tile in range(2):
                ids = lax.broadcasted_iota(jnp.int32, (shard, total), 1)
                hot = (ids == pickc[s, rows, tile : tile + 1]).astype(F32).astype(BF16)
                out = nn(hot, states[s, tile].astype(BF16))
                st[s, me, rows, pl.ds(tile * LANE, LANE)] = out.astype(BF16)
            return carry

        lax.fori_loop(0, 4, pick, 0)
        gs.start(s)
        save(s, states)

    def norm_and_gru(s):
        first_norm(s)
        gru(s)

    each(norm_and_gru)

    def ffn(s):
        gh.forward(s)
        gh.finish(s)
        save(s, h)

        def part(b):
            value, slope = gelu_pair(nn(h[s, b], win[...]))
            act[s, b] = value.astype(BF16)
            dact[s, b] = slope.astype(BF16)
            return nn(act[s, b], wdown[...])

        s_ffn.start(s, part)
        save(s, act, dact)

    each(ffn)

    def second_norm(s):
        unit, spread = normalize(hidden[s] + s_ffn.finish(s))
        unit1[s] = unit
        scale[s, 1] = jnp.broadcast_to(spread, (shard, LANE))
        middle[s] = unit * gain[1:2] + bias[1:2]
        mid[s, me] = middle[s].astype(BF16)
        gm.start(s)
        save(s, unit1, scale)

    each(second_norm)

    def merge(s):
        gs.forward(s)
        gm.forward(s)
        gs.finish(s)
        gm.finish(s)
        save(s, mid, st)
        cols = mg.shape[2]

        def mix(t, carry):
            rows = pl.ds(pl.multiple_of(t * shard, shard), shard)
            total = nn(mid[s, t], wc[pl.ds(0, width), :])
            for u in range(4):
                weights = wc[pl.ds(width + u * 2 * LANE, 2 * LANE), :]
                total = total + nn(st[s, u, rows, :], weights)
            taps[pl.ds(pl.multiple_of(8 + t * shard, 8), shard), :] = total
            return carry

        lax.fori_loop(0, 4, mix, 0)

        def shifted(t, carry):
            rows = pl.ds(pl.multiple_of(t * shard, shard), shard)
            window = taps[pl.ds(pl.multiple_of(t * shard, 8), shard + 16), :]
            before = window[7 : 7 + shard, :cols] * edges[s, rows, 0:1]
            after = window[9 : 9 + shard, 2 * cols :] * edges[s, rows, 1:2]
            value, slope = gelu_pair(before + window[8 : 8 + shard, cols : 2 * cols] + after)
            mg[s, rows, :] = value.astype(BF16)
            dmg[s, rows, :] = slope.astype(BF16)
            return carry

        lax.fori_loop(0, 4, shifted, 0)

        def part(b):
            rows = pl.ds(pl.multiple_of(b * shard, shard), shard)
            return nn(mg[s, rows, :], wm[...])

        s_branch.start(s, part)
        save(s, mg, dmg)

    each(merge)

    def last_norms(s):
        total = s_branch.finish(s)
        rows = pl.ds(pl.multiple_of(me * shard, shard), shard)
        unit, spread = normalize(middle[s] + total[:, :width])
        outs_t[s] = (unit * gain[2:3] + bias[2:3]).astype(BF16)
        cot = cot_t[s]
        norm_grads[0:1] += jnp.sum(cot * unit, axis=0, keepdims=True)
        norm_grads[2:3] += jnp.sum(cot, axis=0, keepdims=True)
        back = normalize_back(unit, spread, cot * gain[2:3])
        res3[s] = back
        branch[s, :, pl.ds(0, width)] = back.astype(BF16)
        mine = total[:, width:]
        for u in range(4):
            mine = mine + nn(st[s, u, rows, :], perm[pl.ds(u * 2 * LANE, 2 * LANE), :])
        unit, spread = normalize(mine)
        outs_c[s] = (unit * gain[3:4] + bias[3:4]).astype(BF16)
        cot = cot_c[s]
        norm_grads[1:2] += jnp.sum(cot * unit, axis=0, keepdims=True)
        norm_grads[3:4] += jnp.sum(cot, axis=0, keepdims=True)
        branch[s, :, pl.ds(width, width)] = normalize_back(unit, spread, cot * gain[3:4]).astype(
            BF16
        )
        save(s, outs_t, outs_c, res3, branch)

    each(last_norms)

    def drain(s):
        for number, (source, target) in enumerate(plan):
            local_copy(2 + number, s, source.at[s], target.at[s]).wait()

    each(drain)


def forward_call(tokens, chars, weights, small, group_slots=27):
    seqs, shard, width = tokens.shape
    length, block_chars = shard * 4, chars.shape[1]
    total = block_chars * 4
    wq, wout, win, wdown, wg, gate_bias, wc, wm = weights
    cols = wq.shape[1] // 3
    heads = small["heads"]
    sds = jax.ShapeDtypeStruct
    big = {
        "x": ((seqs, 4, shard, width), BF16),
        "c": ((seqs, 4, block_chars, chars.shape[2]), BF16),
        "qkv": ((seqs, 3, length, cols), BF16),
        "p": ((seqs, heads, length, length), BF16),
        "ctx": ((seqs, length, cols), BF16),
        "h": ((seqs, 4, shard, width), BF16),
        "act": ((seqs, 4, shard, win.shape[1]), BF16),
        "dact": ((seqs, 4, shard, win.shape[1]), BF16),
        "mid": ((seqs, 4, shard, width), BF16),
        "st": ((seqs, 4, length, 2 * LANE), BF16),
        "mg": ((seqs, length, wm.shape[0]), BF16),
        "dmg": ((seqs, length, wm.shape[0]), BF16),
        "states": ((seqs, 2, total, LANE), F32),
        "unit0": ((seqs, shard, width), F32),
        "unit1": ((seqs, shard, width), F32),
        "scale": ((seqs, 2, shard, LANE), F32),
        "res3": ((seqs, shard, width), F32),
        "branch": ((seqs, shard, 2 * width), BF16),
    }
    rows = ((seqs, shard, width), F32)
    low_rows = ((seqs, shard, width), BF16)
    scratch = list(big.values()) + [
        rows, rows, low_rows, low_rows,
        ((2, total, LANE), F32), ((2, total, LANE), F32),
        ((length + 16, 3 * wm.shape[0]), F32),
        ((8 * LANE, width), BF16),
        ((seqs, 3, shard, 2 * width), BF16), ((seqs, 3, shard, 2 * width), BF16),
        ((seqs, shard, 2 * width), F32), ((shard, 2 * width), F32),
    ]
    anyspace = pl.BlockSpec(memory_space=pl.ANY)
    vmem = pl.BlockSpec(memory_space=pltpu.VMEM)
    out_shapes = [sds(low_rows[0], BF16)] * 2 + [sds(*v) for v in big.values()]
    ins = (
        tokens, chars, wq, wout, win, wdown, wg, gate_bias, wc, wm, small["gain"], small["bias"],
        small["cot_t"], small["cot_c"], small["segc"], small["segr"], small["pickc"],
        small["keep"], small["edges"],
    )
    outs = pl.pallas_call(
        functools.partial(forward_kernel, small["units"]),
        out_shape=out_shapes + [sds((4, width), F32)],
        in_specs=[anyspace] * 2 + [vmem] * (len(ins) - 2),
        out_specs=[anyspace] * len(out_shapes) + [vmem],
        scratch_shapes=[pltpu.VMEM(*v) for v in scratch]
        + [
            pltpu.SemaphoreType.DMA((group_slots * seqs,)),
            pltpu.SemaphoreType.DMA((group_slots * seqs,)),
            pltpu.SemaphoreType.DMA((24 * seqs,)),
        ],
        compiler_params=pltpu.CompilerParams(
            collective_id=0, has_side_effects=True, vmem_limit_bytes=62 * MIB
        ),
    )(*ins)
    names = ["token_out", "char_out"] + list(big) + ["norm_grads"]
    return dict(zip(names, outs))


def reduce_weights(grads):
    low = lax.psum(tuple(g.astype(jnp.bfloat16) for g in grads), "dp")
    return tuple(g.astype(jnp.float32) for g in low)


def local(
    tokens,
    characters,
    doc_lengths,
    token_chars,
    w_qkv,
    w_out,
    w_in,
    w_down,
    w_gru,
    gate_bias,
    w_conv,
    w_merge,
    norm_gain,
    norm_bias,
    token_cot,
    char_cot,
):
    micro_count = tokens.shape[0]
    shard_len = tokens.shape[1]
    model_width = tokens.shape[2]
    char_width = characters.shape[2]
    group_size = lax.axis_size("tensor")
    group_rank = lax.axis_index("tensor")
    length = shard_len * group_size
    char_total = characters.shape[1] * group_size
    head_cols = w_qkv.shape[2]
    heads_here = head_cols // HD
    units_here = w_gru.shape[3]
    merge_here = w_conv.shape[2]
    row_start = group_rank * shard_len
    qkv_matrix = w_qkv.reshape(model_width, 3 * head_cols)
    gru_matrix, gru_bias = gru_weights(w_gru, gate_bias)
    conv_matrix = w_conv.reshape(3 * 2 * model_width, merge_here)
    merge_matrix = w_merge.reshape(merge_here, 2 * model_width)
    spare = -head_cols % LANE
    wq = jnp.pad(w_qkv, ((0, 0), (0, 0), (0, spare))).reshape(model_width, -1)
    wout = jnp.pad(w_out, ((0, spare), (0, 0)))
    more = -merge_here % LANE
    wm = jnp.pad(merge_matrix, ((0, more), (0, 0)))
    conv_pad = jnp.pad(w_conv, ((0, 0), (0, 0), (0, more)))
    conv_mid = jnp.swapaxes(conv_pad[:, :model_width], 0, 1).reshape(model_width, -1)
    conv_char = conv_pad[:, model_width:].reshape(3, 2, group_size, units_here, -1)
    conv_char = jnp.pad(conv_char, ((0, 0),) * 3 + ((0, LANE - units_here), (0, 0)))
    conv_char = conv_char.transpose(2, 1, 3, 0, 4).reshape(group_size * 2 * LANE, -1)
    wc = jnp.concatenate([conv_mid, conv_char], axis=0)
    layouts = [layout(doc_lengths[i], token_chars[i], char_total) for i in range(micro_count)]
    stacked_layout = [jnp.stack(parts) for parts in zip(*layouts)]
    segment, first_char, last_char, keep_forward, keep_backward, prev_ok, next_ok = stacked_layout
    keep = jnp.stack([keep_forward, keep_backward], axis=2)
    picks = jnp.stack([last_char, first_char], axis=2)
    small = dict(
        gain=norm_gain, bias=norm_bias, cot_t=token_cot, cot_c=char_cot,
        segc=segment[:, :, None], segr=segment[:, None, :], pickc=picks, keep=keep,
        edges=jnp.stack([prev_ok, next_ok], axis=2), heads=heads_here, units=units_here,
    )
    fw = forward_call(
        tokens, characters, (wq, wout, w_in, w_down, gru_matrix, gru_bias, wc, wm), small
    )
    token_grads = []
    char_grads = []
    weight_total = None
    gain_total = jnp.zeros((4, model_width), jnp.float32).at[2:].set(fw["norm_grads"][:2])
    bias_total = jnp.zeros((4, model_width), jnp.float32).at[2:].set(fw["norm_grads"][2:])
    for i in range(micro_count):
        all_tokens = fw["x"][i].reshape(length, model_width)
        all_chars = fw["c"][i].reshape(char_total, char_width)
        hidden_all = fw["h"][i].reshape(length, model_width)
        activation = fw["act"][i].reshape(length, -1)
        queries, key_low, value_low = [
            fw["qkv"][i, k, :, :head_cols].reshape(length, heads_here, HD) for k in range(3)
        ]
        context_low = fw["ctx"][i, :, :head_cols]
        merged_low = fw["mg"][i, :, :merge_here]
        char_flat = (
            fw["st"][i].reshape(group_size, length, 2, LANE)[..., :units_here]
            .transpose(1, 2, 0, 3).reshape(length, model_width)
        )
        mid_all = fw["mid"][i].reshape(length, model_width)
        joined = jnp.concatenate([mid_all, char_flat], axis=1)
        stacked = conv_inputs(joined, prev_ok[i], next_ok[i])
        branch_grad = fw["branch"][i]
        grad_res3 = fw["res3"][i]
        grad_res4 = branch_grad[:, model_width:].astype(F32)
        branch_all = lax.all_gather(branch_grad, "tensor", axis=0, tiled=True)
        grad_merge_w = inner_rows(merged_low, branch_all)
        grad_merged = times_transposed(branch_all, merge_matrix)
        grad_pre_merge = (grad_merged * fw["dmg"][i, :, :merge_here]).astype(BF16)
        grad_conv_w = inner_rows(stacked, grad_pre_merge)
        grad_joined = conv_back(
            times_transposed(grad_pre_merge, conv_matrix), prev_ok[i], next_ok[i]
        )
        placed = lax.dynamic_update_slice_in_dim(
            jnp.zeros((length, model_width), F32), grad_res4, row_start, 0
        )
        grad_char_part = (grad_joined[:, model_width:] + placed).reshape(
            length, 2, units_here * group_size
        )
        scatter = lambda part, dim: lax.psum_scatter(
            part.astype(BF16), "tensor", scatter_dimension=dim, tiled=True
        ).astype(F32)
        grad_mid = grad_res3 + scatter(grad_joined[:, :model_width], 0)
        grad_char_tokens = scatter(grad_char_part, 2)

        def norm_grad(k, unit, spread, cot):
            back = normalize_back(unit, spread, cot * norm_gain[k])
            return back, jnp.sum(cot * unit, axis=0), jnp.sum(cot, axis=0)

        grad_res2, grad_g2, grad_b2 = norm_grad(
            1, fw["unit1"][i], fw["scale"][i, 1, :, :1], grad_mid
        )
        ffn_grad_all = lax.all_gather(grad_res2.astype(BF16), "tensor", axis=0, tiled=True)
        grad_down_w = inner_rows(activation, ffn_grad_all)
        slope = fw["dact"][i].reshape(length, -1)
        grad_pre = (times_transposed(ffn_grad_all, w_down) * slope).astype(BF16)
        grad_in_w = inner_rows(hidden_all, grad_pre)
        grad_hidden = grad_res2 + scatter(times_transposed(grad_pre, w_in), 0)
        grad_res1, grad_g1, grad_b1 = norm_grad(
            0, fw["unit0"][i], fw["scale"][i, 0, :, :1], grad_hidden
        )
        attn_grad_all = lax.all_gather(grad_res1.astype(BF16), "tensor", axis=0, tiled=True)
        grad_out_w = inner_rows(context_low, attn_grad_all)
        grad_context = (
            times_transposed(attn_grad_all, w_out).astype(BF16).reshape(length, heads_here, HD)
        )
        prob = fw["p"][i]
        grad_probs = jnp.einsum(
            "qhd,khd->hqk", grad_context, value_low, preferred_element_type=F32
        )
        prob_full = prob.astype(F32)
        row_dot = jnp.sum(prob_full * grad_probs, axis=-1, keepdims=True)
        grad_scores = (prob_full * (grad_probs - row_dot)).astype(BF16)
        query_grads = jnp.einsum(
            "hqk,khd->qhd", grad_scores, key_low, preferred_element_type=F32
        )
        grad_keys = jnp.einsum("hqk,qhd->khd", grad_scores, queries, preferred_element_type=F32)
        grad_values = jnp.einsum("hqk,qhd->khd", prob, grad_context, preferred_element_type=F32)
        grad_qkv_low = jnp.stack(
            [query_grads.astype(BF16) * 0.125, grad_keys.astype(BF16), grad_values.astype(BF16)],
            axis=1,
        ).reshape(length, 3 * head_cols)
        grad_qkv_w = inner_rows(all_tokens, grad_qkv_low)
        token_part = times_transposed(grad_qkv_low, qkv_matrix)
        grad_tok_pad = jnp.pad(
            grad_char_tokens.astype(BF16), ((0, 0), (0, 0), (0, LANE - units_here))
        ).reshape(length, 2 * LANE)
        grad_proj_low, grad_gate = gru_call(
            gru_bwd_kernel,
            (
                jax.ShapeDtypeStruct((char_total, 4 * LANE), BF16),
                jax.ShapeDtypeStruct((1, 2 * LANE), F32),
            ),
            5,
            char_total,
        )(all_chars, gru_matrix, gru_bias, keep[i], picks[i].T, fw["states"][i], grad_tok_pad)
        grad_gate = grad_gate.reshape(2, LANE)[:, :units_here]
        grad_gru_w = jnp.swapaxes(
            inner_rows(all_chars, grad_proj_low).reshape(char_width, 2, 2, LANE)[
                ..., :units_here
            ],
            1,
            2,
        )
        char_part = times_transposed(grad_proj_low, gru_matrix)
        token_grads.append(grad_res1 + scatter(token_part, 0))
        char_grads.append(scatter(char_part, 0))
        gain_total = gain_total.at[:2].add(jnp.stack([grad_g1, grad_g2]))
        bias_total = bias_total.at[:2].add(jnp.stack([grad_b1, grad_b2]))
        micro_grads = (
            grad_qkv_w.reshape(model_width, 3, head_cols),
            grad_out_w,
            grad_in_w,
            grad_down_w,
            grad_gru_w,
            grad_gate,
            grad_conv_w.reshape(3, 2 * model_width, merge_here),
            grad_merge_w.reshape(merge_here, 2, model_width),
        )
        if weight_total is None:
            weight_total = micro_grads
        else:
            weight_total = jax.tree.map(jnp.add, weight_total, micro_grads)
    weight_final = reduce_weights(weight_total)
    gain_grad, bias_grad = lax.psum((gain_total, bias_total), ("dp", "tensor"))
    return (
        fw["token_out"],
        fw["char_out"],
        jnp.stack(token_grads, axis=0),
        jnp.stack(char_grads, axis=0),
        weight_final[0],
        weight_final[1],
        weight_final[2],
        weight_final[3],
        weight_final[4],
        weight_final[5],
        weight_final[6],
        weight_final[7],
        gain_grad,
        bias_grad,
    )


def solution(mesh):
    return jax.shard_map(
        local,
        mesh=mesh,
        in_specs=(
            P("dp", "tensor", None),
            P("dp", "tensor", None),
            P("dp", None),
            P("dp", None),
            P(None, None, "tensor"),
            P("tensor", None),
            P(None, "tensor"),
            P("tensor", None),
            P(None, None, None, "tensor"),
            P(None, "tensor"),
            P(None, None, "tensor"),
            P("tensor", None, None),
            P(),
            P(),
            P("dp", "tensor", None),
            P("dp", "tensor", None),
        ),
        out_specs=(
            P("dp", "tensor", None),
            P("dp", "tensor", None),
            P("dp", "tensor", None),
            P("dp", "tensor", None),
            P(None, None, "tensor"),
            P("tensor", None),
            P(None, "tensor"),
            P("tensor", None),
            P(None, None, None, "tensor"),
            P(None, "tensor"),
            P(None, None, "tensor"),
            P("tensor", None, None),
            P(),
            P(),
        ),
        check_vma=False,
    )
```

```python
import functools

import jax
import jax.numpy as jnp
from jax import lax
from jax.experimental import pallas as pl
from jax.experimental.pallas import tpu as pltpu
from jax.sharding import PartitionSpec as P

HD = 64


NORM_EPSILON = 1e-06
MASK_VALUE = -1e30
HIGH_PRECISION = lax.Precision.HIGHEST


def layout(doc_sizes, char_counts, char_total):
    length = char_counts.shape[0]
    docs = doc_sizes.shape[0]
    doc_ids = jnp.arange(docs, dtype=jnp.int32)
    doc_ends = jnp.sum(
        jnp.where(doc_ids[None, :] <= doc_ids[:, None], doc_sizes[None, :], 0), axis=1
    )
    positions = jnp.arange(length, dtype=jnp.int32)
    segment = jnp.sum(
        (positions[:, None] >= doc_ends[None, :]).astype(jnp.int32), axis=1, dtype=jnp.int32
    )
    token_ends = jnp.sum(
        jnp.where(positions[None, :] <= positions[:, None], char_counts[None, :], 0), axis=1
    )
    last_char = token_ends - 1
    first_char = token_ends - char_counts
    char_ends = jnp.sum(
        jnp.where(positions[None, :] < doc_ends[:, None], char_counts[None, :], 0), axis=1
    )
    char_positions = jnp.arange(char_total, dtype=jnp.int32)
    starts = char_ends - jnp.sum(
        jnp.where(
            (positions[None, :] < doc_ends[:, None])
            & (positions[None, :] >= (doc_ends - doc_sizes)[:, None]),
            char_counts[None, :],
            0,
        ),
        axis=1,
    )
    keep_forward = 1.0 - jnp.any(char_positions[:, None] == starts[None, :], axis=1).astype(
        jnp.float32
    )
    keep_backward = 1.0 - jnp.any(
        char_positions[:, None] == (char_ends - 1)[None, :], axis=1
    ).astype(jnp.float32)
    token_starts = doc_ends - doc_sizes
    prev_ok = 1.0 - jnp.any(positions[:, None] == token_starts[None, :], axis=1).astype(
        jnp.float32
    )
    next_ok = 1.0 - jnp.any(positions[:, None] == (doc_ends - 1)[None, :], axis=1).astype(
        jnp.float32
    )
    return (segment, first_char, last_char, keep_forward, keep_backward, prev_ok, next_ok)


F32 = jnp.float32
BF16 = jnp.bfloat16
LANE = 128
CHUNKS = 32
MIB = 1024 * 1024
VMEM = pl.BlockSpec(memory_space=pltpu.VMEM)


def gru_weights(w_gru, gate_bias):
    width, _, _, units = w_gru.shape
    matrix = jnp.pad(jnp.swapaxes(w_gru, 1, 2), ((0, 0), (0, 0), (0, 0), (0, LANE - units)))
    bias = jnp.pad(gate_bias, ((0, 0), (0, LANE - units)))
    return matrix.reshape(width, 4 * LANE), bias.reshape(1, 2 * LANE)


def nn(left, right):
    return jnp.dot(left, right, preferred_element_type=F32)


def nt(left, right):
    return lax.dot_general(left, right, (((1,), (1,)), ((), ())), preferred_element_type=F32)


def tn(left, right):
    return lax.dot_general(left, right, (((0,), (0,)), ((), ())), preferred_element_type=F32)


def gelu_pair(values):
    cdf = 0.5 * (1.0 + lax.erf(values * 0.7071067811865476))
    density = 0.3989422804014327 * jnp.exp(-0.5 * values * values)
    return values * cdf, cdf + values * density


def normalize(rows):
    centered = rows - jnp.mean(rows, axis=-1, keepdims=True)
    scale = lax.rsqrt(jnp.mean(centered * centered, axis=-1, keepdims=True) + NORM_EPSILON)
    return centered * scale, scale


def normalize_back(unit, scale, grad_unit):
    return scale * (
        grad_unit
        - jnp.mean(grad_unit, axis=-1, keepdims=True)
        - unit * jnp.mean(grad_unit * unit, axis=-1, keepdims=True)
    )


def roll_lanes(value, shift):
    return pltpu.roll(value, shift % value.shape[1], axis=1)


def unpack3(packed, size):
    room = -(-size // LANE) * LANE
    lane = lax.broadcasted_iota(jnp.int32, (packed.shape[0], room), 1)
    parts = []
    for k in range(3):
        first = k * size // LANE * LANE
        inner = k * size - first
        part = packed[:, first : min(first + room + LANE, packed.shape[1])]
        if inner:
            part = roll_lanes(part, -inner)
        parts.append(jnp.where(lane < size, part[:, :room], 0.0))
    return parts


def pack3(parts, size):
    room = parts[0].shape[1]
    columns = -(-3 * size // LANE) * LANE
    tiles = [None] * (columns // LANE)
    for k in range(3):
        first, inner = divmod(k * size, LANE)
        part = parts[k]
        if inner:
            part = jnp.concatenate([part, jnp.zeros_like(part[:, :LANE])], axis=1)
            part = roll_lanes(part, inner)
        for j in range(part.shape[1] // LANE):
            if first + j < len(tiles) and (first + j) * LANE < (k + 1) * size:
                tile = part[:, j * LANE : (j + 1) * LANE]
                old = tiles[first + j]
                tiles[first + j] = tile if old is None else old + tile
    return jnp.concatenate(tiles, axis=1)


class Group:
    def __init__(self, send, recv, seqs):
        self.me = lax.axis_index("tensor")
        self.low = self.me % 2
        self.high = self.me // 2
        self.pair = self.high * 2 + (1 - self.low)
        self.far = (1 - self.high) * 2 + self.low
        self.send, self.recv, self.seqs, self.used = send, recv, seqs, 0

    def block(self, turn):
        left = 3 - turn
        return ((self.high + left // 2) % 2) * 2 + (self.low + left % 2) % 2

    def slots(self, count):
        first = self.used
        self.used += count
        return [first + i for i in range(count)]

    def copy(self, slot, seq, source, target, peer):
        index = slot * self.seqs + seq
        return pltpu.make_async_remote_copy(
            src_ref=source,
            dst_ref=target,
            send_sem=self.send.at[index],
            recv_sem=self.recv.at[index],
            device_id={"tensor": peer},
            device_id_type=pl.DeviceIdType.MESH,
        )

    def greet(self):
        barrier = pltpu.get_barrier_semaphore()
        for peer in (self.pair, self.far):
            pl.semaphore_signal(
                barrier, inc=1, device_id={"tensor": peer}, device_id_type=pl.DeviceIdType.MESH
            )
        pl.semaphore_wait(barrier, 2)


class Gather:
    def __init__(self, group, buf, source=None, place=None):
        self.group, self.source = group, source
        self.at = place or (lambda seq, t: buf.at[seq, t])
        self.near, self.over, self.fwd = group.slots(3)

    def own(self, seq):
        return self.at(seq, self.group.me) if self.source is None else self.source.at[seq]

    def near_copy(self, seq):
        g = self.group
        return g.copy(self.near, seq, self.own(seq), self.at(seq, g.me), g.pair)

    def over_copy(self, seq):
        g = self.group
        return g.copy(self.over, seq, self.own(seq), self.at(seq, g.me), g.far)

    def fwd_copy(self, seq):
        g = self.group
        other = self.at(seq, g.far)
        return g.copy(self.fwd, seq, other, other, g.pair)

    def start(self, seq):
        self.over_copy(seq).start()
        self.near_copy(seq).start()

    def forward(self, seq):
        self.over_copy(seq).wait_recv()
        self.fwd_copy(seq).start()

    def finish(self, seq):
        near = self.near_copy(seq)
        fwd = self.fwd_copy(seq)
        near.wait_recv()
        fwd.wait_recv()
        near.wait_send()
        self.over_copy(seq).wait_send()
        fwd.wait_send()


class Scatter:
    def __init__(self, group, stage, got, own, temp):
        self.group, self.stage, self.got, self.held, self.temp = group, stage, got, own, temp
        self.names = group.slots(3)

    def copies(self, seq):
        g = self.group
        peers = (g.pair, g.pair, g.far)
        return [
            g.copy(self.names[i], seq, self.stage(seq, i), self.got(seq, i), peers[i])
            for i in range(3)
        ]

    def start(self, seq, part):
        mine, other, over = self.copies(seq)

        def turn(step, carry):
            part(self.group.block(step), self.temp)

            @pl.when(step == 0)
            def _():
                self.stage(seq, 1)[...] = self.temp[...].astype(BF16)
                other.start()

            @pl.when(step == 1)
            def _():
                other.wait_recv()
                self.stage(seq, 2)[...] = (self.temp[...] + self.got(seq, 1)[...]).astype(BF16)
                over.start()

            @pl.when(step == 2)
            def _():
                self.stage(seq, 0)[...] = self.temp[...].astype(BF16)
                mine.start()

            @pl.when(step == 3)
            def _():
                self.held(seq)[...] = self.temp[...]

            return carry

        lax.fori_loop(0, 4, turn, 0)

    def finish(self, seq):
        mine, other, over = self.copies(seq)
        mine.wait_recv()
        over.wait_recv()
        total = self.held(seq)[...] + self.got(seq, 0)[...] + self.got(seq, 2)[...]
        mine.wait_send()
        other.wait_send()
        over.wait_send()
        return total


def recur(ups, decays, drives, outs, steps, offsets=(0, 0)):
    def rows(tile, step, offset=0):
        row = step if ups[tile] else steps - 1 - step
        return pl.ds(row + offset, CHUNKS, stride=steps)

    zero = jnp.zeros((CHUNKS, LANE), F32)
    one = jnp.ones((CHUNKS, LANE), F32)

    def summary(step, carry):
        new = []
        for tile in range(2):
            state, mult = carry[2 * tile], carry[2 * tile + 1]
            decay = decays[tile, rows(tile, step, offsets[tile]), :]
            new += [decay * state + drives[tile, rows(tile, step), :], decay * mult]
        return tuple(new)

    ends = lax.fori_loop(0, steps, summary, (zero, one, zero, one), unroll=4)
    starts = []
    for tile in range(2):
        final, mult = ends[2 * tile], ends[2 * tile + 1]
        order = range(CHUNKS) if ups[tile] else range(CHUNKS - 1, -1, -1)
        carry = jnp.zeros((1, LANE), F32)
        heads = [None] * CHUNKS
        for chunk in order:
            heads[chunk] = carry
            carry = mult[chunk : chunk + 1] * carry + final[chunk : chunk + 1]
        starts.append(jnp.concatenate(heads, axis=0))

    def write(step, carry):
        new = []
        for tile in range(2):
            here = rows(tile, step)
            decay = decays[tile, rows(tile, step, offsets[tile]), :]
            state = decay * carry[tile] + drives[tile, here, :]
            outs[tile, here, :] = state
            new.append(state)
        return tuple(new)

    lax.fori_loop(0, steps, write, tuple(starts), unroll=4)


def forward_kernel(
    units, channels, tokens, chars, wq, wout, win, wdown, wg, gate_bias, wc, wm, gain, bias, cot_t, cot_c,
    segc, segr, pickc, keep, edges,
    token_out, char_out, o_x, o_c, o_qkv, o_p, o_ctx, o_h, o_act, o_dact, o_mid, o_st, o_mg,
    o_dmg, o_states, o_decay, o_unit0, o_unit1, o_scale, o_res3, o_res4, o_branch, norm_grads,
    x, c, qkv, p, ctx, h, act, dact, mid, st, mg, dmg, states, decays, unit0, unit1, scale, res3, res4, branch,
    hidden, middle, outs_t, outs_c, drive, taps, perm,
    stage, got, held, temp, send, recv, local,
):
    seqs, length = tokens.shape[0], segr.shape[2]
    shard, width = tokens.shape[1], tokens.shape[2]
    block_chars = chars.shape[1]
    heads = p.shape[1] // 4
    g = Group(send, recv, seqs)
    me = g.me
    saves = []

    def keep_out(seq, source, target):
        saves.append((source, target, len(saves)))

    def local_copy(number, seq, source, target):
        return pltpu.make_async_copy(source, target, local.at[number * seqs + seq])

    gx, gc = Gather(g, x, tokens), Gather(g, c, chars)
    gh, gm, gs = Gather(g, h), Gather(g, mid), Gather(g, st)
    narrow = lambda ref: (lambda s, i: ref.at[s, i, :, pl.ds(0, width)])
    wide = lambda ref: (lambda s, i: ref.at[s, i])
    own_n = lambda s: held.at[s, :, pl.ds(0, width)]
    own_w = lambda s: held.at[s]
    thin = temp.at[:, pl.ds(0, width)]
    s_attn = Scatter(g, narrow(stage), narrow(got), own_n, thin)
    s_ffn = Scatter(g, narrow(stage), narrow(got), own_n, thin)
    s_branch = Scatter(g, wide(stage), wide(got), own_w, temp)

    def own_x(seq):
        return local_copy(0, seq, tokens.at[seq], x.at[seq, me])

    def own_c(seq):
        return local_copy(1, seq, chars.at[seq], c.at[seq, me])

    plan = [
        (x, o_x), (c, o_c), (qkv, o_qkv), (p, o_p), (ctx, o_ctx), (h, o_h), (act, o_act),
        (dact, o_dact), (mid, o_mid), (st, o_st), (mg, o_mg), (dmg, o_dmg), (states, o_states),
        (decays, o_decay), (res4, o_res4), (unit0, o_unit0), (unit1, o_unit1), (scale, o_scale), (res3, o_res3), (branch, o_branch),
        (outs_t, token_out), (outs_c, char_out),
    ]

    def save(seq, *names):
        for name in names:
            for number, (source, target) in enumerate(plan):
                if source is name:
                    local_copy(2 + number, seq, source.at[seq], target.at[seq]).start()

    def each(body):
        def run(seq, carry):
            body(seq)
            return carry

        lax.fori_loop(0, seqs, run, 0)

    each(lambda s: (own_x(s).start(), own_c(s).start()))
    g.greet()
    each(gx.start)
    each(gc.start)

    for t in range(4):
        for d in range(2):
            row = lax.broadcasted_iota(jnp.int32, (LANE, width), 0)
            col = lax.broadcasted_iota(jnp.int32, (LANE, width), 1)
            first = d * 4 * units + t * units
            hit = (col - first == row) & (row < units)
            perm[pl.ds((2 * t + d) * LANE, LANE), :] = hit.astype(F32).astype(BF16)
    taps[...] = jnp.zeros_like(taps)
    norm_grads[...] = jnp.zeros_like(norm_grads)

    lane = lax.broadcasted_iota(jnp.int32, (shard, LANE), 1)
    left = lane < HD

    def attention(s):
        gx.forward(s)
        gx.finish(s)
        own_x(s).wait()
        save(s, x)

        def project(t, carry):
            rows = pl.ds(pl.multiple_of(t * shard, shard), shard)
            first, second, third = unpack3(nn(x[s, t], wq[...]), HD * heads)
            qkv[s, 0, rows, :] = (first * 0.125).astype(BF16)
            qkv[s, 1, rows, :] = second.astype(BF16)
            qkv[s, 2, rows, :] = third.astype(BF16)
            return carry

        lax.fori_loop(0, 4, project, 0)
        save(s, qkv)

        def part(b, out):
            rows = pl.ds(pl.multiple_of(b * shard, shard), shard)
            same = segc[s, rows, :] == segr[s]
            for tile in range(qkv.shape[3] // LANE):
                cols = pl.ds(tile * LANE, LANE)
                result = None
                for half in range(2):
                    head = 2 * tile + half
                    if head >= heads:
                        continue
                    query = qkv[s, 0, rows, cols]
                    if 2 * tile + 1 < heads:
                        query = jnp.where(left if half == 0 else ~left, query, jnp.zeros_like(query))
                    scores = jnp.where(same, nt(query, qkv[s, 1, :, cols]), MASK_VALUE)
                    power = jnp.exp(scores - jnp.max(scores, axis=-1, keepdims=True))
                    probs = (power * (1.0 / jnp.sum(power, axis=-1, keepdims=True))).astype(BF16)
                    p[s, head * 4 + b] = probs
                    mixed = nn(probs, qkv[s, 2, :, cols])
                    result = mixed if result is None else jnp.where(left, result, mixed)
                ctx[s, rows, cols] = result.astype(BF16)
            out[...] = nn(ctx[s, rows, :], wout[...])

        s_attn.start(s, part)
        save(s, p, ctx)

    each(attention)

    def first_norm(s):
        total = x[s, me].astype(F32) + s_attn.finish(s)
        unit, spread = normalize(total)
        unit0[s] = unit
        scale[s, 0] = jnp.broadcast_to(spread, (shard, LANE))
        hidden[s] = unit * gain[0:1] + bias[0:1]
        h[s, me] = hidden[s].astype(BF16)
        gh.start(s)
        save(s, unit0)

    def gru(s):
        gc.forward(s)
        gc.finish(s)
        own_c(s).wait()
        save(s, c)

        def gates(t, carry):
            rows = pl.ds(pl.multiple_of(t * LANE, LANE), LANE)
            per = block_chars // LANE
            inner = pl.ds(pl.multiple_of((t % per) * LANE, LANE), LANE)
            proj = nn(c[s, t // per, inner, :], wg[...])
            for tile in range(2):
                cols = slice(tile * LANE, (tile + 1) * LANE)
                gate = jax.nn.sigmoid(proj[:, cols] + gate_bias_pad(tile))
                cand = proj[:, (2 + tile) * LANE : (3 + tile) * LANE]
                decays[s, tile, rows, :] = (1.0 - gate) * keep[s, rows, tile : tile + 1]
                drive[tile, rows, :] = gate * cand
            return carry

        def gate_bias_pad(tile):
            return gate_bias[:, tile * LANE : (tile + 1) * LANE]

        total = 4 * block_chars
        lax.fori_loop(0, total // LANE, gates, 0)
        recur((True, False), decays.at[s], drive, states.at[s], total // CHUNKS)
        save(s, decays)

        def pick(t, carry):
            rows = pl.ds(pl.multiple_of(t * shard, shard), shard)
            for tile in range(2):
                ids = lax.broadcasted_iota(jnp.int32, (shard, total), 1)
                hot = (ids == pickc[s, rows, tile : tile + 1]).astype(F32).astype(BF16)
                out = nn(hot, states[s, tile].astype(BF16))
                st[s, me, rows, pl.ds(tile * LANE, LANE)] = out.astype(BF16)
            return carry

        lax.fori_loop(0, 4, pick, 0)
        gs.start(s)
        save(s, states)

    def norm_and_gru(s):
        first_norm(s)
        gru(s)

    each(norm_and_gru)

    def ffn(s):
        gh.forward(s)
        gh.finish(s)
        save(s, h)

        def part(b, out):
            value, slope = gelu_pair(nn(h[s, b], win[...]))
            act[s, b] = value.astype(BF16)
            dact[s, b] = slope.astype(BF16)
            out[...] = nn(act[s, b], wdown[...])

        s_ffn.start(s, part)
        save(s, act, dact)

    each(ffn)

    def second_norm(s):
        unit, spread = normalize(hidden[s] + s_ffn.finish(s))
        unit1[s] = unit
        scale[s, 1] = jnp.broadcast_to(spread, (shard, LANE))
        middle[s] = unit * gain[1:2] + bias[1:2]
        mid[s, me] = middle[s].astype(BF16)
        gm.start(s)
        save(s, unit1, scale)

    each(second_norm)

    def merge(s):
        gs.forward(s)
        gm.forward(s)
        gs.finish(s)
        gm.finish(s)
        save(s, mid, st)
        def mix(t, carry):
            rows = pl.ds(pl.multiple_of(t * shard, shard), shard)
            total = nn(mid[s, t], wc[pl.ds(0, width), :])
            for u in range(4):
                weights = wc[pl.ds(width + u * 2 * LANE, 2 * LANE), :]
                total = total + nn(st[s, u, rows, :], weights)
            taps[pl.ds(pl.multiple_of(8 + t * shard, 8), shard), :] = total
            return carry

        lax.fori_loop(0, 4, mix, 0)

        def shifted(t, carry):
            rows = pl.ds(pl.multiple_of(t * shard, shard), shard)
            window = taps[pl.ds(pl.multiple_of(t * shard, 8), shard + 16), :]
            before = unpack3(window[7 : 7 + shard], channels)[0]
            center = unpack3(window[8 : 8 + shard], channels)[1]
            after = unpack3(window[9 : 9 + shard], channels)[2]
            value, slope = gelu_pair(
                before * edges[s, rows, 0:1] + center + after * edges[s, rows, 1:2]
            )
            mg[s, rows, :] = value.astype(BF16)
            dmg[s, rows, :] = slope.astype(BF16)
            return carry

        lax.fori_loop(0, 4, shifted, 0)

        def part(b, out):
            rows = pl.ds(pl.multiple_of(b * shard, shard), shard)
            out[...] = nn(mg[s, rows, :], wm[...])

        s_branch.start(s, part)
        save(s, mg, dmg)

    each(merge)

    def put_branch(s, first, value):
        span = branch.shape[3]
        at = 0
        while at < width:
            part, inner = divmod(first + at, span)
            size = min(span - inner, width - at)
            branch[s, part, :, pl.ds(inner, size)] = value[:, at : at + size]
            at += size

    def last_norms(s):
        total = s_branch.finish(s)
        rows = pl.ds(pl.multiple_of(me * shard, shard), shard)
        unit, spread = normalize(middle[s] + total[:, :width])
        outs_t[s] = (unit * gain[2:3] + bias[2:3]).astype(BF16)
        cot = cot_t[s]
        norm_grads[0:1] += jnp.sum(cot * unit, axis=0, keepdims=True)
        norm_grads[2:3] += jnp.sum(cot, axis=0, keepdims=True)
        back = normalize_back(unit, spread, cot * gain[2:3])
        res3[s] = back
        put_branch(s, 0, back.astype(BF16))
        mine = total[:, width:]
        for u in range(4):
            mine = mine + nn(st[s, u, rows, :], perm[pl.ds(u * 2 * LANE, 2 * LANE), :])
        unit, spread = normalize(mine)
        outs_c[s] = (unit * gain[3:4] + bias[3:4]).astype(BF16)
        cot = cot_c[s]
        norm_grads[1:2] += jnp.sum(cot * unit, axis=0, keepdims=True)
        norm_grads[3:4] += jnp.sum(cot, axis=0, keepdims=True)
        back = normalize_back(unit, spread, cot * gain[3:4]).astype(BF16)
        put_branch(s, width, back)
        for u in range(4):
            res4[s, u] = nt(back, perm[pl.ds(u * 2 * LANE, 2 * LANE), :]).astype(BF16)
        save(s, outs_t, outs_c, res3, res4, branch)

    each(last_norms)

    def drain(s):
        for number, (source, target) in enumerate(plan):
            local_copy(2 + number, s, source.at[s], target.at[s]).wait()

    each(drain)


def forward_call(tokens, chars, weights, small, group_slots=27):
    seqs, shard, width = tokens.shape
    length, block_chars = shard * 4, chars.shape[1]
    total = block_chars * 4
    wq, wout, win, wdown, wg, gate_bias, wc, wm = weights
    cols = wout.shape[0]
    heads = small["heads"]
    sds = jax.ShapeDtypeStruct
    big = {
        "x": ((seqs, 4, shard, width), BF16),
        "c": ((seqs, 4, block_chars, chars.shape[2]), BF16),
        "qkv": ((seqs, 3, length, cols), BF16),
        "p": ((seqs, heads * 4, shard, length), BF16),
        "ctx": ((seqs, length, cols), BF16),
        "h": ((seqs, 4, shard, width), BF16),
        "act": ((seqs, 4, shard, win.shape[1]), BF16),
        "dact": ((seqs, 4, shard, win.shape[1]), BF16),
        "mid": ((seqs, 4, shard, width), BF16),
        "st": ((seqs, 4, length, 2 * LANE), BF16),
        "mg": ((seqs, length, wm.shape[0]), BF16),
        "dmg": ((seqs, length, wm.shape[0]), BF16),
        "states": ((seqs, 2, total, LANE), F32),
        "decay": ((seqs, 2, total, LANE), F32),
        "unit0": ((seqs, shard, width), F32),
        "unit1": ((seqs, shard, width), F32),
        "scale": ((seqs, 2, shard, LANE), F32),
        "res3": ((seqs, shard, width), F32),
        "res4": ((seqs, 4, shard, 2 * LANE), BF16),
        "branch": ((seqs, 2 * width // length, shard, length), BF16),
    }
    rows = ((seqs, shard, width), F32)
    low_rows = ((seqs, shard, width), BF16)
    scratch = list(big.values()) + [
        rows, rows, low_rows, low_rows,
        ((2, total, LANE), F32),
        ((length + 16, wc.shape[1]), F32),
        ((8 * LANE, width), BF16),
        ((seqs, 3, shard, 2 * width), BF16), ((seqs, 3, shard, 2 * width), BF16),
        ((seqs, shard, 2 * width), F32), ((shard, 2 * width), F32),
    ]
    anyspace = pl.BlockSpec(memory_space=pl.ANY)
    vmem = pl.BlockSpec(memory_space=pltpu.VMEM)
    out_shapes = [sds(low_rows[0], BF16)] * 2 + [sds(*v) for v in big.values()]
    ins = (
        tokens, chars, wq, wout, win, wdown, wg, gate_bias, wc, wm, small["gain"], small["bias"],
        small["cot_t"], small["cot_c"], small["segc"], small["segr"], small["pickc"],
        small["keep"], small["edges"],
    )
    outs = pl.pallas_call(
        functools.partial(forward_kernel, small["units"], small["channels"]),
        out_shape=out_shapes + [sds((4, width), F32)],
        in_specs=[anyspace] * 2 + [vmem] * (len(ins) - 2),
        out_specs=[anyspace] * len(out_shapes) + [vmem],
        scratch_shapes=[pltpu.VMEM(*v) for v in scratch]
        + [
            pltpu.SemaphoreType.DMA((group_slots * seqs,)),
            pltpu.SemaphoreType.DMA((group_slots * seqs,)),
            pltpu.SemaphoreType.DMA((26 * seqs,)),
        ],
        compiler_params=pltpu.CompilerParams(
            collective_id=0, has_side_effects=True, vmem_limit_bytes=62 * MIB
        ),
    )(*ins)
    names = ["token_out", "char_out"] + list(big) + ["norm_grads"]
    return dict(zip(names, outs))


class Reduce:
    def __init__(self, net, buf, out, first, land, land_first, rows, order):
        self.net, self.buf, self.out, self.land, self.order = net, buf, out, land, order
        self.first, self.land_first, self.rows = first, land_first, rows
        self.slots = net.take(2 * len(order))
        self.mark = net.mark()

    def start_of(self, level):
        start = self.first
        for i in range(level):
            start = start + self.net.bit(self.order[i]) * (self.rows >> (i + 1))
        return start

    def half(self, level):
        return self.rows >> (level + 1)

    def view(self, start, size, ref=None):
        ref = self.buf if ref is None else ref
        return ref.at[pl.ds(pl.multiple_of(start, 16), size), :]

    def keep(self):
        levels = len(self.order)
        start, size = self.start_of(levels), self.rows >> levels
        return pltpu.make_async_copy(
            self.view(start, size), self.view(start, size, self.out), self.mark
        )

    def landing(self, level):
        start = self.land_first + self.rows - (self.rows >> level)
        return self.land.at[pl.ds(start, self.half(level)), :]

    def down(self, level):
        bit = self.net.bit(self.order[level])
        other = self.start_of(level) + (1 - bit) * self.half(level)
        return self.net.copy(
            self.slots[level],
            self.view(other, self.half(level)),
            self.landing(level),
            self.order[level],
        )

    def up(self, level):
        start, size = self.start_of(level + 1), self.half(level)
        target = self.view(start, size, self.out)
        source = self.view(start, size) if level == len(self.order) - 1 else target
        return self.net.copy(
            self.slots[len(self.order) + level], source, target, self.order[level]
        )

    def step(self, number):
        levels = len(self.order)
        if 0 < number <= levels:
            level = number - 1
            self.down(level).wait()
            start = self.start_of(level + 1)
            start_land = self.land_first + self.rows - (self.rows >> level)

            def add(i, carry):
                rows = pl.ds(pl.multiple_of(start + i * 16, 16), 16)
                more = pl.ds(pl.multiple_of(start_land + i * 16, 16), 16)
                total = self.buf[rows, :].astype(F32) + self.land[more, :].astype(F32)
                self.buf[rows, :] = total.astype(BF16)
                return carry

            lax.fori_loop(0, self.half(level) // 16, add, 0)
            if number == levels:
                self.keep().start()
        elif number > levels:
            self.up(2 * levels - number).wait()
            if number == levels + 1:
                self.keep().wait()
        if number < levels:
            self.down(number).start()
        elif number < 2 * levels:
            self.up(2 * levels - 1 - number).start()


class Plane:
    def __init__(self, send, recv, marks):
        self.index = lax.axis_index("dp")
        self.send, self.recv, self.marks, self.used, self.marked = send, recv, marks, 0, 0

    def mark(self):
        self.marked += 1
        return self.marks.at[self.marked - 1]

    def bit(self, number):
        return (self.index // (1 << number)) % 2

    def peer(self, number):
        return self.index + (1 - 2 * self.bit(number)) * (1 << number)

    def take(self, count):
        first = self.used
        self.used += count
        return [first + i for i in range(count)]

    def copy(self, slot, source, target, number):
        return pltpu.make_async_remote_copy(
            src_ref=source,
            dst_ref=target,
            send_sem=self.send.at[slot],
            recv_sem=self.recv.at[slot],
            device_id={"dp": self.peer(number)},
            device_id_type=pl.DeviceIdType.MESH,
        )


SAVED = (
    "branch", "mg", "dmg", "mid", "st", "res3", "res4", "unit0", "unit1", "scale", "act", "dact",
    "h", "p", "qkv", "ctx", "x", "c", "states", "decay",
)
GRADS = ("merge", "conv", "down", "in", "gru", "out", "qkv")


def backward_kernel(units, channels, dp_size, *refs):
    refs = list(refs)
    take = lambda count: [refs.pop(0) for _ in range(count)]
    hbm = dict(zip(SAVED, take(len(SAVED))))
    wq, wout, win, wdown, wg, gate_bias, wc, wm, gain, pickr, edges, norm_in = take(12)
    grad_tokens, grad_chars = take(2)
    grads_out = dict(zip(GRADS, take(len(GRADS))))
    (small_out,) = take(1)
    names = [n for n in SAVED if n not in ("branch", "states", "decay", "p", "x")]
    v = dict(zip(names, take(len(names))))
    (pb, states, decay, drive, dpre, dyk, fg, gtok, dproj, gru_acc, res2, res1, ds, parts,
     stage, got, held, temp, cstage, cgot, cheld, ctemp) = take(22)
    land = dict(zip(GRADS, take(len(GRADS))))
    big = dict(zip(GRADS, take(len(GRADS))))
    small, small_land, send, recv, dsend, drecv, local, marks = take(8)

    seqs, shard, width = grad_tokens.shape
    length = 4 * shard
    block_chars = grad_chars.shape[1]
    total = 4 * block_chars
    heads = pb.shape[1] // 4
    cols = v["ctx"].shape[2]
    g = Group(send, recv, seqs)
    me = g.me
    inside = dp_size == 8
    plane = Plane(dsend, drecv, marks)

    def each(body):
        def run(seq, carry):
            body(seq)
            return carry

        lax.fori_loop(0, seqs, run, 0)

    def load(name):
        index = names.index(name)
        return pltpu.make_async_copy(hbm[name], v[name], local.at[index])

    spare = len(names)
    p_copy = lambda: pltpu.make_async_copy(hbm["p"], pb, local.at[spare])
    x_copy = lambda: pltpu.make_async_copy(hbm["x"], v["h"], local.at[39])

    def states_copy(s):
        return pltpu.make_async_copy(hbm["states"].at[s], states, local.at[spare + 1])

    def decay_copy(s, tile):
        return pltpu.make_async_copy(
            hbm["decay"].at[s, tile], decay.at[tile, pl.ds(8, total), :], local.at[spare + 2 + tile]
        )

    def out_copy(kind, s):
        source, target = ((res1, grad_tokens), (cheld, grad_chars))[kind]
        return pltpu.make_async_copy(
            source.at[s], target.at[s], local.at[spare + 4 + kind * seqs + s]
        )

    pieces = 2 * width // length
    gb = Gather(
        g, pb, hbm["branch"], place=lambda s, t: pb.at[s, pl.ds(t * pieces, pieces)]
    )
    gf, ga = Gather(g, fg), Gather(g, v["mid"])
    pick = lambda ref: (lambda s, i: ref.at[s, i])
    own = lambda ref: (lambda s: ref.at[s])
    s_mid = Scatter(g, pick(stage), pick(got), own(held), temp)
    s_hid = Scatter(g, pick(stage), pick(got), own(held), temp)
    s_tok = Scatter(g, pick(stage), pick(got), own(held), temp)
    s_chr = Scatter(g, pick(cstage), pick(cgot), own(cheld), ctemp)
    s_cout = Scatter(g, pick(cstage), pick(cgot), own(cheld), ctemp)

    def own_branch(s):
        return pltpu.make_async_copy(
            hbm["branch"].at[s], gb.at(s, me), local.at[spare + 4 + 2 * seqs + s]
        )

    each(lambda s: own_branch(s).start())
    for name in ("dmg", "res4", "mg", "mid", "st"):
        load(name).start()
    states_copy(0).start()
    for tile in range(2):
        decay_copy(0, tile).start()
    for name in names:
        if name not in ("dmg", "res4", "mg", "mid", "st"):
            load(name).start()

    barrier = pltpu.get_barrier_semaphore()
    places = [{"tensor": g.pair}, {"tensor": g.far}]
    if inside:
        places += [{"dp": plane.peer(k)} for k in range(3)]
    for place in places:
        pl.semaphore_signal(barrier, inc=1, device_id=place, device_id_type=pl.DeviceIdType.MESH)
    pl.semaphore_wait(barrier, len(places))
    each(gb.start)
    dpre[...] = jnp.zeros_like(dpre)
    for tile in range(2):
        decay[tile, pl.ds(0, 8), :] = jnp.zeros((8, LANE), F32)
        decay[tile, pl.ds(total + 8, 8), :] = jnp.zeros((8, LANE), F32)
    small[...] = jnp.zeros_like(small)
    small[0, pl.ds(0, 4), :] = norm_in[...]
    lane = lax.broadcasted_iota(jnp.int32, (shard, LANE), 1)
    left = lane < HD
    for name in ("dmg", "res4"):
        load(name).wait()

    def block_rows(t, size):
        return pl.ds(pl.multiple_of(t * size, size), size)

    def merge_back(s):
        gb.forward(s)
        gb.finish(s)
        own_branch(s).wait()

        def inner(t, carry):
            rows = block_rows(t, shard)
            back = None
            for j in range(pieces):
                piece = nt(pb[s, t * pieces + j], wm[:, j * length : (j + 1) * length])
                back = piece if back is None else back + piece
            dpre[pl.ds(pl.multiple_of(8 + t * shard, 8), shard), :] = (
                (back * v["dmg"][s, rows, :].astype(F32)).astype(BF16).astype(F32)
            )
            return carry

        lax.fori_loop(0, 4, inner, 0)

        def taps(t, carry):
            rows = block_rows(t, shard)
            window = dpre[pl.ds(pl.multiple_of(t * shard, 8), shard + 16), :]
            marks = edges[s, rows, :]
            before = window[9 : 9 + shard] * marks[:, 2:3]
            after = window[7 : 7 + shard] * marks[:, 3:4]
            dyk[s, rows, :] = pack3(
                [before, window[8 : 8 + shard], after], channels
            ).astype(BF16)
            return carry

        lax.fori_loop(0, 4, taps, 0)

        def mid_part(b, out):
            out[...] = nt(dyk[s, block_rows(b, shard), :], wc[pl.ds(0, width), :])

        s_mid.start(s, mid_part)

        def char_part(b, out):
            first = pl.multiple_of(width + b * 2 * LANE, 2 * LANE)
            out[...] = nt(dyk[s], wc[pl.ds(first, 2 * LANE), :])
            out[block_rows(me, shard), :] += v["res4"][s, b].astype(F32)

        s_chr.start(s, char_part)

    each(merge_back)
    for name in ("mg", "mid", "st"):
        load(name).wait()

    tokens = seqs * length
    half_w = width
    for j in range(pieces):
        right = jnp.concatenate(
            [pb[s, t * pieces + j] for s in range(seqs) for t in range(4)], axis=0
        )
        out = tn(v["mg"][...].reshape(tokens, -1), right)[:channels].astype(BF16)
        at = 0
        while at < length:
            part, inside_at = divmod(j * length + at, half_w)
            size = min(length - at, half_w - inside_at)
            big["merge"][pl.ds(part * channels, channels), pl.ds(inside_at, size)] = out[
                :, at : at + size
            ]
            at += size
    step_w = 2 * LANE

    def conv_mid(j, carry):
        colsj = pl.ds(pl.multiple_of(j * step_w, step_w), step_w)
        out = tn(v["mid"][:, :, :, colsj].reshape(tokens, step_w), dyk[...].reshape(tokens, -1))
        big["conv"][block_rows(j, step_w), :] = out.astype(BF16)
        return carry

    lax.fori_loop(0, width // step_w, conv_mid, 0)

    def conv_char(t, carry):
        out = tn(v["st"][:, t].reshape(tokens, 2 * LANE), dyk[...].reshape(tokens, -1))
        for d in range(2):
            first = pl.multiple_of(width + d * 4 * units + t * units, 16)
            big["conv"][pl.ds(first, units), :] = out[d * LANE : d * LANE + units].astype(BF16)
        return carry

    lax.fori_loop(0, 4, conv_char, 0)
    p_copy().start()

    near, along = (0, 1, 2), (1, 2, 0)

    def split(name, head):
        rows = big[name].shape[0]
        result = []
        if head:
            result.append(
                Reduce(plane, big[name], grads_out[name], 0, land[name], 0, head, near)
            )
        if rows > head:
            result.append(
                Reduce(
                    plane, big[name], grads_out[name], head, land[name], head * 7 // 8,
                    rows - head, along,
                )
            )
        return result

    if inside:
        first_sums = split("conv", 1024) + split("merge", 0)
        second_sums = split("down", big["down"].shape[0]) + split("in", 256)
        third_sums = split("qkv", 512) + split("out", 0) + split("gru", big["gru"].shape[0])
    else:
        first_sums, second_sums, third_sums = [], [], []

    def advance(sums, number):
        for one in sums:
            one.step(number)

    advance(first_sums, 0)

    def second_back(s):
        incoming = v["res3"][s] + s_mid.finish(s)
        unit = v["unit1"][s]
        small[0, 5:6] += jnp.sum(incoming * unit, axis=0, keepdims=True)
        small[0, 7:8] += jnp.sum(incoming, axis=0, keepdims=True)
        spread = v["scale"][s, 1][:, 0:1]
        res2[s] = normalize_back(unit, spread, incoming * gain[1:2])
        fg[s, me] = res2[s].astype(BF16)
        gtok[s] = s_chr.finish(s).astype(BF16)
        gf.start(s)

    for name in ("res3", "unit1", "scale"):
        load(name).wait()
    each(second_back)
    load("c").wait()

    def gru_back(s):
        def spread_out(t, carry):
            rows = block_rows(t, LANE)
            for tile in range(2):
                ids = lax.broadcasted_iota(jnp.int32, (LANE, length), 0) + t * LANE
                hot = (ids == pickr[s, tile : tile + 1, :]).astype(F32).astype(BF16)
                drive[tile, rows, :] = nn(hot, gtok[s, :, pl.ds(tile * LANE, LANE)])
            return carry

        lax.fori_loop(0, total // LANE, spread_out, 0)
        for tile in range(2):
            decay_copy(s, tile).wait()
        recur((False, True), decay, drive, drive, total // CHUNKS, (9, 7))
        states_copy(s).wait()

        def finish(t, sums):
            rows = block_rows(t, LANE)
            per = block_chars // LANE
            inner = block_rows(t % per, LANE)
            proj = nn(v["c"][s, t // per, inner, :], wg[...])
            new = []
            for tile in range(2):
                colst = slice(tile * LANE, (tile + 1) * LANE)
                gate = jax.nn.sigmoid(proj[:, colst] + gate_bias[:, colst])
                cand = proj[:, (2 + tile) * LANE : (3 + tile) * LANE]
                flow = drive[tile, rows, :] * gate
                logit = flow * (cand - states[tile, rows, :])
                dproj[rows, pl.ds(tile * LANE, LANE)] = logit.astype(BF16)
                dproj[rows, pl.ds((2 + tile) * LANE, LANE)] = flow.astype(BF16)
                new.append(sums[tile] + jnp.sum(logit, axis=0, keepdims=True))
            return tuple(new)

        zero = jnp.zeros((1, LANE), F32)
        sums = lax.fori_loop(0, total // LANE, finish, (zero, zero))
        for tile in range(2):
            small[0, 8:9, pl.ds(tile * LANE, LANE)] += sums[tile]

        @pl.when(s + 1 < seqs)
        def _():
            states_copy(s + 1).start()
            for tile in range(2):
                decay_copy(s + 1, tile).start()

        def part(b, out):
            out[...] = nt(dproj[block_rows(b, block_chars), :], wg[...])

        gf.forward(s)
        gf.finish(s)
        s_cout.start(s, part)
        grad = tn(v["c"][s].reshape(total, -1), dproj[...])

        @pl.when(s == 0)
        def _():
            gru_acc[...] = grad

        @pl.when(s > 0)
        def _():
            gru_acc[...] += grad

    each(gru_back)
    big["gru"][...] = gru_acc[...].astype(BF16)
    advance(first_sums, 1)
    for name in ("dact", "act", "h"):
        load(name).wait()

    def ffn_back(s):
        def part(b, out):
            back = nt(fg[s, b], wdown[...]) * v["dact"][s, b].astype(F32)
            v["dact"][s, b] = back.astype(BF16)
            out[...] = nt(v["dact"][s, b], win[...])

        s_hid.start(s, part)

    each(ffn_back)
    advance(first_sums, 2)

    def ffn_weights(j, carry):
        colsj = pl.ds(pl.multiple_of(j * step_w, step_w), step_w)
        out = tn(v["act"][:, :, :, colsj].reshape(tokens, step_w), fg[...].reshape(tokens, width))
        big["down"][block_rows(j, step_w), :] = out.astype(BF16)
        return carry

    lax.fori_loop(0, big["down"].shape[0] // step_w, ffn_weights, 0)

    def in_weights(j, carry):
        colsj = pl.ds(pl.multiple_of(j * step_w, step_w), step_w)
        out = tn(
            v["h"][:, :, :, colsj].reshape(tokens, step_w), v["dact"][...].reshape(tokens, -1)
        )
        big["in"][block_rows(j, step_w), :] = out.astype(BF16)
        return carry

    lax.fori_loop(0, width // step_w, in_weights, 0)
    x_copy().start()
    advance(second_sums, 0)
    load("unit0").wait()

    def first_back(s):
        incoming = res2[s] + s_hid.finish(s)
        unit = v["unit0"][s]
        small[0, 4:5] += jnp.sum(incoming * unit, axis=0, keepdims=True)
        small[0, 6:7] += jnp.sum(incoming, axis=0, keepdims=True)
        spread = v["scale"][s, 0][:, 0:1]
        res1[s] = normalize_back(unit, spread, incoming * gain[0:1])
        v["mid"][s, me] = res1[s].astype(BF16)
        ga.start(s)

    each(first_back)
    hops = [("t", g.pair), ("t", g.far)] + ([("d", k) for k in range(3)] if inside else [])
    slots_t, slots_d = g.slots(2), plane.take(3)

    def small_copy(number):
        kind, where = hops[number]
        source, target = small.at[number], small_land.at[number]
        if kind == "t":
            return g.copy(slots_t[number], 0, source, target, where)
        return plane.copy(slots_d[where], source, target, where)

    def small_step(number):
        if number > 0:
            small_copy(number - 1).wait()
            keep_rows = 8 if number <= 2 else 16
            value, more = small[number - 1], small_land[number - 1]
            small[number, pl.ds(0, 8), :] = value[:8] + more[:8]
            small[number, pl.ds(8, 8), :] = value[8:] if number <= 2 else value[8:] + more[8:]
        if number < len(hops):
            small_copy(number).start()

    if not inside:
        hops = []
    small_step(0) if hops else None
    advance(first_sums, 3)
    for name in ("qkv", "ctx"):
        load(name).wait()
    p_copy().wait()

    def attention_back(s):
        ga.forward(s)
        ga.finish(s)
        dctx = v["dmg"]

        def context(t, carry):
            dctx[s, block_rows(t, shard), :] = nt(v["mid"][s, t], wout[...]).astype(BF16)
            return carry

        lax.fori_loop(0, 4, context, 0)
        for tile in range(cols // LANE):
            lanes = pl.ds(tile * LANE, LANE)
            for half in range(2):
                head = 2 * tile + half
                if head >= heads:
                    continue
                paired = 2 * tile + 1 < heads

                def rows_of(b, carry):
                    rows = block_rows(b, shard)
                    grad = dctx[s, rows, lanes]
                    if paired:
                        grad = jnp.where(left if half == 0 else ~left, grad, jnp.zeros_like(grad))
                    back = nt(grad, v["qkv"][s, 2, :, lanes])
                    probs = pb[s, head * 4 + b].astype(F32)
                    row_dot = jnp.sum(probs * back, axis=-1, keepdims=True)
                    ds[b] = (probs * (back - row_dot)).astype(BF16)
                    out = nn(ds[b], v["qkv"][s, 1, :, lanes])
                    if half == 1:
                        out = jnp.where(left, ctemp[rows, lanes], out)
                    ctemp[rows, lanes] = out
                    return carry

                lax.fori_loop(0, 4, rows_of, 0)
                keys = tn(ds[...].reshape(length, length), v["qkv"][s, 0, :, lanes])
                values = tn(
                    pb[s, pl.ds(head * 4, 4)].reshape(length, length), dctx[s, :, lanes]
                )
                if half == 1:
                    wide_left = lax.broadcasted_iota(jnp.int32, (length, LANE), 1) < HD
                    keys = jnp.where(wide_left, parts[0, :, lanes], keys)
                    values = jnp.where(wide_left, parts[1, :, lanes], values)
                parts[0, :, lanes] = keys
                parts[1, :, lanes] = values

        def pack(t, carry):
            rows = block_rows(t, shard)
            query = ctemp[rows, :].astype(BF16).astype(F32) * 0.125
            dyk[s, rows, :] = pack3(
                [query, parts[0, rows, :], parts[1, rows, :]], HD * heads
            ).astype(BF16)
            return carry

        lax.fori_loop(0, 4, pack, 0)

        def part(b, out):
            out[...] = nt(dyk[s, block_rows(b, shard), :], wq[...])

        s_tok.start(s, part)

    each(attention_back)
    advance(first_sums, 4)
    advance(second_sums, 1)

    x_copy().wait()

    def qkv_weights(j, carry):
        colsj = pl.ds(pl.multiple_of(j * step_w, step_w), step_w)
        out = tn(v["h"][:, :, :, colsj].reshape(tokens, step_w), dyk[...].reshape(tokens, -1))
        big["qkv"][block_rows(j, step_w), :] = out.astype(BF16)
        return carry

    lax.fori_loop(0, width // step_w, qkv_weights, 0)
    big["out"][...] = tn(
        v["ctx"][...].reshape(tokens, -1), v["mid"][...].reshape(tokens, width)
    ).astype(BF16)
    advance(third_sums, 0)
    if hops:
        small_step(1)

    def last(s):
        res1[s] = res1[s] + s_tok.finish(s)
        out_copy(0, s).start()
        cheld[s] = s_cout.finish(s)
        out_copy(1, s).start()

    each(last)

    def emit(name):
        return pltpu.make_async_copy(
            big[name], grads_out[name], local.at[spare + 4 + 3 * seqs + GRADS.index(name)]
        )

    if inside:
        small_step(2)
        advance(second_sums, 2)
        advance(first_sums, 5)
        advance(third_sums, 1)
        small_step(3)
        advance(second_sums, 3)
        advance(third_sums, 2)
        advance(first_sums, 6)
        small_step(4)
        advance(second_sums, 4)
        advance(third_sums, 3)
        small_step(5)
        advance(second_sums, 5)
        advance(third_sums, 4)
        advance(second_sums, 6)
        advance(third_sums, 5)
        advance(third_sums, 6)
    else:
        for name in GRADS:
            emit(name).start()
        for name in GRADS:
            emit(name).wait()
    small_out[...] = small[len(hops)]
    each(lambda s: (out_copy(0, s).wait(), out_copy(1, s).wait()))


def backward_call(saved, weights, small, dp_size):
    wq, wout, win, wdown, wg, gate_bias, wc, wm = weights
    sds = jax.ShapeDtypeStruct
    seqs, shard, width = saved["res3"].shape
    length = shard * 4
    block_chars, char_width = saved["c"].shape[2:]
    total = 4 * block_chars
    cols, packed = wout.shape[0], wc.shape[1]
    channels = small["channels"]
    saved_in = [saved[n] for n in SAVED]
    names = [n for n in SAVED if n not in ("branch", "states", "decay", "p", "x")]
    shapes = [(saved[n].shape, saved[n].dtype) for n in names]
    grads = {
        "merge": (2 * channels, width), "conv": (2 * width, packed),
        "down": (win.shape[1], width), "in": (width, win.shape[1]),
        "gru": (char_width, 4 * LANE), "out": (cols, width), "qkv": (width, wq.shape[1]),
    }
    pad = (seqs, 3, shard, width)
    cpad = (seqs, 3, length, 2 * LANE)
    scratch = shapes + [
        (saved["p"].shape, BF16),
        ((2, total, LANE), F32),
        ((2, total + 16, LANE), F32),
        ((2, total, LANE), F32),
        ((length + 16, wm.shape[0]), F32),
        ((seqs, length, packed), BF16),
        ((seqs, 4, shard, width), BF16),
        ((seqs, length, 2 * LANE), BF16),
        ((total, 4 * LANE), BF16),
        ((char_width, 4 * LANE), F32),
        ((seqs, shard, width), F32),
        ((seqs, shard, width), F32),
        ((4, shard, length), BF16),
        ((2, length, cols), F32),
        (pad, BF16), (pad, BF16), ((seqs, shard, width), F32), ((shard, width), F32),
        (cpad, BF16), (cpad, BF16), ((seqs, length, 2 * LANE), F32), ((length, 2 * LANE), F32),
    ]
    scratch += [((rows * 7 // 8 if dp_size == 8 else 16, last), BF16) for rows, last in grads.values()]
    scratch += [(shape, BF16) for shape in grads.values()]
    scratch += [((6, 16, width), F32), ((6, 16, width), F32)]
    anyspace = pl.BlockSpec(memory_space=pl.ANY)
    vmem = pl.BlockSpec(memory_space=pltpu.VMEM)
    ins = saved_in + list(weights) + [small["gain"], small["pickr"], small["edges"], saved["norm_grads"]]
    outs = pl.pallas_call(
        functools.partial(backward_kernel, small["units"], channels, dp_size),
        out_shape=[sds((seqs, shard, width), F32), sds((seqs, block_chars, char_width), F32)]
        + [sds(shape, BF16) for shape in grads.values()]
        + [sds((16, width), F32)],
        in_specs=[anyspace] * len(saved_in) + [vmem] * (len(ins) - len(saved_in)),
        out_specs=[anyspace] * (2 + len(grads)) + [vmem],
        scratch_shapes=[pltpu.VMEM(*one) for one in scratch]
        + [
            pltpu.SemaphoreType.DMA((32 * seqs,)),
            pltpu.SemaphoreType.DMA((32 * seqs,)),
            pltpu.SemaphoreType.DMA((72,)),
            pltpu.SemaphoreType.DMA((72,)),
            pltpu.SemaphoreType.DMA((40,)),
            pltpu.SemaphoreType.DMA((12,)),
        ],
        compiler_params=pltpu.CompilerParams(
            collective_id=1, has_side_effects=True, vmem_limit_bytes=63 * MIB
        ),
    )(*ins)
    names = ["grad_tokens", "grad_chars"] + list(grads) + ["small"]
    return dict(zip(names, outs))


def local(
    tokens,
    characters,
    doc_lengths,
    token_chars,
    w_qkv,
    w_out,
    w_in,
    w_down,
    w_gru,
    gate_bias,
    w_conv,
    w_merge,
    norm_gain,
    norm_bias,
    token_cot,
    char_cot,
):
    micro_count = tokens.shape[0]
    shard_len = tokens.shape[1]
    model_width = tokens.shape[2]
    char_width = characters.shape[2]
    group_size = lax.axis_size("tensor")
    group_rank = lax.axis_index("tensor")
    length = shard_len * group_size
    char_total = characters.shape[1] * group_size
    head_cols = w_qkv.shape[2]
    heads_here = head_cols // HD
    units_here = w_gru.shape[3]
    merge_here = w_conv.shape[2]
    gru_matrix, gru_bias = gru_weights(w_gru, gate_bias)
    spare = -head_cols % LANE
    more = -merge_here % LANE
    wq = jnp.pad(
        w_qkv.reshape(model_width, 3 * head_cols), ((0, 0), (0, -3 * head_cols % LANE))
    )
    wout = jnp.pad(w_out, ((0, spare), (0, 0)))
    wm = jnp.pad(w_merge.reshape(merge_here, 2 * model_width), ((0, more), (0, 0)))
    conv = jnp.swapaxes(w_conv, 0, 1).reshape(2 * model_width, 3 * merge_here)
    conv = jnp.pad(conv, ((0, 0), (0, -3 * merge_here % LANE)))
    conv_char = conv[model_width:].reshape(2, group_size, units_here, -1)
    conv_char = jnp.pad(
        jnp.swapaxes(conv_char, 0, 1), ((0, 0), (0, 0), (0, LANE - units_here), (0, 0))
    )
    wc = jnp.concatenate(
        [conv[:model_width], conv_char.reshape(group_size * 2 * LANE, -1)], axis=0
    )
    layouts = [layout(doc_lengths[i], token_chars[i], char_total) for i in range(micro_count)]
    stacked_layout = [jnp.stack(parts) for parts in zip(*layouts)]
    segment, first_char, last_char, keep_forward, keep_backward, prev_ok, next_ok = stacked_layout
    keep = jnp.stack([keep_forward, keep_backward], axis=2)
    picks = jnp.stack([last_char, first_char], axis=2)
    zero = jnp.zeros_like(prev_ok[:, :1])
    small = dict(
        gain=norm_gain, bias=norm_bias, cot_t=token_cot, cot_c=char_cot,
        segc=segment[:, :, None], segr=segment[:, None, :], pickc=picks, keep=keep,
        pickr=jnp.swapaxes(picks, 1, 2),
        edges=jnp.stack(
            [
                prev_ok,
                next_ok,
                jnp.concatenate([prev_ok[:, 1:], zero], axis=1),
                jnp.concatenate([zero, next_ok[:, :-1]], axis=1),
            ],
            axis=2,
        ),
        heads=heads_here, units=units_here, channels=merge_here,
    )
    weights = (wq, wout, w_in, w_down, gru_matrix, gru_bias, wc, wm)
    fw = forward_call(tokens, characters, weights, small)
    dp_size = lax.axis_size("dp")
    bw = backward_call(fw, weights, small, dp_size)
    rows = bw["small"]
    gate_row = rows[8, : 2 * LANE]
    grads = {name: bw[name] for name in GRADS}
    if dp_size != 8:
        grads, gate_row = lax.psum((grads, gate_row), "dp")
        rows = lax.psum(rows, ("dp", "tensor"))
    grads = {name: value.astype(F32) for name, value in grads.items()}
    packed = 3 * merge_here
    grad_conv = grads["conv"][:, :packed].reshape(2 * model_width, 3, merge_here)
    grad_merge = grads["merge"].reshape(2, merge_here, model_width)
    grad_gru = grads["gru"].reshape(char_width, 2, 2, LANE)[..., :units_here]
    return (
        fw["token_out"],
        fw["char_out"],
        bw["grad_tokens"],
        bw["grad_chars"],
        grads["qkv"][:, : 3 * head_cols].reshape(model_width, 3, head_cols),
        grads["out"][:head_cols],
        grads["in"],
        grads["down"],
        jnp.swapaxes(grad_gru, 1, 2),
        gate_row.reshape(2, LANE)[:, :units_here],
        jnp.swapaxes(grad_conv, 0, 1),
        jnp.swapaxes(grad_merge, 0, 1),
        jnp.concatenate([rows[4:6], rows[0:2]], axis=0),
        jnp.concatenate([rows[6:8], rows[2:4]], axis=0),
    )


def solution(mesh):
    return jax.shard_map(
        local,
        mesh=mesh,
        in_specs=(
            P("dp", "tensor", None),
            P("dp", "tensor", None),
            P("dp", None),
            P("dp", None),
            P(None, None, "tensor"),
            P("tensor", None),
            P(None, "tensor"),
            P("tensor", None),
            P(None, None, None, "tensor"),
            P(None, "tensor"),
            P(None, None, "tensor"),
            P("tensor", None, None),
            P(),
            P(),
            P("dp", "tensor", None),
            P("dp", "tensor", None),
        ),
        out_specs=(
            P("dp", "tensor", None),
            P("dp", "tensor", None),
            P("dp", "tensor", None),
            P("dp", "tensor", None),
            P(None, None, "tensor"),
            P("tensor", None),
            P(None, "tensor"),
            P("tensor", None),
            P(None, None, None, "tensor"),
            P(None, "tensor"),
            P(None, None, "tensor"),
            P("tensor", None, None),
            P(),
            P(),
        ),
        check_vma=False,
    )
```

```python
import functools
from types import SimpleNamespace

import jax
import jax.numpy as jnp
from jax import lax
from jax.experimental import pallas as pl
from jax.experimental.pallas import tpu as pltpu
from jax.sharding import PartitionSpec as P

HD = 64


NORM_EPSILON = 1e-06
MASK_VALUE = -1e30
HIGH_PRECISION = lax.Precision.HIGHEST


def layout(doc_sizes, char_counts, char_total):
    length = char_counts.shape[0]
    docs = doc_sizes.shape[0]
    doc_ids = jnp.arange(docs, dtype=jnp.int32)
    doc_ends = jnp.sum(
        jnp.where(doc_ids[None, :] <= doc_ids[:, None], doc_sizes[None, :], 0), axis=1
    )
    positions = jnp.arange(length, dtype=jnp.int32)
    segment = jnp.sum(
        (positions[:, None] >= doc_ends[None, :]).astype(jnp.int32), axis=1, dtype=jnp.int32
    )
    token_ends = jnp.sum(
        jnp.where(positions[None, :] <= positions[:, None], char_counts[None, :], 0), axis=1
    )
    last_char = token_ends - 1
    first_char = token_ends - char_counts
    char_ends = jnp.sum(
        jnp.where(positions[None, :] < doc_ends[:, None], char_counts[None, :], 0), axis=1
    )
    char_positions = jnp.arange(char_total, dtype=jnp.int32)
    starts = char_ends - jnp.sum(
        jnp.where(
            (positions[None, :] < doc_ends[:, None])
            & (positions[None, :] >= (doc_ends - doc_sizes)[:, None]),
            char_counts[None, :],
            0,
        ),
        axis=1,
    )
    keep_forward = 1.0 - jnp.any(char_positions[:, None] == starts[None, :], axis=1).astype(
        jnp.float32
    )
    keep_backward = 1.0 - jnp.any(
        char_positions[:, None] == (char_ends - 1)[None, :], axis=1
    ).astype(jnp.float32)
    token_starts = doc_ends - doc_sizes
    prev_ok = 1.0 - jnp.any(positions[:, None] == token_starts[None, :], axis=1).astype(
        jnp.float32
    )
    next_ok = 1.0 - jnp.any(positions[:, None] == (doc_ends - 1)[None, :], axis=1).astype(
        jnp.float32
    )
    return (segment, first_char, last_char, keep_forward, keep_backward, prev_ok, next_ok)


F32 = jnp.float32
BF16 = jnp.bfloat16
LANE = 128
MIB = 1024 * 1024
VMEM = pl.BlockSpec(memory_space=pltpu.VMEM)


def gru_weights(w_gru, gate_bias):
    width, _, _, units = w_gru.shape
    matrix = jnp.pad(jnp.swapaxes(w_gru, 1, 2), ((0, 0), (0, 0), (0, 0), (0, LANE - units)))
    bias = jnp.pad(gate_bias, ((0, 0), (0, LANE - units)))
    return matrix.reshape(width, 4 * LANE), bias.reshape(1, 2 * LANE)


def nn(left, right):
    return jnp.dot(left, right, preferred_element_type=F32)


def nt(left, right):
    return lax.dot_general(left, right, (((1,), (1,)), ((), ())), preferred_element_type=F32)


def tn(left, right):
    return lax.dot_general(left, right, (((0,), (0,)), ((), ())), preferred_element_type=F32)


def gelu_pair(values):
    cdf = 0.5 * (1.0 + lax.erf(values * 0.7071067811865476))
    density = 0.3989422804014327 * jnp.exp(-0.5 * values * values)
    return values * cdf, cdf + values * density


def normalize(rows):
    centered = rows - jnp.mean(rows, axis=-1, keepdims=True)
    scale = lax.rsqrt(jnp.mean(centered * centered, axis=-1, keepdims=True) + NORM_EPSILON)
    return centered * scale, scale


def normalize_back(unit, scale, grad_unit):
    return scale * (
        grad_unit
        - jnp.mean(grad_unit, axis=-1, keepdims=True)
        - unit * jnp.mean(grad_unit * unit, axis=-1, keepdims=True)
    )


def roll_lanes(value, shift):
    return pltpu.roll(value, shift % value.shape[1], axis=1)


def unpack3(packed, size):
    room = -(-size // LANE) * LANE
    lane = lax.broadcasted_iota(jnp.int32, (packed.shape[0], room), 1)
    parts = []
    for k in range(3):
        first = k * size // LANE * LANE
        inner = k * size - first
        part = packed[:, first : min(first + room + LANE, packed.shape[1])]
        if inner:
            part = roll_lanes(part, -inner)
        parts.append(jnp.where(lane < size, part[:, :room], 0.0))
    return parts


def pack3(parts, size):
    room = parts[0].shape[1]
    columns = -(-3 * size // LANE) * LANE
    tiles = [None] * (columns // LANE)
    for k in range(3):
        first, inner = divmod(k * size, LANE)
        part = parts[k]
        if inner:
            part = jnp.concatenate([part, jnp.zeros_like(part[:, :LANE])], axis=1)
            part = roll_lanes(part, inner)
        for j in range(part.shape[1] // LANE):
            if first + j < len(tiles) and (first + j) * LANE < (k + 1) * size:
                tile = part[:, j * LANE : (j + 1) * LANE]
                old = tiles[first + j]
                tiles[first + j] = tile if old is None else old + tile
    return jnp.concatenate(tiles, axis=1)


class Group:
    def __init__(self, send, recv, seqs):
        self.me = lax.axis_index("tensor")
        self.low = self.me % 2
        self.high = self.me // 2
        self.pair = self.high * 2 + (1 - self.low)
        self.far = (1 - self.high) * 2 + self.low
        self.send, self.recv, self.seqs, self.used = send, recv, seqs, 0

    def block(self, turn):
        left = 3 - turn
        return ((self.high + left // 2) % 2) * 2 + (self.low + left % 2) % 2

    def slots(self, count):
        first = self.used
        self.used += count
        return [first + i for i in range(count)]

    def copy(self, slot, seq, source, target, peer):
        index = slot * self.seqs + seq
        return pltpu.make_async_remote_copy(
            src_ref=source,
            dst_ref=target,
            send_sem=self.send.at[index],
            recv_sem=self.recv.at[index],
            device_id={"tensor": peer},
            device_id_type=pl.DeviceIdType.MESH,
        )

    def greet(self):
        barrier = pltpu.get_barrier_semaphore()
        for peer in (self.pair, self.far):
            pl.semaphore_signal(
                barrier, inc=1, device_id={"tensor": peer}, device_id_type=pl.DeviceIdType.MESH
            )
        pl.semaphore_wait(barrier, 2)


class Gather:
    def __init__(self, group, buf, source=None, place=None):
        self.group, self.source = group, source
        self.at = place or (lambda seq, t: buf.at[seq, t])
        self.near, self.over, self.fwd = group.slots(3)

    def own(self, seq):
        return self.at(seq, self.group.me) if self.source is None else self.source.at[seq]

    def near_copy(self, seq):
        g = self.group
        return g.copy(self.near, seq, self.own(seq), self.at(seq, g.me), g.pair)

    def over_copy(self, seq):
        g = self.group
        return g.copy(self.over, seq, self.own(seq), self.at(seq, g.me), g.far)

    def fwd_copy(self, seq):
        g = self.group
        other = self.at(seq, g.far)
        return g.copy(self.fwd, seq, other, other, g.pair)

    def start(self, seq):
        self.over_copy(seq).start()
        self.near_copy(seq).start()

    def forward(self, seq):
        self.over_copy(seq).wait_recv()
        self.fwd_copy(seq).start()

    def finish(self, seq):
        near = self.near_copy(seq)
        fwd = self.fwd_copy(seq)
        near.wait_recv()
        fwd.wait_recv()
        near.wait_send()
        self.over_copy(seq).wait_send()
        fwd.wait_send()


class Scatter:
    def __init__(self, group, stage, got, own, temp):
        self.group, self.stage, self.got, self.held, self.temp = group, stage, got, own, temp
        self.names = group.slots(3)

    def copies(self, seq):
        g = self.group
        peers = (g.pair, g.pair, g.far)
        return [
            g.copy(self.names[i], seq, self.stage(seq, i), self.got(seq, i), peers[i])
            for i in range(3)
        ]

    def start(self, seq, part):
        mine, other, over = self.copies(seq)

        def turn(step, carry):
            part(self.group.block(step), self.temp)

            @pl.when(step == 0)
            def _():
                self.stage(seq, 1)[...] = self.temp[...].astype(BF16)
                other.start()

            @pl.when(step == 1)
            def _():
                other.wait_recv()
                self.stage(seq, 2)[...] = (self.temp[...] + self.got(seq, 1)[...]).astype(BF16)
                over.start()

            @pl.when(step == 2)
            def _():
                self.stage(seq, 0)[...] = self.temp[...].astype(BF16)
                mine.start()

            @pl.when(step == 3)
            def _():
                self.held(seq)[...] = self.temp[...]

            return carry

        lax.fori_loop(0, 4, turn, 0)

    def finish(self, seq):
        mine, other, over = self.copies(seq)
        mine.wait_recv()
        over.wait_recv()
        total = self.held(seq)[...] + self.got(seq, 0)[...] + self.got(seq, 2)[...]
        mine.wait_send()
        other.wait_send()
        over.wait_send()
        return total


def shift_rows(value, count, up, fill):
    edge = jnp.full((count, value.shape[1]), fill, value.dtype)
    if up:
        return jnp.concatenate([edge, value[:-count]], axis=0)
    return jnp.concatenate([value[count:], edge], axis=0)


def recur(ups, decays, drives, outs, block, back=False):
    steps = block // 8
    pairs = [(tile, t) for tile in range(2) for t in range(4)]

    def rows(tile, t, step):
        row = step if ups[tile] else steps - 1 - step
        return pl.ds(pl.multiple_of(t * block + row * 8, 8), 8)

    def summary(step, carry):
        new = []
        for i, (tile, t) in enumerate(pairs):
            state, mult = carry[2 * i], carry[2 * i + 1]
            here = rows(tile, t, step)
            decay, drive = decays[tile, here, :], drives[tile, here, :]
            state = decay * (state + drive) if back else decay * state + drive
            new += [state, decay * mult]
        return tuple(new)

    zero, one = jnp.zeros((8, LANE), F32), jnp.ones((8, LANE), F32)
    ends = lax.fori_loop(0, steps, summary, (zero, one) * 8, unroll=4)
    starts = []
    for tile in range(2):
        state = jnp.concatenate([ends[2 * (4 * tile + t)] for t in range(4)], axis=0)
        mult = jnp.concatenate([ends[2 * (4 * tile + t) + 1] for t in range(4)], axis=0)
        for count in (1, 2, 4, 8, 16):
            state = mult * shift_rows(state, count, ups[tile], 0.0) + state
            mult = mult * shift_rows(mult, count, ups[tile], 1.0)
        state = shift_rows(state, 1, ups[tile], 0.0)
        starts += [state[8 * t : 8 * t + 8] for t in range(4)]

    def write(step, carry):
        new = []
        for i, (tile, t) in enumerate(pairs):
            here = rows(tile, t, step)
            decay, drive = decays[tile, here, :], drives[tile, here, :]
            if back:
                value = drive + carry[i]
                new.append(decay * value)
            else:
                value = decay * carry[i] + drive
                new.append(value)
            outs[tile, here, :] = value
        return tuple(new)

    lax.fori_loop(0, steps, write, tuple(starts), unroll=4)


def forward_kernel(
    units, channels, tokens, chars, wq, wout, win, wdown, wg, gate_bias, wc, wm, gain, bias, cot_t, cot_c,
    segc, segr, pickc, keep, edges,
    token_out, char_out, o_x, o_c, o_qkv, o_p, o_ctx, o_h, o_act, o_dact, o_mid, o_st, o_mg,
    o_dmg, o_states, o_decay, o_unit0, o_unit1, o_scale, o_res3, o_res4, o_branch, norm_grads,
    x, c, qkv, p, ctx, h, act, dact, mid, st, mg, dmg, low_states, decays, unit0, unit1, scale, res3, res4, branch,
    hidden, middle, outs_t, outs_c, states, drive, taps, perm,
    stage, got, held, temp, send, recv, local,
):
    seqs, length = tokens.shape[0], segr.shape[2]
    shard, width = tokens.shape[1], tokens.shape[2]
    block_chars = chars.shape[1]
    heads = p.shape[1] // 4
    g = Group(send, recv, seqs)
    me = g.me
    saves = []

    def keep_out(seq, source, target):
        saves.append((source, target, len(saves)))

    def local_copy(number, seq, source, target):
        return pltpu.make_async_copy(source, target, local.at[number * seqs + seq])

    gx, gc = Gather(g, x, tokens), Gather(g, c, chars)
    gh, gm, gs = Gather(g, h), Gather(g, mid), Gather(g, st)
    narrow = lambda ref: (lambda s, i: ref.at[s, i, :, pl.ds(0, width)])
    wide = lambda ref: (lambda s, i: ref.at[s, i])
    own_n = lambda s: held.at[s, :, pl.ds(0, width)]
    own_w = lambda s: held.at[s]
    thin = temp.at[:, pl.ds(0, width)]
    s_attn = Scatter(g, narrow(stage), narrow(got), own_n, thin)
    s_ffn = Scatter(g, narrow(stage), narrow(got), own_n, thin)
    s_branch = Scatter(g, wide(stage), wide(got), own_w, temp)

    def own_x(seq):
        return local_copy(0, seq, tokens.at[seq], x.at[seq, me])

    def own_c(seq):
        return local_copy(1, seq, chars.at[seq], c.at[seq, me])

    plan = [
        (x, o_x), (c, o_c), (qkv, o_qkv), (p, o_p), (ctx, o_ctx), (h, o_h), (act, o_act),
        (dact, o_dact), (mid, o_mid), (st, o_st), (mg, o_mg), (dmg, o_dmg), (low_states, o_states),
        (decays, o_decay), (res4, o_res4), (unit0, o_unit0), (unit1, o_unit1), (scale, o_scale), (res3, o_res3), (branch, o_branch),
        (outs_t, token_out), (outs_c, char_out),
    ]

    def save(seq, *names):
        for name in names:
            for number, (source, target) in enumerate(plan):
                if source is name:
                    local_copy(2 + number, seq, source.at[seq], target.at[seq]).start()

    def each(body):
        def run(seq, carry):
            body(seq)
            return carry

        lax.fori_loop(0, seqs, run, 0)

    each(lambda s: (own_x(s).start(), own_c(s).start()))
    g.greet()
    each(gx.start)
    each(gc.start)

    for t in range(4):
        for d in range(2):
            row = lax.broadcasted_iota(jnp.int32, (LANE, width), 0)
            col = lax.broadcasted_iota(jnp.int32, (LANE, width), 1)
            first = d * 4 * units + t * units
            hit = (col - first == row) & (row < units)
            perm[pl.ds((2 * t + d) * LANE, LANE), :] = hit.astype(F32).astype(BF16)
    taps[...] = jnp.zeros_like(taps)
    norm_grads[...] = jnp.zeros_like(norm_grads)

    lane = lax.broadcasted_iota(jnp.int32, (shard, LANE), 1)
    left = lane < HD

    def attention(s):
        gx.forward(s)
        gx.finish(s)
        own_x(s).wait()
        save(s, x)

        def project(t, carry):
            rows = pl.ds(pl.multiple_of(t * shard, shard), shard)
            first, second, third = unpack3(nn(x[s, t], wq[...]), HD * heads)
            qkv[s, 0, rows, :] = (first * 0.125).astype(BF16)
            qkv[s, 1, rows, :] = second.astype(BF16)
            qkv[s, 2, rows, :] = third.astype(BF16)
            return carry

        lax.fori_loop(0, 4, project, 0)
        save(s, qkv)

        def part(b, out):
            rows = pl.ds(pl.multiple_of(b * shard, shard), shard)
            same = segc[s, rows, :] == segr[s]
            for tile in range(qkv.shape[3] // LANE):
                cols = pl.ds(tile * LANE, LANE)
                result = None
                for half in range(2):
                    head = 2 * tile + half
                    if head >= heads:
                        continue
                    query = qkv[s, 0, rows, cols]
                    if 2 * tile + 1 < heads:
                        query = jnp.where(left if half == 0 else ~left, query, jnp.zeros_like(query))
                    scores = jnp.where(same, nt(query, qkv[s, 1, :, cols]), MASK_VALUE)
                    power = jnp.exp(scores - jnp.max(scores, axis=-1, keepdims=True))
                    probs = (power * (1.0 / jnp.sum(power, axis=-1, keepdims=True))).astype(BF16)
                    p[s, head * 4 + b] = probs
                    mixed = nn(probs, qkv[s, 2, :, cols])
                    result = mixed if result is None else jnp.where(left, result, mixed)
                ctx[s, rows, cols] = result.astype(BF16)
            out[...] = nn(ctx[s, rows, :], wout[...])

        s_attn.start(s, part)
        save(s, p, ctx)

    each(attention)

    def first_norm(s):
        total = x[s, me].astype(F32) + s_attn.finish(s)
        unit, spread = normalize(total)
        unit0[s] = unit
        scale[s, 0] = jnp.broadcast_to(spread, (shard, LANE))
        hidden[s] = unit * gain[0:1] + bias[0:1]
        h[s, me] = hidden[s].astype(BF16)
        gh.start(s)
        save(s, unit0)

    def gru(s):
        gc.forward(s)
        gc.finish(s)
        own_c(s).wait()
        save(s, c)

        def gates(t, carry):
            rows = pl.ds(pl.multiple_of(t * LANE, LANE), LANE)
            per = block_chars // LANE
            inner = pl.ds(pl.multiple_of((t % per) * LANE, LANE), LANE)
            proj = nn(c[s, t // per, inner, :], wg[...])
            for tile in range(2):
                cols = slice(tile * LANE, (tile + 1) * LANE)
                gate = jax.nn.sigmoid(proj[:, cols] + gate_bias_pad(tile))
                cand = proj[:, (2 + tile) * LANE : (3 + tile) * LANE]
                decays[s, tile, rows, :] = (1.0 - gate) * keep[s, rows, tile : tile + 1]
                drive[tile, rows, :] = gate * cand
            return carry

        def gate_bias_pad(tile):
            return gate_bias[:, tile * LANE : (tile + 1) * LANE]

        total = 4 * block_chars
        lax.fori_loop(0, total // LANE, gates, 0)
        recur((True, False), decays.at[s], drive, states, block_chars)
        save(s, decays)

        for tile in range(2):
            low_states[s, tile] = states[tile].astype(BF16)

        def pick(t, carry):
            rows = pl.ds(pl.multiple_of(t * shard, shard), shard)
            for tile in range(2):
                ids = lax.broadcasted_iota(jnp.int32, (shard, total), 1)
                hot = (ids == pickc[s, rows, tile : tile + 1]).astype(F32).astype(BF16)
                out = nn(hot, low_states[s, tile])
                st[s, me, rows, pl.ds(tile * LANE, LANE)] = out.astype(BF16)
            return carry

        lax.fori_loop(0, 4, pick, 0)
        gs.start(s)
        save(s, low_states)

    def norm_and_gru(s):
        first_norm(s)
        gru(s)

    each(norm_and_gru)

    def ffn(s):
        gh.forward(s)
        gh.finish(s)
        save(s, h)

        def part(b, out):
            value, slope = gelu_pair(nn(h[s, b], win[...]))
            act[s, b] = value.astype(BF16)
            dact[s, b] = slope.astype(BF16)
            out[...] = nn(act[s, b], wdown[...])

        s_ffn.start(s, part)
        save(s, act, dact)

    each(ffn)

    def second_norm(s):
        unit, spread = normalize(hidden[s] + s_ffn.finish(s))
        unit1[s] = unit
        scale[s, 1] = jnp.broadcast_to(spread, (shard, LANE))
        middle[s] = unit * gain[1:2] + bias[1:2]
        mid[s, me] = middle[s].astype(BF16)
        gm.start(s)
        save(s, unit1, scale)

    each(second_norm)

    def merge(s):
        gs.forward(s)
        gm.forward(s)
        gs.finish(s)
        gm.finish(s)
        save(s, mid, st)
        def mix(t, carry):
            rows = pl.ds(pl.multiple_of(t * shard, shard), shard)
            total = nn(mid[s, t], wc[pl.ds(0, width), :])
            for u in range(4):
                weights = wc[pl.ds(width + u * 2 * LANE, 2 * LANE), :]
                total = total + nn(st[s, u, rows, :], weights)
            taps[pl.ds(pl.multiple_of(8 + t * shard, 8), shard), :] = total
            return carry

        lax.fori_loop(0, 4, mix, 0)

        def shifted(t, carry):
            rows = pl.ds(pl.multiple_of(t * shard, shard), shard)
            window = taps[pl.ds(pl.multiple_of(t * shard, 8), shard + 16), :]
            before = unpack3(window[7 : 7 + shard], channels)[0]
            center = unpack3(window[8 : 8 + shard], channels)[1]
            after = unpack3(window[9 : 9 + shard], channels)[2]
            value, slope = gelu_pair(
                before * edges[s, rows, 0:1] + center + after * edges[s, rows, 1:2]
            )
            mg[s, rows, :] = value.astype(BF16)
            dmg[s, rows, :] = slope.astype(BF16)
            return carry

        lax.fori_loop(0, 4, shifted, 0)

        def part(b, out):
            rows = pl.ds(pl.multiple_of(b * shard, shard), shard)
            out[...] = nn(mg[s, rows, :], wm[...])

        s_branch.start(s, part)
        save(s, mg, dmg)

    each(merge)

    def put_branch(s, first, value):
        span = branch.shape[3]
        at = 0
        while at < width:
            part, inner = divmod(first + at, span)
            size = min(span - inner, width - at)
            branch[s, part, :, pl.ds(inner, size)] = value[:, at : at + size]
            at += size

    def last_norms(s):
        total = s_branch.finish(s)
        rows = pl.ds(pl.multiple_of(me * shard, shard), shard)
        unit, spread = normalize(middle[s] + total[:, :width])
        outs_t[s] = (unit * gain[2:3] + bias[2:3]).astype(BF16)
        cot = cot_t[s]
        norm_grads[0:1] += jnp.sum(cot * unit, axis=0, keepdims=True)
        norm_grads[2:3] += jnp.sum(cot, axis=0, keepdims=True)
        back = normalize_back(unit, spread, cot * gain[2:3])
        res3[s] = back
        put_branch(s, 0, back.astype(BF16))
        mine = total[:, width:]
        for u in range(4):
            mine = mine + nn(st[s, u, rows, :], perm[pl.ds(u * 2 * LANE, 2 * LANE), :])
        unit, spread = normalize(mine)
        outs_c[s] = (unit * gain[3:4] + bias[3:4]).astype(BF16)
        cot = cot_c[s]
        norm_grads[1:2] += jnp.sum(cot * unit, axis=0, keepdims=True)
        norm_grads[3:4] += jnp.sum(cot, axis=0, keepdims=True)
        back = normalize_back(unit, spread, cot * gain[3:4]).astype(BF16)
        put_branch(s, width, back)
        for u in range(4):
            res4[s, u] = nt(back, perm[pl.ds(u * 2 * LANE, 2 * LANE), :]).astype(BF16)
        save(s, outs_t, outs_c, res3, res4, branch)

    each(last_norms)

    def drain(s):
        for number, (source, target) in enumerate(plan):
            local_copy(2 + number, s, source.at[s], target.at[s]).wait()

    each(drain)


def forward_call(tokens, chars, weights, small, group_slots=27):
    seqs, shard, width = tokens.shape
    length, block_chars = shard * 4, chars.shape[1]
    total = block_chars * 4
    wq, wout, win, wdown, wg, gate_bias, wc, wm = weights
    cols = wout.shape[0]
    heads = small["heads"]
    sds = jax.ShapeDtypeStruct
    big = {
        "x": ((seqs, 4, shard, width), BF16),
        "c": ((seqs, 4, block_chars, chars.shape[2]), BF16),
        "qkv": ((seqs, 3, length, cols), BF16),
        "p": ((seqs, heads * 4, shard, length), BF16),
        "ctx": ((seqs, length, cols), BF16),
        "h": ((seqs, 4, shard, width), BF16),
        "act": ((seqs, 4, shard, win.shape[1]), BF16),
        "dact": ((seqs, 4, shard, win.shape[1]), BF16),
        "mid": ((seqs, 4, shard, width), BF16),
        "st": ((seqs, 4, length, 2 * LANE), BF16),
        "mg": ((seqs, length, wm.shape[0]), BF16),
        "dmg": ((seqs, length, wm.shape[0]), BF16),
        "states": ((seqs, 2, total, LANE), BF16),
        "decay": ((seqs, 2, total, LANE), F32),
        "unit0": ((seqs, shard, width), F32),
        "unit1": ((seqs, shard, width), F32),
        "scale": ((seqs, 2, shard, LANE), F32),
        "res3": ((seqs, shard, width), F32),
        "res4": ((seqs, 4, shard, 2 * LANE), BF16),
        "branch": ((seqs, 2 * width // length, shard, length), BF16),
    }
    rows = ((seqs, shard, width), F32)
    low_rows = ((seqs, shard, width), BF16)
    scratch = list(big.values()) + [
        rows, rows, low_rows, low_rows,
        ((2, total, LANE), F32),
        ((2, total, LANE), F32),
        ((length + 16, wc.shape[1]), F32),
        ((8 * LANE, width), BF16),
        ((seqs, 3, shard, 2 * width), BF16), ((seqs, 3, shard, 2 * width), BF16),
        ((seqs, shard, 2 * width), F32), ((shard, 2 * width), F32),
    ]
    anyspace = pl.BlockSpec(memory_space=pl.ANY)
    vmem = pl.BlockSpec(memory_space=pltpu.VMEM)
    out_shapes = [sds(low_rows[0], BF16)] * 2 + [sds(*v) for v in big.values()]
    ins = (
        tokens, chars, wq, wout, win, wdown, wg, gate_bias, wc, wm, small["gain"], small["bias"],
        small["cot_t"], small["cot_c"], small["segc"], small["segr"], small["pickc"],
        small["keep"], small["edges"],
    )
    outs = pl.pallas_call(
        functools.partial(forward_kernel, small["units"], small["channels"]),
        out_shape=out_shapes + [sds((4, width), F32)],
        in_specs=[anyspace] * 2 + [vmem] * (len(ins) - 2),
        out_specs=[anyspace] * len(out_shapes) + [vmem],
        scratch_shapes=[pltpu.VMEM(*v) for v in scratch]
        + [
            pltpu.SemaphoreType.DMA((group_slots * seqs,)),
            pltpu.SemaphoreType.DMA((group_slots * seqs,)),
            pltpu.SemaphoreType.DMA((26 * seqs,)),
        ],
        compiler_params=pltpu.CompilerParams(
            collective_id=0, has_side_effects=True, vmem_limit_bytes=62 * MIB
        ),
    )(*ins)
    names = ["token_out", "char_out"] + list(big) + ["norm_grads"]
    return dict(zip(names, outs))


class Plane:
    def __init__(self, send, recv, marks):
        self.index = lax.axis_index("dp")
        self.x, self.z = self.index % 2, self.index // 2
        self.send, self.recv, self.marks, self.used, self.marked = send, recv, marks, 0, 0

    def mark(self):
        self.marked += 1
        return self.marks.at[self.marked - 1]

    def take(self, count):
        first = self.used
        self.used += count
        return [first + i for i in range(count)]

    def peer(self, way):
        if way == "x":
            return self.index + 1 - 2 * self.x
        return (self.index + (2 if way == "up" else 6)) % 8

    def pair(self, bit):
        digit = self.index // (1 << bit) % 2
        return self.index + (1 - 2 * digit) * (1 << bit)

    def copy(self, slot, source, target, peer):
        return pltpu.make_async_remote_copy(
            src_ref=source,
            dst_ref=target,
            send_sem=self.send.at[slot],
            recv_sem=self.recv.at[slot],
            device_id={"dp": peer},
            device_id_type=pl.DeviceIdType.MESH,
        )


class Reduce:
    steps = 9

    def __init__(self, plane, buf, out, land, first, land_first, rows, x_first):
        self.plane, self.buf, self.out, self.land = plane, buf, out, land
        self.first, self.land_first, self.rows, self.x_first = first, land_first, rows, x_first
        self.slots = plane.take(14)
        self.mark = plane.mark()
        x, z = plane.x, plane.z
        if x_first:
            self.quarter, self.half = rows // 8, rows // 2
            self.z_base, self.x_base = first + x * self.half, first
        else:
            self.quarter, self.half = rows // 4, rows // 8
            self.z_base, self.x_base = first, first + z * self.quarter
        self.x_land = land_first + 5 * self.quarter

    @staticmethod
    def landing_rows(rows, x_first):
        return 5 * rows // 8 + rows // 2 if x_first else 5 * rows // 4 + rows // 8

    def rows_of(self, ref, start, size):
        return ref.at[pl.ds(pl.multiple_of(start, 16), size), :]

    def add(self, start, land_start, size):
        def one(i, carry):
            rows = pl.ds(pl.multiple_of(start + i * 16, 16), 16)
            more = pl.ds(pl.multiple_of(land_start + i * 16, 16), 16)
            total = self.buf[rows, :].astype(F32) + self.land[more, :].astype(F32)
            self.buf[rows, :] = total.astype(BF16)
            return carry

        lax.fori_loop(0, size // 16, one, 0)

    def gather_copy(self, way, step, z):
        piece = 3 - step + z if way == "up" else step - 3 + z
        slot = piece if way == "up" else piece + (4 - piece) * (step // 2)
        return self.plane.copy(
            self.slots[step if way == "up" else 3 + step],
            self.rows_of(self.buf, self.z_base + piece * self.quarter, self.quarter),
            self.rows_of(self.land, self.land_first + slot * self.quarter, self.quarter),
            self.plane.peer(way),
        )

    def gather_send(self, step):
        z = self.plane.z
        pl.when(step >= z)(lambda: self.gather_copy("up", step, z).start())
        pl.when(step >= 3 - z)(lambda: self.gather_copy("down", step, z).start())

    def gather_wait(self, step):
        z = self.plane.z

        @pl.when((z >= 1) & (step >= z - 1))
        def _():
            self.gather_copy("up", step, z - 1).wait_recv()
            piece = 3 - step + z - 1
            self.add(
                self.z_base + piece * self.quarter,
                self.land_first + piece * self.quarter,
                self.quarter,
            )

        @pl.when((z <= 2) & (step >= 2 - z))
        def _():
            self.gather_copy("down", step, z + 1).wait_recv()
            piece = step - 3 + z + 1
            slot = piece if step < 2 else 4
            self.add(
                self.z_base + piece * self.quarter,
                self.land_first + slot * self.quarter,
                self.quarter,
            )

        pl.when(step >= z)(lambda: self.gather_copy("up", step, z).wait_send())
        pl.when(step >= 3 - z)(lambda: self.gather_copy("down", step, z).wait_send())

    def spread_copy(self, way, step, z):
        piece = z - step if way == "up" else z + step
        start = self.z_base + piece * self.quarter
        target = self.rows_of(self.out, start, self.quarter)
        source = target
        if self.x_first and step == 0:
            source = self.rows_of(self.buf, start, self.quarter)
        slot = self.slots[6 + step if way == "up" else 9 + step]
        return self.plane.copy(slot, source, target, self.plane.peer(way))

    def spread_send(self, step):
        z = self.plane.z
        pl.when((z <= 2) & (step <= z))(lambda: self.spread_copy("up", step, z).start())
        pl.when((z >= 1) & (step <= 3 - z))(lambda: self.spread_copy("down", step, z).start())

    def spread_wait(self, step):
        z = self.plane.z
        pl.when((z >= 1) & (step <= z - 1))(lambda: self.spread_copy("up", step, z - 1).wait_recv())
        pl.when((z <= 2) & (step <= 2 - z))(lambda: self.spread_copy("down", step, z + 1).wait_recv())
        pl.when((z <= 2) & (step <= z))(lambda: self.spread_copy("up", step, z).wait_send())
        pl.when((z >= 1) & (step <= 3 - z))(lambda: self.spread_copy("down", step, z).wait_send())

    def halve(self):
        other = self.x_base + (1 - self.plane.x) * self.half
        return self.plane.copy(
            self.slots[12],
            self.rows_of(self.buf, other, self.half),
            self.rows_of(self.land, self.x_land, self.half),
            self.plane.peer("x"),
        )

    def halve_wait(self):
        self.halve().wait()
        self.add(self.x_base + self.plane.x * self.half, self.x_land, self.half)

    def double(self):
        start = self.x_base + self.plane.x * self.half
        target = self.rows_of(self.out, start, self.half)
        source = target if self.x_first else self.rows_of(self.buf, start, self.half)
        return self.plane.copy(self.slots[13], source, target, self.plane.peer("x"))

    def keep(self):
        if self.x_first:
            start, size = self.z_base + self.plane.z * self.quarter, self.quarter
        else:
            start, size = self.x_base + self.plane.x * self.half, self.half
        return pltpu.make_async_copy(
            self.rows_of(self.buf, start, size), self.rows_of(self.out, start, size), self.mark
        )

    def step(self, number):
        if self.x_first:
            if number == 0:
                self.halve().start()
            elif number == 1:
                self.halve_wait()
                self.gather_send(0)
            elif number <= 3:
                self.gather_wait(number - 2)
                self.gather_send(number - 1)
            elif number == 4:
                self.gather_wait(2)
                self.keep().start()
                self.spread_send(0)
            elif number <= 6:
                self.spread_wait(number - 5)
                self.spread_send(number - 4)
            elif number == 7:
                self.spread_wait(2)
                self.keep().wait()
                self.double().start()
            else:
                self.double().wait()
        else:
            if number == 0:
                self.gather_send(0)
            elif number <= 2:
                self.gather_wait(number - 1)
                self.gather_send(number)
            elif number == 3:
                self.gather_wait(2)
                self.halve().start()
            elif number == 4:
                self.halve_wait()
                self.keep().start()
                self.double().start()
            elif number == 5:
                self.double().wait()
                self.keep().wait()
                self.spread_send(0)
            elif number <= 7:
                self.spread_wait(number - 6)
                self.spread_send(number - 5)
            else:
                self.spread_wait(2)


SAVED = (
    "branch", "mg", "dmg", "mid", "st", "res3", "res4", "unit0", "unit1", "scale", "act", "dact",
    "h", "p", "qkv", "ctx", "x", "c", "states", "decay",
)
GRADS = ("merge", "conv", "down", "win", "gru", "out", "qkv")
HEADS_OF = dict(zip(GRADS, (0, 1024, 768, 256, 0, 0, 512)))
SCHEDULE = (
    (0, 10, 20,),
    (),
    (1, 21,),
    (2, 11,),
    (22,),
    (30, 3,),
    (40, 50, 12,),
    (),
    (23,),
    (),
    (51,),
    (13, 31,),
    (4,),
    (52, 41,),
    (24, 14, 5,),
    (32,),
    (25,),
    (70, 80, 90, 53, 15, 42, 6,),
    (33, 71, 26,),
    (91, 43, 16,),
    (81, 34, 7, 54, 72, 92, 27, 44,),
    (82, 17,),
    (55, 73, 35, 93,),
    (60, 83, 8, 28,),
    (45, 61,),
    (84, 56, 18, 62, 74, 36,),
    (94, 46, 85, 63, 75, 95,),
    (64, 57, 65, 37, 47, 86, 76, 96, 58, 66, 87, 38, 77, 97, 67, 48, 78, 98, 68, 88,),
)


def backward_kernel(units, channels, dp_size, *refs):
    refs = list(refs)
    take = lambda count: [refs.pop(0) for _ in range(count)]
    hbm = SimpleNamespace(**dict(zip(SAVED, take(len(SAVED)))))
    wq, wout, win, wdown, wg, gate_bias, wc, wm, gain, pickr, edges, norm_in = take(12)
    grad_tokens, grad_chars = take(2)
    grads_out = dict(zip(GRADS, take(len(GRADS))))
    (small_out,) = take(1)
    names = [n for n in SAVED if n not in ("branch", "states", "decay", "p", "x")]
    v = SimpleNamespace(**dict(zip(names, take(len(names)))))
    (pb, states, decay, drive, dpre, dyk, fg, gtok, dproj, gru_acc, res2, res1, ds, parts,
     stage, got, held, temp, cstage, cgot, cheld, ctemp) = take(22)
    land = dict(zip(GRADS, take(len(GRADS))))
    big = SimpleNamespace(**dict(zip(GRADS, take(len(GRADS)))))
    small, small_land, send, recv, dsend, drecv, local, marks = take(8)

    seqs, shard, width = grad_tokens.shape
    length = 4 * shard
    block_chars = grad_chars.shape[1]
    total = 4 * block_chars
    heads = pb.shape[1] // 4
    cols = v.ctx.shape[2]
    g = Group(send, recv, seqs)
    me = g.me
    inside = dp_size == 8
    plane = Plane(dsend, drecv, marks)

    def each(body):
        def run(seq, carry):
            body(seq)
            return carry

        lax.fori_loop(0, seqs, run, 0)

    def load(name):
        index = names.index(name)
        return pltpu.make_async_copy(getattr(hbm, name), getattr(v, name), local.at[index])

    spare = len(names)
    p_copy = lambda: pltpu.make_async_copy(hbm.p, pb, local.at[spare])
    x_copy = lambda: pltpu.make_async_copy(hbm.x, v.h, local.at[39])

    def states_copy(s):
        return pltpu.make_async_copy(hbm.states.at[s], states, local.at[spare + 1])

    def decay_copy(s, tile):
        return pltpu.make_async_copy(
            hbm.decay.at[s, tile], decay.at[tile], local.at[spare + 2 + tile]
        )

    def out_copy(kind, s):
        source, target = ((res1, grad_tokens), (cheld, grad_chars))[kind]
        return pltpu.make_async_copy(
            source.at[s], target.at[s], local.at[spare + 4 + kind * seqs + s]
        )

    pieces = 2 * width // length
    gb = Gather(
        g, pb, hbm.branch, place=lambda s, t: pb.at[s, pl.ds(t * pieces, pieces)]
    )
    gf, ga = Gather(g, fg), Gather(g, v.mid)
    pick = lambda ref: (lambda s, i: ref.at[s, i])
    own = lambda ref: (lambda s: ref.at[s])
    s_mid = Scatter(g, pick(stage), pick(got), own(held), temp)
    s_hid = Scatter(g, pick(stage), pick(got), own(held), temp)
    s_tok = Scatter(g, pick(stage), pick(got), own(held), temp)
    s_chr = Scatter(g, pick(cstage), pick(cgot), own(cheld), ctemp)
    s_cout = Scatter(g, pick(cstage), pick(cgot), own(cheld), ctemp)

    def own_branch(s):
        return pltpu.make_async_copy(
            hbm.branch.at[s], gb.at(s, me), local.at[spare + 4 + 2 * seqs + s]
        )

    each(lambda s: own_branch(s).start())
    for name in ("dmg", "res4", "mg", "mid", "st"):
        load(name).start()
    states_copy(0).start()
    for tile in range(2):
        decay_copy(0, tile).start()
    for name in names:
        if name not in ("dmg", "res4", "mg", "mid", "st"):
            load(name).start()

    barrier = pltpu.get_barrier_semaphore()
    places = [{"tensor": g.pair}, {"tensor": g.far}]
    if inside:
        places += [{"dp": plane.peer(way)} for way in ("x", "up", "down")]
        places += [{"dp": plane.pair(2)}]
    for place in places:
        pl.semaphore_signal(barrier, inc=1, device_id=place, device_id_type=pl.DeviceIdType.MESH)
    pl.semaphore_wait(barrier, len(places))
    each(gb.start)
    dpre[...] = jnp.zeros_like(dpre)
    small[...] = jnp.zeros_like(small)
    small[0, pl.ds(0, 4), :] = norm_in[...]
    lane = lax.broadcasted_iota(jnp.int32, (shard, LANE), 1)
    left = lane < HD
    for name in ("dmg", "res4"):
        load(name).wait()

    def block_rows(t, size):
        return pl.ds(pl.multiple_of(t * size, size), size)

    def merge_back(s):
        gb.forward(s)
        gb.finish(s)
        own_branch(s).wait()

        def inner(t, carry):
            rows = block_rows(t, shard)
            back = None
            for j in range(pieces):
                piece = nt(pb[s, t * pieces + j], wm[:, j * length : (j + 1) * length])
                back = piece if back is None else back + piece
            dpre[pl.ds(pl.multiple_of(8 + t * shard, 8), shard), :] = (
                (back * v.dmg[s, rows, :].astype(F32)).astype(BF16).astype(F32)
            )
            return carry

        lax.fori_loop(0, 4, inner, 0)

        def taps(t, carry):
            rows = block_rows(t, shard)
            window = dpre[pl.ds(pl.multiple_of(t * shard, 8), shard + 16), :]
            marks = edges[s, rows, :]
            before = window[9 : 9 + shard] * marks[:, 2:3]
            after = window[7 : 7 + shard] * marks[:, 3:4]
            dyk[s, rows, :] = pack3(
                [before, window[8 : 8 + shard], after], channels
            ).astype(BF16)
            return carry

        lax.fori_loop(0, 4, taps, 0)

        def mid_part(b, out):
            out[...] = nt(dyk[s, block_rows(b, shard), :], wc[pl.ds(0, width), :])

        s_mid.start(s, mid_part)

        def char_part(b, out):
            first = pl.multiple_of(width + b * 2 * LANE, 2 * LANE)
            out[...] = nt(dyk[s], wc[pl.ds(first, 2 * LANE), :])
            out[block_rows(me, shard), :] += v.res4[s, b].astype(F32)

        s_chr.start(s, char_part)

    each(merge_back)
    for name in ("mg", "mid", "st"):
        load(name).wait()

    tokens = seqs * length
    half_w = width
    for j in range(pieces):
        right = jnp.concatenate(
            [pb[s, t * pieces + j] for s in range(seqs) for t in range(4)], axis=0
        )
        out = tn(v.mg[...].reshape(tokens, -1), right)[:channels].astype(BF16)
        at = 0
        while at < length:
            part, inside_at = divmod(j * length + at, half_w)
            size = min(length - at, half_w - inside_at)
            big.merge[pl.ds(part * channels, channels), pl.ds(inside_at, size)] = out[
                :, at : at + size
            ]
            at += size
    step_w = 2 * LANE

    def conv_mid(j, carry):
        colsj = pl.ds(pl.multiple_of(j * step_w, step_w), step_w)
        out = tn(v.mid[:, :, :, colsj].reshape(tokens, step_w), dyk[...].reshape(tokens, -1))
        big.conv[block_rows(j, step_w), :] = out.astype(BF16)
        return carry

    lax.fori_loop(0, width // step_w, conv_mid, 0)

    def conv_char(t, carry):
        out = tn(v.st[:, t].reshape(tokens, 2 * LANE), dyk[...].reshape(tokens, -1))
        for d in range(2):
            first = pl.multiple_of(width + d * 4 * units + t * units, 16)
            big.conv[pl.ds(first, units), :] = out[d * LANE : d * LANE + units].astype(BF16)
        return carry

    lax.fori_loop(0, 4, conv_char, 0)
    p_copy().start()

    sums = []
    for name in GRADS if inside else ():
        height, at = getattr(big, name).shape[0], 0
        pieces_of = ((0, HEADS_OF[name], True), (HEADS_OF[name], height - HEADS_OF[name], False))
        for first, size, x_first in pieces_of:
            if size:
                sums.append(
                    Reduce(
                        plane, getattr(big, name), grads_out[name], land[name], first, at, size,
                        x_first,
                    )
                )
                at += Reduce.landing_rows(size, x_first)
    fired = [0] * len(sums)

    def fire(hook):
        for entry in SCHEDULE[hook] if inside else ():
            which, number = divmod(entry, 10)
            fired[which] += 1
            sums[which].step(number)

    def fire_in(seq, hook, stride):
        for k in range(2):
            pl.when(seq == k)(functools.partial(fire, hook + k * stride))

    fire(0)

    def second_back(s):
        incoming = v.res3[s] + s_mid.finish(s)
        unit = v.unit1[s]
        small[0, 5:6] += jnp.sum(incoming * unit, axis=0, keepdims=True)
        small[0, 7:8] += jnp.sum(incoming, axis=0, keepdims=True)
        spread = v.scale[s, 1][:, 0:1]
        res2[s] = normalize_back(unit, spread, incoming * gain[1:2])
        fg[s, me] = res2[s].astype(BF16)
        gtok[s] = s_chr.finish(s).astype(BF16)
        gf.start(s)
        fire_in(s, 1, 1)

    for name in ("res3", "unit1", "scale"):
        load(name).wait()
    each(second_back)
    for name in ("dact", "act", "h"):
        load(name).wait()

    def ffn_back(s):
        gf.forward(s)
        gf.finish(s)

        def part(b, out):
            back = nt(fg[s, b], wdown[...]) * v.dact[s, b].astype(F32)
            v.dact[s, b] = back.astype(BF16)
            out[...] = nt(v.dact[s, b], win[...])

        s_hid.start(s, part)
        fire_in(s, 3, 1)

    each(ffn_back)

    def ffn_weights(j, carry):
        colsj = pl.ds(pl.multiple_of(j * step_w, step_w), step_w)
        out = tn(v.act[:, :, :, colsj].reshape(tokens, step_w), fg[...].reshape(tokens, width))
        big.down[block_rows(j, step_w), :] = out.astype(BF16)
        return carry

    lax.fori_loop(0, big.down.shape[0] // step_w, ffn_weights, 0)
    fire(5)

    def in_weights(j, carry):
        colsj = pl.ds(pl.multiple_of(j * step_w, step_w), step_w)
        out = tn(
            v.h[:, :, :, colsj].reshape(tokens, step_w), v.dact[...].reshape(tokens, -1)
        )
        big.win[block_rows(j, step_w), :] = out.astype(BF16)
        return carry

    lax.fori_loop(0, width // step_w, in_weights, 0)
    x_copy().start()
    fire(6)
    load("unit0").wait()

    def first_back(s):
        incoming = res2[s] + s_hid.finish(s)
        unit = v.unit0[s]
        small[0, 4:5] += jnp.sum(incoming * unit, axis=0, keepdims=True)
        small[0, 6:7] += jnp.sum(incoming, axis=0, keepdims=True)
        spread = v.scale[s, 0][:, 0:1]
        res1[s] = normalize_back(unit, spread, incoming * gain[0:1])
        v.mid[s, me] = res1[s].astype(BF16)
        ga.start(s)
        fire_in(s, 7, 1)

    each(first_back)
    hops = [("t", g.pair), ("t", g.far)] + ([("d", k) for k in range(3)] if inside else [])
    slots_t, slots_d = g.slots(2), plane.take(3)

    def small_copy(number):
        kind, where = hops[number]
        source, target = small.at[number], small_land.at[number]
        if kind == "t":
            return g.copy(slots_t[number], 0, source, target, where)
        return plane.copy(slots_d[where], source, target, plane.pair(where))

    def small_step(number):
        if number > 0:
            small_copy(number - 1).wait()
            value, more = small[number - 1], small_land[number - 1]
            small[number, pl.ds(0, 8), :] = value[:8] + more[:8]
            rest = small[6, pl.ds(0, 8), :] if number <= 2 else value[8:] + more[8:]
            small[number, pl.ds(8, 8), :] = rest
        if number < len(hops):
            small_copy(number).start()

    if not inside:
        hops = []
    small_step(0) if hops else None
    for name in ("qkv", "ctx"):
        load(name).wait()
    p_copy().wait()

    def attention_back(s):
        ga.forward(s)
        ga.finish(s)
        dctx = v.dmg

        def context(t, carry):
            dctx[s, block_rows(t, shard), :] = nt(v.mid[s, t], wout[...]).astype(BF16)
            return carry

        lax.fori_loop(0, 4, context, 0)
        for tile in range(cols // LANE):
            lanes = pl.ds(tile * LANE, LANE)
            for half in range(2):
                head = 2 * tile + half
                if head >= heads:
                    continue
                paired = 2 * tile + 1 < heads

                def rows_of(b, carry):
                    rows = block_rows(b, shard)
                    grad = dctx[s, rows, lanes]
                    if paired:
                        grad = jnp.where(left if half == 0 else ~left, grad, jnp.zeros_like(grad))
                    back = nt(grad, v.qkv[s, 2, :, lanes])
                    probs = pb[s, head * 4 + b].astype(F32)
                    row_dot = jnp.sum(probs * back, axis=-1, keepdims=True)
                    ds[b] = (probs * (back - row_dot)).astype(BF16)
                    out = nn(ds[b], v.qkv[s, 1, :, lanes])
                    if half == 1:
                        out = jnp.where(left, ctemp[rows, lanes], out)
                    ctemp[rows, lanes] = out
                    return carry

                lax.fori_loop(0, 4, rows_of, 0)
                keys = tn(ds[...].reshape(length, length), v.qkv[s, 0, :, lanes])
                values = tn(
                    pb[s, pl.ds(head * 4, 4)].reshape(length, length), dctx[s, :, lanes]
                )
                if half == 1:
                    wide_left = lax.broadcasted_iota(jnp.int32, (length, LANE), 1) < HD
                    keys = jnp.where(wide_left, parts[0, :, lanes], keys)
                    values = jnp.where(wide_left, parts[1, :, lanes], values)
                parts[0, :, lanes] = keys
                parts[1, :, lanes] = values
                fire_in(s, 9 + head, 4)

        def pack(t, carry):
            rows = block_rows(t, shard)
            query = ctemp[rows, :].astype(BF16).astype(F32) * 0.125
            dyk[s, rows, :] = pack3(
                [query, parts[0, rows, :], parts[1, rows, :]], HD * heads
            ).astype(BF16)
            return carry

        lax.fori_loop(0, 4, pack, 0)

        def part(b, out):
            out[...] = nt(dyk[s, block_rows(b, shard), :], wq[...])

        s_tok.start(s, part)

        fire_in(s, 12, 4)

    each(attention_back)
    small_step(1) if hops else None

    x_copy().wait()

    def qkv_weights(j, carry):
        colsj = pl.ds(pl.multiple_of(j * step_w, step_w), step_w)
        out = tn(v.h[:, :, :, colsj].reshape(tokens, step_w), dyk[...].reshape(tokens, -1))
        big.qkv[block_rows(j, step_w), :] = out.astype(BF16)
        return carry

    lax.fori_loop(0, width // step_w, qkv_weights, 0)
    big.out[...] = tn(
        v.ctx[...].reshape(tokens, -1), v.mid[...].reshape(tokens, width)
    ).astype(BF16)
    fire(17)

    load("c").wait()

    def gru_back(s):
        def spread_out(t, carry):
            rows = block_rows(t, LANE)
            for tile in range(2):
                ids = lax.broadcasted_iota(jnp.int32, (LANE, length), 0) + t * LANE
                hot = (ids == pickr[s, tile : tile + 1, :]).astype(F32).astype(BF16)
                drive[tile, rows, :] = nn(hot, gtok[s, :, pl.ds(tile * LANE, LANE)])
            return carry

        lax.fori_loop(0, total // LANE, spread_out, 0)
        fire_in(s, 18, 3)
        for tile in range(2):
            decay_copy(s, tile).wait()
        recur((False, True), decay, drive, drive, block_chars, back=True)
        fire_in(s, 19, 3)
        states_copy(s).wait()

        @pl.when(s == 0)
        def _():
            gru_acc[...] = jnp.zeros_like(gru_acc)

        def part(b, out):
            def finish(t, sums):
                inner = block_rows(t, LANE)
                rows = pl.ds(pl.multiple_of(b * block_chars + t * LANE, LANE), LANE)
                proj = nn(v.c[s, b, inner, :], wg[...])
                new = []
                for tile in range(2):
                    colst = slice(tile * LANE, (tile + 1) * LANE)
                    gate = jax.nn.sigmoid(proj[:, colst] + gate_bias[:, colst])
                    cand = proj[:, (2 + tile) * LANE : (3 + tile) * LANE]
                    flow = drive[tile, rows, :] * gate
                    logit = flow * (cand - states[tile, rows, :].astype(F32))
                    dproj[inner, pl.ds(tile * LANE, LANE)] = logit.astype(BF16)
                    dproj[inner, pl.ds((2 + tile) * LANE, LANE)] = flow.astype(BF16)
                    new.append(sums[tile] + jnp.sum(logit, axis=0, keepdims=True))
                return tuple(new)

            zero = jnp.zeros((1, LANE), F32)
            sums = lax.fori_loop(0, block_chars // LANE, finish, (zero, zero))
            for tile in range(2):
                small[6, 0:1, pl.ds(tile * LANE, LANE)] += sums[tile]
            out[...] = nt(dproj[...], wg[...])
            gru_acc[...] += tn(v.c[s, b], dproj[...])

        s_cout.start(s, part)

        @pl.when(s + 1 < seqs)
        def _():
            states_copy(s + 1).start()
            for tile in range(2):
                decay_copy(s + 1, tile).start()

        if seqs > 1:
            pl.when(s == 0)(functools.partial(fire, 20))

    each(gru_back)
    big.gru[...] = gru_acc[...].astype(BF16)
    small_step(2) if hops else None
    fire(23)

    def last(s):
        res1[s] = res1[s] + s_tok.finish(s)
        out_copy(0, s).start()
        cheld[s] = s_cout.finish(s)
        out_copy(1, s).start()

    each(last)

    def emit(name):
        return pltpu.make_async_copy(
            getattr(big, name), grads_out[name], local.at[spare + 4 + 3 * seqs + GRADS.index(name)]
        )

    if inside:
        fire(24)
        small_step(3)
        fire(25)
        small_step(4)
        fire(26)
        small_step(5)
        fire(27)
        assert all(count == Reduce.steps for count in fired)
    else:
        for name in GRADS:
            emit(name).start()
        for name in GRADS:
            emit(name).wait()
    small_out[...] = small[len(hops)]
    if not inside:
        small_out[pl.ds(8, 8), :] = small[6, pl.ds(0, 8), :]
    each(lambda s: (out_copy(0, s).wait(), out_copy(1, s).wait()))


def backward_call(saved, weights, small, dp_size):
    wq, wout, win, wdown, wg, gate_bias, wc, wm = weights
    sds = jax.ShapeDtypeStruct
    seqs, shard, width = saved["res3"].shape
    length = shard * 4
    block_chars, char_width = saved["c"].shape[2:]
    total = 4 * block_chars
    cols, packed = wout.shape[0], wc.shape[1]
    channels = small["channels"]
    saved_in = [saved[n] for n in SAVED]
    names = [n for n in SAVED if n not in ("branch", "states", "decay", "p", "x")]
    shapes = [(saved[n].shape, saved[n].dtype) for n in names]
    grads = {
        "merge": (2 * channels, width), "conv": (2 * width, packed),
        "down": (win.shape[1], width), "win": (width, win.shape[1]),
        "gru": (char_width, 4 * LANE), "out": (cols, width), "qkv": (width, wq.shape[1]),
    }
    pad = (seqs, 3, shard, width)
    cpad = (seqs, 3, length, 2 * LANE)
    scratch = shapes + [
        (saved["p"].shape, BF16),
        ((2, total, LANE), BF16),
        ((2, total, LANE), F32),
        ((2, total, LANE), F32),
        ((length + 16, wm.shape[0]), F32),
        ((seqs, length, packed), BF16),
        ((seqs, 4, shard, width), BF16),
        ((seqs, length, 2 * LANE), BF16),
        ((block_chars, 4 * LANE), BF16),
        ((char_width, 4 * LANE), F32),
        ((seqs, shard, width), F32),
        ((seqs, shard, width), F32),
        ((4, shard, length), BF16),
        ((2, length, cols), F32),
        (pad, BF16), (pad, BF16), ((seqs, shard, width), F32), ((shard, width), F32),
        (cpad, BF16), (cpad, BF16), ((seqs, length, 2 * LANE), F32), ((length, 2 * LANE), F32),
    ]
    for name, (rows, last) in grads.items():
        head = HEADS_OF[name]
        landing = Reduce.landing_rows(head, True) + Reduce.landing_rows(rows - head, False)
        scratch.append(((landing if dp_size == 8 else 16, last), BF16))
    scratch += [(shape, BF16) for shape in grads.values()]
    scratch += [((7, 16, width), F32), ((5, 16, width), F32)]
    anyspace = pl.BlockSpec(memory_space=pl.ANY)
    vmem = pl.BlockSpec(memory_space=pltpu.VMEM)
    ins = saved_in + list(weights) + [small["gain"], small["pickr"], small["edges"], saved["norm_grads"]]
    outs = pl.pallas_call(
        functools.partial(backward_kernel, small["units"], channels, dp_size),
        out_shape=[sds((seqs, shard, width), F32), sds((seqs, block_chars, char_width), F32)]
        + [sds(shape, BF16) for shape in grads.values()]
        + [sds((16, width), F32)],
        in_specs=[anyspace] * len(saved_in) + [vmem] * (len(ins) - len(saved_in)),
        out_specs=[anyspace] * (2 + len(grads)) + [vmem],
        scratch_shapes=[pltpu.VMEM(*one) for one in scratch]
        + [
            pltpu.SemaphoreType.DMA((32 * seqs,)),
            pltpu.SemaphoreType.DMA((32 * seqs,)),
            pltpu.SemaphoreType.DMA((160,)),
            pltpu.SemaphoreType.DMA((160,)),
            pltpu.SemaphoreType.DMA((40,)),
            pltpu.SemaphoreType.DMA((12,)),
        ],
        compiler_params=pltpu.CompilerParams(
            collective_id=1, has_side_effects=True, vmem_limit_bytes=63 * MIB
        ),
    )(*ins)
    names = ["grad_tokens", "grad_chars"] + list(grads) + ["small"]
    return dict(zip(names, outs))


def local(
    tokens,
    characters,
    doc_lengths,
    token_chars,
    w_qkv,
    w_out,
    w_in,
    w_down,
    w_gru,
    gate_bias,
    w_conv,
    w_merge,
    norm_gain,
    norm_bias,
    token_cot,
    char_cot,
):
    micro_count = tokens.shape[0]
    shard_len = tokens.shape[1]
    model_width = tokens.shape[2]
    char_width = characters.shape[2]
    group_size = lax.axis_size("tensor")
    group_rank = lax.axis_index("tensor")
    length = shard_len * group_size
    char_total = characters.shape[1] * group_size
    head_cols = w_qkv.shape[2]
    heads_here = head_cols // HD
    units_here = w_gru.shape[3]
    merge_here = w_conv.shape[2]
    gru_matrix, gru_bias = gru_weights(w_gru, gate_bias)
    spare = -head_cols % LANE
    more = -merge_here % LANE
    wq = jnp.pad(
        w_qkv.reshape(model_width, 3 * head_cols), ((0, 0), (0, -3 * head_cols % LANE))
    )
    wout = jnp.pad(w_out, ((0, spare), (0, 0)))
    wm = jnp.pad(w_merge.reshape(merge_here, 2 * model_width), ((0, more), (0, 0)))
    conv = jnp.swapaxes(w_conv, 0, 1).reshape(2 * model_width, 3 * merge_here)
    conv = jnp.pad(conv, ((0, 0), (0, -3 * merge_here % LANE)))
    conv_char = conv[model_width:].reshape(2, group_size, units_here, -1)
    conv_char = jnp.pad(
        jnp.swapaxes(conv_char, 0, 1), ((0, 0), (0, 0), (0, LANE - units_here), (0, 0))
    )
    wc = jnp.concatenate(
        [conv[:model_width], conv_char.reshape(group_size * 2 * LANE, -1)], axis=0
    )
    layouts = [layout(doc_lengths[i], token_chars[i], char_total) for i in range(micro_count)]
    stacked_layout = [jnp.stack(parts) for parts in zip(*layouts)]
    segment, first_char, last_char, keep_forward, keep_backward, prev_ok, next_ok = stacked_layout
    block_chars = characters.shape[1]
    steps = block_chars // 8

    def reorder(rows):
        split = rows.reshape(micro_count, -1, 8, steps, rows.shape[-1])
        return jnp.swapaxes(split, 2, 3).reshape(rows.shape)

    keep = reorder(jnp.stack([keep_forward, keep_backward], axis=2))
    picks = jnp.stack([last_char, first_char], axis=2)
    inner = picks % block_chars
    picks = picks - inner + inner % steps * 8 + inner // steps
    zero = jnp.zeros_like(prev_ok[:, :1])
    small = dict(
        gain=norm_gain, bias=norm_bias, cot_t=token_cot, cot_c=char_cot,
        segc=segment[:, :, None], segr=segment[:, None, :], pickc=picks, keep=keep,
        pickr=jnp.swapaxes(picks, 1, 2),
        edges=jnp.stack(
            [
                prev_ok,
                next_ok,
                jnp.concatenate([prev_ok[:, 1:], zero], axis=1),
                jnp.concatenate([zero, next_ok[:, :-1]], axis=1),
            ],
            axis=2,
        ),
        heads=heads_here, units=units_here, channels=merge_here,
    )
    weights = (wq, wout, w_in, w_down, gru_matrix, gru_bias, wc, wm)
    fw = forward_call(tokens, reorder(characters), weights, small)
    dp_size = lax.axis_size("dp")
    bw = backward_call(fw, weights, small, dp_size)
    rows = bw["small"]
    gate_row = rows[8, : 2 * LANE]
    grads = {name: bw[name] for name in GRADS}
    if dp_size != 8:
        grads, gate_row = lax.psum((grads, gate_row), "dp")
        rows = lax.psum(rows, ("dp", "tensor"))
    grads = {name: value.astype(F32) for name, value in grads.items()}
    grad_conv = jnp.stack(
        [grads["conv"][:, k * merge_here : (k + 1) * merge_here] for k in range(3)], axis=0
    )
    grad_merge = grads["merge"].reshape(2, merge_here, model_width)
    grad_gru = grads["gru"].reshape(char_width, 2, 2, LANE)[..., :units_here]
    grad_chars = jnp.swapaxes(
        bw["grad_chars"].reshape(micro_count, steps, 8, char_width), 1, 2
    )
    return (
        fw["token_out"],
        fw["char_out"],
        bw["grad_tokens"],
        grad_chars.reshape(bw["grad_chars"].shape),
        grads["qkv"][:, : 3 * head_cols].reshape(model_width, 3, head_cols),
        grads["out"][:head_cols],
        grads["win"],
        grads["down"],
        jnp.swapaxes(grad_gru, 1, 2),
        gate_row.reshape(2, LANE)[:, :units_here],
        grad_conv,
        jnp.swapaxes(grad_merge, 0, 1),
        jnp.concatenate([rows[4:6], rows[0:2]], axis=0),
        jnp.concatenate([rows[6:8], rows[2:4]], axis=0),
    )


def solution(mesh):
    return jax.shard_map(
        local,
        mesh=mesh,
        in_specs=(
            P("dp", "tensor", None),
            P("dp", "tensor", None),
            P("dp", None),
            P("dp", None),
            P(None, None, "tensor"),
            P("tensor", None),
            P(None, "tensor"),
            P("tensor", None),
            P(None, None, None, "tensor"),
            P(None, "tensor"),
            P(None, None, "tensor"),
            P("tensor", None, None),
            P(),
            P(),
            P("dp", "tensor", None),
            P("dp", "tensor", None),
        ),
        out_specs=(
            P("dp", "tensor", None),
            P("dp", "tensor", None),
            P("dp", "tensor", None),
            P("dp", "tensor", None),
            P(None, None, "tensor"),
            P("tensor", None),
            P(None, "tensor"),
            P("tensor", None),
            P(None, None, None, "tensor"),
            P(None, "tensor"),
            P(None, None, "tensor"),
            P("tensor", None, None),
            P(),
            P(),
        ),
        check_vma=False,
    )
```

```python
import functools
from types import SimpleNamespace

import jax
import jax.numpy as jnp
from jax import lax
from jax.experimental import pallas as pl
from jax.experimental.pallas import tpu as pltpu
from jax.sharding import PartitionSpec as P

HD = 64


NORM_EPSILON = 1e-06
MASK_VALUE = -1e30
HIGH_PRECISION = lax.Precision.HIGHEST


def layout(doc_sizes, char_counts, char_total):
    length = char_counts.shape[0]
    docs = doc_sizes.shape[0]
    doc_ids = jnp.arange(docs, dtype=jnp.int32)
    doc_ends = jnp.sum(
        jnp.where(doc_ids[None, :] <= doc_ids[:, None], doc_sizes[None, :], 0), axis=1
    )
    positions = jnp.arange(length, dtype=jnp.int32)
    segment = jnp.sum(
        (positions[:, None] >= doc_ends[None, :]).astype(jnp.int32), axis=1, dtype=jnp.int32
    )
    token_ends = jnp.sum(
        jnp.where(positions[None, :] <= positions[:, None], char_counts[None, :], 0), axis=1
    )
    last_char = token_ends - 1
    first_char = token_ends - char_counts
    char_ends = jnp.sum(
        jnp.where(positions[None, :] < doc_ends[:, None], char_counts[None, :], 0), axis=1
    )
    char_positions = jnp.arange(char_total, dtype=jnp.int32)
    starts = char_ends - jnp.sum(
        jnp.where(
            (positions[None, :] < doc_ends[:, None])
            & (positions[None, :] >= (doc_ends - doc_sizes)[:, None]),
            char_counts[None, :],
            0,
        ),
        axis=1,
    )
    keep_forward = 1.0 - jnp.any(char_positions[:, None] == starts[None, :], axis=1).astype(
        jnp.float32
    )
    keep_backward = 1.0 - jnp.any(
        char_positions[:, None] == (char_ends - 1)[None, :], axis=1
    ).astype(jnp.float32)
    token_starts = doc_ends - doc_sizes
    prev_ok = 1.0 - jnp.any(positions[:, None] == token_starts[None, :], axis=1).astype(
        jnp.float32
    )
    next_ok = 1.0 - jnp.any(positions[:, None] == (doc_ends - 1)[None, :], axis=1).astype(
        jnp.float32
    )
    return (segment, first_char, last_char, keep_forward, keep_backward, prev_ok, next_ok)


F32 = jnp.float32
BF16 = jnp.bfloat16
LANE = 128
MIB = 1024 * 1024
VMEM = pl.BlockSpec(memory_space=pltpu.VMEM)


def gru_weights(w_gru, gate_bias):
    width, _, _, units = w_gru.shape
    matrix = jnp.pad(jnp.swapaxes(w_gru, 1, 2), ((0, 0), (0, 0), (0, 0), (0, LANE - units)))
    bias = jnp.pad(gate_bias, ((0, 0), (0, LANE - units)))
    return matrix.reshape(width, 4 * LANE), bias.reshape(1, 2 * LANE)


def nn(left, right):
    return jnp.dot(left, right, preferred_element_type=F32)


def nt(left, right):
    return lax.dot_general(left, right, (((1,), (1,)), ((), ())), preferred_element_type=F32)


def tn(left, right):
    return lax.dot_general(left, right, (((0,), (0,)), ((), ())), preferred_element_type=F32)


def gelu_pair(values):
    cdf = 0.5 * (1.0 + lax.erf(values * 0.7071067811865476))
    density = 0.3989422804014327 * jnp.exp(-0.5 * values * values)
    return values * cdf, cdf + values * density


def normalize(rows):
    centered = rows - jnp.mean(rows, axis=-1, keepdims=True)
    scale = lax.rsqrt(jnp.mean(centered * centered, axis=-1, keepdims=True) + NORM_EPSILON)
    return centered * scale, scale


def normalize_back(unit, scale, grad_unit):
    return scale * (
        grad_unit
        - jnp.mean(grad_unit, axis=-1, keepdims=True)
        - unit * jnp.mean(grad_unit * unit, axis=-1, keepdims=True)
    )


def roll_lanes(value, shift):
    return pltpu.roll(value, shift % value.shape[1], axis=1)


def unpack3(packed, size):
    room = -(-size // LANE) * LANE
    lane = lax.broadcasted_iota(jnp.int32, (packed.shape[0], room), 1)
    parts = []
    for k in range(3):
        first = k * size // LANE * LANE
        inner = k * size - first
        part = packed[:, first : min(first + room + LANE, packed.shape[1])]
        if inner:
            part = roll_lanes(part, -inner)
        parts.append(jnp.where(lane < size, part[:, :room], 0.0))
    return parts


def pack3(parts, size):
    room = parts[0].shape[1]
    columns = -(-3 * size // LANE) * LANE
    tiles = [None] * (columns // LANE)
    for k in range(3):
        first, inner = divmod(k * size, LANE)
        part = parts[k]
        if inner:
            part = jnp.concatenate([part, jnp.zeros_like(part[:, :LANE])], axis=1)
            part = roll_lanes(part, inner)
        for j in range(part.shape[1] // LANE):
            if first + j < len(tiles) and (first + j) * LANE < (k + 1) * size:
                tile = part[:, j * LANE : (j + 1) * LANE]
                old = tiles[first + j]
                tiles[first + j] = tile if old is None else old + tile
    return jnp.concatenate(tiles, axis=1)


class Group:
    def __init__(self, send, recv, seqs):
        self.me = lax.axis_index("tensor")
        self.low = self.me % 2
        self.high = self.me // 2
        self.pair = self.high * 2 + (1 - self.low)
        self.far = (1 - self.high) * 2 + self.low
        self.send, self.recv, self.seqs, self.used = send, recv, seqs, 0

    def block(self, turn):
        left = 3 - turn
        return ((self.high + left // 2) % 2) * 2 + (self.low + left % 2) % 2

    def slots(self, count):
        first = self.used
        self.used += count
        return [first + i for i in range(count)]

    def copy(self, slot, seq, source, target, peer):
        index = slot * self.seqs + seq
        return pltpu.make_async_remote_copy(
            src_ref=source,
            dst_ref=target,
            send_sem=self.send.at[index],
            recv_sem=self.recv.at[index],
            device_id={"tensor": peer},
            device_id_type=pl.DeviceIdType.MESH,
        )

    def greet(self):
        barrier = pltpu.get_barrier_semaphore()
        for peer in (self.pair, self.far):
            pl.semaphore_signal(
                barrier, inc=1, device_id={"tensor": peer}, device_id_type=pl.DeviceIdType.MESH
            )
        pl.semaphore_wait(barrier, 2)


class Gather:
    def __init__(self, group, buf, source=None, place=None):
        self.group, self.source = group, source
        self.at = place or (lambda seq, t: buf.at[seq, t])
        self.near, self.over, self.fwd = group.slots(3)

    def own(self, seq):
        return self.at(seq, self.group.me) if self.source is None else self.source.at[seq]

    def near_copy(self, seq):
        g = self.group
        return g.copy(self.near, seq, self.own(seq), self.at(seq, g.me), g.pair)

    def over_copy(self, seq):
        g = self.group
        return g.copy(self.over, seq, self.own(seq), self.at(seq, g.me), g.far)

    def fwd_copy(self, seq):
        g = self.group
        other = self.at(seq, g.far)
        return g.copy(self.fwd, seq, other, other, g.pair)

    def start(self, seq):
        self.over_copy(seq).start()
        self.near_copy(seq).start()

    def forward(self, seq):
        self.over_copy(seq).wait_recv()
        self.fwd_copy(seq).start()

    def finish(self, seq):
        near = self.near_copy(seq)
        fwd = self.fwd_copy(seq)
        near.wait_recv()
        fwd.wait_recv()
        near.wait_send()
        self.over_copy(seq).wait_send()
        fwd.wait_send()


class Scatter:
    def __init__(self, group, stage, got, own, temp):
        self.group, self.stage, self.got, self.held, self.temp = group, stage, got, own, temp
        self.names = group.slots(3)

    def copies(self, seq):
        g = self.group
        peers = (g.pair, g.pair, g.far)
        return [
            g.copy(self.names[i], seq, self.stage(seq, i), self.got(seq, i), peers[i])
            for i in range(3)
        ]

    def start(self, seq, part):
        mine, other, over = self.copies(seq)

        def turn(step, carry):
            part(self.group.block(step), self.temp)

            @pl.when(step == 0)
            def _():
                self.stage(seq, 1)[...] = self.temp[...].astype(BF16)
                other.start()

            @pl.when(step == 1)
            def _():
                other.wait_recv()
                self.stage(seq, 2)[...] = (self.temp[...] + self.got(seq, 1)[...]).astype(BF16)
                over.start()

            @pl.when(step == 2)
            def _():
                self.stage(seq, 0)[...] = self.temp[...].astype(BF16)
                mine.start()

            @pl.when(step == 3)
            def _():
                self.held(seq)[...] = self.temp[...]

            return carry

        lax.fori_loop(0, 4, turn, 0)

    def finish(self, seq):
        mine, other, over = self.copies(seq)
        mine.wait_recv()
        over.wait_recv()
        total = self.held(seq)[...] + self.got(seq, 0)[...] + self.got(seq, 2)[...]
        mine.wait_send()
        other.wait_send()
        over.wait_send()
        return total


def shift_rows(value, count, up, fill):
    edge = jnp.full((count, value.shape[1]), fill, value.dtype)
    if up:
        return jnp.concatenate([edge, value[:-count]], axis=0)
    return jnp.concatenate([value[count:], edge], axis=0)


def recur(ups, decays, drives, outs, block, back=False):
    steps = block // 8
    pairs = [(tile, t) for tile in range(2) for t in range(4)]

    def rows(tile, t, step):
        row = step if ups[tile] else steps - 1 - step
        return pl.ds(pl.multiple_of(t * block + row * 8, 8), 8)

    def summary(step, carry):
        new = []
        for i, (tile, t) in enumerate(pairs):
            state, mult = carry[2 * i], carry[2 * i + 1]
            here = rows(tile, t, step)
            decay, drive = decays[tile, here, :], drives[tile, here, :]
            state = decay * (state + drive) if back else decay * state + drive
            new += [state, decay * mult]
        return tuple(new)

    zero, one = jnp.zeros((8, LANE), F32), jnp.ones((8, LANE), F32)
    ends = lax.fori_loop(0, steps, summary, (zero, one) * 8, unroll=4)
    starts = []
    for tile in range(2):
        state = jnp.concatenate([ends[2 * (4 * tile + t)] for t in range(4)], axis=0)
        mult = jnp.concatenate([ends[2 * (4 * tile + t) + 1] for t in range(4)], axis=0)
        for count in (1, 2, 4, 8, 16):
            state = mult * shift_rows(state, count, ups[tile], 0.0) + state
            mult = mult * shift_rows(mult, count, ups[tile], 1.0)
        state = shift_rows(state, 1, ups[tile], 0.0)
        starts += [state[8 * t : 8 * t + 8] for t in range(4)]

    def write(step, carry):
        new = []
        for i, (tile, t) in enumerate(pairs):
            here = rows(tile, t, step)
            decay, drive = decays[tile, here, :], drives[tile, here, :]
            if back:
                value = drive + carry[i]
                new.append(decay * value)
            else:
                value = decay * carry[i] + drive
                new.append(value)
            outs[tile, here, :] = value
        return tuple(new)

    lax.fori_loop(0, steps, write, tuple(starts), unroll=4)


def forward_kernel(
    units, channels, tokens, chars, wq, wout, win, wdown, wg, gate_bias, wc, wm, gain, bias, cot_t, cot_c,
    segc, segr, pickc, keep, edges,
    token_out, char_out, o_x, o_c, o_qkv, o_p, o_ctx, o_h, o_act, o_dact, o_mid, o_st, o_mg,
    o_dmg, o_states, o_decay, o_unit0, o_unit1, o_scale, o_res3, o_res4, o_branch, norm_grads,
    x, c, qkv, p, ctx, h, act, dact, mid, st, mg, dmg, low_states, decays, unit0, unit1, scale, res3, res4, branch,
    hidden, middle, outs_t, outs_c, states, drive, taps, perm,
    stage, got, held, temp, send, recv, local,
):
    seqs, length = tokens.shape[0], segr.shape[2]
    shard, width = tokens.shape[1], tokens.shape[2]
    block_chars = chars.shape[1]
    heads = p.shape[1] // 4
    g = Group(send, recv, seqs)
    me = g.me
    saves = []

    def keep_out(seq, source, target):
        saves.append((source, target, len(saves)))

    def local_copy(number, seq, source, target):
        return pltpu.make_async_copy(source, target, local.at[number * seqs + seq])

    gx, gc = Gather(g, x, tokens), Gather(g, c, chars)
    gh, gm, gs = Gather(g, h), Gather(g, mid), Gather(g, st)
    narrow = lambda ref: (lambda s, i: ref.at[s, i, :, pl.ds(0, width)])
    wide = lambda ref: (lambda s, i: ref.at[s, i])
    own_n = lambda s: held.at[s, :, pl.ds(0, width)]
    own_w = lambda s: held.at[s]
    thin = temp.at[:, pl.ds(0, width)]
    s_attn = Scatter(g, narrow(stage), narrow(got), own_n, thin)
    s_ffn = Scatter(g, narrow(stage), narrow(got), own_n, thin)
    s_branch = Scatter(g, wide(stage), wide(got), own_w, temp)

    def own_x(seq):
        return local_copy(0, seq, tokens.at[seq], x.at[seq, me])

    def own_c(seq):
        return local_copy(1, seq, chars.at[seq], c.at[seq, me])

    plan = [
        (x, o_x), (c, o_c), (qkv, o_qkv), (p, o_p), (ctx, o_ctx), (h, o_h), (act, o_act),
        (dact, o_dact), (mid, o_mid), (st, o_st), (mg, o_mg), (dmg, o_dmg), (low_states, o_states),
        (decays, o_decay), (res4, o_res4), (unit0, o_unit0), (unit1, o_unit1), (scale, o_scale), (res3, o_res3), (branch, o_branch),
        (outs_t, token_out), (outs_c, char_out),
    ]

    def save(seq, *names):
        for name in names:
            for number, (source, target) in enumerate(plan):
                if source is name:
                    local_copy(2 + number, seq, source.at[seq], target.at[seq]).start()

    def each(body):
        def run(seq, carry):
            body(seq)
            return carry

        lax.fori_loop(0, seqs, run, 0)

    each(lambda s: (own_x(s).start(), own_c(s).start()))
    g.greet()
    each(gx.start)
    each(gc.start)

    for t in range(4):
        for d in range(2):
            row = lax.broadcasted_iota(jnp.int32, (LANE, width), 0)
            col = lax.broadcasted_iota(jnp.int32, (LANE, width), 1)
            first = d * 4 * units + t * units
            hit = (col - first == row) & (row < units)
            perm[pl.ds((2 * t + d) * LANE, LANE), :] = hit.astype(F32).astype(BF16)
    taps[...] = jnp.zeros_like(taps)
    norm_grads[...] = jnp.zeros_like(norm_grads)

    lane = lax.broadcasted_iota(jnp.int32, (shard, LANE), 1)
    left = lane < HD

    def attention(s):
        gx.forward(s)
        gx.finish(s)
        own_x(s).wait()
        save(s, x)

        def project(t, carry):
            rows = pl.ds(pl.multiple_of(t * shard, shard), shard)
            first, second, third = unpack3(nn(x[s, t], wq[...]), HD * heads)
            qkv[s, 0, rows, :] = (first * 0.125).astype(BF16)
            qkv[s, 1, rows, :] = second.astype(BF16)
            qkv[s, 2, rows, :] = third.astype(BF16)
            return carry

        lax.fori_loop(0, 4, project, 0)
        save(s, qkv)

        def part(b, out):
            rows = pl.ds(pl.multiple_of(b * shard, shard), shard)
            same = segc[s, rows, :] == segr[s]
            for tile in range(qkv.shape[3] // LANE):
                cols = pl.ds(tile * LANE, LANE)
                result = None
                for half in range(2):
                    head = 2 * tile + half
                    if head >= heads:
                        continue
                    query = qkv[s, 0, rows, cols]
                    if 2 * tile + 1 < heads:
                        query = jnp.where(left if half == 0 else ~left, query, jnp.zeros_like(query))
                    scores = jnp.where(same, nt(query, qkv[s, 1, :, cols]), MASK_VALUE)
                    power = jnp.exp(scores - jnp.max(scores, axis=-1, keepdims=True))
                    probs = (power * (1.0 / jnp.sum(power, axis=-1, keepdims=True))).astype(BF16)
                    p[s, head * 4 + b] = probs
                    mixed = nn(probs, qkv[s, 2, :, cols])
                    result = mixed if result is None else jnp.where(left, result, mixed)
                ctx[s, rows, cols] = result.astype(BF16)
            out[...] = nn(ctx[s, rows, :], wout[...])

        s_attn.start(s, part)
        save(s, p, ctx)

    each(attention)

    def first_norm(s):
        total = x[s, me].astype(F32) + s_attn.finish(s)
        unit, spread = normalize(total)
        unit0[s] = unit
        scale[s, 0] = jnp.broadcast_to(spread, (shard, LANE))
        hidden[s] = unit * gain[0:1] + bias[0:1]
        h[s, me] = hidden[s].astype(BF16)
        gh.start(s)
        save(s, unit0)

    def gru(s):
        gc.forward(s)
        gc.finish(s)
        own_c(s).wait()
        save(s, c)

        def gates(t, carry):
            rows = pl.ds(pl.multiple_of(t * LANE, LANE), LANE)
            per = block_chars // LANE
            inner = pl.ds(pl.multiple_of((t % per) * LANE, LANE), LANE)
            proj = nn(c[s, t // per, inner, :], wg[...])
            for tile in range(2):
                cols = slice(tile * LANE, (tile + 1) * LANE)
                gate = jax.nn.sigmoid(proj[:, cols] + gate_bias_pad(tile))
                cand = proj[:, (2 + tile) * LANE : (3 + tile) * LANE]
                decays[s, tile, rows, :] = (1.0 - gate) * keep[s, rows, tile : tile + 1]
                drive[tile, rows, :] = gate * cand
            return carry

        def gate_bias_pad(tile):
            return gate_bias[:, tile * LANE : (tile + 1) * LANE]

        total = 4 * block_chars
        lax.fori_loop(0, total // LANE, gates, 0)
        recur((True, False), decays.at[s], drive, states, block_chars)
        save(s, decays)

        for tile in range(2):
            low_states[s, tile] = states[tile].astype(BF16)

        def pick(t, carry):
            rows = pl.ds(pl.multiple_of(t * shard, shard), shard)
            for tile in range(2):
                ids = lax.broadcasted_iota(jnp.int32, (shard, total), 1)
                hot = (ids == pickc[s, rows, tile : tile + 1]).astype(F32).astype(BF16)
                out = nn(hot, low_states[s, tile])
                st[s, me, rows, pl.ds(tile * LANE, LANE)] = out.astype(BF16)
            return carry

        lax.fori_loop(0, 4, pick, 0)
        gs.start(s)
        save(s, low_states)

    def norm_and_gru(s):
        first_norm(s)
        gru(s)

    each(norm_and_gru)

    def ffn(s):
        gh.forward(s)
        gh.finish(s)
        save(s, h)

        def part(b, out):
            value, slope = gelu_pair(nn(h[s, b], win[...]))
            act[s, b] = value.astype(BF16)
            dact[s, b] = slope.astype(BF16)
            out[...] = nn(act[s, b], wdown[...])

        s_ffn.start(s, part)
        save(s, act, dact)

    each(ffn)

    def second_norm(s):
        unit, spread = normalize(hidden[s] + s_ffn.finish(s))
        unit1[s] = unit
        scale[s, 1] = jnp.broadcast_to(spread, (shard, LANE))
        middle[s] = unit * gain[1:2] + bias[1:2]
        mid[s, me] = middle[s].astype(BF16)
        gm.start(s)
        save(s, unit1, scale)

    each(second_norm)

    def merge(s):
        gs.forward(s)
        gm.forward(s)
        gs.finish(s)
        gm.finish(s)
        save(s, mid, st)
        def mix(t, carry):
            rows = pl.ds(pl.multiple_of(t * shard, shard), shard)
            total = nn(mid[s, t], wc[pl.ds(0, width), :])
            for u in range(4):
                weights = wc[pl.ds(width + u * 2 * LANE, 2 * LANE), :]
                total = total + nn(st[s, u, rows, :], weights)
            taps[pl.ds(pl.multiple_of(8 + t * shard, 8), shard), :] = total
            return carry

        lax.fori_loop(0, 4, mix, 0)

        def shifted(t, carry):
            rows = pl.ds(pl.multiple_of(t * shard, shard), shard)
            window = taps[pl.ds(pl.multiple_of(t * shard, 8), shard + 16), :]
            before = unpack3(window[7 : 7 + shard], channels)[0]
            center = unpack3(window[8 : 8 + shard], channels)[1]
            after = unpack3(window[9 : 9 + shard], channels)[2]
            value, slope = gelu_pair(
                before * edges[s, rows, 0:1] + center + after * edges[s, rows, 1:2]
            )
            mg[s, rows, :] = value.astype(BF16)
            dmg[s, rows, :] = slope.astype(BF16)
            return carry

        lax.fori_loop(0, 4, shifted, 0)

        def part(b, out):
            rows = pl.ds(pl.multiple_of(b * shard, shard), shard)
            out[...] = nn(mg[s, rows, :], wm[...])

        s_branch.start(s, part)
        save(s, mg, dmg)

    each(merge)

    def put_branch(s, first, value):
        span = branch.shape[3]
        at = 0
        while at < width:
            part, inner = divmod(first + at, span)
            size = min(span - inner, width - at)
            branch[s, part, :, pl.ds(inner, size)] = value[:, at : at + size]
            at += size

    def last_norms(s):
        total = s_branch.finish(s)
        rows = pl.ds(pl.multiple_of(me * shard, shard), shard)
        unit, spread = normalize(middle[s] + total[:, :width])
        outs_t[s] = (unit * gain[2:3] + bias[2:3]).astype(BF16)
        cot = cot_t[s]
        norm_grads[0:1] += jnp.sum(cot * unit, axis=0, keepdims=True)
        norm_grads[2:3] += jnp.sum(cot, axis=0, keepdims=True)
        back = normalize_back(unit, spread, cot * gain[2:3])
        res3[s] = back
        put_branch(s, 0, back.astype(BF16))
        mine = total[:, width:]
        for u in range(4):
            mine = mine + nn(st[s, u, rows, :], perm[pl.ds(u * 2 * LANE, 2 * LANE), :])
        unit, spread = normalize(mine)
        outs_c[s] = (unit * gain[3:4] + bias[3:4]).astype(BF16)
        cot = cot_c[s]
        norm_grads[1:2] += jnp.sum(cot * unit, axis=0, keepdims=True)
        norm_grads[3:4] += jnp.sum(cot, axis=0, keepdims=True)
        back = normalize_back(unit, spread, cot * gain[3:4]).astype(BF16)
        put_branch(s, width, back)
        for u in range(4):
            res4[s, u] = nt(back, perm[pl.ds(u * 2 * LANE, 2 * LANE), :]).astype(BF16)
        save(s, outs_t, outs_c, res3, res4, branch)

    each(last_norms)

    def drain(s):
        for number, (source, target) in enumerate(plan):
            local_copy(2 + number, s, source.at[s], target.at[s]).wait()

    each(drain)


def forward_call(tokens, chars, weights, small, group_slots=27):
    seqs, shard, width = tokens.shape
    length, block_chars = shard * 4, chars.shape[1]
    total = block_chars * 4
    wq, wout, win, wdown, wg, gate_bias, wc, wm = weights
    cols = wout.shape[0]
    heads = small["heads"]
    sds = jax.ShapeDtypeStruct
    big = {
        "x": ((seqs, 4, shard, width), BF16),
        "c": ((seqs, 4, block_chars, chars.shape[2]), BF16),
        "qkv": ((seqs, 3, length, cols), BF16),
        "p": ((seqs, heads * 4, shard, length), BF16),
        "ctx": ((seqs, length, cols), BF16),
        "h": ((seqs, 4, shard, width), BF16),
        "act": ((seqs, 4, shard, win.shape[1]), BF16),
        "dact": ((seqs, 4, shard, win.shape[1]), BF16),
        "mid": ((seqs, 4, shard, width), BF16),
        "st": ((seqs, 4, length, 2 * LANE), BF16),
        "mg": ((seqs, length, wm.shape[0]), BF16),
        "dmg": ((seqs, length, wm.shape[0]), BF16),
        "states": ((seqs, 2, total, LANE), BF16),
        "decay": ((seqs, 2, total, LANE), F32),
        "unit0": ((seqs, shard, width), F32),
        "unit1": ((seqs, shard, width), F32),
        "scale": ((seqs, 2, shard, LANE), F32),
        "res3": ((seqs, shard, width), F32),
        "res4": ((seqs, 4, shard, 2 * LANE), BF16),
        "branch": ((seqs, 2 * width // length, shard, length), BF16),
    }
    rows = ((seqs, shard, width), F32)
    low_rows = ((seqs, shard, width), BF16)
    scratch = list(big.values()) + [
        rows, rows, low_rows, low_rows,
        ((2, total, LANE), F32),
        ((2, total, LANE), F32),
        ((length + 16, wc.shape[1]), F32),
        ((8 * LANE, width), BF16),
        ((seqs, 3, shard, 2 * width), BF16), ((seqs, 3, shard, 2 * width), BF16),
        ((seqs, shard, 2 * width), F32), ((shard, 2 * width), F32),
    ]
    anyspace = pl.BlockSpec(memory_space=pl.ANY)
    vmem = pl.BlockSpec(memory_space=pltpu.VMEM)
    out_shapes = [sds(low_rows[0], BF16)] * 2 + [sds(*v) for v in big.values()]
    ins = (
        tokens, chars, wq, wout, win, wdown, wg, gate_bias, wc, wm, small["gain"], small["bias"],
        small["cot_t"], small["cot_c"], small["segc"], small["segr"], small["pickc"],
        small["keep"], small["edges"],
    )
    outs = pl.pallas_call(
        functools.partial(forward_kernel, small["units"], small["channels"]),
        out_shape=out_shapes + [sds((4, width), F32)],
        in_specs=[anyspace] * 2 + [vmem] * (len(ins) - 2),
        out_specs=[anyspace] * len(out_shapes) + [vmem],
        scratch_shapes=[pltpu.VMEM(*v) for v in scratch]
        + [
            pltpu.SemaphoreType.DMA((group_slots * seqs,)),
            pltpu.SemaphoreType.DMA((group_slots * seqs,)),
            pltpu.SemaphoreType.DMA((26 * seqs,)),
        ],
        compiler_params=pltpu.CompilerParams(
            collective_id=0, has_side_effects=True, vmem_limit_bytes=62 * MIB
        ),
    )(*ins)
    names = ["token_out", "char_out"] + list(big) + ["norm_grads"]
    return dict(zip(names, outs))


class Plane:
    def __init__(self, send, recv, marks):
        self.index = lax.axis_index("dp")
        self.x, self.z = self.index % 2, self.index // 2
        self.send, self.recv, self.marks, self.used, self.marked = send, recv, marks, 0, 0

    def mark(self):
        self.marked += 1
        return self.marks.at[self.marked - 1]

    def take(self, count):
        first = self.used
        self.used += count
        return [first + i for i in range(count)]

    def peer(self, way):
        if way == "x":
            return self.index + 1 - 2 * self.x
        return (self.index + (2 if way == "up" else 6)) % 8

    def pair(self, bit):
        digit = self.index // (1 << bit) % 2
        return self.index + (1 - 2 * digit) * (1 << bit)

    def copy(self, slot, source, target, peer):
        return pltpu.make_async_remote_copy(
            src_ref=source,
            dst_ref=target,
            send_sem=self.send.at[slot],
            recv_sem=self.recv.at[slot],
            device_id={"dp": peer},
            device_id_type=pl.DeviceIdType.MESH,
        )


class Reduce:
    steps = 9

    def __init__(self, plane, buf, out, land, first, land_first, rows, x_first):
        self.plane, self.buf, self.out, self.land = plane, buf, out, land
        self.first, self.land_first, self.rows, self.x_first = first, land_first, rows, x_first
        self.slots = plane.take(14)
        self.mark = plane.mark()
        x, z = plane.x, plane.z
        if x_first:
            self.quarter, self.half = rows // 8, rows // 2
            self.z_base, self.x_base = first + x * self.half, first
        else:
            self.quarter, self.half = rows // 4, rows // 8
            self.z_base, self.x_base = first, first + z * self.quarter
        self.x_land = land_first + 5 * self.quarter

    @staticmethod
    def landing_rows(rows, x_first):
        return 5 * rows // 8 + rows // 2 if x_first else 5 * rows // 4 + rows // 8

    def rows_of(self, ref, start, size):
        return ref.at[pl.ds(pl.multiple_of(start, 16), size), :]

    def add(self, start, land_start, size):
        def one(i, carry):
            rows = pl.ds(pl.multiple_of(start + i * 16, 16), 16)
            more = pl.ds(pl.multiple_of(land_start + i * 16, 16), 16)
            total = self.buf[rows, :].astype(F32) + self.land[more, :].astype(F32)
            self.buf[rows, :] = total.astype(BF16)
            return carry

        lax.fori_loop(0, size // 16, one, 0)

    def gather_copy(self, way, step, z):
        piece = 3 - step + z if way == "up" else step - 3 + z
        slot = piece if way == "up" else piece + (4 - piece) * (step // 2)
        return self.plane.copy(
            self.slots[step if way == "up" else 3 + step],
            self.rows_of(self.buf, self.z_base + piece * self.quarter, self.quarter),
            self.rows_of(self.land, self.land_first + slot * self.quarter, self.quarter),
            self.plane.peer(way),
        )

    def gather_send(self, step):
        z = self.plane.z
        pl.when(step >= z)(lambda: self.gather_copy("up", step, z).start())
        pl.when(step >= 3 - z)(lambda: self.gather_copy("down", step, z).start())

    def gather_wait(self, step):
        z = self.plane.z

        @pl.when((z >= 1) & (step >= z - 1))
        def _():
            self.gather_copy("up", step, z - 1).wait_recv()
            piece = 3 - step + z - 1
            self.add(
                self.z_base + piece * self.quarter,
                self.land_first + piece * self.quarter,
                self.quarter,
            )

        @pl.when((z <= 2) & (step >= 2 - z))
        def _():
            self.gather_copy("down", step, z + 1).wait_recv()
            piece = step - 3 + z + 1
            slot = piece if step < 2 else 4
            self.add(
                self.z_base + piece * self.quarter,
                self.land_first + slot * self.quarter,
                self.quarter,
            )

        pl.when(step >= z)(lambda: self.gather_copy("up", step, z).wait_send())
        pl.when(step >= 3 - z)(lambda: self.gather_copy("down", step, z).wait_send())

    def spread_copy(self, way, step, z):
        piece = z - step if way == "up" else z + step
        start = self.z_base + piece * self.quarter
        target = self.rows_of(self.out, start, self.quarter)
        source = target
        if self.x_first and step == 0:
            source = self.rows_of(self.buf, start, self.quarter)
        slot = self.slots[6 + step if way == "up" else 9 + step]
        return self.plane.copy(slot, source, target, self.plane.peer(way))

    def spread_send(self, step):
        z = self.plane.z
        pl.when((z <= 2) & (step <= z))(lambda: self.spread_copy("up", step, z).start())
        pl.when((z >= 1) & (step <= 3 - z))(lambda: self.spread_copy("down", step, z).start())

    def spread_wait(self, step):
        z = self.plane.z
        pl.when((z >= 1) & (step <= z - 1))(lambda: self.spread_copy("up", step, z - 1).wait_recv())
        pl.when((z <= 2) & (step <= 2 - z))(lambda: self.spread_copy("down", step, z + 1).wait_recv())
        pl.when((z <= 2) & (step <= z))(lambda: self.spread_copy("up", step, z).wait_send())
        pl.when((z >= 1) & (step <= 3 - z))(lambda: self.spread_copy("down", step, z).wait_send())

    def halve(self):
        other = self.x_base + (1 - self.plane.x) * self.half
        return self.plane.copy(
            self.slots[12],
            self.rows_of(self.buf, other, self.half),
            self.rows_of(self.land, self.x_land, self.half),
            self.plane.peer("x"),
        )

    def halve_wait(self):
        self.halve().wait()
        self.add(self.x_base + self.plane.x * self.half, self.x_land, self.half)

    def double(self):
        start = self.x_base + self.plane.x * self.half
        target = self.rows_of(self.out, start, self.half)
        source = target if self.x_first else self.rows_of(self.buf, start, self.half)
        return self.plane.copy(self.slots[13], source, target, self.plane.peer("x"))

    def keep(self):
        if self.x_first:
            start, size = self.z_base + self.plane.z * self.quarter, self.quarter
        else:
            start, size = self.x_base + self.plane.x * self.half, self.half
        return pltpu.make_async_copy(
            self.rows_of(self.buf, start, size), self.rows_of(self.out, start, size), self.mark
        )

    def step(self, number):
        if self.x_first:
            if number == 0:
                self.halve().start()
            elif number == 1:
                self.halve_wait()
                self.gather_send(0)
            elif number <= 3:
                self.gather_wait(number - 2)
                self.gather_send(number - 1)
            elif number == 4:
                self.gather_wait(2)
                self.keep().start()
                self.spread_send(0)
            elif number <= 6:
                self.spread_wait(number - 5)
                self.spread_send(number - 4)
            elif number == 7:
                self.spread_wait(2)
                self.keep().wait()
                self.double().start()
            else:
                self.double().wait()
        else:
            if number == 0:
                self.gather_send(0)
            elif number <= 2:
                self.gather_wait(number - 1)
                self.gather_send(number)
            elif number == 3:
                self.gather_wait(2)
                self.halve().start()
            elif number == 4:
                self.halve_wait()
                self.keep().start()
                self.double().start()
            elif number == 5:
                self.double().wait()
                self.keep().wait()
                self.spread_send(0)
            elif number <= 7:
                self.spread_wait(number - 6)
                self.spread_send(number - 5)
            else:
                self.spread_wait(2)


SAVED = (
    "branch", "mg", "dmg", "mid", "st", "res3", "res4", "unit0", "unit1", "scale", "act", "dact",
    "h", "p", "qkv", "ctx", "x", "c", "states", "decay",
)
GRADS = ("merge", "conv", "down", "win", "gru", "out", "qkv")
PIECES = (
    (0, 384, True),
    (1, 640, False),
    (1, 768, True),
    (1, 128, True),
    (2, 384, True),
    (2, 384, True),
    (3, 768, True),
    (4, 128, True),
    (4, 128, True),
    (5, 256, False),
    (6, 512, True),
    (6, 256, False),
)
SCHEDULE = (
    (),
    (0, 10, 20, 30,),
    (),
    (11,),
    (1,),
    (),
    (40, 50, 12,),
    (60, 2,),
    (21,),
    (31,),
    (13,),
    (3, 22, 41, 32,),
    (4,),
    (51, 23, 42, 33,),
    (5,),
    (52, 24,),
    (43, 34, 6, 61, 53, 14,),
    (25, 44, 35, 7,),
    (15, 62,),
    (90, 100, 110, 54, 26, 45, 36,),
    (8, 16,),
    (),
    (63, 91, 27, 111, 101, 37, 46, 55, 17,),
    (64,),
    (47, 92, 112,),
    (70, 80, 56, 102, 18, 28, 38, 65, 93,),
    (113, 103, 57, 48,),
    (71, 81, 66, 94, 104, 114, 72,),
    (82, 67, 73, 83, 105, 58, 95,),
    (74, 115, 84, 106, 96, 75, 116, 85, 107, 97, 76, 68, 117, 86, 98, 77, 118, 87, 108, 78, 88,),
)


def backward_kernel(units, channels, dp_size, *refs):
    refs = list(refs)
    take = lambda count: [refs.pop(0) for _ in range(count)]
    hbm = SimpleNamespace(**dict(zip(SAVED, take(len(SAVED)))))
    wq, wout, win, wdown, wg, gate_bias, wc, wm, gain, pickr, edges, norm_in = take(12)
    grad_tokens, grad_chars = take(2)
    grads_out = dict(zip(GRADS, take(len(GRADS))))
    (small_out,) = take(1)
    names = [n for n in SAVED if n not in ("branch", "states", "decay", "p", "x")]
    v = SimpleNamespace(**dict(zip(names, take(len(names)))))
    (pb, states, decay, drive, dpre, dyk, fg, gtok, dproj, gru_acc, res2, res1, ds, parts,
     stage, got, held, temp, cstage, cgot, cheld, ctemp) = take(22)
    land = dict(zip(GRADS, take(len(GRADS))))
    big = SimpleNamespace(**dict(zip(GRADS, take(len(GRADS)))))
    small, small_land, send, recv, dsend, drecv, local, marks, credit = take(9)

    seqs, shard, width = grad_tokens.shape
    length = 4 * shard
    block_chars = grad_chars.shape[1]
    total = 4 * block_chars
    heads = pb.shape[1] // 4
    cols = v.ctx.shape[2]
    g = Group(send, recv, seqs)
    me = g.me
    inside = dp_size == 8
    plane = Plane(dsend, drecv, marks)

    def each(body):
        def run(seq, carry):
            body(seq)
            return carry

        lax.fori_loop(0, seqs, run, 0)

    def load(name):
        index = names.index(name)
        return pltpu.make_async_copy(getattr(hbm, name), getattr(v, name), local.at[index])

    spare = len(names)
    p_copy = lambda: pltpu.make_async_copy(hbm.p, pb, local.at[spare])
    x_copy = lambda: pltpu.make_async_copy(hbm.x, v.h, local.at[39])

    def states_copy(s):
        return pltpu.make_async_copy(hbm.states.at[s], states, local.at[spare + 1])

    def decay_copy(s, tile):
        return pltpu.make_async_copy(
            hbm.decay.at[s, tile], decay.at[tile], local.at[spare + 2 + tile]
        )

    def out_copy(kind, s):
        source, target = ((res1, grad_tokens), (cheld, grad_chars))[kind]
        return pltpu.make_async_copy(
            source.at[s], target.at[s], local.at[spare + 4 + kind * seqs + s]
        )

    pieces = 2 * width // length
    gb = Gather(
        g, pb, hbm.branch, place=lambda s, t: pb.at[s, pl.ds(t * pieces, pieces)]
    )
    gf, ga = Gather(g, fg), Gather(g, v.mid)
    pick = lambda ref: (lambda s, i: ref.at[s, i])
    own = lambda ref: (lambda s: ref.at[s])
    s_mid = Scatter(g, pick(stage), pick(got), own(held), temp)
    s_hid = Scatter(g, pick(stage), pick(got), own(held), temp)
    s_tok = Scatter(g, pick(stage), pick(got), own(held), temp)
    s_chr = Scatter(g, pick(cstage), pick(cgot), own(cheld), ctemp)
    s_cout = Scatter(g, pick(cstage), pick(cgot), own(cheld), ctemp)

    def own_branch(s):
        return pltpu.make_async_copy(
            hbm.branch.at[s], gb.at(s, me), local.at[spare + 4 + 2 * seqs + s]
        )

    each(lambda s: own_branch(s).start())
    for name in ("dmg", "res4", "mg", "mid", "st"):
        load(name).start()
    states_copy(0).start()
    for tile in range(2):
        decay_copy(0, tile).start()
    for name in names:
        if name not in ("dmg", "res4", "mg", "mid", "st"):
            load(name).start()

    barrier = pltpu.get_barrier_semaphore()
    places = [{"tensor": g.pair}, {"tensor": g.far}]
    if inside:
        places += [{"dp": plane.peer(way)} for way in ("x", "up", "down")]
        places += [{"dp": plane.pair(2)}]
    for place in places:
        pl.semaphore_signal(barrier, inc=1, device_id=place, device_id_type=pl.DeviceIdType.MESH)
    pl.semaphore_wait(barrier, len(places))
    each(gb.start)
    dpre[...] = jnp.zeros_like(dpre)
    small[...] = jnp.zeros_like(small)
    small[0, pl.ds(0, 4), :] = norm_in[...]
    lane = lax.broadcasted_iota(jnp.int32, (shard, LANE), 1)
    left = lane < HD
    for name in ("dmg", "res4"):
        load(name).wait()

    def block_rows(t, size):
        return pl.ds(pl.multiple_of(t * size, size), size)

    def merge_back(s):
        gb.forward(s)
        gb.finish(s)
        own_branch(s).wait()

        def inner(t, carry):
            rows = block_rows(t, shard)
            back = None
            for j in range(pieces):
                piece = nt(pb[s, t * pieces + j], wm[:, j * length : (j + 1) * length])
                back = piece if back is None else back + piece
            dpre[pl.ds(pl.multiple_of(8 + t * shard, 8), shard), :] = (
                (back * v.dmg[s, rows, :].astype(F32)).astype(BF16).astype(F32)
            )
            return carry

        lax.fori_loop(0, 4, inner, 0)

        def taps(t, carry):
            rows = block_rows(t, shard)
            window = dpre[pl.ds(pl.multiple_of(t * shard, 8), shard + 16), :]
            marks = edges[s, rows, :]
            before = window[9 : 9 + shard] * marks[:, 2:3]
            after = window[7 : 7 + shard] * marks[:, 3:4]
            dyk[s, rows, :] = pack3(
                [before, window[8 : 8 + shard], after], channels
            ).astype(BF16)
            return carry

        lax.fori_loop(0, 4, taps, 0)

        def mid_part(b, out):
            out[...] = nt(dyk[s, block_rows(b, shard), :], wc[pl.ds(0, width), :])

        s_mid.start(s, mid_part)

    each(merge_back)
    sums, marks_at = [], {}
    for which, height, x_first in PIECES if inside else ():
        name = GRADS[which]
        first, at = marks_at.get(name, (0, 0))
        sums.append(
            Reduce(
                plane, getattr(big, name), grads_out[name], land[name], first, at, height, x_first
            )
        )
        marks_at[name] = (first + height, at + Reduce.landing_rows(height, x_first))
    fired = [0] * len(sums)

    def fire(hook):
        for entry in SCHEDULE[hook] if inside else ():
            which, number = divmod(entry, 10)
            fired[which] += 1
            sums[which].step(number)

    def fire_in(seq, hook, stride):
        for k in range(2):
            pl.when(seq == k)(functools.partial(fire, hook + k * stride))

    tokens = seqs * length
    step_w = 2 * LANE

    def merge_weights():
        for name in ("mg", "mid", "st"):
            load(name).wait()

        half_w = width
        for j in range(pieces):
            right = jnp.concatenate(
                [pb[s, t * pieces + j] for s in range(seqs) for t in range(4)], axis=0
            )
            out = tn(v.mg[...].reshape(tokens, -1), right)[:channels].astype(BF16)
            at = 0
            while at < length:
                part, inside_at = divmod(j * length + at, half_w)
                size = min(length - at, half_w - inside_at)
                big.merge[pl.ds(part * channels, channels), pl.ds(inside_at, size)] = out[
                    :, at : at + size
                ]
                at += size
        def conv_mid(j, carry):
            colsj = pl.ds(pl.multiple_of(j * step_w, step_w), step_w)
            out = tn(v.mid[:, :, :, colsj].reshape(tokens, step_w), dyk[...].reshape(tokens, -1))
            big.conv[block_rows(j, step_w), :] = out.astype(BF16)
            return carry

        lax.fori_loop(0, width // step_w, conv_mid, 0)

        def conv_char(t, carry):
            out = tn(v.st[:, t].reshape(tokens, 2 * LANE), dyk[...].reshape(tokens, -1))
            for d in range(2):
                first = pl.multiple_of(width + d * 4 * units + t * units, 16)
                big.conv[pl.ds(first, units), :] = out[d * LANE : d * LANE + units].astype(BF16)
            return carry

        lax.fori_loop(0, 4, conv_char, 0)
        p_copy().start()
        fire(1)

    def second_back(s):
        incoming = v.res3[s] + s_mid.finish(s)
        unit = v.unit1[s]
        small[0, 5:6] += jnp.sum(incoming * unit, axis=0, keepdims=True)
        small[0, 7:8] += jnp.sum(incoming, axis=0, keepdims=True)
        spread = v.scale[s, 1][:, 0:1]
        res2[s] = normalize_back(unit, spread, incoming * gain[1:2])
        fg[s, me] = res2[s].astype(BF16)
        gf.start(s)
        fire_in(s, 0, 2)
        pl.when(s == 0)(merge_weights)

    for name in ("res3", "unit1", "scale"):
        load(name).wait()
    each(second_back)
    for name in ("dact", "act", "h"):
        load(name).wait()

    def ffn_back(s):
        gf.forward(s)
        gf.finish(s)

        def part(b, out):
            back = nt(fg[s, b], wdown[...]) * v.dact[s, b].astype(F32)
            v.dact[s, b] = back.astype(BF16)
            out[...] = nt(v.dact[s, b], win[...])

        s_hid.start(s, part)
        fire_in(s, 3, 1)

    each(ffn_back)

    def all_ffn_weights():
        def ffn_weights(j, carry):
            colsj = pl.ds(pl.multiple_of(j * step_w, step_w), step_w)
            out = tn(v.act[:, :, :, colsj].reshape(tokens, step_w), fg[...].reshape(tokens, width))
            big.down[block_rows(j, step_w), :] = out.astype(BF16)
            return carry

        lax.fori_loop(0, big.down.shape[0] // step_w, ffn_weights, 0)
        fire(6)

        def in_weights(j, carry):
            colsj = pl.ds(pl.multiple_of(j * step_w, step_w), step_w)
            out = tn(
                v.h[:, :, :, colsj].reshape(tokens, step_w), v.dact[...].reshape(tokens, -1)
            )
            big.win[block_rows(j, step_w), :] = out.astype(BF16)
            return carry

        lax.fori_loop(0, width // step_w, in_weights, 0)
        x_copy().start()
        fire(7)

    load("unit0").wait()

    def first_back(s):
        incoming = res2[s] + s_hid.finish(s)
        unit = v.unit0[s]
        small[0, 4:5] += jnp.sum(incoming * unit, axis=0, keepdims=True)
        small[0, 6:7] += jnp.sum(incoming, axis=0, keepdims=True)
        spread = v.scale[s, 0][:, 0:1]
        res1[s] = normalize_back(unit, spread, incoming * gain[0:1])
        v.mid[s, me] = res1[s].astype(BF16)
        ga.start(s)
        fire_in(s, 5, 3)
        pl.when(s == 0)(all_ffn_weights)

    each(first_back)

    def chars_back(s):
        def char_part(b, out):
            first = pl.multiple_of(width + b * 2 * LANE, 2 * LANE)
            out[...] = nt(dyk[s], wc[pl.ds(first, 2 * LANE), :])
            out[block_rows(me, shard), :] += v.res4[s, b].astype(F32)

        s_chr.start(s, char_part)
        fire_in(s, 9, 1)

    each(chars_back)
    hops = [("t", g.pair), ("t", g.far)] + ([("d", k) for k in range(3)] if inside else [])
    slots_t, slots_d = g.slots(2), plane.take(3)

    def small_copy(number):
        kind, where = hops[number]
        source, target = small.at[number], small_land.at[number]
        if kind == "t":
            return g.copy(slots_t[number], 0, source, target, where)
        return plane.copy(slots_d[where], source, target, plane.pair(where))

    def small_step(number):
        if number > 0:
            small_copy(number - 1).wait()
            value, more = small[number - 1], small_land[number - 1]
            small[number, pl.ds(0, 8), :] = value[:8] + more[:8]
            rest = small[6, pl.ds(0, 8), :] if number <= 2 else value[8:] + more[8:]
            small[number, pl.ds(8, 8), :] = rest
        if number < len(hops):
            small_copy(number).start()

    if not inside:
        hops = []
    small_step(0) if hops else None
    for name in ("qkv", "ctx"):
        load(name).wait()
    p_copy().wait()

    def attention_back(s):
        ga.forward(s)
        ga.finish(s)
        dctx = v.dmg

        def context(t, carry):
            dctx[s, block_rows(t, shard), :] = nt(v.mid[s, t], wout[...]).astype(BF16)
            return carry

        lax.fori_loop(0, 4, context, 0)
        for tile in range(cols // LANE):
            lanes = pl.ds(tile * LANE, LANE)
            for half in range(2):
                head = 2 * tile + half
                if head >= heads:
                    continue
                paired = 2 * tile + 1 < heads

                def rows_of(b, carry):
                    rows = block_rows(b, shard)
                    grad = dctx[s, rows, lanes]
                    if paired:
                        grad = jnp.where(left if half == 0 else ~left, grad, jnp.zeros_like(grad))
                    back = nt(grad, v.qkv[s, 2, :, lanes])
                    probs = pb[s, head * 4 + b].astype(F32)
                    row_dot = jnp.sum(probs * back, axis=-1, keepdims=True)
                    ds[b] = (probs * (back - row_dot)).astype(BF16)
                    out = nn(ds[b], v.qkv[s, 1, :, lanes])
                    if half == 1:
                        out = jnp.where(left, ctemp[rows, lanes], out)
                    ctemp[rows, lanes] = out
                    return carry

                lax.fori_loop(0, 4, rows_of, 0)
                keys = tn(ds[...].reshape(length, length), v.qkv[s, 0, :, lanes])
                values = tn(
                    pb[s, pl.ds(head * 4, 4)].reshape(length, length), dctx[s, :, lanes]
                )
                if half == 1:
                    wide_left = lax.broadcasted_iota(jnp.int32, (length, LANE), 1) < HD
                    keys = jnp.where(wide_left, parts[0, :, lanes], keys)
                    values = jnp.where(wide_left, parts[1, :, lanes], values)
                parts[0, :, lanes] = keys
                parts[1, :, lanes] = values
                fire_in(s, 11 + head, 4)

        def pack(t, carry):
            rows = block_rows(t, shard)
            query = ctemp[rows, :].astype(BF16).astype(F32) * 0.125
            dyk[s, rows, :] = pack3(
                [query, parts[0, rows, :], parts[1, rows, :]], HD * heads
            ).astype(BF16)
            return carry

        lax.fori_loop(0, 4, pack, 0)

        def part(b, out):
            out[...] = nt(dyk[s, block_rows(b, shard), :], wq[...])

        s_tok.start(s, part)

        fire_in(s, 14, 4)

    each(attention_back)
    small_step(1) if hops else None

    x_copy().wait()

    def qkv_weights(j, carry):
        colsj = pl.ds(pl.multiple_of(j * step_w, step_w), step_w)
        out = tn(v.h[:, :, :, colsj].reshape(tokens, step_w), dyk[...].reshape(tokens, -1))
        big.qkv[block_rows(j, step_w), :] = out.astype(BF16)
        return carry

    lax.fori_loop(0, width // step_w, qkv_weights, 0)
    big.out[...] = tn(
        v.ctx[...].reshape(tokens, -1), v.mid[...].reshape(tokens, width)
    ).astype(BF16)
    fire(19)

    load("c").wait()

    def gru_back(s):
        gtok[...] = s_chr.finish(s).astype(BF16)
        for peer in (g.pair, g.far):
            pl.semaphore_signal(
                credit.at[s], inc=1, device_id={"tensor": peer},
                device_id_type=pl.DeviceIdType.MESH,
            )
        def spread_out(t, carry):
            rows = block_rows(t, LANE)
            for tile in range(2):
                ids = lax.broadcasted_iota(jnp.int32, (LANE, length), 0) + t * LANE
                hot = (ids == pickr[s, tile : tile + 1, :]).astype(F32).astype(BF16)
                drive[tile, rows, :] = nn(hot, gtok[:, pl.ds(tile * LANE, LANE)])
            return carry

        lax.fori_loop(0, total // LANE, spread_out, 0)
        fire_in(s, 20, 3)
        for tile in range(2):
            decay_copy(s, tile).wait()
        recur((False, True), decay, drive, drive, block_chars, back=True)
        fire_in(s, 21, 3)
        states_copy(s).wait()

        @pl.when(s == 0)
        def _():
            gru_acc[...] = jnp.zeros_like(gru_acc)

        def part(b, out):
            def finish(t, sums):
                inner = block_rows(t, LANE)
                rows = pl.ds(pl.multiple_of(b * block_chars + t * LANE, LANE), LANE)
                proj = nn(v.c[s, b, inner, :], wg[...])
                new = []
                for tile in range(2):
                    colst = slice(tile * LANE, (tile + 1) * LANE)
                    gate = jax.nn.sigmoid(proj[:, colst] + gate_bias[:, colst])
                    cand = proj[:, (2 + tile) * LANE : (3 + tile) * LANE]
                    flow = drive[tile, rows, :] * gate
                    logit = flow * (cand - states[tile, rows, :].astype(F32))
                    dproj[inner, pl.ds(tile * LANE, LANE)] = logit.astype(BF16)
                    dproj[inner, pl.ds((2 + tile) * LANE, LANE)] = flow.astype(BF16)
                    new.append(sums[tile] + jnp.sum(logit, axis=0, keepdims=True))
                return tuple(new)

            zero = jnp.zeros((1, LANE), F32)
            sums = lax.fori_loop(0, block_chars // LANE, finish, (zero, zero))
            for tile in range(2):
                small[6, 0:1, pl.ds(tile * LANE, LANE)] += sums[tile]
            out[...] = nt(dproj[...], wg[...])
            gru_acc[...] += tn(v.c[s, b], dproj[...])

        pl.semaphore_wait(credit.at[s], 2)
        s_cout.start(s, part)

        @pl.when(s + 1 < seqs)
        def _():
            states_copy(s + 1).start()
            for tile in range(2):
                decay_copy(s + 1, tile).start()

        if seqs > 1:
            pl.when(s == 0)(functools.partial(fire, 22))

    each(gru_back)
    big.gru[...] = gru_acc[...].astype(BF16)
    small_step(2) if hops else None
    fire(25)

    def last(s):
        res1[s] = res1[s] + s_tok.finish(s)
        out_copy(0, s).start()
        cheld[s] = s_cout.finish(s)
        out_copy(1, s).start()

    each(last)

    def emit(name):
        return pltpu.make_async_copy(
            getattr(big, name), grads_out[name], local.at[spare + 4 + 3 * seqs + GRADS.index(name)]
        )

    if inside:
        fire(26)
        small_step(3)
        fire(27)
        small_step(4)
        fire(28)
        small_step(5)
        fire(29)
        assert all(count == Reduce.steps for count in fired)
    else:
        for name in GRADS:
            emit(name).start()
        for name in GRADS:
            emit(name).wait()
    small_out[...] = small[len(hops)]
    if not inside:
        small_out[pl.ds(8, 8), :] = small[6, pl.ds(0, 8), :]
    each(lambda s: (out_copy(0, s).wait(), out_copy(1, s).wait()))


def backward_call(saved, weights, small, dp_size):
    wq, wout, win, wdown, wg, gate_bias, wc, wm = weights
    sds = jax.ShapeDtypeStruct
    seqs, shard, width = saved["res3"].shape
    length = shard * 4
    block_chars, char_width = saved["c"].shape[2:]
    total = 4 * block_chars
    cols, packed = wout.shape[0], wc.shape[1]
    channels = small["channels"]
    saved_in = [saved[n] for n in SAVED]
    names = [n for n in SAVED if n not in ("branch", "states", "decay", "p", "x")]
    shapes = [(saved[n].shape, saved[n].dtype) for n in names]
    grads = {
        "merge": (2 * channels, width), "conv": (2 * width, packed),
        "down": (win.shape[1], width), "win": (width, win.shape[1]),
        "gru": (char_width, 4 * LANE), "out": (cols, width), "qkv": (width, wq.shape[1]),
    }
    pad = (seqs, 3, shard, width)
    cpad = (seqs, 3, length, 2 * LANE)
    scratch = shapes + [
        (saved["p"].shape, BF16),
        ((2, total, LANE), BF16),
        ((2, total, LANE), F32),
        ((2, total, LANE), F32),
        ((length + 16, wm.shape[0]), F32),
        ((seqs, length, packed), BF16),
        ((seqs, 4, shard, width), BF16),
        ((length, 2 * LANE), BF16),
        ((block_chars, 4 * LANE), BF16),
        ((char_width, 4 * LANE), F32),
        ((seqs, shard, width), F32),
        ((seqs, shard, width), F32),
        ((4, shard, length), BF16),
        ((2, length, cols), F32),
        (pad, BF16), (pad, BF16), ((seqs, shard, width), F32), ((shard, width), F32),
        (cpad, BF16), (cpad, BF16), ((seqs, length, 2 * LANE), F32), ((length, 2 * LANE), F32),
    ]
    for which, name in enumerate(GRADS):
        landing = sum(Reduce.landing_rows(n, way) for k, n, way in PIECES if k == which)
        scratch.append(((landing if dp_size == 8 else 16, grads[name][1]), BF16))
    scratch += [(shape, BF16) for shape in grads.values()]
    scratch += [((7, 16, width), F32), ((5, 16, width), F32)]
    anyspace = pl.BlockSpec(memory_space=pl.ANY)
    vmem = pl.BlockSpec(memory_space=pltpu.VMEM)
    ins = saved_in + list(weights) + [small["gain"], small["pickr"], small["edges"], saved["norm_grads"]]
    outs = pl.pallas_call(
        functools.partial(backward_kernel, small["units"], channels, dp_size),
        out_shape=[sds((seqs, shard, width), F32), sds((seqs, block_chars, char_width), F32)]
        + [sds(shape, BF16) for shape in grads.values()]
        + [sds((16, width), F32)],
        in_specs=[anyspace] * len(saved_in) + [vmem] * (len(ins) - len(saved_in)),
        out_specs=[anyspace] * (2 + len(grads)) + [vmem],
        scratch_shapes=[pltpu.VMEM(*one) for one in scratch]
        + [
            pltpu.SemaphoreType.DMA((32 * seqs,)),
            pltpu.SemaphoreType.DMA((32 * seqs,)),
            pltpu.SemaphoreType.DMA((14 * len(PIECES) + 4,)),
            pltpu.SemaphoreType.DMA((14 * len(PIECES) + 4,)),
            pltpu.SemaphoreType.DMA((40,)),
            pltpu.SemaphoreType.DMA((len(PIECES),)),
            pltpu.SemaphoreType.REGULAR((seqs,)),
        ],
        compiler_params=pltpu.CompilerParams(
            collective_id=1, has_side_effects=True, vmem_limit_bytes=63 * MIB
        ),
    )(*ins)
    names = ["grad_tokens", "grad_chars"] + list(grads) + ["small"]
    return dict(zip(names, outs))


def local(
    tokens,
    characters,
    doc_lengths,
    token_chars,
    w_qkv,
    w_out,
    w_in,
    w_down,
    w_gru,
    gate_bias,
    w_conv,
    w_merge,
    norm_gain,
    norm_bias,
    token_cot,
    char_cot,
):
    micro_count = tokens.shape[0]
    shard_len = tokens.shape[1]
    model_width = tokens.shape[2]
    char_width = characters.shape[2]
    group_size = lax.axis_size("tensor")
    group_rank = lax.axis_index("tensor")
    length = shard_len * group_size
    char_total = characters.shape[1] * group_size
    head_cols = w_qkv.shape[2]
    heads_here = head_cols // HD
    units_here = w_gru.shape[3]
    merge_here = w_conv.shape[2]
    gru_matrix, gru_bias = gru_weights(w_gru, gate_bias)
    spare = -head_cols % LANE
    more = -merge_here % LANE
    wq = jnp.pad(
        w_qkv.reshape(model_width, 3 * head_cols), ((0, 0), (0, -3 * head_cols % LANE))
    )
    wout = jnp.pad(w_out, ((0, spare), (0, 0)))
    wm = jnp.pad(w_merge.reshape(merge_here, 2 * model_width), ((0, more), (0, 0)))
    conv = jnp.swapaxes(w_conv, 0, 1).reshape(2 * model_width, 3 * merge_here)
    conv = jnp.pad(conv, ((0, 0), (0, -3 * merge_here % LANE)))
    conv_char = conv[model_width:].reshape(2, group_size, units_here, -1)
    conv_char = jnp.pad(
        jnp.swapaxes(conv_char, 0, 1), ((0, 0), (0, 0), (0, LANE - units_here), (0, 0))
    )
    wc = jnp.concatenate(
        [conv[:model_width], conv_char.reshape(group_size * 2 * LANE, -1)], axis=0
    )
    layouts = [layout(doc_lengths[i], token_chars[i], char_total) for i in range(micro_count)]
    stacked_layout = [jnp.stack(parts) for parts in zip(*layouts)]
    segment, first_char, last_char, keep_forward, keep_backward, prev_ok, next_ok = stacked_layout
    block_chars = characters.shape[1]
    steps = block_chars // 8

    def reorder(rows):
        split = rows.reshape(micro_count, -1, 8, steps, rows.shape[-1])
        return jnp.swapaxes(split, 2, 3).reshape(rows.shape)

    keep = reorder(jnp.stack([keep_forward, keep_backward], axis=2))
    picks = jnp.stack([last_char, first_char], axis=2)
    inner = picks % block_chars
    picks = picks - inner + inner % steps * 8 + inner // steps
    zero = jnp.zeros_like(prev_ok[:, :1])
    small = dict(
        gain=norm_gain, bias=norm_bias, cot_t=token_cot, cot_c=char_cot,
        segc=segment[:, :, None], segr=segment[:, None, :], pickc=picks, keep=keep,
        pickr=jnp.swapaxes(picks, 1, 2),
        edges=jnp.stack(
            [
                prev_ok,
                next_ok,
                jnp.concatenate([prev_ok[:, 1:], zero], axis=1),
                jnp.concatenate([zero, next_ok[:, :-1]], axis=1),
            ],
            axis=2,
        ),
        heads=heads_here, units=units_here, channels=merge_here,
    )
    weights = (wq, wout, w_in, w_down, gru_matrix, gru_bias, wc, wm)
    fw = forward_call(tokens, reorder(characters), weights, small)
    dp_size = lax.axis_size("dp")
    bw = backward_call(fw, weights, small, dp_size)
    rows = bw["small"]
    gate_row = rows[8, : 2 * LANE]
    grads = {name: bw[name] for name in GRADS}
    if dp_size != 8:
        grads, gate_row = lax.psum((grads, gate_row), "dp")
        rows = lax.psum(rows, ("dp", "tensor"))
    grads = {name: value.astype(F32) for name, value in grads.items()}
    grad_conv = jnp.stack(
        [grads["conv"][:, k * merge_here : (k + 1) * merge_here] for k in range(3)], axis=0
    )
    grad_merge = grads["merge"].reshape(2, merge_here, model_width)
    grad_gru = grads["gru"].reshape(char_width, 2, 2, LANE)[..., :units_here]
    grad_chars = jnp.swapaxes(
        bw["grad_chars"].reshape(micro_count, steps, 8, char_width), 1, 2
    )
    return (
        fw["token_out"],
        fw["char_out"],
        bw["grad_tokens"],
        grad_chars.reshape(bw["grad_chars"].shape),
        grads["qkv"][:, : 3 * head_cols].reshape(model_width, 3, head_cols),
        grads["out"][:head_cols],
        grads["win"],
        grads["down"],
        jnp.swapaxes(grad_gru, 1, 2),
        gate_row.reshape(2, LANE)[:, :units_here],
        grad_conv,
        jnp.swapaxes(grad_merge, 0, 1),
        jnp.concatenate([rows[4:6], rows[0:2]], axis=0),
        jnp.concatenate([rows[6:8], rows[2:4]], axis=0),
    )


def solution(mesh):
    return jax.shard_map(
        local,
        mesh=mesh,
        in_specs=(
            P("dp", "tensor", None),
            P("dp", "tensor", None),
            P("dp", None),
            P("dp", None),
            P(None, None, "tensor"),
            P("tensor", None),
            P(None, "tensor"),
            P("tensor", None),
            P(None, None, None, "tensor"),
            P(None, "tensor"),
            P(None, None, "tensor"),
            P("tensor", None, None),
            P(),
            P(),
            P("dp", "tensor", None),
            P("dp", "tensor", None),
        ),
        out_specs=(
            P("dp", "tensor", None),
            P("dp", "tensor", None),
            P("dp", "tensor", None),
            P("dp", "tensor", None),
            P(None, None, "tensor"),
            P("tensor", None),
            P(None, "tensor"),
            P("tensor", None),
            P(None, None, None, "tensor"),
            P(None, "tensor"),
            P(None, None, "tensor"),
            P("tensor", None, None),
            P(),
            P(),
        ),
        check_vma=False,
    )
```

```python
import functools
from types import SimpleNamespace

import jax
import jax.numpy as jnp
from jax import lax
from jax.experimental import pallas as pl
from jax.experimental.pallas import tpu as pltpu
from jax.sharding import PartitionSpec as P

HD = 64


NORM_EPSILON = 1e-06
MASK_VALUE = -1e30
HIGH_PRECISION = lax.Precision.HIGHEST


def layout(doc_sizes, char_counts, char_total):
    length = char_counts.shape[0]
    docs = doc_sizes.shape[0]
    doc_ids = jnp.arange(docs, dtype=jnp.int32)
    doc_ends = jnp.sum(
        jnp.where(doc_ids[None, :] <= doc_ids[:, None], doc_sizes[None, :], 0), axis=1
    )
    positions = jnp.arange(length, dtype=jnp.int32)
    segment = jnp.sum(
        (positions[:, None] >= doc_ends[None, :]).astype(jnp.int32), axis=1, dtype=jnp.int32
    )
    token_ends = jnp.sum(
        jnp.where(positions[None, :] <= positions[:, None], char_counts[None, :], 0), axis=1
    )
    last_char = token_ends - 1
    first_char = token_ends - char_counts
    char_ends = jnp.sum(
        jnp.where(positions[None, :] < doc_ends[:, None], char_counts[None, :], 0), axis=1
    )
    char_positions = jnp.arange(char_total, dtype=jnp.int32)
    starts = char_ends - jnp.sum(
        jnp.where(
            (positions[None, :] < doc_ends[:, None])
            & (positions[None, :] >= (doc_ends - doc_sizes)[:, None]),
            char_counts[None, :],
            0,
        ),
        axis=1,
    )
    keep_forward = 1.0 - jnp.any(char_positions[:, None] == starts[None, :], axis=1).astype(
        jnp.float32
    )
    keep_backward = 1.0 - jnp.any(
        char_positions[:, None] == (char_ends - 1)[None, :], axis=1
    ).astype(jnp.float32)
    token_starts = doc_ends - doc_sizes
    prev_ok = 1.0 - jnp.any(positions[:, None] == token_starts[None, :], axis=1).astype(
        jnp.float32
    )
    next_ok = 1.0 - jnp.any(positions[:, None] == (doc_ends - 1)[None, :], axis=1).astype(
        jnp.float32
    )
    return (segment, first_char, last_char, keep_forward, keep_backward, prev_ok, next_ok)


F32 = jnp.float32
BF16 = jnp.bfloat16
LANE = 128
MIB = 1024 * 1024
VMEM = pl.BlockSpec(memory_space=pltpu.VMEM)


def nn(left, right):
    return jnp.dot(left, right, preferred_element_type=F32)


def nt(left, right):
    return lax.dot_general(left, right, (((1,), (1,)), ((), ())), preferred_element_type=F32)


def tn(left, right):
    return lax.dot_general(left, right, (((0,), (0,)), ((), ())), preferred_element_type=F32)


def gelu_pair(values):
    cdf = 0.5 * (1.0 + lax.erf(values * 0.7071067811865476))
    density = 0.3989422804014327 * jnp.exp(-0.5 * values * values)
    return values * cdf, cdf + values * density


def normalize(rows):
    centered = rows - jnp.mean(rows, axis=-1, keepdims=True)
    scale = lax.rsqrt(jnp.mean(centered * centered, axis=-1, keepdims=True) + NORM_EPSILON)
    return centered * scale, scale


def normalize_back(unit, scale, grad_unit):
    return scale * (
        grad_unit
        - jnp.mean(grad_unit, axis=-1, keepdims=True)
        - unit * jnp.mean(grad_unit * unit, axis=-1, keepdims=True)
    )


def roll_lanes(value, shift):
    return pltpu.roll(value, shift % value.shape[1], axis=1)


def unpack3(packed, size):
    room = -(-size // LANE) * LANE
    lane = lax.broadcasted_iota(jnp.int32, (packed.shape[0], room), 1)
    parts = []
    for k in range(3):
        first = k * size // LANE * LANE
        inner = k * size - first
        part = packed[:, first : min(first + room + LANE, packed.shape[1])]
        if inner:
            part = roll_lanes(part, -inner)
        parts.append(jnp.where(lane < size, part[:, :room], 0.0))
    return parts


def pack3(parts, size):
    room = parts[0].shape[1]
    columns = -(-3 * size // LANE) * LANE
    tiles = [None] * (columns // LANE)
    for k in range(3):
        first, inner = divmod(k * size, LANE)
        part = parts[k]
        if inner:
            part = jnp.concatenate([part, jnp.zeros_like(part[:, :LANE])], axis=1)
            part = roll_lanes(part, inner)
        for j in range(part.shape[1] // LANE):
            if first + j < len(tiles) and (first + j) * LANE < (k + 1) * size:
                tile = part[:, j * LANE : (j + 1) * LANE]
                old = tiles[first + j]
                tiles[first + j] = tile if old is None else old + tile
    return jnp.concatenate(tiles, axis=1)


class Group:
    def __init__(self, send, recv, seqs):
        self.me = lax.axis_index("tensor")
        self.low = self.me % 2
        self.high = self.me // 2
        self.pair = self.high * 2 + (1 - self.low)
        self.far = (1 - self.high) * 2 + self.low
        self.send, self.recv, self.seqs, self.used = send, recv, seqs, 0

    def block(self, turn):
        left = 3 - turn
        return ((self.high + left // 2) % 2) * 2 + (self.low + left % 2) % 2

    def slots(self, count):
        first = self.used
        self.used += count
        return [first + i for i in range(count)]

    def copy(self, slot, seq, source, target, peer):
        index = slot * self.seqs + seq
        return pltpu.make_async_remote_copy(
            src_ref=source,
            dst_ref=target,
            send_sem=self.send.at[index],
            recv_sem=self.recv.at[index],
            device_id={"tensor": peer},
            device_id_type=pl.DeviceIdType.MESH,
        )

    def greet(self):
        barrier = pltpu.get_barrier_semaphore()
        for peer in (self.pair, self.far):
            pl.semaphore_signal(
                barrier, inc=1, device_id={"tensor": peer}, device_id_type=pl.DeviceIdType.MESH
            )
        pl.semaphore_wait(barrier, 2)


class Gather:
    def __init__(self, group, buf, source=None, place=None):
        self.group, self.source = group, source
        self.at = place or (lambda seq, t: buf.at[seq, t])
        self.near, self.over, self.fwd = group.slots(3)

    def own(self, seq):
        return self.at(seq, self.group.me) if self.source is None else self.source.at[seq]

    def near_copy(self, seq):
        g = self.group
        return g.copy(self.near, seq, self.own(seq), self.at(seq, g.me), g.pair)

    def over_copy(self, seq):
        g = self.group
        return g.copy(self.over, seq, self.own(seq), self.at(seq, g.me), g.far)

    def fwd_copy(self, seq):
        g = self.group
        other = self.at(seq, g.far)
        return g.copy(self.fwd, seq, other, other, g.pair)

    def start(self, seq):
        self.over_copy(seq).start()
        self.near_copy(seq).start()

    def forward(self, seq):
        self.over_copy(seq).wait_recv()
        self.fwd_copy(seq).start()

    def finish(self, seq):
        near = self.near_copy(seq)
        fwd = self.fwd_copy(seq)
        near.wait_recv()
        fwd.wait_recv()
        near.wait_send()
        self.over_copy(seq).wait_send()
        fwd.wait_send()


class Scatter:
    def __init__(self, group, stage, got, own, temp):
        self.group, self.stage, self.got, self.held, self.temp = group, stage, got, own, temp
        self.names = group.slots(3)

    def copies(self, seq):
        g = self.group
        peers = (g.pair, g.pair, g.far)
        return [
            g.copy(self.names[i], seq, self.stage(seq, i), self.got(seq, i), peers[i])
            for i in range(3)
        ]

    def start(self, seq, part):
        mine, other, over = self.copies(seq)

        def turn(step, carry):
            part(self.group.block(step), self.temp)

            @pl.when(step == 0)
            def _():
                self.stage(seq, 1)[...] = self.temp[...].astype(BF16)
                other.start()

            @pl.when(step == 1)
            def _():
                other.wait_recv()
                self.stage(seq, 2)[...] = (self.temp[...] + self.got(seq, 1)[...]).astype(BF16)
                over.start()

            @pl.when(step == 2)
            def _():
                self.stage(seq, 0)[...] = self.temp[...].astype(BF16)
                mine.start()

            @pl.when(step == 3)
            def _():
                self.held(seq)[...] = self.temp[...]

            return carry

        lax.fori_loop(0, 4, turn, 0)

    def finish(self, seq):
        mine, other, over = self.copies(seq)
        mine.wait_recv()
        over.wait_recv()
        total = self.held(seq)[...] + self.got(seq, 0)[...] + self.got(seq, 2)[...]
        mine.wait_send()
        other.wait_send()
        over.wait_send()
        return total


def shift_rows(value, count, up, fill):
    edge = jnp.full((count, value.shape[1]), fill, value.dtype)
    if up:
        return jnp.concatenate([edge, value[:-count]], axis=0)
    return jnp.concatenate([value[count:], edge], axis=0)


def recur(ups, decays, drives, outs, block, back=False):
    steps = block // 8
    pairs = [(tile, t) for tile in range(2) for t in range(4)]

    def rows(tile, t, step):
        row = step if ups[tile] else steps - 1 - step
        return pl.ds(pl.multiple_of(t * block + row * 8, 8), 8)

    def summary(step, carry):
        new = []
        for i, (tile, t) in enumerate(pairs):
            state, mult = carry[2 * i], carry[2 * i + 1]
            here = rows(tile, t, step)
            decay, drive = decays[tile, here, :], drives[tile, here, :]
            state = decay * (state + drive) if back else decay * state + drive
            new += [state, decay * mult]
        return tuple(new)

    zero, one = jnp.zeros((8, LANE), F32), jnp.ones((8, LANE), F32)
    ends = lax.fori_loop(0, steps, summary, (zero, one) * 8, unroll=4)
    starts = []
    for tile in range(2):
        state = jnp.concatenate([ends[2 * (4 * tile + t)] for t in range(4)], axis=0)
        mult = jnp.concatenate([ends[2 * (4 * tile + t) + 1] for t in range(4)], axis=0)
        for count in (1, 2, 4, 8, 16):
            state = mult * shift_rows(state, count, ups[tile], 0.0) + state
            mult = mult * shift_rows(mult, count, ups[tile], 1.0)
        state = shift_rows(state, 1, ups[tile], 0.0)
        starts += [state[8 * t : 8 * t + 8] for t in range(4)]

    def write(step, carry):
        new = []
        for i, (tile, t) in enumerate(pairs):
            here = rows(tile, t, step)
            decay, drive = decays[tile, here, :], drives[tile, here, :]
            if back:
                value = drive + carry[i]
                new.append(decay * value)
            else:
                value = decay * carry[i] + drive
                new.append(value)
            outs[tile, here, :] = value
        return tuple(new)

    lax.fori_loop(0, steps, write, tuple(starts), unroll=4)


def forward_kernel(
    units, channels, tokens, chars, wq_in, wout_in, win, wdown, wg_in, gate_in, wc_in, wm, gain, bias,
    cot_t, cot_c,
    segc, segr, pickc, keep, edges,
    token_out, char_out, o_x, o_c, o_qkv, o_p, o_ctx, o_h, o_act, o_dact, o_mid, o_st, o_mg,
    o_dmg, o_states, o_decay, o_unit0, o_unit1, o_scale, o_res3, o_res4, o_branch,
    o_wq, o_wout, o_wg, o_wc, norm_grads,
    x, c, qkv, p, ctx, h, act, dact, mid, st, mg, dmg, low_states, decays, unit0, unit1, scale, res3, res4, branch,
    wq, wout, wg, wc, hidden, middle, outs_t, outs_c, states, drive, taps, perm, gate_bias,
    stage, got, held, temp, send, recv, local,
):
    seqs, length = tokens.shape[0], segr.shape[2]
    shard, width = tokens.shape[1], tokens.shape[2]
    block_chars = chars.shape[1]
    heads = p.shape[1] // 4
    g = Group(send, recv, seqs)
    me = g.me
    saves = []

    def keep_out(seq, source, target):
        saves.append((source, target, len(saves)))

    def local_copy(number, seq, source, target):
        return pltpu.make_async_copy(source, target, local.at[number * seqs + seq])

    gx, gc = Gather(g, x, tokens), Gather(g, c, chars)
    gh, gm, gs = Gather(g, h), Gather(g, mid), Gather(g, st)
    narrow = lambda ref: (lambda s, i: ref.at[s, i, :, pl.ds(0, width)])
    wide = lambda ref: (lambda s, i: ref.at[s, i])
    own_n = lambda s: held.at[s, :, pl.ds(0, width)]
    own_w = lambda s: held.at[s]
    thin = temp.at[:, pl.ds(0, width)]
    s_attn = Scatter(g, narrow(stage), narrow(got), own_n, thin)
    s_ffn = Scatter(g, narrow(stage), narrow(got), own_n, thin)
    s_branch = Scatter(g, wide(stage), wide(got), own_w, temp)

    def own_x(seq):
        return local_copy(0, seq, tokens.at[seq], x.at[seq, me])

    def own_c(seq):
        return local_copy(1, seq, chars.at[seq], c.at[seq, me])

    plan = [
        (x, o_x), (c, o_c), (qkv, o_qkv), (p, o_p), (ctx, o_ctx), (h, o_h), (act, o_act),
        (dact, o_dact), (mid, o_mid), (st, o_st), (mg, o_mg), (dmg, o_dmg), (low_states, o_states),
        (decays, o_decay), (res4, o_res4), (unit0, o_unit0), (unit1, o_unit1), (scale, o_scale), (res3, o_res3), (branch, o_branch),
        (outs_t, token_out), (outs_c, char_out),
    ]

    def save(seq, *names):
        for name in names:
            for number, (source, target) in enumerate(plan):
                if source is name:
                    local_copy(2 + number, seq, source.at[seq], target.at[seq]).start()

    def each(body):
        def run(seq, carry):
            body(seq)
            return carry

        lax.fori_loop(0, seqs, run, 0)

    each(lambda s: (own_x(s).start(), own_c(s).start()))
    base = (2 + len(plan)) * seqs
    rows_in = wq_in.shape[0]
    fills = [
        (wq_in, wq.at[pl.ds(0, rows_in), :]),
        (wout_in, wout.at[pl.ds(0, wout_in.shape[0]), :]),
        (wc_in.at[:, pl.ds(0, width)], wc.at[pl.ds(0, rows_in), pl.ds(0, width)]),
    ]
    for d in range(2):
        for k in range(2):
            fills.append((wg_in.at[d, k], wg.at[pl.ds((2 * k + d) * LANE, units), :]))
    pieces = -(-rows_in // shard)
    for j in range(pieces):
        size = min(shard, rows_in - j * shard)
        fills.append(
            (
                wc_in.at[pl.ds(j * shard, size), pl.ds(width, width)],
                mid.at[j // 4, j % 4, pl.ds(0, size), :],
            )
        )

    def fill(number):
        return pltpu.make_async_copy(*fills[number], local.at[base + number])

    keeps = [(wq, o_wq), (wout, o_wout), (wg, o_wg), (wc, o_wc)]

    def keep_weights(number):
        return pltpu.make_async_copy(*keeps[number], local.at[base + len(fills) + number])

    for number in range(len(fills)):
        fill(number).start()
    g.greet()
    each(gx.start)
    each(gc.start)

    for t in range(4):
        for d in range(2):
            row = lax.broadcasted_iota(jnp.int32, (LANE, width), 0)
            col = lax.broadcasted_iota(jnp.int32, (LANE, width), 1)
            first = d * 4 * units + t * units
            hit = (col - first == row) & (row < units)
            perm[pl.ds((2 * t + d) * LANE, LANE), :] = hit.astype(F32).astype(BF16)
    taps[...] = jnp.zeros_like(taps)
    norm_grads[...] = jnp.zeros_like(norm_grads)
    gate_bias[...] = jnp.zeros_like(gate_bias)
    gate_bias[:, pl.ds(0, units)] = gate_in[...]
    rest = wq.shape[0] - rows_in
    wq[pl.ds(rows_in, rest), :] = jnp.zeros((rest, width), BF16)
    wc[pl.ds(rows_in, rest), :] = jnp.zeros((rest, wc.shape[1]), BF16)
    more = wout.shape[0] - wout_in.shape[0]
    wout[pl.ds(wout_in.shape[0], more), :] = jnp.zeros((more, width), BF16)
    for j in range(4):
        wg[pl.ds(j * LANE + units, LANE - units), :] = jnp.zeros(
            (LANE - units, wg.shape[1]), BF16
        )
    for number in range(len(fills)):
        fill(number).wait()
    for j in range(pieces):
        size = min(shard, rows_in - j * shard)
        wc[pl.ds(j * shard, size), pl.ds(width, 8 * LANE)] = nt(
            mid[j // 4, j % 4, pl.ds(0, size), :], perm[...]
        ).astype(BF16)
    for number in range(len(keeps)):
        keep_weights(number).start()

    lane = lax.broadcasted_iota(jnp.int32, (shard, LANE), 1)
    left = lane < HD

    def attention(s):
        gx.forward(s)
        gx.finish(s)
        own_x(s).wait()
        save(s, x)

        def project(t, carry):
            rows = pl.ds(pl.multiple_of(t * shard, shard), shard)
            first, second, third = unpack3(nt(x[s, t], wq[...]), HD * heads)
            qkv[s, 0, rows, :] = (first * 0.125).astype(BF16)
            qkv[s, 1, rows, :] = second.astype(BF16)
            qkv[s, 2, rows, :] = third.astype(BF16)
            return carry

        lax.fori_loop(0, 4, project, 0)
        save(s, qkv)

        def part(b, out):
            rows = pl.ds(pl.multiple_of(b * shard, shard), shard)
            same = segc[s, rows, :] == segr[s]
            for tile in range(qkv.shape[3] // LANE):
                cols = pl.ds(tile * LANE, LANE)
                result = None
                for half in range(2):
                    head = 2 * tile + half
                    if head >= heads:
                        continue
                    query = qkv[s, 0, rows, cols]
                    if 2 * tile + 1 < heads:
                        query = jnp.where(left if half == 0 else ~left, query, jnp.zeros_like(query))
                    scores = jnp.where(same, nt(query, qkv[s, 1, :, cols]), MASK_VALUE)
                    power = jnp.exp(scores - jnp.max(scores, axis=-1, keepdims=True))
                    probs = (power * (1.0 / jnp.sum(power, axis=-1, keepdims=True))).astype(BF16)
                    p[s, head * 4 + b] = probs
                    mixed = nn(probs, qkv[s, 2, :, cols])
                    result = mixed if result is None else jnp.where(left, result, mixed)
                ctx[s, rows, cols] = result.astype(BF16)
            out[...] = nn(ctx[s, rows, :], wout[...])

        s_attn.start(s, part)
        save(s, p, ctx)

    each(attention)

    def first_norm(s):
        total = x[s, me].astype(F32) + s_attn.finish(s)
        unit, spread = normalize(total)
        unit0[s] = unit
        scale[s, 0] = jnp.broadcast_to(spread, (shard, LANE))
        hidden[s] = unit * gain[0:1] + bias[0:1]
        h[s, me] = hidden[s].astype(BF16)
        gh.start(s)
        save(s, unit0)

    def gru(s):
        gc.forward(s)
        gc.finish(s)
        own_c(s).wait()
        save(s, c)

        def gates(t, carry):
            rows = pl.ds(pl.multiple_of(t * LANE, LANE), LANE)
            per = block_chars // LANE
            inner = pl.ds(pl.multiple_of((t % per) * LANE, LANE), LANE)
            proj = nt(c[s, t // per, inner, :], wg[...])
            for tile in range(2):
                cols = slice(tile * LANE, (tile + 1) * LANE)
                gate = jax.nn.sigmoid(proj[:, cols] + gate_bias[tile : tile + 1])
                cand = proj[:, (2 + tile) * LANE : (3 + tile) * LANE]
                decays[s, tile, rows, :] = (1.0 - gate) * keep[s, rows, tile : tile + 1]
                drive[tile, rows, :] = gate * cand
            return carry

        total = 4 * block_chars
        lax.fori_loop(0, total // LANE, gates, 0)
        recur((True, False), decays.at[s], drive, states, block_chars)
        save(s, decays)

        for tile in range(2):
            low_states[s, tile] = states[tile].astype(BF16)

        def pick(t, carry):
            rows = pl.ds(pl.multiple_of(t * shard, shard), shard)
            for tile in range(2):
                ids = lax.broadcasted_iota(jnp.int32, (shard, total), 1)
                hot = (ids == pickc[s, rows, tile : tile + 1]).astype(F32).astype(BF16)
                out = nn(hot, low_states[s, tile])
                st[s, me, rows, pl.ds(tile * LANE, LANE)] = out.astype(BF16)
            return carry

        lax.fori_loop(0, 4, pick, 0)
        gs.start(s)
        save(s, low_states)

    def norm_and_gru(s):
        first_norm(s)
        gru(s)

    each(norm_and_gru)

    def ffn(s):
        gh.forward(s)
        gh.finish(s)
        save(s, h)

        def part(b, out):
            value, slope = gelu_pair(nn(h[s, b], win[...]))
            act[s, b] = value.astype(BF16)
            dact[s, b] = slope.astype(BF16)
            out[...] = nn(act[s, b], wdown[...])

        s_ffn.start(s, part)
        save(s, act, dact)

    each(ffn)

    def second_norm(s):
        unit, spread = normalize(hidden[s] + s_ffn.finish(s))
        unit1[s] = unit
        scale[s, 1] = jnp.broadcast_to(spread, (shard, LANE))
        middle[s] = unit * gain[1:2] + bias[1:2]
        mid[s, me] = middle[s].astype(BF16)
        gm.start(s)
        save(s, unit1, scale)

    each(second_norm)

    def merge(s):
        gs.forward(s)
        gm.forward(s)
        gs.finish(s)
        gm.finish(s)
        save(s, mid, st)
        def mix(t, carry):
            rows = pl.ds(pl.multiple_of(t * shard, shard), shard)
            total = nt(mid[s, t], wc[:, pl.ds(0, width)])
            for u in range(4):
                weights = wc[:, pl.ds(width + u * 2 * LANE, 2 * LANE)]
                total = total + nt(st[s, u, rows, :], weights)
            taps[pl.ds(pl.multiple_of(8 + t * shard, 8), shard), :] = total
            return carry

        lax.fori_loop(0, 4, mix, 0)

        def shifted(t, carry):
            rows = pl.ds(pl.multiple_of(t * shard, shard), shard)
            window = taps[pl.ds(pl.multiple_of(t * shard, 8), shard + 16), :]
            before = unpack3(window[7 : 7 + shard], channels)[0]
            center = unpack3(window[8 : 8 + shard], channels)[1]
            after = unpack3(window[9 : 9 + shard], channels)[2]
            value, slope = gelu_pair(
                before * edges[s, rows, 0:1] + center + after * edges[s, rows, 1:2]
            )
            mg[s, rows, :] = value.astype(BF16)
            dmg[s, rows, :] = slope.astype(BF16)
            return carry

        lax.fori_loop(0, 4, shifted, 0)

        def part(b, out):
            rows = pl.ds(pl.multiple_of(b * shard, shard), shard)
            out[...] = nn(mg[s, rows, :], wm[...])

        s_branch.start(s, part)
        save(s, mg, dmg)

    each(merge)

    def put_branch(s, first, value):
        span = branch.shape[3]
        at = 0
        while at < width:
            part, inner = divmod(first + at, span)
            size = min(span - inner, width - at)
            branch[s, part, :, pl.ds(inner, size)] = value[:, at : at + size]
            at += size

    def last_norms(s):
        total = s_branch.finish(s)
        rows = pl.ds(pl.multiple_of(me * shard, shard), shard)
        unit, spread = normalize(middle[s] + total[:, :width])
        outs_t[s] = (unit * gain[2:3] + bias[2:3]).astype(BF16)
        cot = cot_t[s]
        norm_grads[0:1] += jnp.sum(cot * unit, axis=0, keepdims=True)
        norm_grads[2:3] += jnp.sum(cot, axis=0, keepdims=True)
        back = normalize_back(unit, spread, cot * gain[2:3])
        res3[s] = back
        put_branch(s, 0, back.astype(BF16))
        mine = total[:, width:]
        for u in range(4):
            mine = mine + nn(st[s, u, rows, :], perm[pl.ds(u * 2 * LANE, 2 * LANE), :])
        unit, spread = normalize(mine)
        outs_c[s] = (unit * gain[3:4] + bias[3:4]).astype(BF16)
        cot = cot_c[s]
        norm_grads[1:2] += jnp.sum(cot * unit, axis=0, keepdims=True)
        norm_grads[3:4] += jnp.sum(cot, axis=0, keepdims=True)
        back = normalize_back(unit, spread, cot * gain[3:4]).astype(BF16)
        put_branch(s, width, back)
        for u in range(4):
            res4[s, u] = nt(back, perm[pl.ds(u * 2 * LANE, 2 * LANE), :]).astype(BF16)
        save(s, outs_t, outs_c, res3, res4, branch)

    each(last_norms)

    def drain(s):
        for number, (source, target) in enumerate(plan):
            local_copy(2 + number, s, source.at[s], target.at[s]).wait()

    each(drain)
    for number in range(len(keeps)):
        keep_weights(number).wait()


def forward_call(tokens, chars, weights, small, group_slots=27):
    seqs, shard, width = tokens.shape
    length, block_chars = shard * 4, chars.shape[1]
    total = block_chars * 4
    wq, wout, win, wdown, wg, gate_bias, wc, wm = weights
    cols = -(-wout.shape[0] // LANE) * LANE
    packed = -(-wq.shape[0] // LANE) * LANE
    heads = small["heads"]
    kept = [
        ((packed, width), BF16), ((cols, width), BF16), ((4 * LANE, chars.shape[2]), BF16),
        ((packed, width + 8 * LANE), BF16),
    ]
    sds = jax.ShapeDtypeStruct
    big = {
        "x": ((seqs, 4, shard, width), BF16),
        "c": ((seqs, 4, block_chars, chars.shape[2]), BF16),
        "qkv": ((seqs, 3, length, cols), BF16),
        "p": ((seqs, heads * 4, shard, length), BF16),
        "ctx": ((seqs, length, cols), BF16),
        "h": ((seqs, 4, shard, width), BF16),
        "act": ((seqs, 4, shard, win.shape[1]), BF16),
        "dact": ((seqs, 4, shard, win.shape[1]), BF16),
        "mid": ((seqs, 4, shard, width), BF16),
        "st": ((seqs, 4, length, 2 * LANE), BF16),
        "mg": ((seqs, length, wm.shape[0]), BF16),
        "dmg": ((seqs, length, wm.shape[0]), BF16),
        "states": ((seqs, 2, total, LANE), BF16),
        "decay": ((seqs, 2, total, LANE), F32),
        "unit0": ((seqs, shard, width), F32),
        "unit1": ((seqs, shard, width), F32),
        "scale": ((seqs, 2, shard, LANE), F32),
        "res3": ((seqs, shard, width), F32),
        "res4": ((seqs, 4, shard, 2 * LANE), BF16),
        "branch": ((seqs, 2 * width // length, shard, length), BF16),
    }
    rows = ((seqs, shard, width), F32)
    low_rows = ((seqs, shard, width), BF16)
    scratch = list(big.values()) + kept + [
        rows, rows, low_rows, low_rows,
        ((2, total, LANE), F32),
        ((2, total, LANE), F32),
        ((length + 16, packed), F32),
        ((8 * LANE, width), BF16),
        ((2, LANE), F32),
        ((seqs, 3, shard, 2 * width), BF16), ((seqs, 3, shard, 2 * width), BF16),
        ((seqs, shard, 2 * width), F32), ((shard, 2 * width), F32),
    ]
    anyspace = pl.BlockSpec(memory_space=pl.ANY)
    vmem = pl.BlockSpec(memory_space=pltpu.VMEM)
    out_shapes = [sds(low_rows[0], BF16)] * 2 + [sds(*v) for v in list(big.values()) + kept]
    ins = (
        tokens, chars, wq, wout, win, wdown, wg, gate_bias, wc, wm, small["gain"], small["bias"],
        small["cot_t"], small["cot_c"], small["segc"], small["segr"], small["pickc"],
        small["keep"], small["edges"],
    )
    outs = pl.pallas_call(
        functools.partial(forward_kernel, small["units"], small["channels"]),
        out_shape=out_shapes + [sds((4, width), F32)],
        in_specs=[
            anyspace if k in (0, 1, 2, 3, 6, 8) else vmem for k in range(len(ins))
        ],
        out_specs=[anyspace] * len(out_shapes) + [vmem],
        scratch_shapes=[pltpu.VMEM(*v) for v in scratch]
        + [
            pltpu.SemaphoreType.DMA((group_slots * seqs,)),
            pltpu.SemaphoreType.DMA((group_slots * seqs,)),
            pltpu.SemaphoreType.DMA((26 * seqs + 24,)),
        ],
        compiler_params=pltpu.CompilerParams(
            collective_id=0, has_side_effects=True, vmem_limit_bytes=62 * MIB
        ),
    )(*ins)
    names = ["token_out", "char_out"] + list(big) + ["wq", "wout", "wg", "wc", "norm_grads"]
    return dict(zip(names, outs))


class Plane:
    def __init__(self, send, recv, marks):
        self.index = lax.axis_index("dp")
        self.x, self.z = self.index % 2, self.index // 2
        self.send, self.recv, self.marks, self.used, self.marked = send, recv, marks, 0, 0

    def mark(self):
        self.marked += 1
        return self.marks.at[self.marked - 1]

    def take(self, count):
        first = self.used
        self.used += count
        return [first + i for i in range(count)]

    def peer(self, way):
        if way == "x":
            return self.index + 1 - 2 * self.x
        return (self.index + (2 if way == "up" else 6)) % 8

    def pair(self, bit):
        digit = self.index // (1 << bit) % 2
        return self.index + (1 - 2 * digit) * (1 << bit)

    def copy(self, slot, source, target, peer):
        return pltpu.make_async_remote_copy(
            src_ref=source,
            dst_ref=target,
            send_sem=self.send.at[slot],
            recv_sem=self.recv.at[slot],
            device_id={"dp": peer},
            device_id_type=pl.DeviceIdType.MESH,
        )


class Reduce:
    steps = 9

    def __init__(self, plane, buf, out, land, first, land_first, rows, x_first):
        self.plane, self.buf, self.out, self.land = plane, buf, out, land
        self.first, self.land_first, self.rows, self.x_first = first, land_first, rows, x_first
        self.slots = plane.take(14)
        self.mark = plane.mark()
        x, z = plane.x, plane.z
        if x_first:
            self.quarter, self.half = rows // 8, rows // 2
            self.z_base, self.x_base = first + x * self.half, first
        else:
            self.quarter, self.half = rows // 4, rows // 8
            self.z_base, self.x_base = first, first + z * self.quarter
        self.x_land = land_first + 5 * self.quarter

    @staticmethod
    def landing_rows(rows, x_first):
        return 5 * rows // 8 + rows // 2 if x_first else 5 * rows // 4 + rows // 8

    def rows_of(self, ref, start, size):
        return ref.at[pl.ds(pl.multiple_of(start, 16), size), :]

    def add(self, start, land_start, size):
        def one(i, carry):
            rows = pl.ds(pl.multiple_of(start + i * 16, 16), 16)
            more = pl.ds(pl.multiple_of(land_start + i * 16, 16), 16)
            total = self.buf[rows, :].astype(F32) + self.land[more, :].astype(F32)
            self.buf[rows, :] = total.astype(BF16)
            return carry

        lax.fori_loop(0, size // 16, one, 0)

    def gather_copy(self, way, step, z):
        piece = 3 - step + z if way == "up" else step - 3 + z
        slot = piece if way == "up" else piece + (4 - piece) * (step // 2)
        return self.plane.copy(
            self.slots[step if way == "up" else 3 + step],
            self.rows_of(self.buf, self.z_base + piece * self.quarter, self.quarter),
            self.rows_of(self.land, self.land_first + slot * self.quarter, self.quarter),
            self.plane.peer(way),
        )

    def gather_send(self, step):
        z = self.plane.z
        pl.when(step >= z)(lambda: self.gather_copy("up", step, z).start())
        pl.when(step >= 3 - z)(lambda: self.gather_copy("down", step, z).start())

    def gather_wait(self, step):
        z = self.plane.z

        @pl.when((z >= 1) & (step >= z - 1))
        def _():
            self.gather_copy("up", step, z - 1).wait_recv()
            piece = 3 - step + z - 1
            self.add(
                self.z_base + piece * self.quarter,
                self.land_first + piece * self.quarter,
                self.quarter,
            )

        @pl.when((z <= 2) & (step >= 2 - z))
        def _():
            self.gather_copy("down", step, z + 1).wait_recv()
            piece = step - 3 + z + 1
            slot = piece if step < 2 else 4
            self.add(
                self.z_base + piece * self.quarter,
                self.land_first + slot * self.quarter,
                self.quarter,
            )

        pl.when(step >= z)(lambda: self.gather_copy("up", step, z).wait_send())
        pl.when(step >= 3 - z)(lambda: self.gather_copy("down", step, z).wait_send())

    def spread_copy(self, way, step, z):
        piece = z - step if way == "up" else z + step
        start = self.z_base + piece * self.quarter
        target = self.rows_of(self.out, start, self.quarter)
        source = target
        if self.x_first and step == 0:
            source = self.rows_of(self.buf, start, self.quarter)
        slot = self.slots[6 + step if way == "up" else 9 + step]
        return self.plane.copy(slot, source, target, self.plane.peer(way))

    def spread_send(self, step):
        z = self.plane.z
        pl.when((z <= 2) & (step <= z))(lambda: self.spread_copy("up", step, z).start())
        pl.when((z >= 1) & (step <= 3 - z))(lambda: self.spread_copy("down", step, z).start())

    def spread_wait(self, step):
        z = self.plane.z
        pl.when((z >= 1) & (step <= z - 1))(lambda: self.spread_copy("up", step, z - 1).wait_recv())
        pl.when((z <= 2) & (step <= 2 - z))(lambda: self.spread_copy("down", step, z + 1).wait_recv())
        pl.when((z <= 2) & (step <= z))(lambda: self.spread_copy("up", step, z).wait_send())
        pl.when((z >= 1) & (step <= 3 - z))(lambda: self.spread_copy("down", step, z).wait_send())

    def halve(self):
        other = self.x_base + (1 - self.plane.x) * self.half
        return self.plane.copy(
            self.slots[12],
            self.rows_of(self.buf, other, self.half),
            self.rows_of(self.land, self.x_land, self.half),
            self.plane.peer("x"),
        )

    def halve_wait(self):
        self.halve().wait()
        self.add(self.x_base + self.plane.x * self.half, self.x_land, self.half)

    def double(self):
        start = self.x_base + self.plane.x * self.half
        target = self.rows_of(self.out, start, self.half)
        source = target if self.x_first else self.rows_of(self.buf, start, self.half)
        return self.plane.copy(self.slots[13], source, target, self.plane.peer("x"))

    def keep(self):
        if self.x_first:
            start, size = self.z_base + self.plane.z * self.quarter, self.quarter
        else:
            start, size = self.x_base + self.plane.x * self.half, self.half
        return pltpu.make_async_copy(
            self.rows_of(self.buf, start, size), self.rows_of(self.out, start, size), self.mark
        )

    def step(self, number):
        if self.x_first:
            if number == 0:
                self.halve().start()
            elif number == 1:
                self.halve_wait()
                self.gather_send(0)
            elif number <= 3:
                self.gather_wait(number - 2)
                self.gather_send(number - 1)
            elif number == 4:
                self.gather_wait(2)
                self.keep().start()
                self.spread_send(0)
            elif number <= 6:
                self.spread_wait(number - 5)
                self.spread_send(number - 4)
            elif number == 7:
                self.spread_wait(2)
                self.keep().wait()
                self.double().start()
            else:
                self.double().wait()
        else:
            if number == 0:
                self.gather_send(0)
            elif number <= 2:
                self.gather_wait(number - 1)
                self.gather_send(number)
            elif number == 3:
                self.gather_wait(2)
                self.halve().start()
            elif number == 4:
                self.halve_wait()
                self.keep().start()
                self.double().start()
            elif number == 5:
                self.double().wait()
                self.keep().wait()
                self.spread_send(0)
            elif number <= 7:
                self.spread_wait(number - 6)
                self.spread_send(number - 5)
            else:
                self.spread_wait(2)


SAVED = (
    "branch", "mg", "dmg", "mid", "st", "res3", "res4", "unit0", "unit1", "scale", "act", "dact",
    "h", "p", "qkv", "ctx", "x", "c", "states", "decay",
)
GRADS = ("merge", "conv", "down", "win", "gru", "out", "qkv")
PIECES = (
    (0, 384, False),
    (1, 256, False),
    (1, 512, True),
    (1, 384, True),
    (2, 512, True),
    (2, 256, True),
    (3, 768, True),
    (4, 384, True),
    (5, 384, True),
    (6, 384, False),
    (6, 768, False),
)
SCHEDULE = (
    (),
    (0, 10, 20, 30,),
    (),
    (1, 11,),
    (21,),
    (2,),
    (40, 50, 12,),
    (60, 22, 31,),
    (3,),
    (13,),
    (23,),
    (32, 41, 24,),
    (51, 33,),
    (42,),
    (25, 52,),
    (34, 43,),
    (61, 26, 53, 4, 14, 35, 44,),
    (27, 5, 62, 15, 54, 36,),
    (),
    (80, 90, 100, 45, 6,),
    (63, 28, 16, 37, 55,),
    (81, 91, 46,),
    (101, 7, 64, 38, 82, 17, 56,),
    (92, 47,),
    (102, 8,),
    (70, 65, 83, 18, 57, 93, 48,),
    (103, 71,),
    (66, 84, 72, 58, 94,),
    (104, 73, 67, 85, 95,),
    (74, 105, 86, 96, 75, 106, 87, 97, 76, 107, 68, 98, 77, 88, 108, 78,),
)


def backward_kernel(units, channels, dp_size, *refs):
    refs = list(refs)
    take = lambda count: [refs.pop(0) for _ in range(count)]
    hbm = SimpleNamespace(**dict(zip(SAVED, take(len(SAVED)))))
    wq, wout, win, wdown, wg, gate_in, wc, wm, gain, pickr, edges, norm_in = take(12)
    grad_tokens, grad_chars = take(2)
    grads_out = dict(zip(GRADS, take(len(GRADS))))
    (small_out,) = take(1)
    names = [n for n in SAVED if n not in ("branch", "states", "decay", "p", "x")]
    v = SimpleNamespace(**dict(zip(names, take(len(names)))))
    (pb, states, decay, drive, dpre, dyk, fg, gtok, dproj, gru_acc, res2, res1, ds, parts,
     stage, got, held, temp, cstage, cgot, cheld, ctemp) = take(22)
    land = dict(zip(GRADS, take(len(GRADS))))
    big = SimpleNamespace(**dict(zip(GRADS, take(len(GRADS)))))
    small, small_land, gate_bias, send, recv, dsend, drecv, local, marks, credit = take(10)

    seqs, shard, width = grad_tokens.shape
    length = 4 * shard
    block_chars = grad_chars.shape[1]
    total = 4 * block_chars
    heads = pb.shape[1] // 4
    cols = v.ctx.shape[2]
    g = Group(send, recv, seqs)
    me = g.me
    inside = dp_size == 8
    plane = Plane(dsend, drecv, marks)

    def each(body):
        def run(seq, carry):
            body(seq)
            return carry

        lax.fori_loop(0, seqs, run, 0)

    def load(name):
        index = names.index(name)
        return pltpu.make_async_copy(getattr(hbm, name), getattr(v, name), local.at[index])

    spare = len(names)
    p_copy = lambda: pltpu.make_async_copy(hbm.p, pb, local.at[spare])
    x_copy = lambda: pltpu.make_async_copy(hbm.x, v.h, local.at[39])

    def states_copy(s):
        return pltpu.make_async_copy(hbm.states.at[s], states, local.at[spare + 1])

    def decay_copy(s, tile):
        return pltpu.make_async_copy(
            hbm.decay.at[s, tile], decay.at[tile], local.at[spare + 2 + tile]
        )

    def out_copy(kind, s):
        source, target = ((res1, grad_tokens), (cheld, grad_chars))[kind]
        return pltpu.make_async_copy(
            source.at[s], target.at[s], local.at[spare + 4 + kind * seqs + s]
        )

    pieces = 2 * width // length
    gb = Gather(
        g, pb, hbm.branch, place=lambda s, t: pb.at[s, pl.ds(t * pieces, pieces)]
    )
    gf, ga = Gather(g, fg), Gather(g, v.mid)
    pick = lambda ref: (lambda s, i: ref.at[s, i])
    own = lambda ref: (lambda s: ref.at[s])
    s_mid = Scatter(g, pick(stage), pick(got), own(held), temp)
    s_hid = Scatter(g, pick(stage), pick(got), own(held), temp)
    s_tok = Scatter(g, pick(stage), pick(got), own(held), temp)
    s_chr = Scatter(g, pick(cstage), pick(cgot), own(cheld), ctemp)
    s_cout = Scatter(g, pick(cstage), pick(cgot), own(cheld), ctemp)

    def own_branch(s):
        return pltpu.make_async_copy(
            hbm.branch.at[s], gb.at(s, me), local.at[spare + 4 + 2 * seqs + s]
        )

    each(lambda s: own_branch(s).start())
    for name in ("dmg", "res4", "mg", "mid", "st"):
        load(name).start()
    states_copy(0).start()
    for tile in range(2):
        decay_copy(0, tile).start()
    for name in names:
        if name not in ("dmg", "res4", "mg", "mid", "st"):
            load(name).start()

    barrier = pltpu.get_barrier_semaphore()
    places = [{"tensor": g.pair}, {"tensor": g.far}]
    if inside:
        places += [{"dp": plane.peer(way)} for way in ("x", "up", "down")]
        places += [{"dp": plane.pair(2)}]
    for place in places:
        pl.semaphore_signal(barrier, inc=1, device_id=place, device_id_type=pl.DeviceIdType.MESH)
    pl.semaphore_wait(barrier, len(places))
    each(gb.start)
    dpre[...] = jnp.zeros_like(dpre)
    gate_bias[...] = jnp.zeros_like(gate_bias)
    gate_bias[:, pl.ds(0, units)] = gate_in[...]
    side = 2 * LANE
    for t in range(4):
        for j in range(width // side):
            row = lax.broadcasted_iota(jnp.int32, (side, side), 0)
            col = lax.broadcasted_iota(jnp.int32, (side, side), 1) + j * side
            unit = row % LANE
            hit = (col == row // LANE * 4 * units + t * units + unit) & (unit < units)
            cstage[t // 2, j, pl.ds(t % 2 * side, side), :] = hit.astype(F32).astype(BF16)
    small[...] = jnp.zeros_like(small)
    small[0, pl.ds(0, 4), :] = norm_in[...]
    lane = lax.broadcasted_iota(jnp.int32, (shard, LANE), 1)
    left = lane < HD
    for name in ("dmg", "res4"):
        load(name).wait()

    def block_rows(t, size):
        return pl.ds(pl.multiple_of(t * size, size), size)

    def merge_back(s):
        gb.forward(s)
        gb.finish(s)
        own_branch(s).wait()

        def inner(t, carry):
            rows = block_rows(t, shard)
            back = None
            for j in range(pieces):
                piece = nt(pb[s, t * pieces + j], wm[:, j * length : (j + 1) * length])
                back = piece if back is None else back + piece
            dpre[pl.ds(pl.multiple_of(8 + t * shard, 8), shard), :] = (
                (back * v.dmg[s, rows, :].astype(F32)).astype(BF16).astype(F32)
            )
            return carry

        lax.fori_loop(0, 4, inner, 0)

        def taps(t, carry):
            rows = block_rows(t, shard)
            window = dpre[pl.ds(pl.multiple_of(t * shard, 8), shard + 16), :]
            marks = edges[s, rows, :]
            before = window[9 : 9 + shard] * marks[:, 2:3]
            after = window[7 : 7 + shard] * marks[:, 3:4]
            dyk[s, rows, :] = pack3(
                [before, window[8 : 8 + shard], after], channels
            ).astype(BF16)
            return carry

        lax.fori_loop(0, 4, taps, 0)

        def mid_part(b, out):
            out[...] = nn(dyk[s, block_rows(b, shard), :], wc[:, pl.ds(0, width)])

        s_mid.start(s, mid_part)

    each(merge_back)
    sums, marks_at = [], {}
    for which, height, x_first in PIECES if inside else ():
        name = GRADS[which]
        first, at = marks_at.get(name, (0, 0))
        sums.append(
            Reduce(
                plane, getattr(big, name), grads_out[name], land[name], first, at, height, x_first
            )
        )
        marks_at[name] = (first + height, at + Reduce.landing_rows(height, x_first))
    fired = [0] * len(sums)

    def fire(hook):
        for entry in SCHEDULE[hook] if inside else ():
            which, number = divmod(entry, 10)
            fired[which] += 1
            sums[which].step(number)

    def fire_in(seq, hook, stride):
        for k in range(2):
            pl.when(seq == k)(functools.partial(fire, hook + k * stride))

    tokens = seqs * length
    step_w = 2 * LANE

    def merge_weights():
        for name in ("mg", "mid", "st"):
            load(name).wait()

        half_w = width
        for j in range(pieces):
            right = jnp.concatenate(
                [pb[s, t * pieces + j] for s in range(seqs) for t in range(4)], axis=0
            )
            out = tn(v.mg[...].reshape(tokens, -1), right)[:channels].astype(BF16)
            at = 0
            while at < length:
                part, inside_at = divmod(j * length + at, half_w)
                size = min(length - at, half_w - inside_at)
                big.merge[pl.ds(part * channels, channels), pl.ds(inside_at, size)] = out[
                    :, at : at + size
                ]
                at += size
        taps = 3 * channels

        def conv_rows(j, carry):
            lanes = pl.ds(pl.multiple_of(j * LANE, LANE), LANE)
            left_rows = dyk[:, :, lanes].reshape(tokens, LANE)
            size = min(LANE, taps - LANE * j) if isinstance(j, int) else LANE
            first = j * LANE if isinstance(j, int) else pl.multiple_of(j * LANE, LANE)
            out = tn(left_rows, v.mid[...].reshape(tokens, width))
            big.conv[pl.ds(first, size), :] = out[:size].astype(BF16)
            padded = [
                tn(left_rows, v.st[:, t].reshape(tokens, side)).astype(BF16) for t in range(4)
            ]
            first = taps + j * LANE if isinstance(j, int) else pl.multiple_of(taps + j * LANE, 64)
            for k in range(width // side):
                out = None
                for t in range(4):
                    piece = nn(padded[t], cstage[t // 2, k, pl.ds(t % 2 * side, side), :])
                    out = piece if out is None else out + piece
                big.conv[pl.ds(first, size), pl.ds(k * side, side)] = out[:size].astype(BF16)
            return carry

        lax.fori_loop(0, taps // LANE, conv_rows, 0)
        if taps % LANE:
            conv_rows(taps // LANE, 0)
        p_copy().start()
        fire(1)

    def second_back(s):
        incoming = v.res3[s] + s_mid.finish(s)
        unit = v.unit1[s]
        small[0, 5:6] += jnp.sum(incoming * unit, axis=0, keepdims=True)
        small[0, 7:8] += jnp.sum(incoming, axis=0, keepdims=True)
        spread = v.scale[s, 1][:, 0:1]
        res2[s] = normalize_back(unit, spread, incoming * gain[1:2])
        fg[s, me] = res2[s].astype(BF16)
        gf.start(s)
        fire_in(s, 0, 2)
        pl.when(s == 0)(merge_weights)

    for name in ("res3", "unit1", "scale"):
        load(name).wait()
    each(second_back)
    for name in ("dact", "act", "h"):
        load(name).wait()

    def ffn_back(s):
        gf.forward(s)
        gf.finish(s)

        def part(b, out):
            back = nt(fg[s, b], wdown[...]) * v.dact[s, b].astype(F32)
            v.dact[s, b] = back.astype(BF16)
            out[...] = nt(v.dact[s, b], win[...])

        s_hid.start(s, part)
        fire_in(s, 3, 1)

    each(ffn_back)

    def all_ffn_weights():
        def ffn_weights(j, carry):
            colsj = pl.ds(pl.multiple_of(j * step_w, step_w), step_w)
            out = tn(v.act[:, :, :, colsj].reshape(tokens, step_w), fg[...].reshape(tokens, width))
            big.down[block_rows(j, step_w), :] = out.astype(BF16)
            return carry

        lax.fori_loop(0, big.down.shape[0] // step_w, ffn_weights, 0)
        fire(6)

        def in_weights(j, carry):
            colsj = pl.ds(pl.multiple_of(j * step_w, step_w), step_w)
            out = tn(
                v.h[:, :, :, colsj].reshape(tokens, step_w), v.dact[...].reshape(tokens, -1)
            )
            big.win[block_rows(j, step_w), :] = out.astype(BF16)
            return carry

        lax.fori_loop(0, width // step_w, in_weights, 0)
        x_copy().start()
        fire(7)

    load("unit0").wait()

    def first_back(s):
        incoming = res2[s] + s_hid.finish(s)
        unit = v.unit0[s]
        small[0, 4:5] += jnp.sum(incoming * unit, axis=0, keepdims=True)
        small[0, 6:7] += jnp.sum(incoming, axis=0, keepdims=True)
        spread = v.scale[s, 0][:, 0:1]
        res1[s] = normalize_back(unit, spread, incoming * gain[0:1])
        v.mid[s, me] = res1[s].astype(BF16)
        ga.start(s)
        fire_in(s, 5, 3)
        pl.when(s == 0)(all_ffn_weights)

    each(first_back)

    def chars_back(s):
        def char_part(b, out):
            first = pl.multiple_of(width + b * 2 * LANE, 2 * LANE)
            out[...] = nn(dyk[s], wc[:, pl.ds(first, 2 * LANE)])
            out[block_rows(me, shard), :] += v.res4[s, b].astype(F32)

        s_chr.start(s, char_part)
        fire_in(s, 9, 1)

    each(chars_back)
    hops = [("t", g.pair), ("t", g.far)] + ([("d", k) for k in range(3)] if inside else [])
    slots_t, slots_d = g.slots(2), plane.take(3)

    def small_copy(number):
        kind, where = hops[number]
        source, target = small.at[number], small_land.at[number]
        if kind == "t":
            return g.copy(slots_t[number], 0, source, target, where)
        return plane.copy(slots_d[where], source, target, plane.pair(where))

    def small_step(number):
        if number > 0:
            small_copy(number - 1).wait()
            value, more = small[number - 1], small_land[number - 1]
            small[number, pl.ds(0, 8), :] = value[:8] + more[:8]
            rest = small[6, pl.ds(0, 8), :] if number <= 2 else value[8:] + more[8:]
            small[number, pl.ds(8, 8), :] = rest
        if number < len(hops):
            small_copy(number).start()

    if not inside:
        hops = []
    small_step(0) if hops else None
    for name in ("qkv", "ctx"):
        load(name).wait()
    p_copy().wait()

    def attention_back(s):
        ga.forward(s)
        ga.finish(s)
        dctx = v.dmg

        def context(t, carry):
            dctx[s, block_rows(t, shard), :] = nt(v.mid[s, t], wout[...]).astype(BF16)
            return carry

        lax.fori_loop(0, 4, context, 0)
        for tile in range(cols // LANE):
            lanes = pl.ds(tile * LANE, LANE)
            for half in range(2):
                head = 2 * tile + half
                if head >= heads:
                    continue
                paired = 2 * tile + 1 < heads

                def rows_of(b, carry):
                    rows = block_rows(b, shard)
                    grad = dctx[s, rows, lanes]
                    if paired:
                        grad = jnp.where(left if half == 0 else ~left, grad, jnp.zeros_like(grad))
                    back = nt(grad, v.qkv[s, 2, :, lanes])
                    probs = pb[s, head * 4 + b].astype(F32)
                    row_dot = jnp.sum(probs * back, axis=-1, keepdims=True)
                    ds[b] = (probs * (back - row_dot)).astype(BF16)
                    out = nn(ds[b], v.qkv[s, 1, :, lanes])
                    if half == 1:
                        out = jnp.where(left, ctemp[rows, lanes], out)
                    ctemp[rows, lanes] = out
                    return carry

                lax.fori_loop(0, 4, rows_of, 0)
                keys = tn(ds[...].reshape(length, length), v.qkv[s, 0, :, lanes])
                values = tn(
                    pb[s, pl.ds(head * 4, 4)].reshape(length, length), dctx[s, :, lanes]
                )
                if half == 1:
                    wide_left = lax.broadcasted_iota(jnp.int32, (length, LANE), 1) < HD
                    keys = jnp.where(wide_left, parts[0, :, lanes], keys)
                    values = jnp.where(wide_left, parts[1, :, lanes], values)
                parts[0, :, lanes] = keys
                parts[1, :, lanes] = values
                fire_in(s, 11 + head, 4)

        def pack(t, carry):
            rows = block_rows(t, shard)
            query = ctemp[rows, :].astype(BF16).astype(F32) * 0.125
            dyk[s, rows, :] = pack3(
                [query, parts[0, rows, :], parts[1, rows, :]], HD * heads
            ).astype(BF16)
            return carry

        lax.fori_loop(0, 4, pack, 0)

        def part(b, out):
            out[...] = nn(dyk[s, block_rows(b, shard), :], wq[...])

        s_tok.start(s, part)

        fire_in(s, 14, 4)

    each(attention_back)
    small_step(1) if hops else None

    x_copy().wait()

    tall = 3 * HD * heads
    half_w = width // 2

    def qkv_weights(j, carry):
        lanes = pl.ds(pl.multiple_of(j * LANE, LANE), LANE)
        size = min(LANE, tall - LANE * j) if isinstance(j, int) else LANE
        out = tn(dyk[:, :, lanes].reshape(tokens, LANE), v.h[...].reshape(tokens, width))
        for k in range(2):
            first = k * tall + j * LANE
            first = first if isinstance(j, int) else pl.multiple_of(first, 64)
            big.qkv[pl.ds(first, size), :] = out[:size, k * half_w : (k + 1) * half_w].astype(BF16)
        return carry

    lax.fori_loop(0, tall // LANE, qkv_weights, 0)
    if tall % LANE:
        qkv_weights(tall // LANE, 0)
    out = tn(v.ctx[...].reshape(tokens, -1), v.mid[...].reshape(tokens, width))
    for k in range(2):
        big.out[pl.ds(k * HD * heads, HD * heads), :] = out[
            : HD * heads, k * half_w : (k + 1) * half_w
        ].astype(BF16)
    fire(19)

    load("c").wait()

    def gru_back(s):
        gtok[...] = s_chr.finish(s).astype(BF16)
        for peer in (g.pair, g.far):
            pl.semaphore_signal(
                credit.at[s], inc=1, device_id={"tensor": peer},
                device_id_type=pl.DeviceIdType.MESH,
            )
        def spread_out(t, carry):
            rows = block_rows(t, LANE)
            for tile in range(2):
                ids = lax.broadcasted_iota(jnp.int32, (LANE, length), 0) + t * LANE
                hot = (ids == pickr[s, tile : tile + 1, :]).astype(F32).astype(BF16)
                drive[tile, rows, :] = nn(hot, gtok[:, pl.ds(tile * LANE, LANE)])
            return carry

        lax.fori_loop(0, total // LANE, spread_out, 0)
        fire_in(s, 20, 3)
        for tile in range(2):
            decay_copy(s, tile).wait()
        recur((False, True), decay, drive, drive, block_chars, back=True)
        fire_in(s, 21, 3)
        states_copy(s).wait()

        @pl.when(s == 0)
        def _():
            gru_acc[...] = jnp.zeros_like(gru_acc)

        def part(b, out):
            def finish(t, sums):
                inner = block_rows(t, LANE)
                rows = pl.ds(pl.multiple_of(b * block_chars + t * LANE, LANE), LANE)
                proj = nt(v.c[s, b, inner, :], wg[...])
                new = []
                for tile in range(2):
                    colst = slice(tile * LANE, (tile + 1) * LANE)
                    gate = jax.nn.sigmoid(proj[:, colst] + gate_bias[tile : tile + 1])
                    cand = proj[:, (2 + tile) * LANE : (3 + tile) * LANE]
                    flow = drive[tile, rows, :] * gate
                    logit = flow * (cand - states[tile, rows, :].astype(F32))
                    dproj[inner, pl.ds(tile * LANE, LANE)] = logit.astype(BF16)
                    dproj[inner, pl.ds((2 + tile) * LANE, LANE)] = flow.astype(BF16)
                    new.append(sums[tile] + jnp.sum(logit, axis=0, keepdims=True))
                return tuple(new)

            zero = jnp.zeros((1, LANE), F32)
            sums = lax.fori_loop(0, block_chars // LANE, finish, (zero, zero))
            for tile in range(2):
                small[6, 0:1, pl.ds(tile * LANE, LANE)] += sums[tile]
            out[...] = nn(dproj[...], wg[...])
            gru_acc[...] += tn(dproj[...], v.c[s, b])

        pl.semaphore_wait(credit.at[s], 2)
        s_cout.start(s, part)

        @pl.when(s + 1 < seqs)
        def _():
            states_copy(s + 1).start()
            for tile in range(2):
                decay_copy(s + 1, tile).start()

        if seqs > 1:
            pl.when(s == 0)(functools.partial(fire, 22))

    each(gru_back)
    for d in range(2):
        for k in range(2):
            big.gru[pl.ds((2 * d + k) * units, units), :] = gru_acc[
                pl.ds((2 * k + d) * LANE, units), :
            ].astype(BF16)
    small_step(2) if hops else None
    fire(25)

    def last(s):
        res1[s] = res1[s] + s_tok.finish(s)
        out_copy(0, s).start()
        cheld[s] = s_cout.finish(s)
        out_copy(1, s).start()

    each(last)

    def emit(name):
        return pltpu.make_async_copy(
            getattr(big, name), grads_out[name], local.at[spare + 4 + 3 * seqs + GRADS.index(name)]
        )

    if inside:
        fire(26)
        small_step(3)
        fire(27)
        small_step(4)
        fire(28)
        small_step(5)
        fire(29)
        assert all(count == Reduce.steps for count in fired)
    else:
        for name in GRADS:
            emit(name).start()
        for name in GRADS:
            emit(name).wait()
    small_out[...] = small[len(hops)]
    if not inside:
        small_out[pl.ds(8, 8), :] = small[6, pl.ds(0, 8), :]
    each(lambda s: (out_copy(0, s).wait(), out_copy(1, s).wait()))


def backward_call(saved, weights, small, dp_size):
    wq, wout, win, wdown, wg, gate_bias, wc, wm = weights
    sds = jax.ShapeDtypeStruct
    seqs, shard, width = saved["res3"].shape
    length = shard * 4
    block_chars, char_width = saved["c"].shape[2:]
    total = 4 * block_chars
    cols, packed = wout.shape[0], wc.shape[0]
    tall = 3 * HD * small["heads"]
    channels = small["channels"]
    saved_in = [saved[n] for n in SAVED]
    names = [n for n in SAVED if n not in ("branch", "states", "decay", "p", "x")]
    shapes = [(saved[n].shape, saved[n].dtype) for n in names]
    grads = {
        "merge": (2 * channels, width), "conv": (2 * 3 * channels, width),
        "down": (win.shape[1], width), "win": (width, win.shape[1]),
        "gru": (4 * small["units"], char_width), "out": (2 * tall // 3, width // 2),
        "qkv": (2 * tall, width // 2),
    }
    pad = (seqs, 3, shard, width)
    cpad = (seqs, 3, length, 2 * LANE)
    scratch = shapes + [
        (saved["p"].shape, BF16),
        ((2, total, LANE), BF16),
        ((2, total, LANE), F32),
        ((2, total, LANE), F32),
        ((length + 16, wm.shape[0]), F32),
        ((seqs, length, packed), BF16),
        ((seqs, 4, shard, width), BF16),
        ((length, 2 * LANE), BF16),
        ((block_chars, 4 * LANE), BF16),
        ((4 * LANE, char_width), F32),
        ((seqs, shard, width), F32),
        ((seqs, shard, width), F32),
        ((4, shard, length), BF16),
        ((2, length, cols), F32),
        (pad, BF16), (pad, BF16), ((seqs, shard, width), F32), ((shard, width), F32),
        (cpad, BF16), (cpad, BF16), ((seqs, length, 2 * LANE), F32), ((length, 2 * LANE), F32),
    ]
    for which, name in enumerate(GRADS):
        landing = sum(Reduce.landing_rows(n, way) for k, n, way in PIECES if k == which)
        scratch.append(((landing if dp_size == 8 else 16, grads[name][1]), BF16))
    scratch += [(shape, BF16) for shape in grads.values()]
    scratch += [((7, 16, width), F32), ((5, 16, width), F32), ((2, LANE), F32)]
    anyspace = pl.BlockSpec(memory_space=pl.ANY)
    vmem = pl.BlockSpec(memory_space=pltpu.VMEM)
    ins = saved_in + list(weights) + [small["gain"], small["pickr"], small["edges"], saved["norm_grads"]]
    outs = pl.pallas_call(
        functools.partial(backward_kernel, small["units"], channels, dp_size),
        out_shape=[sds((seqs, shard, width), F32), sds((seqs, block_chars, char_width), F32)]
        + [sds(shape, BF16) for shape in grads.values()]
        + [sds((16, width), F32)],
        in_specs=[anyspace] * len(saved_in) + [vmem] * (len(ins) - len(saved_in)),
        out_specs=[anyspace] * (2 + len(grads)) + [vmem],
        scratch_shapes=[pltpu.VMEM(*one) for one in scratch]
        + [
            pltpu.SemaphoreType.DMA((32 * seqs,)),
            pltpu.SemaphoreType.DMA((32 * seqs,)),
            pltpu.SemaphoreType.DMA((14 * len(PIECES) + 4,)),
            pltpu.SemaphoreType.DMA((14 * len(PIECES) + 4,)),
            pltpu.SemaphoreType.DMA((40,)),
            pltpu.SemaphoreType.DMA((len(PIECES),)),
            pltpu.SemaphoreType.REGULAR((seqs,)),
        ],
        compiler_params=pltpu.CompilerParams(
            collective_id=1, has_side_effects=True, vmem_limit_bytes=63 * MIB
        ),
    )(*ins)
    names = ["grad_tokens", "grad_chars"] + list(grads) + ["small"]
    return dict(zip(names, outs))


def finish_kernel(
    conv, qkv, out, down, win, gru, chars, tokens, first, second,
    o_conv, o_qkv, o_out, o_down, o_win, o_gru, o_chars, o_tokens, o_first, o_second,
):
    for source, target in ((conv, o_conv), (qkv, o_qkv), (out, o_out)):
        half = source.shape[2]
        for k in range(2):
            target[:, k * half : (k + 1) * half] = source[k].astype(F32)
    for source, target in ((down, o_down), (win, o_win), (gru, o_gru)):
        target[...] = source[...].astype(F32)
    for j in range(8):
        o_chars[0, j] = chars[0, :, j, :]
    for source, target in ((tokens, o_tokens), (first, o_first), (second, o_second)):
        target[...] = source[...]


def finish_call(grads, grad_chars, grad_tokens, token_out, char_out):
    seqs, block_chars, char_width = grad_chars.shape
    steps = block_chars // 8
    turns = 2 * seqs
    chars = grad_chars.reshape(seqs, steps, 8, char_width)
    pairs = [a.reshape(2, -1, a.shape[1]) for a in (grads["conv"], grads["qkv"], grads["out"])]
    plain = [grads["down"], grads["win"], grads["gru"]]
    copied = [grad_tokens, token_out, char_out]
    flat = [(a.shape[1], 2 * a.shape[2]) for a in pairs] + [a.shape for a in plain]

    def rows_spec(shape):
        return pl.BlockSpec((shape[0] // turns, shape[1]), lambda i: (i, 0))

    def pair_spec(shape):
        return pl.BlockSpec((2, shape[1] // turns, shape[2]), lambda i: (0, i, 0))

    def halves(shape):
        return pl.BlockSpec((1, shape[1] // 2, shape[2]), lambda i: (i // 2, i % 2, 0))

    return pl.pallas_call(
        finish_kernel,
        grid=(turns,),
        out_shape=[jax.ShapeDtypeStruct(shape, F32) for shape in flat]
        + [jax.ShapeDtypeStruct((seqs, 8, steps, char_width), F32)]
        + [jax.ShapeDtypeStruct(a.shape, a.dtype) for a in copied],
        in_specs=[pair_spec(a.shape) for a in pairs]
        + [rows_spec(a.shape) for a in plain]
        + [pl.BlockSpec((1, steps // 2, 8, char_width), lambda i: (i // 2, i % 2, 0, 0))]
        + [halves(a.shape) for a in copied],
        out_specs=[rows_spec(shape) for shape in flat]
        + [pl.BlockSpec((1, 8, steps // 2, char_width), lambda i: (i // 2, 0, i % 2, 0))]
        + [halves(a.shape) for a in copied],
        compiler_params=pltpu.CompilerParams(vmem_limit_bytes=62 * MIB),
    )(*pairs, *plain, chars, *copied)


def local(
    tokens,
    characters,
    doc_lengths,
    token_chars,
    w_qkv,
    w_out,
    w_in,
    w_down,
    w_gru,
    gate_bias,
    w_conv,
    w_merge,
    norm_gain,
    norm_bias,
    token_cot,
    char_cot,
):
    micro_count = tokens.shape[0]
    shard_len = tokens.shape[1]
    model_width = tokens.shape[2]
    char_width = characters.shape[2]
    group_size = lax.axis_size("tensor")
    group_rank = lax.axis_index("tensor")
    length = shard_len * group_size
    char_total = characters.shape[1] * group_size
    head_cols = w_qkv.shape[2]
    heads_here = head_cols // HD
    units_here = w_gru.shape[3]
    merge_here = w_conv.shape[2]
    wq = jnp.transpose(w_qkv, (1, 2, 0)).reshape(3 * head_cols, model_width)
    wc = jnp.transpose(w_conv, (0, 2, 1)).reshape(3 * merge_here, 2 * model_width)
    wg = jnp.transpose(w_gru, (1, 2, 3, 0))
    more = -merge_here % LANE
    wm = jnp.pad(w_merge.reshape(merge_here, 2 * model_width), ((0, more), (0, 0)))
    layouts = [layout(doc_lengths[i], token_chars[i], char_total) for i in range(micro_count)]
    stacked_layout = [jnp.stack(parts) for parts in zip(*layouts)]
    segment, first_char, last_char, keep_forward, keep_backward, prev_ok, next_ok = stacked_layout
    block_chars = characters.shape[1]
    steps = block_chars // 8

    def reorder(rows):
        split = rows.reshape(micro_count, -1, 8, steps, rows.shape[-1])
        return jnp.swapaxes(split, 2, 3).reshape(rows.shape)

    keep = reorder(jnp.stack([keep_forward, keep_backward], axis=2))
    picks = jnp.stack([last_char, first_char], axis=2)
    inner = picks % block_chars
    picks = picks - inner + inner % steps * 8 + inner // steps
    zero = jnp.zeros_like(prev_ok[:, :1])
    small = dict(
        gain=norm_gain, bias=norm_bias, cot_t=token_cot, cot_c=char_cot,
        segc=segment[:, :, None], segr=segment[:, None, :], pickc=picks, keep=keep,
        pickr=jnp.swapaxes(picks, 1, 2),
        edges=jnp.stack(
            [
                prev_ok,
                next_ok,
                jnp.concatenate([prev_ok[:, 1:], zero], axis=1),
                jnp.concatenate([zero, next_ok[:, :-1]], axis=1),
            ],
            axis=2,
        ),
        heads=heads_here, units=units_here, channels=merge_here,
    )
    weights = (wq, w_out, w_in, w_down, wg, gate_bias, wc, wm)
    fw = forward_call(tokens, reorder(characters), weights, small)
    weights = (fw["wq"], fw["wout"], w_in, w_down, fw["wg"], gate_bias, fw["wc"], wm)
    dp_size = lax.axis_size("dp")
    bw = backward_call(fw, weights, small, dp_size)
    rows = bw["small"]
    gate_row = rows[8, : 2 * LANE]
    grads = {name: bw[name] for name in GRADS}
    if dp_size != 8:
        grads, gate_row = lax.psum((grads, gate_row), "dp")
        rows = lax.psum(rows, ("dp", "tensor"))
    grad_merge = grads["merge"].astype(F32).reshape(2, merge_here, model_width)
    conv, qkv, out, down, win, gru, chars, tokens_grad, first, second = finish_call(
        grads, bw["grad_chars"], bw["grad_tokens"], fw["token_out"], fw["char_out"]
    )
    conv = conv.reshape(3, merge_here, 2 * model_width)
    qkv = qkv.reshape(3, head_cols, model_width)
    gru = gru.reshape(2, 2, units_here, char_width)
    return (
        first,
        second,
        tokens_grad,
        chars.reshape(bw["grad_chars"].shape),
        jnp.transpose(qkv, (2, 0, 1)),
        out,
        win,
        down,
        jnp.transpose(gru, (3, 0, 1, 2)),
        gate_row.reshape(2, LANE)[:, :units_here],
        jnp.transpose(conv, (0, 2, 1)),
        jnp.swapaxes(grad_merge, 0, 1),
        jnp.concatenate([rows[4:6], rows[0:2]], axis=0),
        jnp.concatenate([rows[6:8], rows[2:4]], axis=0),
    )


def solution(mesh):
    return jax.shard_map(
        local,
        mesh=mesh,
        in_specs=(
            P("dp", "tensor", None),
            P("dp", "tensor", None),
            P("dp", None),
            P("dp", None),
            P(None, None, "tensor"),
            P("tensor", None),
            P(None, "tensor"),
            P("tensor", None),
            P(None, None, None, "tensor"),
            P(None, "tensor"),
            P(None, None, "tensor"),
            P("tensor", None, None),
            P(),
            P(),
            P("dp", "tensor", None),
            P("dp", "tensor", None),
        ),
        out_specs=(
            P("dp", "tensor", None),
            P("dp", "tensor", None),
            P("dp", "tensor", None),
            P("dp", "tensor", None),
            P(None, None, "tensor"),
            P("tensor", None),
            P(None, "tensor"),
            P("tensor", None),
            P(None, None, None, "tensor"),
            P(None, "tensor"),
            P(None, None, "tensor"),
            P("tensor", None, None),
            P(),
            P(),
        ),
        check_vma=False,
    )
```

```python
import functools
from types import SimpleNamespace

import jax
import jax.numpy as jnp
from jax import lax
from jax.experimental import pallas as pl
from jax.experimental.pallas import tpu as pltpu
from jax.sharding import PartitionSpec as P

HD = 64


NORM_EPSILON = 1e-06
MASK_VALUE = -1e30
HIGH_PRECISION = lax.Precision.HIGHEST


F32 = jnp.float32
BF16 = jnp.bfloat16
LANE = 128
MIB = 1024 * 1024


def nn(left, right):
    return jnp.dot(left, right, preferred_element_type=F32)


def nt(left, right):
    return lax.dot_general(left, right, (((1,), (1,)), ((), ())), preferred_element_type=F32)


def tn(left, right):
    return lax.dot_general(left, right, (((0,), (0,)), ((), ())), preferred_element_type=F32)


def gelu_pair(values):
    cdf = 0.5 * (1.0 + lax.erf(values * 0.7071067811865476))
    density = 0.3989422804014327 * jnp.exp(-0.5 * values * values)
    return values * cdf, cdf + values * density


def normalize(rows):
    centered = rows - jnp.mean(rows, axis=-1, keepdims=True)
    scale = lax.rsqrt(jnp.mean(centered * centered, axis=-1, keepdims=True) + NORM_EPSILON)
    return centered * scale, scale


def normalize_back(unit, scale, grad_unit):
    return scale * (
        grad_unit
        - jnp.mean(grad_unit, axis=-1, keepdims=True)
        - unit * jnp.mean(grad_unit * unit, axis=-1, keepdims=True)
    )


def roll_lanes(value, shift):
    return pltpu.roll(value, shift % value.shape[1], axis=1)


def unpack3(packed, size):
    room = -(-size // LANE) * LANE
    lane = lax.broadcasted_iota(jnp.int32, (packed.shape[0], room), 1)
    parts = []
    for k in range(3):
        first = k * size // LANE * LANE
        inner = k * size - first
        part = packed[:, first : min(first + room + LANE, packed.shape[1])]
        if inner:
            part = roll_lanes(part, -inner)
        parts.append(jnp.where(lane < size, part[:, :room], 0.0))
    return parts


def pack3(parts, size):
    room = parts[0].shape[1]
    columns = -(-3 * size // LANE) * LANE
    tiles = [None] * (columns // LANE)
    for k in range(3):
        first, inner = divmod(k * size, LANE)
        part = parts[k]
        if inner:
            part = jnp.concatenate([part, jnp.zeros_like(part[:, :LANE])], axis=1)
            part = roll_lanes(part, inner)
        for j in range(part.shape[1] // LANE):
            if first + j < len(tiles) and (first + j) * LANE < (k + 1) * size:
                tile = part[:, j * LANE : (j + 1) * LANE]
                old = tiles[first + j]
                tiles[first + j] = tile if old is None else old + tile
    return jnp.concatenate(tiles, axis=1)


class Group:
    def __init__(self, send, recv, seqs):
        self.me = lax.axis_index("tensor")
        self.low = self.me % 2
        self.high = self.me // 2
        self.pair = self.high * 2 + (1 - self.low)
        self.far = (1 - self.high) * 2 + self.low
        self.send, self.recv, self.seqs, self.used = send, recv, seqs, 0

    def block(self, turn):
        left = 3 - turn
        return ((self.high + left // 2) % 2) * 2 + (self.low + left % 2) % 2

    def slots(self, count):
        first = self.used
        self.used += count
        return [first + i for i in range(count)]

    def copy(self, slot, seq, source, target, peer):
        index = slot * self.seqs + seq
        return pltpu.make_async_remote_copy(
            src_ref=source,
            dst_ref=target,
            send_sem=self.send.at[index],
            recv_sem=self.recv.at[index],
            device_id={"tensor": peer},
            device_id_type=pl.DeviceIdType.MESH,
        )

    def greet(self):
        barrier = pltpu.get_barrier_semaphore()
        for peer in (self.pair, self.far):
            pl.semaphore_signal(
                barrier, inc=1, device_id={"tensor": peer}, device_id_type=pl.DeviceIdType.MESH
            )
        pl.semaphore_wait(barrier, 2)


class Gather:
    def __init__(self, group, buf, source=None, place=None):
        self.group, self.source = group, source
        self.at = place or (lambda seq, t: buf.at[seq, t])
        self.near, self.over, self.fwd = group.slots(3)

    def own(self, seq):
        return self.at(seq, self.group.me) if self.source is None else self.source.at[seq]

    def near_copy(self, seq):
        g = self.group
        return g.copy(self.near, seq, self.own(seq), self.at(seq, g.me), g.pair)

    def over_copy(self, seq):
        g = self.group
        return g.copy(self.over, seq, self.own(seq), self.at(seq, g.me), g.far)

    def fwd_copy(self, seq):
        g = self.group
        other = self.at(seq, g.far)
        return g.copy(self.fwd, seq, other, other, g.pair)

    def start(self, seq):
        self.over_copy(seq).start()
        self.near_copy(seq).start()

    def forward(self, seq):
        self.over_copy(seq).wait_recv()
        self.fwd_copy(seq).start()

    def finish(self, seq):
        near = self.near_copy(seq)
        fwd = self.fwd_copy(seq)
        near.wait_recv()
        fwd.wait_recv()
        near.wait_send()
        self.over_copy(seq).wait_send()
        fwd.wait_send()


class Scatter:
    def __init__(self, group, stage, got, own, temp):
        self.group, self.stage, self.got, self.held, self.temp = group, stage, got, own, temp
        self.names = group.slots(3)

    def copies(self, seq):
        g = self.group
        peers = (g.pair, g.pair, g.far)
        return [
            g.copy(self.names[i], seq, self.stage(seq, i), self.got(seq, i), peers[i])
            for i in range(3)
        ]

    def start(self, seq, part):
        mine, other, over = self.copies(seq)

        def turn(step, carry):
            part(self.group.block(step), self.temp)

            @pl.when(step == 0)
            def _():
                self.stage(seq, 1)[...] = self.temp[...].astype(BF16)
                other.start()

            @pl.when(step == 1)
            def _():
                other.wait_recv()
                self.stage(seq, 2)[...] = (self.temp[...] + self.got(seq, 1)[...]).astype(BF16)
                over.start()

            @pl.when(step == 2)
            def _():
                self.stage(seq, 0)[...] = self.temp[...].astype(BF16)
                mine.start()

            @pl.when(step == 3)
            def _():
                self.held(seq)[...] = self.temp[...]

            return carry

        lax.fori_loop(0, 4, turn, 0)

    def finish(self, seq):
        mine, other, over = self.copies(seq)
        mine.wait_recv()
        over.wait_recv()
        total = self.held(seq)[...] + self.got(seq, 0)[...] + self.got(seq, 2)[...]
        mine.wait_send()
        other.wait_send()
        over.wait_send()
        return total


def shift_rows(value, count, up, fill):
    edge = jnp.full((count, value.shape[1]), fill, value.dtype)
    if up:
        return jnp.concatenate([edge, value[:-count]], axis=0)
    return jnp.concatenate([value[count:], edge], axis=0)


def recur(ups, decays, drives, outs, block, back=False):
    steps = block // 8
    pairs = [(tile, t) for tile in range(2) for t in range(4)]

    def rows(tile, t, step):
        row = step if ups[tile] else steps - 1 - step
        return pl.ds(pl.multiple_of(t * block + row * 8, 8), 8)

    def summary(step, carry):
        new = []
        for i, (tile, t) in enumerate(pairs):
            state, mult = carry[2 * i], carry[2 * i + 1]
            here = rows(tile, t, step)
            decay, drive = decays[tile, here, :], drives[tile, here, :]
            state = decay * (state + drive) if back else decay * state + drive
            new += [state, decay * mult]
        return tuple(new)

    zero, one = jnp.zeros((8, LANE), F32), jnp.ones((8, LANE), F32)
    ends = lax.fori_loop(0, steps, summary, (zero, one) * 8, unroll=4)
    starts = []
    for tile in range(2):
        state = jnp.concatenate([ends[2 * (4 * tile + t)] for t in range(4)], axis=0)
        mult = jnp.concatenate([ends[2 * (4 * tile + t) + 1] for t in range(4)], axis=0)
        for count in (1, 2, 4, 8, 16):
            state = mult * shift_rows(state, count, ups[tile], 0.0) + state
            mult = mult * shift_rows(mult, count, ups[tile], 1.0)
        state = shift_rows(state, 1, ups[tile], 0.0)
        starts += [state[8 * t : 8 * t + 8] for t in range(4)]

    def write(step, carry):
        new = []
        for i, (tile, t) in enumerate(pairs):
            here = rows(tile, t, step)
            decay, drive = decays[tile, here, :], drives[tile, here, :]
            if back:
                value = drive + carry[i]
                new.append(decay * value)
            else:
                value = decay * carry[i] + drive
                new.append(value)
            outs[tile, here, :] = value
        return tuple(new)

    lax.fori_loop(0, steps, write, tuple(starts), unroll=4)


def forward_kernel(
    units, channels, docs, counts, tokens, chars, wq_in, wout_in, win_in, wdown_in, wg_in, gate_in,
    wc_in, wm_in, gain, bias, cot_t_in, cot_c_in,
    token_out, char_out, o_x, o_c, o_qkv, o_p, o_ctx, o_h, o_act, o_dact, o_mid, o_st, o_mg,
    o_dmg, o_states, o_decay, o_unit0, o_unit1, o_scale, o_res3, o_res4, o_branch,
    o_wq, o_wout, o_wg, o_wc, norm_grads, pickr, edges,
    x, c, qkv, p, ctx, h, act, dact, mid, st, mg, dmg, low_states, decays, unit0, unit1, scale, res3, res4, branch,
    wq, wout, wg, wc, hidden, middle, outs_t, outs_c, states, drive, taps, perm, gate_bias,
    win, wdown, wm, cot_t, cot_c, segc, segr, pickc, keep,
    stage, got, held, temp, send, recv, local,
):
    seqs, length = counts.shape[0], counts.shape[2]
    shard, width = tokens.shape[1], tokens.shape[2]
    block_chars = chars.shape[1]
    heads = p.shape[1] // 4
    g = Group(send, recv, seqs)
    me = g.me
    saves = []

    def keep_out(seq, source, target):
        saves.append((source, target, len(saves)))

    def local_copy(number, seq, source, target):
        return pltpu.make_async_copy(source, target, local.at[number * seqs + seq])

    gx, gc = Gather(g, x, tokens), Gather(g, c, chars)
    gh, gm, gs = Gather(g, h), Gather(g, mid), Gather(g, st)
    narrow = lambda ref: (lambda s, i: ref.at[s, i, :, pl.ds(0, width)])
    wide = lambda ref: (lambda s, i: ref.at[s, i])
    own_n = lambda s: held.at[s, :, pl.ds(0, width)]
    own_w = lambda s: held.at[s]
    thin = temp.at[:, pl.ds(0, width)]
    s_attn = Scatter(g, narrow(stage), narrow(got), own_n, thin)
    s_ffn = Scatter(g, narrow(stage), narrow(got), own_n, thin)
    s_branch = Scatter(g, wide(stage), wide(got), own_w, temp)

    def own_x(seq):
        return local_copy(0, seq, tokens.at[seq], x.at[seq, me])

    def own_c(seq):
        return local_copy(1, seq, chars.at[seq], c.at[seq, me])

    plan = [
        (x, o_x), (c, o_c), (qkv, o_qkv), (p, o_p), (ctx, o_ctx), (h, o_h), (act, o_act),
        (dact, o_dact), (mid, o_mid), (st, o_st), (mg, o_mg), (dmg, o_dmg), (low_states, o_states),
        (decays, o_decay), (res4, o_res4), (unit0, o_unit0), (unit1, o_unit1), (scale, o_scale), (res3, o_res3), (branch, o_branch),
        (outs_t, token_out), (outs_c, char_out),
    ]

    def save(seq, *names):
        for name in names:
            for number, (source, target) in enumerate(plan):
                if source is name:
                    local_copy(2 + number, seq, source.at[seq], target.at[seq]).start()

    def each(body):
        def run(seq, carry):
            body(seq)
            return carry

        lax.fori_loop(0, seqs, run, 0)

    each(lambda s: (own_x(s).start(), own_c(s).start()))
    base = (2 + len(plan)) * seqs
    late = [(win_in, win), (wdown_in, wdown), (wm_in, wm), (cot_t_in, cot_t), (cot_c_in, cot_c)]
    rows_in = wq_in.shape[0]
    fills = [
        (wq_in, wq.at[pl.ds(0, rows_in), :]),
        (wout_in, wout.at[pl.ds(0, wout_in.shape[0]), :]),
        (wc_in.at[:, pl.ds(0, width)], wc.at[pl.ds(0, rows_in), pl.ds(0, width)]),
    ]
    for d in range(2):
        for k in range(2):
            fills.append((wg_in.at[d, k], wg.at[pl.ds((2 * k + d) * LANE, units), :]))
    pieces = -(-rows_in // shard)
    for j in range(pieces):
        size = min(shard, rows_in - j * shard)
        fills.append(
            (
                wc_in.at[pl.ds(j * shard, size), pl.ds(width, width)],
                mid.at[j // 4, j % 4, pl.ds(0, size), :],
            )
        )

    fills += late

    def fill(number):
        return pltpu.make_async_copy(*fills[number], local.at[base + number])

    keeps = [(wq, o_wq), (wout, o_wout), (wg, o_wg), (wc, o_wc)]

    def keep_weights(number):
        return pltpu.make_async_copy(*keeps[number], local.at[base + len(fills) + number])

    for number in range(len(fills)):
        fill(number).start()
    g.greet()
    each(gx.start)
    each(gc.start)

    for t in range(4):
        for d in range(2):
            row = lax.broadcasted_iota(jnp.int32, (LANE, width), 0)
            col = lax.broadcasted_iota(jnp.int32, (LANE, width), 1)
            first = d * 4 * units + t * units
            hit = (col - first == row) & (row < units)
            perm[pl.ds((2 * t + d) * LANE, LANE), :] = hit.astype(F32).astype(BF16)
    taps[...] = jnp.zeros_like(taps)
    norm_grads[...] = jnp.zeros_like(norm_grads)
    gate_bias[...] = jnp.zeros_like(gate_bias)
    gate_bias[:, pl.ds(0, units)] = gate_in[...]
    rest = wq.shape[0] - rows_in
    wq[pl.ds(rows_in, rest), :] = jnp.zeros((rest, width), BF16)
    wc[pl.ds(rows_in, rest), :] = jnp.zeros((rest, wc.shape[1]), BF16)
    more = wout.shape[0] - wout_in.shape[0]
    wout[pl.ds(wout_in.shape[0], more), :] = jnp.zeros((more, width), BF16)
    for j in range(4):
        wg[pl.ds(j * LANE + units, LANE - units), :] = jnp.zeros(
            (LANE - units, wg.shape[1]), BF16
        )
    for number in range(len(fills) - len(late)):
        fill(number).wait()
    for j in range(pieces):
        size = min(shard, rows_in - j * shard)
        wc[pl.ds(j * shard, size), pl.ds(width, 8 * LANE)] = nt(
            mid[j // 4, j % 4, pl.ds(0, size), :], perm[...]
        ).astype(BF16)
    for number in range(len(keeps)):
        keep_weights(number).start()

    lane = lax.broadcasted_iota(jnp.int32, (shard, LANE), 1)
    left = lane < HD
    steps = block_chars // 8
    assert steps & (steps - 1) == 0

    def place(char):
        inner = char & (block_chars - 1)
        return char - inner + ((inner & (steps - 1)) << 3) + (inner >> (steps.bit_length() - 1))

    def hits(positions, marks):
        total = jnp.zeros(positions.shape, F32)
        for mark in marks:
            total = total + (positions == mark).astype(F32)
        return total

    def structure(s):
        ends, running = [], 0
        for d in range(docs.shape[1]):
            running = running + docs[s, d]
            ends.append(running)
        along = lax.broadcasted_iota(jnp.int32, (1, length), 1)
        down = lax.broadcasted_iota(jnp.int32, (length, 1), 0)
        seg_row, seg_col = jnp.zeros_like(along), jnp.zeros_like(down)
        for end in ends:
            seg_row = seg_row + (along >= end).astype(jnp.int32)
            seg_col = seg_col + (down >= end).astype(jnp.int32)
        segr[s] = seg_row
        segc[s] = seg_col
        edges[s, :, 0:1] = 1.0 - hits(down, [0] + ends[:-1])
        edges[s, :, 1:2] = 1.0 - hits(down + 1, ends)
        count = counts[s].astype(F32)
        many = jnp.broadcast_to(count, (LANE, length)).astype(BF16)
        rows = lax.broadcasted_iota(jnp.int32, (length, length), 0)
        cols = lax.broadcasted_iota(jnp.int32, (length, length), 1)
        ends_row = nn(many[:16], (rows <= cols).astype(F32).astype(BF16))[0:1]
        ends_col = nt((cols <= rows).astype(F32).astype(BF16), many)[:, 0:1]
        starts_col = nt((cols < rows).astype(F32).astype(BF16), many)[:, 0:1]
        pickr[s, 0:1, :] = place(ends_row.astype(jnp.int32) - 1)
        pickr[s, 1:2, :] = place((ends_row - count).astype(jnp.int32))
        pickc[s, :, 0:1] = place(ends_col.astype(jnp.int32) - 1)
        pickc[s, :, 1:2] = place(starts_col.astype(jnp.int32))
        cuts = [
            jnp.sum(jnp.where(along < end, count, 0.0), axis=1, keepdims=True) for end in ends
        ]
        row = lax.broadcasted_iota(jnp.int32, (4 * block_chars, 1), 0)
        inner = row & (block_chars - 1)
        char = (row - inner + (inner & 7) * steps + (inner >> 3)).astype(F32)
        keep[s, :, 0:1] = 1.0 - hits(char, [0.0] + cuts[:-1])
        keep[s, :, 1:2] = 1.0 - hits(char + 1.0, cuts)

    each(structure)
    for number in range(len(fills) - len(late), len(fills)):
        fill(number).wait()

    def attention(s):
        gx.forward(s)
        gx.finish(s)
        own_x(s).wait()
        save(s, x)

        def project(t, carry):
            rows = pl.ds(pl.multiple_of(t * shard, shard), shard)
            first, second, third = unpack3(nt(x[s, t], wq[...]), HD * heads)
            qkv[s, 0, rows, :] = (first * 0.125).astype(BF16)
            qkv[s, 1, rows, :] = second.astype(BF16)
            qkv[s, 2, rows, :] = third.astype(BF16)
            return carry

        lax.fori_loop(0, 4, project, 0)
        save(s, qkv)

        def part(b, out):
            rows = pl.ds(pl.multiple_of(b * shard, shard), shard)
            same = segc[s, rows, :] == segr[s]
            for tile in range(qkv.shape[3] // LANE):
                cols = pl.ds(tile * LANE, LANE)
                result = None
                for half in range(2):
                    head = 2 * tile + half
                    if head >= heads:
                        continue
                    query = qkv[s, 0, rows, cols]
                    if 2 * tile + 1 < heads:
                        query = jnp.where(left if half == 0 else ~left, query, jnp.zeros_like(query))
                    scores = jnp.where(same, nt(query, qkv[s, 1, :, cols]), MASK_VALUE)
                    power = jnp.exp(scores - jnp.max(scores, axis=-1, keepdims=True))
                    probs = (power * (1.0 / jnp.sum(power, axis=-1, keepdims=True))).astype(BF16)
                    p[s, head * 4 + b] = probs
                    mixed = nn(probs, qkv[s, 2, :, cols])
                    result = mixed if result is None else jnp.where(left, result, mixed)
                ctx[s, rows, cols] = result.astype(BF16)
            out[...] = nn(ctx[s, rows, :], wout[...])

        s_attn.start(s, part)
        save(s, p, ctx)

    each(attention)

    def first_norm(s):
        total = x[s, me].astype(F32) + s_attn.finish(s)
        unit, spread = normalize(total)
        unit0[s] = unit
        scale[s, 0] = jnp.broadcast_to(spread, (shard, LANE))
        hidden[s] = unit * gain[0:1] + bias[0:1]
        h[s, me] = hidden[s].astype(BF16)
        gh.start(s)
        save(s, unit0)

    def gru(s):
        gc.forward(s)
        gc.finish(s)
        own_c(s).wait()
        save(s, c)

        def gates(t, carry):
            rows = pl.ds(pl.multiple_of(t * LANE, LANE), LANE)
            per = block_chars // LANE
            inner = pl.ds(pl.multiple_of((t % per) * LANE, LANE), LANE)
            proj = nt(c[s, t // per, inner, :], wg[...])
            for tile in range(2):
                cols = slice(tile * LANE, (tile + 1) * LANE)
                gate = jax.nn.sigmoid(proj[:, cols] + gate_bias[tile : tile + 1])
                cand = proj[:, (2 + tile) * LANE : (3 + tile) * LANE]
                decays[s, tile, rows, :] = (1.0 - gate) * keep[s, rows, tile : tile + 1]
                drive[tile, rows, :] = gate * cand
            return carry

        total = 4 * block_chars
        lax.fori_loop(0, total // LANE, gates, 0)
        recur((True, False), decays.at[s], drive, states, block_chars)
        save(s, decays)

        for tile in range(2):
            low_states[s, tile] = states[tile].astype(BF16)

        def pick(t, carry):
            rows = pl.ds(pl.multiple_of(t * shard, shard), shard)
            for tile in range(2):
                ids = lax.broadcasted_iota(jnp.int32, (shard, total), 1)
                hot = (ids == pickc[s, rows, tile : tile + 1]).astype(F32).astype(BF16)
                out = nn(hot, low_states[s, tile])
                st[s, me, rows, pl.ds(tile * LANE, LANE)] = out.astype(BF16)
            return carry

        lax.fori_loop(0, 4, pick, 0)
        gs.start(s)
        save(s, low_states)

    def norm_and_gru(s):
        first_norm(s)
        gru(s)

    each(norm_and_gru)

    def ffn(s):
        gh.forward(s)
        gh.finish(s)
        save(s, h)

        def part(b, out):
            value, slope = gelu_pair(nn(h[s, b], win[...]))
            act[s, b] = value.astype(BF16)
            dact[s, b] = slope.astype(BF16)
            out[...] = nn(act[s, b], wdown[...])

        s_ffn.start(s, part)
        save(s, act, dact)

    each(ffn)

    def second_norm(s):
        unit, spread = normalize(hidden[s] + s_ffn.finish(s))
        unit1[s] = unit
        scale[s, 1] = jnp.broadcast_to(spread, (shard, LANE))
        middle[s] = unit * gain[1:2] + bias[1:2]
        mid[s, me] = middle[s].astype(BF16)
        gm.start(s)
        save(s, unit1, scale)

    each(second_norm)

    def merge(s):
        gs.forward(s)
        gm.forward(s)
        gs.finish(s)
        gm.finish(s)
        save(s, mid, st)
        def mix(t, carry):
            rows = pl.ds(pl.multiple_of(t * shard, shard), shard)
            total = nt(mid[s, t], wc[:, pl.ds(0, width)])
            for u in range(4):
                weights = wc[:, pl.ds(width + u * 2 * LANE, 2 * LANE)]
                total = total + nt(st[s, u, rows, :], weights)
            taps[pl.ds(pl.multiple_of(8 + t * shard, 8), shard), :] = total
            return carry

        lax.fori_loop(0, 4, mix, 0)

        def shifted(t, carry):
            rows = pl.ds(pl.multiple_of(t * shard, shard), shard)
            window = taps[pl.ds(pl.multiple_of(t * shard, 8), shard + 16), :]
            before = unpack3(window[7 : 7 + shard], channels)[0]
            center = unpack3(window[8 : 8 + shard], channels)[1]
            after = unpack3(window[9 : 9 + shard], channels)[2]
            value, slope = gelu_pair(
                before * edges[s, rows, 0:1] + center + after * edges[s, rows, 1:2]
            )
            mg[s, rows, :] = value.astype(BF16)
            dmg[s, rows, :] = slope.astype(BF16)
            return carry

        lax.fori_loop(0, 4, shifted, 0)

        def part(b, out):
            rows = pl.ds(pl.multiple_of(b * shard, shard), shard)
            out[...] = nn(mg[s, rows, :], wm[...])

        s_branch.start(s, part)
        save(s, mg, dmg)

    each(merge)

    def put_branch(s, first, value):
        span = branch.shape[3]
        at = 0
        while at < width:
            part, inner = divmod(first + at, span)
            size = min(span - inner, width - at)
            branch[s, part, :, pl.ds(inner, size)] = value[:, at : at + size]
            at += size

    def last_norms(s):
        total = s_branch.finish(s)
        rows = pl.ds(pl.multiple_of(me * shard, shard), shard)
        unit, spread = normalize(middle[s] + total[:, :width])
        outs_t[s] = (unit * gain[2:3] + bias[2:3]).astype(BF16)
        cot = cot_t[s]
        norm_grads[0:1] += jnp.sum(cot * unit, axis=0, keepdims=True)
        norm_grads[2:3] += jnp.sum(cot, axis=0, keepdims=True)
        back = normalize_back(unit, spread, cot * gain[2:3])
        res3[s] = back
        put_branch(s, 0, back.astype(BF16))
        mine = total[:, width:]
        for u in range(4):
            mine = mine + nn(st[s, u, rows, :], perm[pl.ds(u * 2 * LANE, 2 * LANE), :])
        unit, spread = normalize(mine)
        outs_c[s] = (unit * gain[3:4] + bias[3:4]).astype(BF16)
        cot = cot_c[s]
        norm_grads[1:2] += jnp.sum(cot * unit, axis=0, keepdims=True)
        norm_grads[3:4] += jnp.sum(cot, axis=0, keepdims=True)
        back = normalize_back(unit, spread, cot * gain[3:4]).astype(BF16)
        put_branch(s, width, back)
        for u in range(4):
            res4[s, u] = nt(back, perm[pl.ds(u * 2 * LANE, 2 * LANE), :]).astype(BF16)
        save(s, outs_t, outs_c, res3, res4, branch)

    each(last_norms)

    def drain(s):
        for number, (source, target) in enumerate(plan):
            local_copy(2 + number, s, source.at[s], target.at[s]).wait()

    each(drain)
    for number in range(len(keeps)):
        keep_weights(number).wait()


def forward_call(tokens, chars, weights, small, group_slots=27):
    seqs, shard, width = tokens.shape
    length, block_chars = shard * 4, chars.shape[1]
    total = block_chars * 4
    wq, wout, win, wdown, wg, gate_bias, wc, wm = weights
    cols = -(-wout.shape[0] // LANE) * LANE
    packed = -(-wq.shape[0] // LANE) * LANE
    heads = small["heads"]
    kept = [
        ((packed, width), BF16), ((cols, width), BF16), ((4 * LANE, chars.shape[2]), BF16),
        ((packed, width + 8 * LANE), BF16),
    ]
    sds = jax.ShapeDtypeStruct
    big = {
        "x": ((seqs, 4, shard, width), BF16),
        "c": ((seqs, 4, block_chars, chars.shape[2]), BF16),
        "qkv": ((seqs, 3, length, cols), BF16),
        "p": ((seqs, heads * 4, shard, length), BF16),
        "ctx": ((seqs, length, cols), BF16),
        "h": ((seqs, 4, shard, width), BF16),
        "act": ((seqs, 4, shard, win.shape[1]), BF16),
        "dact": ((seqs, 4, shard, win.shape[1]), BF16),
        "mid": ((seqs, 4, shard, width), BF16),
        "st": ((seqs, 4, length, 2 * LANE), BF16),
        "mg": ((seqs, length, wm.shape[0]), BF16),
        "dmg": ((seqs, length, wm.shape[0]), BF16),
        "states": ((seqs, 2, total, LANE), BF16),
        "decay": ((seqs, 2, total, LANE), F32),
        "unit0": ((seqs, shard, width), F32),
        "unit1": ((seqs, shard, width), F32),
        "scale": ((seqs, 2, shard, LANE), F32),
        "res3": ((seqs, shard, width), F32),
        "res4": ((seqs, 4, shard, 2 * LANE), BF16),
        "branch": ((seqs, 2 * width // length, shard, length), BF16),
    }
    rows = ((seqs, shard, width), F32)
    low_rows = ((seqs, shard, width), BF16)
    total = block_chars * 4
    scratch = list(big.values()) + kept + [
        rows, rows, low_rows, low_rows,
        ((2, total, LANE), F32),
        ((2, total, LANE), F32),
        ((length + 16, packed), F32),
        ((8 * LANE, width), BF16),
        ((2, LANE), F32),
        (win.shape, BF16), (wdown.shape, BF16), (wm.shape, BF16), rows, rows,
        ((seqs, length, 1), jnp.int32), ((seqs, 1, length), jnp.int32),
        ((seqs, length, 2), jnp.int32), ((seqs, total, 2), F32),
        ((seqs, 3, shard, 2 * width), BF16), ((seqs, 3, shard, 2 * width), BF16),
        ((seqs, shard, 2 * width), F32), ((shard, 2 * width), F32),
    ]
    anyspace = pl.BlockSpec(memory_space=pl.ANY)
    vmem = pl.BlockSpec(memory_space=pltpu.VMEM)
    out_shapes = [sds(low_rows[0], BF16)] * 2 + [sds(*v) for v in list(big.values()) + kept]
    ins = (
        small["docs"], small["counts"], tokens, chars, wq, wout, win, wdown, wg, gate_bias, wc, wm,
        small["gain"], small["bias"], small["cot_t"], small["cot_c"],
    )
    smem = pl.BlockSpec(memory_space=pltpu.SMEM)
    places = [smem, vmem] + [anyspace] * 7 + [vmem] + [anyspace] * 2 + [vmem] * 2 + [anyspace] * 2
    outs = pl.pallas_call(
        functools.partial(forward_kernel, small["units"], small["channels"]),
        out_shape=out_shapes
        + [
            sds((4, width), F32),
            sds((seqs, 2, length), jnp.int32),
            sds((seqs, length, 2), F32),
        ],
        in_specs=places,
        out_specs=[anyspace] * len(out_shapes) + [vmem] * 3,
        scratch_shapes=[pltpu.VMEM(*v) for v in scratch]
        + [
            pltpu.SemaphoreType.DMA((group_slots * seqs,)),
            pltpu.SemaphoreType.DMA((group_slots * seqs,)),
            pltpu.SemaphoreType.DMA((26 * seqs + 24,)),
        ],
        compiler_params=pltpu.CompilerParams(
            collective_id=0, has_side_effects=True, vmem_limit_bytes=62 * MIB
        ),
    )(*ins)
    names = ["token_out", "char_out"] + list(big) + ["wq", "wout", "wg", "wc", "norm_grads"]
    names += ["pickr", "edges"]
    return dict(zip(names, outs))


class Plane:
    def __init__(self, send, recv, marks):
        self.index = lax.axis_index("dp")
        self.x, self.z = self.index % 2, self.index // 2
        self.send, self.recv, self.marks, self.used, self.marked = send, recv, marks, 0, 0

    def mark(self):
        self.marked += 1
        return self.marks.at[self.marked - 1]

    def take(self, count):
        first = self.used
        self.used += count
        return [first + i for i in range(count)]

    def peer(self, way):
        if way == "x":
            return self.index + 1 - 2 * self.x
        return (self.index + (2 if way == "up" else 6)) % 8

    def pair(self, bit):
        digit = self.index // (1 << bit) % 2
        return self.index + (1 - 2 * digit) * (1 << bit)

    def copy(self, slot, source, target, peer):
        return pltpu.make_async_remote_copy(
            src_ref=source,
            dst_ref=target,
            send_sem=self.send.at[slot],
            recv_sem=self.recv.at[slot],
            device_id={"dp": peer},
            device_id_type=pl.DeviceIdType.MESH,
        )


class Reduce:
    steps = 9

    def __init__(self, plane, buf, out, land, first, land_first, rows, x_first):
        self.plane, self.buf, self.out, self.land = plane, buf, out, land
        self.first, self.land_first, self.rows, self.x_first = first, land_first, rows, x_first
        self.slots = plane.take(14)
        self.mark = plane.mark()
        x, z = plane.x, plane.z
        if x_first:
            self.quarter, self.half = rows // 8, rows // 2
            self.z_base, self.x_base = first + x * self.half, first
        else:
            self.quarter, self.half = rows // 4, rows // 8
            self.z_base, self.x_base = first, first + z * self.quarter
        self.x_land = land_first + 5 * self.quarter

    @staticmethod
    def landing_rows(rows, x_first):
        return 5 * rows // 8 + rows // 2 if x_first else 5 * rows // 4 + rows // 8

    def rows_of(self, ref, start, size):
        return ref.at[pl.ds(pl.multiple_of(start, 16), size), :]

    def add(self, start, land_start, size):
        def one(i, carry):
            rows = pl.ds(pl.multiple_of(start + i * 16, 16), 16)
            more = pl.ds(pl.multiple_of(land_start + i * 16, 16), 16)
            total = self.buf[rows, :].astype(F32) + self.land[more, :].astype(F32)
            self.buf[rows, :] = total.astype(BF16)
            return carry

        lax.fori_loop(0, size // 16, one, 0)

    def gather_copy(self, way, step, z):
        piece = 3 - step + z if way == "up" else step - 3 + z
        slot = piece if way == "up" else piece + (4 - piece) * (step // 2)
        return self.plane.copy(
            self.slots[step if way == "up" else 3 + step],
            self.rows_of(self.buf, self.z_base + piece * self.quarter, self.quarter),
            self.rows_of(self.land, self.land_first + slot * self.quarter, self.quarter),
            self.plane.peer(way),
        )

    def gather_send(self, step):
        z = self.plane.z
        pl.when(step >= z)(lambda: self.gather_copy("up", step, z).start())
        pl.when(step >= 3 - z)(lambda: self.gather_copy("down", step, z).start())

    def gather_wait(self, step):
        z = self.plane.z

        @pl.when((z >= 1) & (step >= z - 1))
        def _():
            self.gather_copy("up", step, z - 1).wait_recv()
            piece = 3 - step + z - 1
            self.add(
                self.z_base + piece * self.quarter,
                self.land_first + piece * self.quarter,
                self.quarter,
            )

        @pl.when((z <= 2) & (step >= 2 - z))
        def _():
            self.gather_copy("down", step, z + 1).wait_recv()
            piece = step - 3 + z + 1
            slot = piece if step < 2 else 4
            self.add(
                self.z_base + piece * self.quarter,
                self.land_first + slot * self.quarter,
                self.quarter,
            )

        pl.when(step >= z)(lambda: self.gather_copy("up", step, z).wait_send())
        pl.when(step >= 3 - z)(lambda: self.gather_copy("down", step, z).wait_send())

    def spread_copy(self, way, step, z):
        piece = z - step if way == "up" else z + step
        start = self.z_base + piece * self.quarter
        target = self.rows_of(self.out, start, self.quarter)
        source = target
        if self.x_first and step == 0:
            source = self.rows_of(self.buf, start, self.quarter)
        slot = self.slots[6 + step if way == "up" else 9 + step]
        return self.plane.copy(slot, source, target, self.plane.peer(way))

    def spread_send(self, step):
        z = self.plane.z
        pl.when((z <= 2) & (step <= z))(lambda: self.spread_copy("up", step, z).start())
        pl.when((z >= 1) & (step <= 3 - z))(lambda: self.spread_copy("down", step, z).start())

    def spread_wait(self, step):
        z = self.plane.z
        pl.when((z >= 1) & (step <= z - 1))(lambda: self.spread_copy("up", step, z - 1).wait_recv())
        pl.when((z <= 2) & (step <= 2 - z))(lambda: self.spread_copy("down", step, z + 1).wait_recv())
        pl.when((z <= 2) & (step <= z))(lambda: self.spread_copy("up", step, z).wait_send())
        pl.when((z >= 1) & (step <= 3 - z))(lambda: self.spread_copy("down", step, z).wait_send())

    def halve(self):
        other = self.x_base + (1 - self.plane.x) * self.half
        return self.plane.copy(
            self.slots[12],
            self.rows_of(self.buf, other, self.half),
            self.rows_of(self.land, self.x_land, self.half),
            self.plane.peer("x"),
        )

    def halve_wait(self):
        self.halve().wait()
        self.add(self.x_base + self.plane.x * self.half, self.x_land, self.half)

    def double(self):
        start = self.x_base + self.plane.x * self.half
        target = self.rows_of(self.out, start, self.half)
        source = target if self.x_first else self.rows_of(self.buf, start, self.half)
        return self.plane.copy(self.slots[13], source, target, self.plane.peer("x"))

    def keep(self):
        if self.x_first:
            start, size = self.z_base + self.plane.z * self.quarter, self.quarter
        else:
            start, size = self.x_base + self.plane.x * self.half, self.half
        return pltpu.make_async_copy(
            self.rows_of(self.buf, start, size), self.rows_of(self.out, start, size), self.mark
        )

    def step(self, number):
        if self.x_first:
            if number == 0:
                self.halve().start()
            elif number == 1:
                self.halve_wait()
                self.gather_send(0)
            elif number <= 3:
                self.gather_wait(number - 2)
                self.gather_send(number - 1)
            elif number == 4:
                self.gather_wait(2)
                self.keep().start()
                self.spread_send(0)
            elif number <= 6:
                self.spread_wait(number - 5)
                self.spread_send(number - 4)
            elif number == 7:
                self.spread_wait(2)
                self.keep().wait()
                self.double().start()
            else:
                self.double().wait()
        else:
            if number == 0:
                self.gather_send(0)
            elif number <= 2:
                self.gather_wait(number - 1)
                self.gather_send(number)
            elif number == 3:
                self.gather_wait(2)
                self.halve().start()
            elif number == 4:
                self.halve_wait()
                self.keep().start()
                self.double().start()
            elif number == 5:
                self.double().wait()
                self.keep().wait()
                self.spread_send(0)
            elif number <= 7:
                self.spread_wait(number - 6)
                self.spread_send(number - 5)
            else:
                self.spread_wait(2)


SAVED = (
    "branch", "mg", "dmg", "mid", "st", "res3", "res4", "unit0", "unit1", "scale", "act", "dact",
    "h", "p", "qkv", "ctx", "x", "c", "states", "decay",
)
GRADS = ("merge", "conv", "down", "win", "gru", "out", "qkv")
PIECES = (
    (0, 384, False),
    (1, 256, False),
    (1, 512, True),
    (1, 384, True),
    (2, 512, True),
    (2, 256, True),
    (3, 768, True),
    (4, 384, True),
    (5, 384, True),
    (6, 384, False),
    (6, 768, False),
)
SCHEDULE = (
    (),
    (0, 10, 20, 30,),
    (),
    (1, 11,),
    (21,),
    (2,),
    (40, 50, 12,),
    (60, 22, 31,),
    (3,),
    (13,),
    (23,),
    (32, 41, 24,),
    (51, 33,),
    (42,),
    (25, 52,),
    (34, 43,),
    (61, 26, 53, 4, 14, 35, 44,),
    (27, 5, 62, 15, 54, 36,),
    (),
    (80, 90, 100, 45, 6,),
    (63, 28, 16, 37, 55,),
    (81, 91, 46,),
    (101, 7, 64, 38, 82, 17, 56,),
    (92, 47,),
    (102, 8,),
    (70, 65, 83, 18, 57, 93, 48,),
    (103, 71,),
    (66, 84, 72, 58, 94,),
    (104, 73, 67, 85, 95,),
    (74, 105, 86, 96, 75, 106, 87, 97, 76, 107, 68, 98, 77, 88, 108, 78,),
)


def backward_kernel(units, channels, dp_size, *refs):
    refs = list(refs)
    take = lambda count: [refs.pop(0) for _ in range(count)]
    hbm = SimpleNamespace(**dict(zip(SAVED, take(len(SAVED)))))
    weights_in = take(7)
    gate_in, gain, pickr, edges, norm_in = take(5)
    grad_tokens, grad_chars = take(2)
    grads_out = dict(zip(GRADS, take(len(GRADS))))
    (small_out,) = take(1)
    names = [n for n in SAVED if n not in ("branch", "states", "decay", "p", "x")]
    v = SimpleNamespace(**dict(zip(names, take(len(names)))))
    weights = take(7)
    wq, wout, win, wdown, wg, wc, wm = weights
    (pb, states, decay, drive, dpre, dyk, fg, gtok, dproj, gru_acc, res2, res1, ds, parts,
     stage, got, held, temp, cstage, cgot, cheld, ctemp) = take(22)
    land = dict(zip(GRADS, take(len(GRADS))))
    big = SimpleNamespace(**dict(zip(GRADS, take(len(GRADS)))))
    small, small_land, gate_bias, send, recv, dsend, drecv, local, marks, credit = take(10)

    seqs, shard, width = grad_tokens.shape
    length = 4 * shard
    block_chars = grad_chars.shape[1]
    total = 4 * block_chars
    heads = pb.shape[1] // 4
    cols = v.ctx.shape[2]
    g = Group(send, recv, seqs)
    me = g.me
    inside = dp_size == 8
    plane = Plane(dsend, drecv, marks)

    def each(body):
        def run(seq, carry):
            body(seq)
            return carry

        lax.fori_loop(0, seqs, run, 0)

    def load(name):
        index = names.index(name)
        return pltpu.make_async_copy(getattr(hbm, name), getattr(v, name), local.at[index])

    spare = len(names)
    p_copy = lambda: pltpu.make_async_copy(hbm.p, pb, local.at[spare])
    x_copy = lambda: pltpu.make_async_copy(hbm.x, v.h, local.at[39])

    def states_copy(s):
        return pltpu.make_async_copy(hbm.states.at[s], states, local.at[spare + 1])

    def decay_copy(s, tile):
        return pltpu.make_async_copy(
            hbm.decay.at[s, tile], decay.at[tile], local.at[spare + 2 + tile]
        )

    def out_copy(kind, s):
        source, target = ((res1, grad_tokens), (cheld, grad_chars))[kind]
        return pltpu.make_async_copy(
            source.at[s], target.at[s], local.at[spare + 4 + kind * seqs + s]
        )

    pieces = 2 * width // length
    gb = Gather(
        g, pb, hbm.branch, place=lambda s, t: pb.at[s, pl.ds(t * pieces, pieces)]
    )
    gf, ga = Gather(g, fg), Gather(g, v.mid)
    pick = lambda ref: (lambda s, i: ref.at[s, i])
    own = lambda ref: (lambda s: ref.at[s])
    s_mid = Scatter(g, pick(stage), pick(got), own(held), temp)
    s_hid = Scatter(g, pick(stage), pick(got), own(held), temp)
    s_tok = Scatter(g, pick(stage), pick(got), own(held), temp)
    s_chr = Scatter(g, pick(cstage), pick(cgot), own(cheld), ctemp)
    s_cout = Scatter(g, pick(cstage), pick(cgot), own(cheld), ctemp)

    def own_branch(s):
        return pltpu.make_async_copy(
            hbm.branch.at[s], gb.at(s, me), local.at[spare + 4 + 2 * seqs + s]
        )

    def weight(number):
        return pltpu.make_async_copy(weights_in[number], weights[number], local.at[40 + number])

    each(lambda s: own_branch(s).start())
    weight(6).start()
    for name in ("dmg", "res4", "mg", "mid", "st"):
        load(name).start()
    for number in (5, 3, 2, 1, 0, 4):
        weight(number).start()
    states_copy(0).start()
    for tile in range(2):
        decay_copy(0, tile).start()
    for name in names:
        if name not in ("dmg", "res4", "mg", "mid", "st"):
            load(name).start()

    barrier = pltpu.get_barrier_semaphore()
    places = [{"tensor": g.pair}, {"tensor": g.far}]
    if inside:
        places += [{"dp": plane.peer(way)} for way in ("x", "up", "down")]
        places += [{"dp": plane.pair(2)}]
    for place in places:
        pl.semaphore_signal(barrier, inc=1, device_id=place, device_id_type=pl.DeviceIdType.MESH)
    pl.semaphore_wait(barrier, len(places))
    each(gb.start)
    dpre[...] = jnp.zeros_like(dpre)
    gate_bias[...] = jnp.zeros_like(gate_bias)
    gate_bias[:, pl.ds(0, units)] = gate_in[...]
    side = 2 * LANE
    for t in range(4):
        for j in range(width // side):
            row = lax.broadcasted_iota(jnp.int32, (side, side), 0)
            col = lax.broadcasted_iota(jnp.int32, (side, side), 1) + j * side
            unit = row % LANE
            hit = (col == row // LANE * 4 * units + t * units + unit) & (unit < units)
            cstage[t // 2, j, pl.ds(t % 2 * side, side), :] = hit.astype(F32).astype(BF16)
    small[...] = jnp.zeros_like(small)
    small[0, pl.ds(0, 4), :] = norm_in[...]
    lane = lax.broadcasted_iota(jnp.int32, (shard, LANE), 1)
    left = lane < HD
    for name in ("dmg", "res4"):
        load(name).wait()
    weight(6).wait()
    weight(5).wait()

    def block_rows(t, size):
        return pl.ds(pl.multiple_of(t * size, size), size)

    def merge_back(s):
        gb.forward(s)
        gb.finish(s)
        own_branch(s).wait()

        def inner(t, carry):
            rows = block_rows(t, shard)
            back = None
            for j in range(pieces):
                piece = nt(pb[s, t * pieces + j], wm[:, j * length : (j + 1) * length])
                back = piece if back is None else back + piece
            dpre[pl.ds(pl.multiple_of(8 + t * shard, 8), shard), :] = (
                (back * v.dmg[s, rows, :].astype(F32)).astype(BF16).astype(F32)
            )
            return carry

        lax.fori_loop(0, 4, inner, 0)

        def taps(t, carry):
            rows = block_rows(t, shard)
            window = dpre[pl.ds(pl.multiple_of(t * shard, 8), shard + 16), :]
            marks = edges[s, rows, :]
            before = window[9 : 9 + shard] * marks[:, 1:2]
            after = window[7 : 7 + shard] * marks[:, 0:1]
            dyk[s, rows, :] = pack3(
                [before, window[8 : 8 + shard], after], channels
            ).astype(BF16)
            return carry

        lax.fori_loop(0, 4, taps, 0)

        def mid_part(b, out):
            out[...] = nn(dyk[s, block_rows(b, shard), :], wc[:, pl.ds(0, width)])

        s_mid.start(s, mid_part)

    each(merge_back)
    sums, marks_at = [], {}
    for which, height, x_first in PIECES if inside else ():
        name = GRADS[which]
        first, at = marks_at.get(name, (0, 0))
        sums.append(
            Reduce(
                plane, getattr(big, name), grads_out[name], land[name], first, at, height, x_first
            )
        )
        marks_at[name] = (first + height, at + Reduce.landing_rows(height, x_first))
    fired = [0] * len(sums)

    def fire(hook):
        for entry in SCHEDULE[hook] if inside else ():
            which, number = divmod(entry, 10)
            fired[which] += 1
            sums[which].step(number)

    def fire_in(seq, hook, stride):
        for k in range(2):
            pl.when(seq == k)(functools.partial(fire, hook + k * stride))

    tokens = seqs * length
    step_w = 2 * LANE

    def merge_weights():
        for name in ("mg", "mid", "st"):
            load(name).wait()

        half_w = width
        for j in range(pieces):
            right = jnp.concatenate(
                [pb[s, t * pieces + j] for s in range(seqs) for t in range(4)], axis=0
            )
            out = tn(v.mg[...].reshape(tokens, -1), right)[:channels].astype(BF16)
            at = 0
            while at < length:
                part, inside_at = divmod(j * length + at, half_w)
                size = min(length - at, half_w - inside_at)
                big.merge[pl.ds(part * channels, channels), pl.ds(inside_at, size)] = out[
                    :, at : at + size
                ]
                at += size
        taps = 3 * channels

        def conv_rows(j, carry):
            lanes = pl.ds(pl.multiple_of(j * LANE, LANE), LANE)
            left_rows = dyk[:, :, lanes].reshape(tokens, LANE)
            size = min(LANE, taps - LANE * j) if isinstance(j, int) else LANE
            first = j * LANE if isinstance(j, int) else pl.multiple_of(j * LANE, LANE)
            out = tn(left_rows, v.mid[...].reshape(tokens, width))
            big.conv[pl.ds(first, size), :] = out[:size].astype(BF16)
            padded = [
                tn(left_rows, v.st[:, t].reshape(tokens, side)).astype(BF16) for t in range(4)
            ]
            first = taps + j * LANE if isinstance(j, int) else pl.multiple_of(taps + j * LANE, 64)
            for k in range(width // side):
                out = None
                for t in range(4):
                    piece = nn(padded[t], cstage[t // 2, k, pl.ds(t % 2 * side, side), :])
                    out = piece if out is None else out + piece
                big.conv[pl.ds(first, size), pl.ds(k * side, side)] = out[:size].astype(BF16)
            return carry

        lax.fori_loop(0, taps // LANE, conv_rows, 0)
        if taps % LANE:
            conv_rows(taps // LANE, 0)
        p_copy().start()
        fire(1)

    def second_back(s):
        incoming = v.res3[s] + s_mid.finish(s)
        unit = v.unit1[s]
        small[0, 5:6] += jnp.sum(incoming * unit, axis=0, keepdims=True)
        small[0, 7:8] += jnp.sum(incoming, axis=0, keepdims=True)
        spread = v.scale[s, 1][:, 0:1]
        res2[s] = normalize_back(unit, spread, incoming * gain[1:2])
        fg[s, me] = res2[s].astype(BF16)
        gf.start(s)
        fire_in(s, 0, 2)
        pl.when(s == 0)(merge_weights)

    for name in ("res3", "unit1", "scale"):
        load(name).wait()
    each(second_back)
    for name in ("dact", "act", "h"):
        load(name).wait()
    weight(3).wait()
    weight(2).wait()

    def ffn_back(s):
        gf.forward(s)
        gf.finish(s)

        def part(b, out):
            back = nt(fg[s, b], wdown[...]) * v.dact[s, b].astype(F32)
            v.dact[s, b] = back.astype(BF16)
            out[...] = nt(v.dact[s, b], win[...])

        s_hid.start(s, part)
        fire_in(s, 3, 1)

    each(ffn_back)

    def all_ffn_weights():
        def ffn_weights(j, carry):
            colsj = pl.ds(pl.multiple_of(j * step_w, step_w), step_w)
            out = tn(v.act[:, :, :, colsj].reshape(tokens, step_w), fg[...].reshape(tokens, width))
            big.down[block_rows(j, step_w), :] = out.astype(BF16)
            return carry

        lax.fori_loop(0, big.down.shape[0] // step_w, ffn_weights, 0)
        fire(6)

        def in_weights(j, carry):
            colsj = pl.ds(pl.multiple_of(j * step_w, step_w), step_w)
            out = tn(
                v.h[:, :, :, colsj].reshape(tokens, step_w), v.dact[...].reshape(tokens, -1)
            )
            big.win[block_rows(j, step_w), :] = out.astype(BF16)
            return carry

        lax.fori_loop(0, width // step_w, in_weights, 0)
        x_copy().start()
        fire(7)

    load("unit0").wait()

    def first_back(s):
        incoming = res2[s] + s_hid.finish(s)
        unit = v.unit0[s]
        small[0, 4:5] += jnp.sum(incoming * unit, axis=0, keepdims=True)
        small[0, 6:7] += jnp.sum(incoming, axis=0, keepdims=True)
        spread = v.scale[s, 0][:, 0:1]
        res1[s] = normalize_back(unit, spread, incoming * gain[0:1])
        v.mid[s, me] = res1[s].astype(BF16)
        ga.start(s)
        fire_in(s, 5, 3)
        pl.when(s == 0)(all_ffn_weights)

    each(first_back)

    def chars_back(s):
        def char_part(b, out):
            first = pl.multiple_of(width + b * 2 * LANE, 2 * LANE)
            out[...] = nn(dyk[s], wc[:, pl.ds(first, 2 * LANE)])
            out[block_rows(me, shard), :] += v.res4[s, b].astype(F32)

        s_chr.start(s, char_part)
        fire_in(s, 9, 1)

    each(chars_back)
    hops = [("t", g.pair), ("t", g.far)] + ([("d", k) for k in range(3)] if inside else [])
    slots_t, slots_d = g.slots(2), plane.take(3)

    def small_copy(number):
        kind, where = hops[number]
        source, target = small.at[number], small_land.at[number]
        if kind == "t":
            return g.copy(slots_t[number], 0, source, target, where)
        return plane.copy(slots_d[where], source, target, plane.pair(where))

    def small_step(number):
        if number > 0:
            small_copy(number - 1).wait()
            value, more = small[number - 1], small_land[number - 1]
            small[number, pl.ds(0, 8), :] = value[:8] + more[:8]
            rest = small[6, pl.ds(0, 8), :] if number <= 2 else value[8:] + more[8:]
            small[number, pl.ds(8, 8), :] = rest
        if number < len(hops):
            small_copy(number).start()

    if not inside:
        hops = []
    small_step(0) if hops else None
    for name in ("qkv", "ctx"):
        load(name).wait()
    weight(1).wait()
    weight(0).wait()
    p_copy().wait()

    def attention_back(s):
        ga.forward(s)
        ga.finish(s)
        dctx = v.dmg

        def context(t, carry):
            dctx[s, block_rows(t, shard), :] = nt(v.mid[s, t], wout[...]).astype(BF16)
            return carry

        lax.fori_loop(0, 4, context, 0)
        for tile in range(cols // LANE):
            lanes = pl.ds(tile * LANE, LANE)
            for half in range(2):
                head = 2 * tile + half
                if head >= heads:
                    continue
                paired = 2 * tile + 1 < heads

                def rows_of(b, carry):
                    rows = block_rows(b, shard)
                    grad = dctx[s, rows, lanes]
                    if paired:
                        grad = jnp.where(left if half == 0 else ~left, grad, jnp.zeros_like(grad))
                    back = nt(grad, v.qkv[s, 2, :, lanes])
                    probs = pb[s, head * 4 + b].astype(F32)
                    row_dot = jnp.sum(probs * back, axis=-1, keepdims=True)
                    ds[b] = (probs * (back - row_dot)).astype(BF16)
                    out = nn(ds[b], v.qkv[s, 1, :, lanes])
                    if half == 1:
                        out = jnp.where(left, ctemp[rows, lanes], out)
                    ctemp[rows, lanes] = out
                    return carry

                lax.fori_loop(0, 4, rows_of, 0)
                keys = tn(ds[...].reshape(length, length), v.qkv[s, 0, :, lanes])
                values = tn(
                    pb[s, pl.ds(head * 4, 4)].reshape(length, length), dctx[s, :, lanes]
                )
                if half == 1:
                    wide_left = lax.broadcasted_iota(jnp.int32, (length, LANE), 1) < HD
                    keys = jnp.where(wide_left, parts[0, :, lanes], keys)
                    values = jnp.where(wide_left, parts[1, :, lanes], values)
                parts[0, :, lanes] = keys
                parts[1, :, lanes] = values
                fire_in(s, 11 + head, 4)

        def pack(t, carry):
            rows = block_rows(t, shard)
            query = ctemp[rows, :].astype(BF16).astype(F32) * 0.125
            dyk[s, rows, :] = pack3(
                [query, parts[0, rows, :], parts[1, rows, :]], HD * heads
            ).astype(BF16)
            return carry

        lax.fori_loop(0, 4, pack, 0)

        def part(b, out):
            out[...] = nn(dyk[s, block_rows(b, shard), :], wq[...])

        s_tok.start(s, part)

        fire_in(s, 14, 4)

    each(attention_back)
    small_step(1) if hops else None

    x_copy().wait()

    tall = 3 * HD * heads
    half_w = width // 2

    def qkv_weights(j, carry):
        lanes = pl.ds(pl.multiple_of(j * LANE, LANE), LANE)
        size = min(LANE, tall - LANE * j) if isinstance(j, int) else LANE
        out = tn(dyk[:, :, lanes].reshape(tokens, LANE), v.h[...].reshape(tokens, width))
        for k in range(2):
            first = k * tall + j * LANE
            first = first if isinstance(j, int) else pl.multiple_of(first, 64)
            big.qkv[pl.ds(first, size), :] = out[:size, k * half_w : (k + 1) * half_w].astype(BF16)
        return carry

    lax.fori_loop(0, tall // LANE, qkv_weights, 0)
    if tall % LANE:
        qkv_weights(tall // LANE, 0)
    out = tn(v.ctx[...].reshape(tokens, -1), v.mid[...].reshape(tokens, width))
    for k in range(2):
        big.out[pl.ds(k * HD * heads, HD * heads), :] = out[
            : HD * heads, k * half_w : (k + 1) * half_w
        ].astype(BF16)
    fire(19)

    load("c").wait()
    weight(4).wait()

    def gru_back(s):
        gtok[...] = s_chr.finish(s).astype(BF16)
        for peer in (g.pair, g.far):
            pl.semaphore_signal(
                credit.at[s], inc=1, device_id={"tensor": peer},
                device_id_type=pl.DeviceIdType.MESH,
            )
        def spread_out(t, carry):
            rows = block_rows(t, LANE)
            for tile in range(2):
                ids = lax.broadcasted_iota(jnp.int32, (LANE, length), 0) + t * LANE
                hot = (ids == pickr[s, tile : tile + 1, :]).astype(F32).astype(BF16)
                drive[tile, rows, :] = nn(hot, gtok[:, pl.ds(tile * LANE, LANE)])
            return carry

        lax.fori_loop(0, total // LANE, spread_out, 0)
        fire_in(s, 20, 3)
        for tile in range(2):
            decay_copy(s, tile).wait()
        recur((False, True), decay, drive, drive, block_chars, back=True)
        fire_in(s, 21, 3)
        states_copy(s).wait()

        @pl.when(s == 0)
        def _():
            gru_acc[...] = jnp.zeros_like(gru_acc)

        def part(b, out):
            def finish(t, sums):
                inner = block_rows(t, LANE)
                rows = pl.ds(pl.multiple_of(b * block_chars + t * LANE, LANE), LANE)
                proj = nt(v.c[s, b, inner, :], wg[...])
                new = []
                for tile in range(2):
                    colst = slice(tile * LANE, (tile + 1) * LANE)
                    gate = jax.nn.sigmoid(proj[:, colst] + gate_bias[tile : tile + 1])
                    cand = proj[:, (2 + tile) * LANE : (3 + tile) * LANE]
                    flow = drive[tile, rows, :] * gate
                    logit = flow * (cand - states[tile, rows, :].astype(F32))
                    dproj[inner, pl.ds(tile * LANE, LANE)] = logit.astype(BF16)
                    dproj[inner, pl.ds((2 + tile) * LANE, LANE)] = flow.astype(BF16)
                    new.append(sums[tile] + jnp.sum(logit, axis=0, keepdims=True))
                return tuple(new)

            zero = jnp.zeros((1, LANE), F32)
            sums = lax.fori_loop(0, block_chars // LANE, finish, (zero, zero))
            for tile in range(2):
                small[6, 0:1, pl.ds(tile * LANE, LANE)] += sums[tile]
            out[...] = nn(dproj[...], wg[...])
            gru_acc[...] += tn(dproj[...], v.c[s, b])

        pl.semaphore_wait(credit.at[s], 2)
        s_cout.start(s, part)

        @pl.when(s + 1 < seqs)
        def _():
            states_copy(s + 1).start()
            for tile in range(2):
                decay_copy(s + 1, tile).start()

        if seqs > 1:
            pl.when(s == 0)(functools.partial(fire, 22))

    each(gru_back)
    for d in range(2):
        for k in range(2):
            big.gru[pl.ds((2 * d + k) * units, units), :] = gru_acc[
                pl.ds((2 * k + d) * LANE, units), :
            ].astype(BF16)
    small_step(2) if hops else None
    fire(25)

    def last(s):
        res1[s] = res1[s] + s_tok.finish(s)
        out_copy(0, s).start()
        cheld[s] = s_cout.finish(s)
        out_copy(1, s).start()

    each(last)

    def emit(name):
        return pltpu.make_async_copy(
            getattr(big, name), grads_out[name], local.at[spare + 4 + 3 * seqs + GRADS.index(name)]
        )

    if inside:
        fire(26)
        small_step(3)
        fire(27)
        small_step(4)
        fire(28)
        small_step(5)
        fire(29)
        assert all(count == Reduce.steps for count in fired)
    else:
        for name in GRADS:
            emit(name).start()
        for name in GRADS:
            emit(name).wait()
    small_out[...] = small[len(hops)]
    if not inside:
        small_out[pl.ds(8, 8), :] = small[6, pl.ds(0, 8), :]
    each(lambda s: (out_copy(0, s).wait(), out_copy(1, s).wait()))


def backward_call(saved, weights, small, dp_size):
    wq, wout, win, wdown, wg, wc, wm, gate_bias = weights
    sds = jax.ShapeDtypeStruct
    seqs, shard, width = saved["res3"].shape
    length = shard * 4
    block_chars, char_width = saved["c"].shape[2:]
    total = 4 * block_chars
    cols, packed = wout.shape[0], wc.shape[0]
    tall = 3 * HD * small["heads"]
    channels = small["channels"]
    saved_in = [saved[n] for n in SAVED]
    names = [n for n in SAVED if n not in ("branch", "states", "decay", "p", "x")]
    shapes = [(saved[n].shape, saved[n].dtype) for n in names]
    grads = {
        "merge": (2 * channels, width), "conv": (2 * 3 * channels, width),
        "down": (win.shape[1], width), "win": (width, win.shape[1]),
        "gru": (4 * small["units"], char_width), "out": (2 * tall // 3, width // 2),
        "qkv": (2 * tall, width // 2),
    }
    pad = (seqs, 3, shard, width)
    cpad = (seqs, 3, length, 2 * LANE)
    scratch = shapes + [(w.shape, BF16) for w in weights[:7]] + [
        (saved["p"].shape, BF16),
        ((2, total, LANE), BF16),
        ((2, total, LANE), F32),
        ((2, total, LANE), F32),
        ((length + 16, wm.shape[0]), F32),
        ((seqs, length, packed), BF16),
        ((seqs, 4, shard, width), BF16),
        ((length, 2 * LANE), BF16),
        ((block_chars, 4 * LANE), BF16),
        ((4 * LANE, char_width), F32),
        ((seqs, shard, width), F32),
        ((seqs, shard, width), F32),
        ((4, shard, length), BF16),
        ((2, length, cols), F32),
        (pad, BF16), (pad, BF16), ((seqs, shard, width), F32), ((shard, width), F32),
        (cpad, BF16), (cpad, BF16), ((seqs, length, 2 * LANE), F32), ((length, 2 * LANE), F32),
    ]
    for which, name in enumerate(GRADS):
        landing = sum(Reduce.landing_rows(n, way) for k, n, way in PIECES if k == which)
        scratch.append(((landing if dp_size == 8 else 16, grads[name][1]), BF16))
    scratch += [(shape, BF16) for shape in grads.values()]
    scratch += [((7, 16, width), F32), ((5, 16, width), F32), ((2, LANE), F32)]
    anyspace = pl.BlockSpec(memory_space=pl.ANY)
    vmem = pl.BlockSpec(memory_space=pltpu.VMEM)
    ins = saved_in + list(weights) + [small["gain"]]
    ins += [saved["pickr"], saved["edges"], saved["norm_grads"]]
    outs = pl.pallas_call(
        functools.partial(backward_kernel, small["units"], channels, dp_size),
        out_shape=[sds((seqs, shard, width), F32), sds((seqs, block_chars, char_width), F32)]
        + [sds(shape, BF16) for shape in grads.values()]
        + [sds((16, width), F32)],
        in_specs=[anyspace] * (len(saved_in) + 7) + [vmem] * 5,
        out_specs=[anyspace] * (2 + len(grads)) + [vmem],
        scratch_shapes=[pltpu.VMEM(*one) for one in scratch]
        + [
            pltpu.SemaphoreType.DMA((32 * seqs,)),
            pltpu.SemaphoreType.DMA((32 * seqs,)),
            pltpu.SemaphoreType.DMA((14 * len(PIECES) + 4,)),
            pltpu.SemaphoreType.DMA((14 * len(PIECES) + 4,)),
            pltpu.SemaphoreType.DMA((48,)),
            pltpu.SemaphoreType.DMA((len(PIECES),)),
            pltpu.SemaphoreType.REGULAR((seqs,)),
        ],
        compiler_params=pltpu.CompilerParams(
            collective_id=1, has_side_effects=True, vmem_limit_bytes=63 * MIB
        ),
    )(*ins)
    names = ["grad_tokens", "grad_chars"] + list(grads) + ["small"]
    return dict(zip(names, outs))


def finish_kernel(
    units, conv, qkv, out, merge, down, win, gru, chars, tokens, first, second, rows,
    o_conv, o_qkv, o_out, o_merge, o_down, o_win, o_gru, o_chars, o_tokens, o_first, o_second,
    o_gain, o_bias, o_gate,
):
    for source, target in ((conv, o_conv), (qkv, o_qkv), (out, o_out)):
        half = source.shape[2]
        for k in range(2):
            target[:, k * half : (k + 1) * half] = source[k].astype(F32)
    for k in range(2):
        o_merge[:, k, :] = merge[k].astype(F32)
        o_gate[k : k + 1, :] = rows[8:9, k * LANE : k * LANE + units]
    for target, at in ((o_gain, 0), (o_bias, 2)):
        target[0:2] = rows[4 + at : 6 + at]
        target[2:4] = rows[at : at + 2]
    for source, target in ((down, o_down), (win, o_win), (gru, o_gru)):
        target[...] = source[...].astype(F32)
    for j in range(8):
        o_chars[0, j] = chars[0, :, j, :]
    for source, target in ((tokens, o_tokens), (first, o_first), (second, o_second)):
        target[...] = source[...]


def finish_call(grads, grad_chars, grad_tokens, token_out, char_out, rows, units):
    seqs, block_chars, char_width = grad_chars.shape
    steps = block_chars // 8
    turns = 2 * seqs
    chars = grad_chars.reshape(seqs, steps, 8, char_width)
    pairs = [
        grads[n].reshape(2, -1, grads[n].shape[1]) for n in ("conv", "qkv", "out", "merge")
    ]
    plain = [grads["down"], grads["win"], grads["gru"]]
    copied = [grad_tokens, token_out, char_out]
    flat = [(a.shape[1], 2 * a.shape[2]) for a in pairs[:3]]
    channels, width = pairs[3].shape[1:]
    merged = (channels, 2, width)
    plain_shapes = [a.shape for a in plain]
    ends = [(4, width), (4, width), (2, units)]

    def rows_spec(shape):
        return pl.BlockSpec((shape[0] // turns, shape[1]), lambda i: (i, 0))

    def pair_spec(shape):
        return pl.BlockSpec((2, shape[1] // turns, shape[2]), lambda i: (0, i, 0))

    def halves(shape):
        return pl.BlockSpec((1, shape[1] // 2, shape[2]), lambda i: (i // 2, i % 2, 0))

    return pl.pallas_call(
        functools.partial(finish_kernel, units),
        grid=(turns,),
        out_shape=[jax.ShapeDtypeStruct(shape, F32) for shape in flat + [merged] + plain_shapes]
        + [jax.ShapeDtypeStruct((seqs, 8, steps, char_width), F32)]
        + [jax.ShapeDtypeStruct(a.shape, a.dtype) for a in copied]
        + [jax.ShapeDtypeStruct(shape, F32) for shape in ends],
        in_specs=[pair_spec(a.shape) for a in pairs]
        + [rows_spec(a.shape) for a in plain]
        + [pl.BlockSpec((1, steps // 2, 8, char_width), lambda i: (i // 2, i % 2, 0, 0))]
        + [halves(a.shape) for a in copied]
        + [pl.BlockSpec(rows.shape, lambda i: (0, 0))],
        out_specs=[rows_spec(shape) for shape in flat]
        + [pl.BlockSpec((channels // turns, 2, width), lambda i: (i, 0, 0))]
        + [rows_spec(shape) for shape in plain_shapes]
        + [pl.BlockSpec((1, 8, steps // 2, char_width), lambda i: (i // 2, 0, i % 2, 0))]
        + [halves(a.shape) for a in copied]
        + [pl.BlockSpec(shape, lambda i: (0, 0)) for shape in ends],
        compiler_params=pltpu.CompilerParams(vmem_limit_bytes=62 * MIB),
    )(*pairs, *plain, chars, *copied, rows)


def local(
    tokens,
    characters,
    doc_lengths,
    token_chars,
    w_qkv,
    w_out,
    w_in,
    w_down,
    w_gru,
    gate_bias,
    w_conv,
    w_merge,
    norm_gain,
    norm_bias,
    token_cot,
    char_cot,
):
    micro_count = tokens.shape[0]
    shard_len = tokens.shape[1]
    model_width = tokens.shape[2]
    char_width = characters.shape[2]
    group_size = lax.axis_size("tensor")
    group_rank = lax.axis_index("tensor")
    length = shard_len * group_size
    char_total = characters.shape[1] * group_size
    head_cols = w_qkv.shape[2]
    heads_here = head_cols // HD
    units_here = w_gru.shape[3]
    merge_here = w_conv.shape[2]
    wq = jnp.transpose(w_qkv, (1, 2, 0)).reshape(3 * head_cols, model_width)
    wc = jnp.transpose(w_conv, (0, 2, 1)).reshape(3 * merge_here, 2 * model_width)
    wg = jnp.transpose(w_gru, (1, 2, 3, 0))
    more = -merge_here % LANE
    wm = jnp.pad(w_merge.reshape(merge_here, 2 * model_width), ((0, more), (0, 0)))
    block_chars = characters.shape[1]
    steps = block_chars // 8
    chars = jnp.swapaxes(
        characters.reshape(micro_count, 8, steps, char_width), 1, 2
    ).reshape(characters.shape)
    small = dict(
        gain=norm_gain, bias=norm_bias, cot_t=token_cot, cot_c=char_cot, docs=doc_lengths,
        counts=token_chars[:, None, :], heads=heads_here, units=units_here, channels=merge_here,
    )
    weights = (wq, w_out, w_in, w_down, wg, gate_bias, wc, wm)
    fw = forward_call(tokens, chars, weights, small)
    weights = (fw["wq"], fw["wout"], w_in, w_down, fw["wg"], fw["wc"], wm, gate_bias)
    dp_size = lax.axis_size("dp")
    bw = backward_call(fw, weights, small, dp_size)
    rows = bw["small"]
    grads = {name: bw[name] for name in GRADS}
    if dp_size != 8:
        grads, gate_rows = lax.psum((grads, rows[8:]), "dp")
        rows = jnp.concatenate([lax.psum(rows[:8], ("dp", "tensor")), gate_rows], axis=0)
    (conv, qkv, out, merge, down, win, gru, chars, tokens_grad, first, second, gain_grad, bias_grad,
     gate_grad) = finish_call(
        grads, bw["grad_chars"], bw["grad_tokens"], fw["token_out"], fw["char_out"], rows,
        units_here,
    )
    conv = conv.reshape(3, merge_here, 2 * model_width)
    qkv = qkv.reshape(3, head_cols, model_width)
    gru = gru.reshape(2, 2, units_here, char_width)
    return (
        first,
        second,
        tokens_grad,
        chars.reshape(bw["grad_chars"].shape),
        jnp.transpose(qkv, (2, 0, 1)),
        out,
        win,
        down,
        jnp.transpose(gru, (3, 0, 1, 2)),
        gate_grad,
        jnp.transpose(conv, (0, 2, 1)),
        merge,
        gain_grad,
        bias_grad,
    )


def solution(mesh):
    return jax.shard_map(
        local,
        mesh=mesh,
        in_specs=(
            P("dp", "tensor", None),
            P("dp", "tensor", None),
            P("dp", None),
            P("dp", None),
            P(None, None, "tensor"),
            P("tensor", None),
            P(None, "tensor"),
            P("tensor", None),
            P(None, None, None, "tensor"),
            P(None, "tensor"),
            P(None, None, "tensor"),
            P("tensor", None, None),
            P(),
            P(),
            P("dp", "tensor", None),
            P("dp", "tensor", None),
        ),
        out_specs=(
            P("dp", "tensor", None),
            P("dp", "tensor", None),
            P("dp", "tensor", None),
            P("dp", "tensor", None),
            P(None, None, "tensor"),
            P("tensor", None),
            P(None, "tensor"),
            P("tensor", None),
            P(None, None, None, "tensor"),
            P(None, "tensor"),
            P(None, None, "tensor"),
            P("tensor", None, None),
            P(),
            P(),
        ),
        check_vma=False,
    )
```

```python
import functools
from types import SimpleNamespace

import jax
import jax.numpy as jnp
from jax import lax
from jax.experimental import pallas as pl
from jax.experimental.pallas import tpu as pltpu
from jax.sharding import PartitionSpec as P

HD = 64


NORM_EPSILON = 1e-06
MASK_VALUE = -1e30
HIGH_PRECISION = lax.Precision.HIGHEST


F32 = jnp.float32
BF16 = jnp.bfloat16
LANE = 128
MIB = 1024 * 1024


def nn(left, right):
    return jnp.dot(left, right, preferred_element_type=F32)


def nt(left, right):
    return lax.dot_general(left, right, (((1,), (1,)), ((), ())), preferred_element_type=F32)


def tn(left, right):
    return lax.dot_general(left, right, (((0,), (0,)), ((), ())), preferred_element_type=F32)


def gelu_pair(values):
    cdf = 0.5 * (1.0 + lax.erf(values * 0.7071067811865476))
    density = 0.3989422804014327 * jnp.exp(-0.5 * values * values)
    return values * cdf, cdf + values * density


def normalize(rows):
    centered = rows - jnp.mean(rows, axis=-1, keepdims=True)
    scale = lax.rsqrt(jnp.mean(centered * centered, axis=-1, keepdims=True) + NORM_EPSILON)
    return centered * scale, scale


def normalize_back(unit, scale, grad_unit):
    return scale * (
        grad_unit
        - jnp.mean(grad_unit, axis=-1, keepdims=True)
        - unit * jnp.mean(grad_unit * unit, axis=-1, keepdims=True)
    )


def roll_lanes(value, shift):
    return pltpu.roll(value, shift % value.shape[1], axis=1)


def unpack3(packed, size):
    room = -(-size // LANE) * LANE
    lane = lax.broadcasted_iota(jnp.int32, (packed.shape[0], room), 1)
    parts = []
    for k in range(3):
        first = k * size // LANE * LANE
        inner = k * size - first
        part = packed[:, first : min(first + room + LANE, packed.shape[1])]
        if inner:
            part = roll_lanes(part, -inner)
        parts.append(jnp.where(lane < size, part[:, :room], 0.0))
    return parts


def pack3(parts, size):
    room = parts[0].shape[1]
    columns = -(-3 * size // LANE) * LANE
    tiles = [None] * (columns // LANE)
    for k in range(3):
        first, inner = divmod(k * size, LANE)
        part = parts[k]
        if inner:
            part = jnp.concatenate([part, jnp.zeros_like(part[:, :LANE])], axis=1)
            part = roll_lanes(part, inner)
        for j in range(part.shape[1] // LANE):
            if first + j < len(tiles) and (first + j) * LANE < (k + 1) * size:
                tile = part[:, j * LANE : (j + 1) * LANE]
                old = tiles[first + j]
                tiles[first + j] = tile if old is None else old + tile
    return jnp.concatenate(tiles, axis=1)


class Group:
    def __init__(self, send, recv, seqs):
        self.me = lax.axis_index("tensor")
        self.low = self.me % 2
        self.high = self.me // 2
        self.pair = self.high * 2 + (1 - self.low)
        self.far = (1 - self.high) * 2 + self.low
        self.send, self.recv, self.seqs, self.used = send, recv, seqs, 0

    def block(self, turn):
        left = 3 - turn
        return ((self.high + left // 2) % 2) * 2 + (self.low + left % 2) % 2

    def slots(self, count):
        first = self.used
        self.used += count
        return [first + i for i in range(count)]

    def copy(self, slot, seq, source, target, peer):
        index = slot * self.seqs + seq
        return pltpu.make_async_remote_copy(
            src_ref=source,
            dst_ref=target,
            send_sem=self.send.at[index],
            recv_sem=self.recv.at[index],
            device_id={"tensor": peer},
            device_id_type=pl.DeviceIdType.MESH,
        )

    def greet(self):
        barrier = pltpu.get_barrier_semaphore()
        for peer in (self.pair, self.far):
            pl.semaphore_signal(
                barrier, inc=1, device_id={"tensor": peer}, device_id_type=pl.DeviceIdType.MESH
            )
        pl.semaphore_wait(barrier, 2)


class Gather:
    def __init__(self, group, buf, source=None, place=None):
        self.group, self.source = group, source
        self.at = place or (lambda seq, t: buf.at[seq, t])
        self.near, self.over, self.fwd = group.slots(3)

    def own(self, seq):
        return self.at(seq, self.group.me) if self.source is None else self.source.at[seq]

    def near_copy(self, seq):
        g = self.group
        return g.copy(self.near, seq, self.own(seq), self.at(seq, g.me), g.pair)

    def over_copy(self, seq):
        g = self.group
        return g.copy(self.over, seq, self.own(seq), self.at(seq, g.me), g.far)

    def fwd_copy(self, seq):
        g = self.group
        other = self.at(seq, g.far)
        return g.copy(self.fwd, seq, other, other, g.pair)

    def start(self, seq):
        self.over_copy(seq).start()
        self.near_copy(seq).start()

    def forward(self, seq):
        self.over_copy(seq).wait_recv()
        self.fwd_copy(seq).start()

    def finish(self, seq):
        near = self.near_copy(seq)
        fwd = self.fwd_copy(seq)
        near.wait_recv()
        fwd.wait_recv()
        near.wait_send()
        self.over_copy(seq).wait_send()
        fwd.wait_send()


class Scatter:
    def __init__(self, group, stage, got, own, temp):
        self.group, self.stage, self.got, self.held, self.temp = group, stage, got, own, temp
        self.names = group.slots(3)

    def copies(self, seq):
        g = self.group
        peers = (g.pair, g.pair, g.far)
        return [
            g.copy(self.names[i], seq, self.stage(seq, i), self.got(seq, i), peers[i])
            for i in range(3)
        ]

    def start(self, seq, part):
        mine, other, over = self.copies(seq)

        def turn(step, carry):
            part(self.group.block(step), self.temp)

            @pl.when(step == 0)
            def _():
                self.stage(seq, 1)[...] = self.temp[...].astype(BF16)
                other.start()

            @pl.when(step == 1)
            def _():
                other.wait_recv()
                self.stage(seq, 2)[...] = (self.temp[...] + self.got(seq, 1)[...]).astype(BF16)
                over.start()

            @pl.when(step == 2)
            def _():
                self.stage(seq, 0)[...] = self.temp[...].astype(BF16)
                mine.start()

            @pl.when(step == 3)
            def _():
                self.held(seq)[...] = self.temp[...]

            return carry

        lax.fori_loop(0, 4, turn, 0)

    def finish(self, seq):
        mine, other, over = self.copies(seq)
        mine.wait_recv()
        over.wait_recv()
        total = self.held(seq)[...] + self.got(seq, 0)[...] + self.got(seq, 2)[...]
        mine.wait_send()
        other.wait_send()
        over.wait_send()
        return total


def shift_rows(value, count, up, fill):
    edge = jnp.full((count, value.shape[1]), fill, value.dtype)
    if up:
        return jnp.concatenate([edge, value[:-count]], axis=0)
    return jnp.concatenate([value[count:], edge], axis=0)


def recur(ups, decays, drives, outs, block, back=False):
    steps = block // 8
    pairs = [(tile, t) for tile in range(2) for t in range(4)]

    def rows(tile, t, step):
        row = step if ups[tile] else steps - 1 - step
        return pl.ds(pl.multiple_of(t * block + row * 8, 8), 8)

    def summary(step, carry):
        new = []
        for i, (tile, t) in enumerate(pairs):
            state, mult = carry[2 * i], carry[2 * i + 1]
            here = rows(tile, t, step)
            decay, drive = decays[tile, here, :], drives[tile, here, :]
            state = decay * (state + drive) if back else decay * state + drive
            new += [state, decay * mult]
        return tuple(new)

    zero, one = jnp.zeros((8, LANE), F32), jnp.ones((8, LANE), F32)
    ends = lax.fori_loop(0, steps, summary, (zero, one) * 8, unroll=4)
    starts = []
    for tile in range(2):
        state = jnp.concatenate([ends[2 * (4 * tile + t)] for t in range(4)], axis=0)
        mult = jnp.concatenate([ends[2 * (4 * tile + t) + 1] for t in range(4)], axis=0)
        for count in (1, 2, 4, 8, 16):
            state = mult * shift_rows(state, count, ups[tile], 0.0) + state
            mult = mult * shift_rows(mult, count, ups[tile], 1.0)
        state = shift_rows(state, 1, ups[tile], 0.0)
        starts += [state[8 * t : 8 * t + 8] for t in range(4)]

    def write(step, carry):
        new = []
        for i, (tile, t) in enumerate(pairs):
            here = rows(tile, t, step)
            decay, drive = decays[tile, here, :], drives[tile, here, :]
            if back:
                value = drive + carry[i]
                new.append(decay * value)
            else:
                value = decay * carry[i] + drive
                new.append(value)
            outs[tile, here, :] = value
        return tuple(new)

    lax.fori_loop(0, steps, write, tuple(starts), unroll=4)


def forward_kernel(
    units, channels, docs, counts, tokens, chars, wq_in, wout_in, win_in, wdown_in, wg_in, gate_in,
    wc_in, wm_in, gain, bias, cot_t_in, cot_c_in,
    token_out, char_out, o_x, o_c, o_qkv, o_p, o_ctx, o_h, o_act, o_dact, o_mid, o_st, o_mg,
    o_dmg, o_states, o_decay, o_unit0, o_unit1, o_scale, o_res3, o_res4, o_branch,
    o_wq, o_wout, o_wg, o_wc, norm_grads, pickr, edges,
    x, c, qkv, p, ctx, h, act, dact, mid, st, mg, dmg, low_states, decays, unit0, unit1, scale, res3, res4, branch,
    wq, wout, wg, wc, hidden, middle, outs_t, outs_c, states, drive, taps, perm, gate_bias,
    win, wdown, wm, cot_t, cot_c, segc, segr, pickc, keep,
    stage, got, held, temp, send, recv, local,
):
    seqs, length = counts.shape
    shard, width = tokens.shape[1], tokens.shape[2]
    block_chars = chars.shape[1]
    heads = p.shape[1] // 4
    g = Group(send, recv, seqs)
    me = g.me
    saves = []

    def keep_out(seq, source, target):
        saves.append((source, target, len(saves)))

    def local_copy(number, seq, source, target):
        return pltpu.make_async_copy(source, target, local.at[number * seqs + seq])

    gx, gc = Gather(g, x, tokens), Gather(g, c)
    gh, gm, gs = Gather(g, h), Gather(g, mid), Gather(g, st)
    narrow = lambda ref: (lambda s, i: ref.at[s, i, :, pl.ds(0, width)])
    wide = lambda ref: (lambda s, i: ref.at[s, i])
    own_n = lambda s: held.at[s, :, pl.ds(0, width)]
    own_w = lambda s: held.at[s]
    thin = temp.at[:, pl.ds(0, width)]
    s_attn = Scatter(g, narrow(stage), narrow(got), own_n, thin)
    s_ffn = Scatter(g, narrow(stage), narrow(got), own_n, thin)
    s_branch = Scatter(g, wide(stage), wide(got), own_w, temp)

    def own_x(seq):
        return local_copy(0, seq, tokens.at[seq], x.at[seq, me])

    def own_c(seq):
        return local_copy(1, seq, chars.at[seq], c.at[seq, me])

    plan = [
        (x, o_x), (c, o_c), (qkv, o_qkv), (p, o_p), (ctx, o_ctx), (h, o_h), (act, o_act),
        (dact, o_dact), (mid, o_mid), (st, o_st), (mg, o_mg), (dmg, o_dmg), (low_states, o_states),
        (decays, o_decay), (res4, o_res4), (unit0, o_unit0), (unit1, o_unit1), (scale, o_scale), (res3, o_res3), (branch, o_branch),
        (outs_t, token_out), (outs_c, char_out),
    ]

    def save(seq, *names):
        for name in names:
            for number, (source, target) in enumerate(plan):
                if source is name:
                    local_copy(2 + number, seq, source.at[seq], target.at[seq]).start()

    def each(body):
        def run(seq, carry):
            body(seq)
            return carry

        lax.fori_loop(0, seqs, run, 0)

    each(lambda s: (own_x(s).start(), own_c(s).start()))
    base = (2 + len(plan)) * seqs
    late = [(win_in, win), (wdown_in, wdown), (wm_in, wm), (cot_t_in, cot_t), (cot_c_in, cot_c)]
    rows_in = wq_in.shape[0]
    fills = [
        (wq_in, wq.at[pl.ds(0, rows_in), :]),
        (wout_in, wout.at[pl.ds(0, wout_in.shape[0]), :]),
        (wc_in.at[:, pl.ds(0, width)], wc.at[pl.ds(0, rows_in), pl.ds(0, width)]),
    ]
    for d in range(2):
        for k in range(2):
            fills.append((wg_in.at[d, k], wg.at[pl.ds((2 * k + d) * LANE, units), :]))
    pieces = -(-rows_in // shard)
    for j in range(pieces):
        size = min(shard, rows_in - j * shard)
        fills.append(
            (
                wc_in.at[pl.ds(j * shard, size), pl.ds(width, width)],
                mid.at[j // 4, j % 4, pl.ds(0, size), :],
            )
        )

    fills += late

    def fill(number):
        return pltpu.make_async_copy(*fills[number], local.at[base + number])

    keeps = [(wq, o_wq), (wout, o_wout), (wg, o_wg), (wc, o_wc)]

    def keep_weights(number):
        return pltpu.make_async_copy(*keeps[number], local.at[base + len(fills) + number])

    for number in range(len(fills)):
        fill(number).start()
    g.greet()
    each(gx.start)
    steps = block_chars // 8
    assert steps & (steps - 1) == 0

    def reorder(s):
        own_c(s).wait()
        row = lax.broadcasted_iota(jnp.int32, (block_chars, block_chars), 0)
        col = lax.broadcasted_iota(jnp.int32, (block_chars, block_chars), 1)
        hit = (col == (row & 7) * steps + (row >> 3)).astype(F32).astype(BF16)
        c[s, me] = nn(hit, c[s, me]).astype(BF16)
        gc.start(s)

    each(reorder)

    taps[...] = jnp.zeros_like(taps)
    norm_grads[...] = jnp.zeros_like(norm_grads)
    gate_bias[...] = jnp.zeros_like(gate_bias)
    gate_bias[:, pl.ds(0, units)] = gate_in[...]
    rest = wq.shape[0] - rows_in
    wq[pl.ds(rows_in, rest), :] = jnp.zeros((rest, width), BF16)
    wc[pl.ds(rows_in, rest), :] = jnp.zeros((rest, wc.shape[1]), BF16)
    more = wout.shape[0] - wout_in.shape[0]
    wout[pl.ds(wout_in.shape[0], more), :] = jnp.zeros((more, width), BF16)
    for j in range(4):
        wg[pl.ds(j * LANE + units, LANE - units), :] = jnp.zeros(
            (LANE - units, wg.shape[1]), BF16
        )
    fill(0).wait()
    fill(1).wait()
    lane = lax.broadcasted_iota(jnp.int32, (shard, LANE), 1)
    left = lane < HD

    def place(char):
        inner = char & (block_chars - 1)
        return char - inner + ((inner & (steps - 1)) << 3) + (inner >> (steps.bit_length() - 1))

    def hits(positions, marks):
        total = jnp.zeros(positions.shape, F32)
        for mark in marks:
            total = total + (positions == mark).astype(F32)
        return total

    def structure(s):
        ends, running = [], 0
        for d in range(docs.shape[1]):
            running = running + docs[s, d]
            ends.append(running)
        along = lax.broadcasted_iota(jnp.int32, (1, length), 1)
        down = lax.broadcasted_iota(jnp.int32, (length, 1), 0)
        seg_row, seg_col = jnp.zeros_like(along), jnp.zeros_like(down)
        for end in ends:
            seg_row = seg_row + (along >= end).astype(jnp.int32)
            seg_col = seg_col + (down >= end).astype(jnp.int32)
        segr[s] = seg_row
        segc[s] = seg_col
        edges[s, :, 0:1] = 1.0 - hits(down, [0] + ends[:-1])
        edges[s, :, 1:2] = 1.0 - hits(down + 1, ends)
        count = counts[pl.ds(s, 1), :].astype(F32)
        many = jnp.broadcast_to(count, (LANE, length)).astype(BF16)
        rows = lax.broadcasted_iota(jnp.int32, (length, length), 0)
        cols = lax.broadcasted_iota(jnp.int32, (length, length), 1)
        ends_row = nn(many[:16], (rows <= cols).astype(F32).astype(BF16))[0:1]
        ends_col = nt((cols <= rows).astype(F32).astype(BF16), many)[:, 0:1]
        starts_col = nt((cols < rows).astype(F32).astype(BF16), many)[:, 0:1]
        pickr[s, 0:1, :] = place(ends_row.astype(jnp.int32) - 1)
        pickr[s, 1:2, :] = place((ends_row - count).astype(jnp.int32))
        pickc[s, :, 0:1] = place(ends_col.astype(jnp.int32) - 1)
        pickc[s, :, 1:2] = place(starts_col.astype(jnp.int32))
        cuts = [
            jnp.sum(jnp.where(along < end, count, 0.0), axis=1, keepdims=True) for end in ends
        ]
        row = lax.broadcasted_iota(jnp.int32, (4 * block_chars, 1), 0)
        inner = row & (block_chars - 1)
        char = (row - inner + (inner & 7) * steps + (inner >> 3)).astype(F32)
        keep[s, :, 0:1] = 1.0 - hits(char, [0.0] + cuts[:-1])
        keep[s, :, 1:2] = 1.0 - hits(char + 1.0, cuts)

    each(structure)
    for number in (3, 4, 5, 6):
        fill(number).wait()

    def attention(s):
        gx.forward(s)
        gx.finish(s)
        own_x(s).wait()
        save(s, x)

        def project(t, carry):
            rows = pl.ds(pl.multiple_of(t * shard, shard), shard)
            first, second, third = unpack3(nt(x[s, t], wq[...]), HD * heads)
            qkv[s, 0, rows, :] = (first * 0.125).astype(BF16)
            qkv[s, 1, rows, :] = second.astype(BF16)
            qkv[s, 2, rows, :] = third.astype(BF16)
            return carry

        lax.fori_loop(0, 4, project, 0)
        save(s, qkv)

        def part(b, out):
            rows = pl.ds(pl.multiple_of(b * shard, shard), shard)
            same = segc[s, rows, :] == segr[s]
            for tile in range(qkv.shape[3] // LANE):
                cols = pl.ds(tile * LANE, LANE)
                result = None
                for half in range(2):
                    head = 2 * tile + half
                    if head >= heads:
                        continue
                    query = qkv[s, 0, rows, cols]
                    if 2 * tile + 1 < heads:
                        query = jnp.where(left if half == 0 else ~left, query, jnp.zeros_like(query))
                    scores = jnp.where(same, nt(query, qkv[s, 1, :, cols]), MASK_VALUE)
                    power = jnp.exp(scores - jnp.max(scores, axis=-1, keepdims=True))
                    probs = (power * (1.0 / jnp.sum(power, axis=-1, keepdims=True))).astype(BF16)
                    p[s, head * 4 + b] = probs
                    mixed = nn(probs, qkv[s, 2, :, cols])
                    result = mixed if result is None else jnp.where(left, result, mixed)
                ctx[s, rows, cols] = result.astype(BF16)
            out[...] = nn(ctx[s, rows, :], wout[...])

        s_attn.start(s, part)
        save(s, p, ctx)

    each(attention)

    def first_norm(s):
        total = x[s, me].astype(F32) + s_attn.finish(s)
        unit, spread = normalize(total)
        unit0[s] = unit
        scale[s, 0] = jnp.broadcast_to(spread, (shard, LANE))
        hidden[s] = unit * gain[0:1] + bias[0:1]
        h[s, me] = hidden[s].astype(BF16)
        gh.start(s)
        save(s, unit0)

    def gru(s):
        gc.forward(s)
        gc.finish(s)
        save(s, c)

        def gates(t, carry):
            rows = pl.ds(pl.multiple_of(t * LANE, LANE), LANE)
            per = block_chars // LANE
            inner = pl.ds(pl.multiple_of((t % per) * LANE, LANE), LANE)
            proj = nt(c[s, t // per, inner, :], wg[...])
            for tile in range(2):
                cols = slice(tile * LANE, (tile + 1) * LANE)
                gate = jax.nn.sigmoid(proj[:, cols] + gate_bias[tile : tile + 1])
                cand = proj[:, (2 + tile) * LANE : (3 + tile) * LANE]
                decays[s, tile, rows, :] = (1.0 - gate) * keep[s, rows, tile : tile + 1]
                drive[tile, rows, :] = gate * cand
            return carry

        total = 4 * block_chars
        lax.fori_loop(0, total // LANE, gates, 0)
        recur((True, False), decays.at[s], drive, states, block_chars)
        save(s, decays)

        for tile in range(2):
            low_states[s, tile] = states[tile].astype(BF16)

        def pick(t, carry):
            rows = pl.ds(pl.multiple_of(t * shard, shard), shard)
            for tile in range(2):
                ids = lax.broadcasted_iota(jnp.int32, (shard, total), 1)
                hot = (ids == pickc[s, rows, tile : tile + 1]).astype(F32).astype(BF16)
                out = nn(hot, low_states[s, tile])
                st[s, me, rows, pl.ds(tile * LANE, LANE)] = out.astype(BF16)
            return carry

        lax.fori_loop(0, 4, pick, 0)
        gs.start(s)
        save(s, low_states)

    def norm_and_gru(s):
        first_norm(s)
        gru(s)

    each(norm_and_gru)

    def ffn(s):
        gh.forward(s)
        gh.finish(s)
        save(s, h)

        def part(b, out):
            value, slope = gelu_pair(nn(h[s, b], win[...]))
            act[s, b] = value.astype(BF16)
            dact[s, b] = slope.astype(BF16)
            out[...] = nn(act[s, b], wdown[...])

        s_ffn.start(s, part)
        save(s, act, dact)

    for t in range(4):
        for d in range(2):
            row = lax.broadcasted_iota(jnp.int32, (LANE, width), 0)
            col = lax.broadcasted_iota(jnp.int32, (LANE, width), 1)
            first = d * 4 * units + t * units
            hit = (col - first == row) & (row < units)
            perm[pl.ds((2 * t + d) * LANE, LANE), :] = hit.astype(F32).astype(BF16)
    for number in range(2, len(fills)):
        if number not in (3, 4, 5, 6):
            fill(number).wait()
    for j in range(pieces):
        size = min(shard, rows_in - j * shard)
        wc[pl.ds(j * shard, size), pl.ds(width, 8 * LANE)] = nt(
            mid[j // 4, j % 4, pl.ds(0, size), :], perm[...]
        ).astype(BF16)
    for number in range(len(keeps)):
        keep_weights(number).start()

    each(ffn)

    def second_norm(s):
        unit, spread = normalize(hidden[s] + s_ffn.finish(s))
        unit1[s] = unit
        scale[s, 1] = jnp.broadcast_to(spread, (shard, LANE))
        middle[s] = unit * gain[1:2] + bias[1:2]
        mid[s, me] = middle[s].astype(BF16)
        gm.start(s)
        save(s, unit1, scale)

    each(second_norm)

    def merge(s):
        gs.forward(s)
        gm.forward(s)
        gs.finish(s)
        gm.finish(s)
        save(s, mid, st)
        def mix(t, carry):
            rows = pl.ds(pl.multiple_of(t * shard, shard), shard)
            total = nt(mid[s, t], wc[:, pl.ds(0, width)])
            for u in range(4):
                weights = wc[:, pl.ds(width + u * 2 * LANE, 2 * LANE)]
                total = total + nt(st[s, u, rows, :], weights)
            taps[pl.ds(pl.multiple_of(8 + t * shard, 8), shard), :] = total
            return carry

        lax.fori_loop(0, 4, mix, 0)

        def shifted(t, carry):
            rows = pl.ds(pl.multiple_of(t * shard, shard), shard)
            window = taps[pl.ds(pl.multiple_of(t * shard, 8), shard + 16), :]
            before = unpack3(window[7 : 7 + shard], channels)[0]
            center = unpack3(window[8 : 8 + shard], channels)[1]
            after = unpack3(window[9 : 9 + shard], channels)[2]
            value, slope = gelu_pair(
                before * edges[s, rows, 0:1] + center + after * edges[s, rows, 1:2]
            )
            mg[s, rows, :] = value.astype(BF16)
            dmg[s, rows, :] = slope.astype(BF16)
            return carry

        lax.fori_loop(0, 4, shifted, 0)

        def part(b, out):
            rows = pl.ds(pl.multiple_of(b * shard, shard), shard)
            out[...] = nn(mg[s, rows, :], wm[...])

        s_branch.start(s, part)
        save(s, mg, dmg)

    each(merge)

    def put_branch(s, first, value):
        span = branch.shape[3]
        at = 0
        while at < width:
            part, inner = divmod(first + at, span)
            size = min(span - inner, width - at)
            branch[s, part, :, pl.ds(inner, size)] = value[:, at : at + size]
            at += size

    def last_norms(s):
        total = s_branch.finish(s)
        rows = pl.ds(pl.multiple_of(me * shard, shard), shard)
        unit, spread = normalize(middle[s] + total[:, :width])
        outs_t[s] = (unit * gain[2:3] + bias[2:3]).astype(BF16)
        cot = cot_t[s]
        norm_grads[0:1] += jnp.sum(cot * unit, axis=0, keepdims=True)
        norm_grads[2:3] += jnp.sum(cot, axis=0, keepdims=True)
        back = normalize_back(unit, spread, cot * gain[2:3])
        res3[s] = back
        put_branch(s, 0, back.astype(BF16))
        mine = total[:, width:]
        for u in range(4):
            mine = mine + nn(st[s, u, rows, :], perm[pl.ds(u * 2 * LANE, 2 * LANE), :])
        unit, spread = normalize(mine)
        outs_c[s] = (unit * gain[3:4] + bias[3:4]).astype(BF16)
        cot = cot_c[s]
        norm_grads[1:2] += jnp.sum(cot * unit, axis=0, keepdims=True)
        norm_grads[3:4] += jnp.sum(cot, axis=0, keepdims=True)
        back = normalize_back(unit, spread, cot * gain[3:4]).astype(BF16)
        put_branch(s, width, back)
        for u in range(4):
            res4[s, u] = nt(back, perm[pl.ds(u * 2 * LANE, 2 * LANE), :]).astype(BF16)
        save(s, outs_t, outs_c, res3, res4, branch)

    each(last_norms)

    def drain(s):
        for number, (source, target) in enumerate(plan):
            local_copy(2 + number, s, source.at[s], target.at[s]).wait()

    each(drain)
    for number in range(len(keeps)):
        keep_weights(number).wait()


def forward_call(tokens, chars, weights, small, group_slots=27):
    seqs, shard, width = tokens.shape
    length, block_chars = shard * 4, chars.shape[1]
    total = block_chars * 4
    wq, wout, win, wdown, wg, gate_bias, wc, wm = weights
    cols = -(-wout.shape[0] // LANE) * LANE
    packed = -(-wq.shape[0] // LANE) * LANE
    heads = small["heads"]
    kept = [
        ((packed, width), BF16), ((cols, width), BF16), ((4 * LANE, chars.shape[2]), BF16),
        ((packed, width + 8 * LANE), BF16),
    ]
    sds = jax.ShapeDtypeStruct
    big = {
        "x": ((seqs, 4, shard, width), BF16),
        "c": ((seqs, 4, block_chars, chars.shape[2]), BF16),
        "qkv": ((seqs, 3, length, cols), BF16),
        "p": ((seqs, heads * 4, shard, length), BF16),
        "ctx": ((seqs, length, cols), BF16),
        "h": ((seqs, 4, shard, width), BF16),
        "act": ((seqs, 4, shard, win.shape[1]), BF16),
        "dact": ((seqs, 4, shard, win.shape[1]), BF16),
        "mid": ((seqs, 4, shard, width), BF16),
        "st": ((seqs, 4, length, 2 * LANE), BF16),
        "mg": ((seqs, length, wm.shape[0]), BF16),
        "dmg": ((seqs, length, wm.shape[0]), BF16),
        "states": ((seqs, 2, total, LANE), BF16),
        "decay": ((seqs, 2, total, LANE), F32),
        "unit0": ((seqs, shard, width), F32),
        "unit1": ((seqs, shard, width), F32),
        "scale": ((seqs, 2, shard, LANE), F32),
        "res3": ((seqs, shard, width), F32),
        "res4": ((seqs, 4, shard, 2 * LANE), BF16),
        "branch": ((seqs, 2 * width // length, shard, length), BF16),
    }
    rows = ((seqs, shard, width), F32)
    low_rows = ((seqs, shard, width), BF16)
    total = block_chars * 4
    scratch = list(big.values()) + kept + [
        rows, rows, low_rows, low_rows,
        ((2, total, LANE), F32),
        ((2, total, LANE), F32),
        ((length + 16, packed), F32),
        ((8 * LANE, width), BF16),
        ((2, LANE), F32),
        (win.shape, BF16), (wdown.shape, BF16), (wm.shape, BF16), rows, rows,
        ((seqs, length, 1), jnp.int32), ((seqs, 1, length), jnp.int32),
        ((seqs, length, 2), jnp.int32), ((seqs, total, 2), F32),
        ((seqs, 3, shard, 2 * width), BF16), ((seqs, 3, shard, 2 * width), BF16),
        ((seqs, shard, 2 * width), F32), ((shard, 2 * width), F32),
    ]
    anyspace = pl.BlockSpec(memory_space=pl.ANY)
    vmem = pl.BlockSpec(memory_space=pltpu.VMEM)
    out_shapes = [sds(low_rows[0], BF16)] * 2 + [sds(*v) for v in list(big.values()) + kept]
    ins = (
        small["docs"], small["counts"], tokens, chars, wq, wout, win, wdown, wg, gate_bias, wc, wm,
        small["gain"], small["bias"], small["cot_t"], small["cot_c"],
    )
    smem = pl.BlockSpec(memory_space=pltpu.SMEM)
    places = [smem, vmem] + [anyspace] * 7 + [vmem] + [anyspace] * 2 + [vmem] * 2 + [anyspace] * 2
    outs = pl.pallas_call(
        functools.partial(forward_kernel, small["units"], small["channels"]),
        out_shape=out_shapes
        + [
            sds((4, width), F32),
            sds((seqs, 2, length), jnp.int32),
            sds((seqs, length, 2), F32),
        ],
        in_specs=places,
        out_specs=[anyspace] * len(out_shapes) + [vmem] * 3,
        scratch_shapes=[pltpu.VMEM(*v) for v in scratch]
        + [
            pltpu.SemaphoreType.DMA((group_slots * seqs,)),
            pltpu.SemaphoreType.DMA((group_slots * seqs,)),
            pltpu.SemaphoreType.DMA((26 * seqs + 24,)),
        ],
        compiler_params=pltpu.CompilerParams(
            collective_id=0, has_side_effects=True, vmem_limit_bytes=62 * MIB
        ),
    )(*ins)
    names = ["token_out", "char_out"] + list(big) + ["wq", "wout", "wg", "wc", "norm_grads"]
    names += ["pickr", "edges"]
    return dict(zip(names, outs))


class Plane:
    def __init__(self, send, recv, marks):
        self.index = lax.axis_index("dp")
        self.x, self.z = self.index % 2, self.index // 2
        self.send, self.recv, self.marks, self.used, self.marked = send, recv, marks, 0, 0

    def mark(self):
        self.marked += 1
        return self.marks.at[self.marked - 1]

    def take(self, count):
        first = self.used
        self.used += count
        return [first + i for i in range(count)]

    def peer(self, way):
        if way == "x":
            return self.index + 1 - 2 * self.x
        return (self.index + (2 if way == "up" else 6)) % 8

    def pair(self, bit):
        digit = self.index // (1 << bit) % 2
        return self.index + (1 - 2 * digit) * (1 << bit)

    def copy(self, slot, source, target, peer):
        return pltpu.make_async_remote_copy(
            src_ref=source,
            dst_ref=target,
            send_sem=self.send.at[slot],
            recv_sem=self.recv.at[slot],
            device_id={"dp": peer},
            device_id_type=pl.DeviceIdType.MESH,
        )


class Reduce:
    steps = 9

    def __init__(self, plane, buf, out, land, first, land_first, rows, x_first):
        self.plane, self.buf, self.out, self.land = plane, buf, out, land
        self.first, self.land_first, self.rows, self.x_first = first, land_first, rows, x_first
        self.slots = plane.take(14)
        self.mark = plane.mark()
        x, z = plane.x, plane.z
        if x_first:
            self.quarter, self.half = rows // 8, rows // 2
            self.z_base, self.x_base = first + x * self.half, first
        else:
            self.quarter, self.half = rows // 4, rows // 8
            self.z_base, self.x_base = first, first + z * self.quarter
        self.x_land = land_first + 5 * self.quarter

    @staticmethod
    def landing_rows(rows, x_first):
        return 5 * rows // 8 + rows // 2 if x_first else 5 * rows // 4 + rows // 8

    def rows_of(self, ref, start, size):
        return ref.at[pl.ds(pl.multiple_of(start, 16), size), :]

    def add(self, start, land_start, size):
        def one(i, carry):
            rows = pl.ds(pl.multiple_of(start + i * 16, 16), 16)
            more = pl.ds(pl.multiple_of(land_start + i * 16, 16), 16)
            total = self.buf[rows, :].astype(F32) + self.land[more, :].astype(F32)
            self.buf[rows, :] = total.astype(BF16)
            return carry

        lax.fori_loop(0, size // 16, one, 0)

    def gather_copy(self, way, step, z):
        piece = 3 - step + z if way == "up" else step - 3 + z
        slot = piece if way == "up" else piece + (4 - piece) * (step // 2)
        return self.plane.copy(
            self.slots[step if way == "up" else 3 + step],
            self.rows_of(self.buf, self.z_base + piece * self.quarter, self.quarter),
            self.rows_of(self.land, self.land_first + slot * self.quarter, self.quarter),
            self.plane.peer(way),
        )

    def gather_send(self, step):
        z = self.plane.z
        pl.when(step >= z)(lambda: self.gather_copy("up", step, z).start())
        pl.when(step >= 3 - z)(lambda: self.gather_copy("down", step, z).start())

    def gather_wait(self, step):
        z = self.plane.z

        @pl.when((z >= 1) & (step >= z - 1))
        def _():
            self.gather_copy("up", step, z - 1).wait_recv()
            piece = 3 - step + z - 1
            self.add(
                self.z_base + piece * self.quarter,
                self.land_first + piece * self.quarter,
                self.quarter,
            )

        @pl.when((z <= 2) & (step >= 2 - z))
        def _():
            self.gather_copy("down", step, z + 1).wait_recv()
            piece = step - 3 + z + 1
            slot = piece if step < 2 else 4
            self.add(
                self.z_base + piece * self.quarter,
                self.land_first + slot * self.quarter,
                self.quarter,
            )

        pl.when(step >= z)(lambda: self.gather_copy("up", step, z).wait_send())
        pl.when(step >= 3 - z)(lambda: self.gather_copy("down", step, z).wait_send())

    def spread_copy(self, way, step, z):
        piece = z - step if way == "up" else z + step
        start = self.z_base + piece * self.quarter
        target = self.rows_of(self.out, start, self.quarter)
        source = target
        if self.x_first and step == 0:
            source = self.rows_of(self.buf, start, self.quarter)
        slot = self.slots[6 + step if way == "up" else 9 + step]
        return self.plane.copy(slot, source, target, self.plane.peer(way))

    def spread_send(self, step):
        z = self.plane.z
        pl.when((z <= 2) & (step <= z))(lambda: self.spread_copy("up", step, z).start())
        pl.when((z >= 1) & (step <= 3 - z))(lambda: self.spread_copy("down", step, z).start())

    def spread_wait(self, step):
        z = self.plane.z
        pl.when((z >= 1) & (step <= z - 1))(lambda: self.spread_copy("up", step, z - 1).wait_recv())
        pl.when((z <= 2) & (step <= 2 - z))(lambda: self.spread_copy("down", step, z + 1).wait_recv())
        pl.when((z <= 2) & (step <= z))(lambda: self.spread_copy("up", step, z).wait_send())
        pl.when((z >= 1) & (step <= 3 - z))(lambda: self.spread_copy("down", step, z).wait_send())

    def halve(self):
        other = self.x_base + (1 - self.plane.x) * self.half
        return self.plane.copy(
            self.slots[12],
            self.rows_of(self.buf, other, self.half),
            self.rows_of(self.land, self.x_land, self.half),
            self.plane.peer("x"),
        )

    def halve_wait(self):
        self.halve().wait()
        self.add(self.x_base + self.plane.x * self.half, self.x_land, self.half)

    def double(self):
        start = self.x_base + self.plane.x * self.half
        target = self.rows_of(self.out, start, self.half)
        source = target if self.x_first else self.rows_of(self.buf, start, self.half)
        return self.plane.copy(self.slots[13], source, target, self.plane.peer("x"))

    def keep(self):
        if self.x_first:
            start, size = self.z_base + self.plane.z * self.quarter, self.quarter
        else:
            start, size = self.x_base + self.plane.x * self.half, self.half
        return pltpu.make_async_copy(
            self.rows_of(self.buf, start, size), self.rows_of(self.out, start, size), self.mark
        )

    def step(self, number):
        if self.x_first:
            if number == 0:
                self.halve().start()
            elif number == 1:
                self.halve_wait()
                self.gather_send(0)
            elif number <= 3:
                self.gather_wait(number - 2)
                self.gather_send(number - 1)
            elif number == 4:
                self.gather_wait(2)
                self.keep().start()
                self.spread_send(0)
            elif number <= 6:
                self.spread_wait(number - 5)
                self.spread_send(number - 4)
            elif number == 7:
                self.spread_wait(2)
                self.keep().wait()
                self.double().start()
            else:
                self.double().wait()
        else:
            if number == 0:
                self.gather_send(0)
            elif number <= 2:
                self.gather_wait(number - 1)
                self.gather_send(number)
            elif number == 3:
                self.gather_wait(2)
                self.halve().start()
            elif number == 4:
                self.halve_wait()
                self.keep().start()
                self.double().start()
            elif number == 5:
                self.double().wait()
                self.keep().wait()
                self.spread_send(0)
            elif number <= 7:
                self.spread_wait(number - 6)
                self.spread_send(number - 5)
            else:
                self.spread_wait(2)


SAVED = (
    "branch", "mg", "dmg", "mid", "st", "res3", "res4", "unit0", "unit1", "scale", "act", "dact",
    "h", "p", "qkv", "ctx", "x", "c", "states", "decay",
)
GRADS = ("merge", "conv", "down", "win", "gru", "out", "qkv")
PIECES = (
    (0, 384, True),
    (1, 640, True),
    (1, 384, False),
    (1, 128, True),
    (2, 256, True),
    (2, 512, True),
    (3, 384, True),
    (3, 384, True),
    (4, 384, True),
    (5, 384, True),
    (6, 256, True),
    (6, 896, False),
)
SCHEDULE = (
    (),
    (0, 10, 20, 30,),
    (),
    (21,),
    (1,),
    (),
    (40, 50, 22,),
    (60, 70, 2,),
    (11,),
    (23, 31,),
    (3,),
    (12, 41, 32, 4,),
    (),
    (13, 42, 51, 33,),
    (5,),
    (14, 43, 61,),
    (6, 52, 34,),
    (15, 44, 71, 7, 62, 24,),
    (53, 35,),
    (90, 100, 110, 16, 72, 45, 63,),
    (54, 8, 36, 25,),
    (17, 111, 46, 91, 73,),
    (64, 101, 37, 55, 26, 47,),
    (112,),
    (92, 18, 74, 56,),
    (80, 38, 65, 102, 27, 48, 113, 93,),
    (75, 57, 81,),
    (66, 103, 114, 82, 28, 94,),
    (76, 83, 67, 104, 95, 77,),
    (58, 84, 105, 96, 115, 85, 106, 97, 68, 116, 86, 107, 78, 117, 87, 98, 108, 118, 88,),
)


def backward_kernel(units, channels, dp_size, *refs):
    refs = list(refs)
    take = lambda count: [refs.pop(0) for _ in range(count)]
    hbm = SimpleNamespace(**dict(zip(SAVED, take(len(SAVED)))))
    weights_in = take(7)
    gate_in, gain, pickr, edges, norm_in = take(5)
    grad_tokens, grad_chars = take(2)
    grads_out = dict(zip(GRADS, take(len(GRADS))))
    (small_out,) = take(1)
    names = [n for n in SAVED if n not in ("branch", "states", "decay", "p", "x")]
    v = SimpleNamespace(**dict(zip(names, take(len(names)))))
    weights = take(7)
    wq, wout, win, wdown, wg, wc, wm = weights
    (pb, states, decay, drive, dpre, dyk, fg, gtok, dproj, gru_acc, res2, res1, ds, parts,
     stage, got, held, temp, cstage, cgot, cheld, ctemp) = take(22)
    land = dict(zip(GRADS, take(len(GRADS))))
    big = SimpleNamespace(**dict(zip(GRADS, take(len(GRADS)))))
    small, small_land, gate_bias, send, recv, dsend, drecv, local, marks, credit = take(10)

    seqs, shard, width = grad_tokens.shape
    length = 4 * shard
    block_chars = grad_chars.shape[1]
    total = 4 * block_chars
    heads = pb.shape[1] // 4
    cols = v.ctx.shape[2]
    g = Group(send, recv, seqs)
    me = g.me
    inside = dp_size == 8
    plane = Plane(dsend, drecv, marks)

    def each(body):
        def run(seq, carry):
            body(seq)
            return carry

        lax.fori_loop(0, seqs, run, 0)

    def load(name):
        index = names.index(name)
        return pltpu.make_async_copy(getattr(hbm, name), getattr(v, name), local.at[index])

    spare = len(names)
    p_copy = lambda: pltpu.make_async_copy(hbm.p, pb, local.at[spare])
    x_copy = lambda: pltpu.make_async_copy(hbm.x, v.h, local.at[39])

    def states_copy(s):
        return pltpu.make_async_copy(hbm.states.at[s], states, local.at[spare + 1])

    def decay_copy(s, tile):
        return pltpu.make_async_copy(
            hbm.decay.at[s, tile], decay.at[tile], local.at[spare + 2 + tile]
        )

    def out_copy(kind, s):
        source, target = ((res1, grad_tokens), (cheld, grad_chars))[kind]
        return pltpu.make_async_copy(
            source.at[s], target.at[s], local.at[spare + 4 + kind * seqs + s]
        )

    pieces = 2 * width // length
    gb = Gather(
        g, pb, hbm.branch, place=lambda s, t: pb.at[s, pl.ds(t * pieces, pieces)]
    )
    gf, ga = Gather(g, fg), Gather(g, v.mid)
    pick = lambda ref: (lambda s, i: ref.at[s, i])
    own = lambda ref: (lambda s: ref.at[s])
    s_mid = Scatter(g, pick(stage), pick(got), own(held), temp)
    s_hid = Scatter(g, pick(stage), pick(got), own(held), temp)
    s_tok = Scatter(g, pick(stage), pick(got), own(held), temp)
    s_chr = Scatter(g, pick(cstage), pick(cgot), own(cheld), ctemp)
    s_cout = Scatter(g, pick(cstage), pick(cgot), own(cheld), ctemp)

    def own_branch(s):
        return pltpu.make_async_copy(
            hbm.branch.at[s], gb.at(s, me), local.at[spare + 4 + 2 * seqs + s]
        )

    def weight(number):
        return pltpu.make_async_copy(weights_in[number], weights[number], local.at[40 + number])

    each(lambda s: own_branch(s).start())
    weight(6).start()
    for name in ("dmg", "res4", "mg", "mid", "st"):
        load(name).start()
    for number in (5, 3, 2, 1, 0, 4):
        weight(number).start()
    states_copy(0).start()
    for tile in range(2):
        decay_copy(0, tile).start()
    for name in names:
        if name not in ("dmg", "res4", "mg", "mid", "st"):
            load(name).start()

    barrier = pltpu.get_barrier_semaphore()
    places = [{"tensor": g.pair}, {"tensor": g.far}]
    if inside:
        places += [{"dp": plane.peer(way)} for way in ("x", "up", "down")]
        places += [{"dp": plane.pair(2)}]
    for place in places:
        pl.semaphore_signal(barrier, inc=1, device_id=place, device_id_type=pl.DeviceIdType.MESH)
    pl.semaphore_wait(barrier, len(places))
    each(gb.start)
    dpre[...] = jnp.zeros_like(dpre)
    gate_bias[...] = jnp.zeros_like(gate_bias)
    gate_bias[:, pl.ds(0, units)] = gate_in[...]
    side = 2 * LANE
    for t in range(4):
        for j in range(width // side):
            row = lax.broadcasted_iota(jnp.int32, (side, side), 0)
            col = lax.broadcasted_iota(jnp.int32, (side, side), 1) + j * side
            unit = row % LANE
            hit = (col == row // LANE * 4 * units + t * units + unit) & (unit < units)
            cstage[t // 2, j, pl.ds(t % 2 * side, side), :] = hit.astype(F32).astype(BF16)
    small[...] = jnp.zeros_like(small)
    small[0, pl.ds(0, 4), :] = norm_in[...]
    lane = lax.broadcasted_iota(jnp.int32, (shard, LANE), 1)
    left = lane < HD
    for name in ("dmg", "res4"):
        load(name).wait()
    weight(6).wait()
    weight(5).wait()

    def block_rows(t, size):
        return pl.ds(pl.multiple_of(t * size, size), size)

    def merge_back(s):
        gb.forward(s)
        gb.finish(s)
        own_branch(s).wait()

        def inner(t, carry):
            rows = block_rows(t, shard)
            back = None
            for j in range(pieces):
                piece = nt(pb[s, t * pieces + j], wm[:, j * length : (j + 1) * length])
                back = piece if back is None else back + piece
            dpre[pl.ds(pl.multiple_of(8 + t * shard, 8), shard), :] = (
                (back * v.dmg[s, rows, :].astype(F32)).astype(BF16).astype(F32)
            )
            return carry

        lax.fori_loop(0, 4, inner, 0)

        def taps(t, carry):
            rows = block_rows(t, shard)
            window = dpre[pl.ds(pl.multiple_of(t * shard, 8), shard + 16), :]
            marks = edges[s, rows, :]
            before = window[9 : 9 + shard] * marks[:, 1:2]
            after = window[7 : 7 + shard] * marks[:, 0:1]
            dyk[s, rows, :] = pack3(
                [before, window[8 : 8 + shard], after], channels
            ).astype(BF16)
            return carry

        lax.fori_loop(0, 4, taps, 0)

        def mid_part(b, out):
            out[...] = nn(dyk[s, block_rows(b, shard), :], wc[:, pl.ds(0, width)])

        s_mid.start(s, mid_part)

    each(merge_back)
    sums, marks_at = [], {}
    for which, height, x_first in PIECES if inside else ():
        name = GRADS[which]
        first, at = marks_at.get(name, (0, 0))
        sums.append(
            Reduce(
                plane, getattr(big, name), grads_out[name], land[name], first, at, height, x_first
            )
        )
        marks_at[name] = (first + height, at + Reduce.landing_rows(height, x_first))
    fired = [0] * len(sums)

    def fire(hook):
        for entry in SCHEDULE[hook] if inside else ():
            which, number = divmod(entry, 10)
            fired[which] += 1
            sums[which].step(number)

    def fire_in(seq, hook, stride):
        for k in range(2):
            pl.when(seq == k)(functools.partial(fire, hook + k * stride))

    tokens = seqs * length
    step_w = 2 * LANE

    def merge_weights():
        for name in ("mg", "mid", "st"):
            load(name).wait()

        half_w = width
        for j in range(pieces):
            right = jnp.concatenate(
                [pb[s, t * pieces + j] for s in range(seqs) for t in range(4)], axis=0
            )
            out = tn(v.mg[...].reshape(tokens, -1), right)[:channels].astype(BF16)
            at = 0
            while at < length:
                part, inside_at = divmod(j * length + at, half_w)
                size = min(length - at, half_w - inside_at)
                big.merge[pl.ds(part * channels, channels), pl.ds(inside_at, size)] = out[
                    :, at : at + size
                ]
                at += size
        taps = 3 * channels

        def conv_rows(j, carry):
            lanes = pl.ds(pl.multiple_of(j * LANE, LANE), LANE)
            left_rows = dyk[:, :, lanes].reshape(tokens, LANE)
            size = min(LANE, taps - LANE * j) if isinstance(j, int) else LANE
            first = j * LANE if isinstance(j, int) else pl.multiple_of(j * LANE, LANE)
            out = tn(left_rows, v.mid[...].reshape(tokens, width))
            big.conv[pl.ds(first, size), :] = out[:size].astype(BF16)
            padded = [
                tn(left_rows, v.st[:, t].reshape(tokens, side)).astype(BF16) for t in range(4)
            ]
            first = taps + j * LANE if isinstance(j, int) else pl.multiple_of(taps + j * LANE, 64)
            for k in range(width // side):
                out = None
                for t in range(4):
                    piece = nn(padded[t], cstage[t // 2, k, pl.ds(t % 2 * side, side), :])
                    out = piece if out is None else out + piece
                big.conv[pl.ds(first, size), pl.ds(k * side, side)] = out[:size].astype(BF16)
            return carry

        lax.fori_loop(0, taps // LANE, conv_rows, 0)
        if taps % LANE:
            conv_rows(taps // LANE, 0)
        p_copy().start()
        fire(1)

    def second_back(s):
        incoming = v.res3[s] + s_mid.finish(s)
        unit = v.unit1[s]
        small[0, 5:6] += jnp.sum(incoming * unit, axis=0, keepdims=True)
        small[0, 7:8] += jnp.sum(incoming, axis=0, keepdims=True)
        spread = v.scale[s, 1][:, 0:1]
        res2[s] = normalize_back(unit, spread, incoming * gain[1:2])
        fg[s, me] = res2[s].astype(BF16)
        gf.start(s)
        fire_in(s, 0, 2)
        pl.when(s == 0)(merge_weights)

    for name in ("res3", "unit1", "scale"):
        load(name).wait()
    each(second_back)
    for name in ("dact", "act", "h"):
        load(name).wait()
    weight(3).wait()
    weight(2).wait()

    def ffn_back(s):
        gf.forward(s)
        gf.finish(s)

        def part(b, out):
            back = nt(fg[s, b], wdown[...]) * v.dact[s, b].astype(F32)
            v.dact[s, b] = back.astype(BF16)
            out[...] = nt(v.dact[s, b], win[...])

        s_hid.start(s, part)
        fire_in(s, 3, 1)

    each(ffn_back)

    def all_ffn_weights():
        def ffn_weights(j, carry):
            colsj = pl.ds(pl.multiple_of(j * step_w, step_w), step_w)
            out = tn(v.act[:, :, :, colsj].reshape(tokens, step_w), fg[...].reshape(tokens, width))
            big.down[block_rows(j, step_w), :] = out.astype(BF16)
            return carry

        lax.fori_loop(0, big.down.shape[0] // step_w, ffn_weights, 0)
        fire(6)

        def in_weights(j, carry):
            colsj = pl.ds(pl.multiple_of(j * step_w, step_w), step_w)
            out = tn(
                v.h[:, :, :, colsj].reshape(tokens, step_w), v.dact[...].reshape(tokens, -1)
            )
            big.win[block_rows(j, step_w), :] = out.astype(BF16)
            return carry

        lax.fori_loop(0, width // step_w, in_weights, 0)
        x_copy().start()
        fire(7)

    load("unit0").wait()

    def first_back(s):
        incoming = res2[s] + s_hid.finish(s)
        unit = v.unit0[s]
        small[0, 4:5] += jnp.sum(incoming * unit, axis=0, keepdims=True)
        small[0, 6:7] += jnp.sum(incoming, axis=0, keepdims=True)
        spread = v.scale[s, 0][:, 0:1]
        res1[s] = normalize_back(unit, spread, incoming * gain[0:1])
        v.mid[s, me] = res1[s].astype(BF16)
        ga.start(s)
        fire_in(s, 5, 3)
        pl.when(s == 0)(all_ffn_weights)

    each(first_back)

    def chars_back(s):
        def char_part(b, out):
            first = pl.multiple_of(width + b * 2 * LANE, 2 * LANE)
            out[...] = nn(dyk[s], wc[:, pl.ds(first, 2 * LANE)])
            out[block_rows(me, shard), :] += v.res4[s, b].astype(F32)

        s_chr.start(s, char_part)
        fire_in(s, 9, 1)

    each(chars_back)
    hops = [("t", g.pair), ("t", g.far)] + ([("d", k) for k in range(3)] if inside else [])
    slots_t, slots_d = g.slots(2), plane.take(3)

    def small_copy(number):
        kind, where = hops[number]
        source, target = small.at[number], small_land.at[number]
        if kind == "t":
            return g.copy(slots_t[number], 0, source, target, where)
        return plane.copy(slots_d[where], source, target, plane.pair(where))

    def small_step(number):
        if number > 0:
            small_copy(number - 1).wait()
            value, more = small[number - 1], small_land[number - 1]
            small[number, pl.ds(0, 8), :] = value[:8] + more[:8]
            rest = small[6, pl.ds(0, 8), :] if number <= 2 else value[8:] + more[8:]
            small[number, pl.ds(8, 8), :] = rest
        if number < len(hops):
            small_copy(number).start()

    if not inside:
        hops = []
    small_step(0) if hops else None
    for name in ("qkv", "ctx"):
        load(name).wait()
    weight(1).wait()
    weight(0).wait()
    p_copy().wait()

    def attention_back(s):
        ga.forward(s)
        ga.finish(s)
        dctx = v.dmg

        def context(t, carry):
            dctx[s, block_rows(t, shard), :] = nt(v.mid[s, t], wout[...]).astype(BF16)
            return carry

        lax.fori_loop(0, 4, context, 0)
        for tile in range(cols // LANE):
            lanes = pl.ds(tile * LANE, LANE)
            for half in range(2):
                head = 2 * tile + half
                if head >= heads:
                    continue
                paired = 2 * tile + 1 < heads

                def rows_of(b, carry):
                    rows = block_rows(b, shard)
                    grad = dctx[s, rows, lanes]
                    if paired:
                        grad = jnp.where(left if half == 0 else ~left, grad, jnp.zeros_like(grad))
                    back = nt(grad, v.qkv[s, 2, :, lanes])
                    probs = pb[s, head * 4 + b].astype(F32)
                    row_dot = jnp.sum(probs * back, axis=-1, keepdims=True)
                    ds[b] = (probs * (back - row_dot)).astype(BF16)
                    out = nn(ds[b], v.qkv[s, 1, :, lanes])
                    if half == 1:
                        out = jnp.where(left, ctemp[rows, lanes], out)
                    ctemp[rows, lanes] = out
                    return carry

                lax.fori_loop(0, 4, rows_of, 0)
                keys = tn(ds[...].reshape(length, length), v.qkv[s, 0, :, lanes])
                values = tn(
                    pb[s, pl.ds(head * 4, 4)].reshape(length, length), dctx[s, :, lanes]
                )
                if half == 1:
                    wide_left = lax.broadcasted_iota(jnp.int32, (length, LANE), 1) < HD
                    keys = jnp.where(wide_left, parts[0, :, lanes], keys)
                    values = jnp.where(wide_left, parts[1, :, lanes], values)
                parts[0, :, lanes] = keys
                parts[1, :, lanes] = values
                fire_in(s, 11 + head, 4)

        def pack(t, carry):
            rows = block_rows(t, shard)
            query = ctemp[rows, :].astype(BF16).astype(F32) * 0.125
            dyk[s, rows, :] = pack3(
                [query, parts[0, rows, :], parts[1, rows, :]], HD * heads
            ).astype(BF16)
            return carry

        lax.fori_loop(0, 4, pack, 0)

        def part(b, out):
            out[...] = nn(dyk[s, block_rows(b, shard), :], wq[...])

        s_tok.start(s, part)

        fire_in(s, 14, 4)

    each(attention_back)
    small_step(1) if hops else None

    x_copy().wait()

    tall = 3 * HD * heads
    half_w = width // 2

    def qkv_weights(j, carry):
        lanes = pl.ds(pl.multiple_of(j * LANE, LANE), LANE)
        size = min(LANE, tall - LANE * j) if isinstance(j, int) else LANE
        out = tn(dyk[:, :, lanes].reshape(tokens, LANE), v.h[...].reshape(tokens, width))
        for k in range(2):
            first = k * tall + j * LANE
            first = first if isinstance(j, int) else pl.multiple_of(first, 64)
            big.qkv[pl.ds(first, size), :] = out[:size, k * half_w : (k + 1) * half_w].astype(BF16)
        return carry

    lax.fori_loop(0, tall // LANE, qkv_weights, 0)
    if tall % LANE:
        qkv_weights(tall // LANE, 0)
    out = tn(v.ctx[...].reshape(tokens, -1), v.mid[...].reshape(tokens, width))
    for k in range(2):
        big.out[pl.ds(k * HD * heads, HD * heads), :] = out[
            : HD * heads, k * half_w : (k + 1) * half_w
        ].astype(BF16)
    fire(19)

    load("c").wait()
    weight(4).wait()

    def gru_back(s):
        gtok[...] = s_chr.finish(s).astype(BF16)
        for peer in (g.pair, g.far):
            pl.semaphore_signal(
                credit.at[s], inc=1, device_id={"tensor": peer},
                device_id_type=pl.DeviceIdType.MESH,
            )
        def spread_out(t, carry):
            rows = block_rows(t, LANE)
            for tile in range(2):
                ids = lax.broadcasted_iota(jnp.int32, (LANE, length), 0) + t * LANE
                hot = (ids == pickr[s, tile : tile + 1, :]).astype(F32).astype(BF16)
                drive[tile, rows, :] = nn(hot, gtok[:, pl.ds(tile * LANE, LANE)])
            return carry

        lax.fori_loop(0, total // LANE, spread_out, 0)
        fire_in(s, 20, 3)
        for tile in range(2):
            decay_copy(s, tile).wait()
        recur((False, True), decay, drive, drive, block_chars, back=True)
        fire_in(s, 21, 3)
        states_copy(s).wait()

        @pl.when(s == 0)
        def _():
            gru_acc[...] = jnp.zeros_like(gru_acc)

        def part(b, out):
            def finish(t, sums):
                inner = block_rows(t, LANE)
                rows = pl.ds(pl.multiple_of(b * block_chars + t * LANE, LANE), LANE)
                proj = nt(v.c[s, b, inner, :], wg[...])
                new = []
                for tile in range(2):
                    colst = slice(tile * LANE, (tile + 1) * LANE)
                    gate = jax.nn.sigmoid(proj[:, colst] + gate_bias[tile : tile + 1])
                    cand = proj[:, (2 + tile) * LANE : (3 + tile) * LANE]
                    flow = drive[tile, rows, :] * gate
                    logit = flow * (cand - states[tile, rows, :].astype(F32))
                    dproj[inner, pl.ds(tile * LANE, LANE)] = logit.astype(BF16)
                    dproj[inner, pl.ds((2 + tile) * LANE, LANE)] = flow.astype(BF16)
                    new.append(sums[tile] + jnp.sum(logit, axis=0, keepdims=True))
                return tuple(new)

            zero = jnp.zeros((1, LANE), F32)
            sums = lax.fori_loop(0, block_chars // LANE, finish, (zero, zero))
            for tile in range(2):
                small[6, 0:1, pl.ds(tile * LANE, LANE)] += sums[tile]
            out[...] = nn(dproj[...], wg[...])
            gru_acc[...] += tn(dproj[...], v.c[s, b])

        pl.semaphore_wait(credit.at[s], 2)
        s_cout.start(s, part)

        @pl.when(s + 1 < seqs)
        def _():
            states_copy(s + 1).start()
            for tile in range(2):
                decay_copy(s + 1, tile).start()

        if seqs > 1:
            pl.when(s == 0)(functools.partial(fire, 22))

    each(gru_back)
    for d in range(2):
        for k in range(2):
            big.gru[pl.ds((2 * d + k) * units, units), :] = gru_acc[
                pl.ds((2 * k + d) * LANE, units), :
            ].astype(BF16)
    small_step(2) if hops else None
    fire(25)

    def last(s):
        res1[s] = res1[s] + s_tok.finish(s)
        out_copy(0, s).start()
        cheld[s] = s_cout.finish(s)
        out_copy(1, s).start()

    each(last)

    def emit(name):
        return pltpu.make_async_copy(
            getattr(big, name), grads_out[name], local.at[spare + 4 + 3 * seqs + GRADS.index(name)]
        )

    if inside:
        fire(26)
        small_step(3)
        fire(27)
        small_step(4)
        fire(28)
        small_step(5)
        fire(29)
        assert all(count == Reduce.steps for count in fired)
    else:
        for name in GRADS:
            emit(name).start()
        for name in GRADS:
            emit(name).wait()
    small_out[...] = small[len(hops)]
    if not inside:
        small_out[pl.ds(8, 8), :] = small[6, pl.ds(0, 8), :]
    each(lambda s: (out_copy(0, s).wait(), out_copy(1, s).wait()))


def backward_call(saved, weights, small, dp_size):
    wq, wout, win, wdown, wg, wc, wm, gate_bias = weights
    sds = jax.ShapeDtypeStruct
    seqs, shard, width = saved["res3"].shape
    length = shard * 4
    block_chars, char_width = saved["c"].shape[2:]
    total = 4 * block_chars
    cols, packed = wout.shape[0], wc.shape[0]
    tall = 3 * HD * small["heads"]
    channels = small["channels"]
    saved_in = [saved[n] for n in SAVED]
    names = [n for n in SAVED if n not in ("branch", "states", "decay", "p", "x")]
    shapes = [(saved[n].shape, saved[n].dtype) for n in names]
    grads = {
        "merge": (2 * channels, width), "conv": (2 * 3 * channels, width),
        "down": (win.shape[1], width), "win": (width, win.shape[1]),
        "gru": (4 * small["units"], char_width), "out": (2 * tall // 3, width // 2),
        "qkv": (2 * tall, width // 2),
    }
    pad = (seqs, 3, shard, width)
    cpad = (seqs, 3, length, 2 * LANE)
    scratch = shapes + [(w.shape, BF16) for w in weights[:7]] + [
        (saved["p"].shape, BF16),
        ((2, total, LANE), BF16),
        ((2, total, LANE), F32),
        ((2, total, LANE), F32),
        ((length + 16, wm.shape[0]), F32),
        ((seqs, length, packed), BF16),
        ((seqs, 4, shard, width), BF16),
        ((length, 2 * LANE), BF16),
        ((block_chars, 4 * LANE), BF16),
        ((4 * LANE, char_width), F32),
        ((seqs, shard, width), F32),
        ((seqs, shard, width), F32),
        ((4, shard, length), BF16),
        ((2, length, cols), F32),
        (pad, BF16), (pad, BF16), ((seqs, shard, width), F32), ((shard, width), F32),
        (cpad, BF16), (cpad, BF16), ((seqs, length, 2 * LANE), F32), ((length, 2 * LANE), F32),
    ]
    for which, name in enumerate(GRADS):
        landing = sum(Reduce.landing_rows(n, way) for k, n, way in PIECES if k == which)
        scratch.append(((landing if dp_size == 8 else 16, grads[name][1]), BF16))
    scratch += [(shape, BF16) for shape in grads.values()]
    scratch += [((7, 16, width), F32), ((5, 16, width), F32), ((2, LANE), F32)]
    anyspace = pl.BlockSpec(memory_space=pl.ANY)
    vmem = pl.BlockSpec(memory_space=pltpu.VMEM)
    ins = saved_in + list(weights) + [small["gain"]]
    ins += [saved["pickr"], saved["edges"], saved["norm_grads"]]
    outs = pl.pallas_call(
        functools.partial(backward_kernel, small["units"], channels, dp_size),
        out_shape=[sds((seqs, shard, width), F32), sds((seqs, block_chars, char_width), F32)]
        + [sds(shape, BF16) for shape in grads.values()]
        + [sds((16, width), F32)],
        in_specs=[anyspace] * (len(saved_in) + 7) + [vmem] * 5,
        out_specs=[anyspace] * (2 + len(grads)) + [vmem],
        scratch_shapes=[pltpu.VMEM(*one) for one in scratch]
        + [
            pltpu.SemaphoreType.DMA((32 * seqs,)),
            pltpu.SemaphoreType.DMA((32 * seqs,)),
            pltpu.SemaphoreType.DMA((14 * len(PIECES) + 4,)),
            pltpu.SemaphoreType.DMA((14 * len(PIECES) + 4,)),
            pltpu.SemaphoreType.DMA((48,)),
            pltpu.SemaphoreType.DMA((len(PIECES),)),
            pltpu.SemaphoreType.REGULAR((seqs,)),
        ],
        compiler_params=pltpu.CompilerParams(
            collective_id=1, has_side_effects=True, vmem_limit_bytes=63 * MIB
        ),
    )(*ins)
    names = ["grad_tokens", "grad_chars"] + list(grads) + ["small"]
    return dict(zip(names, outs))


def finish_kernel(
    units, conv, qkv, out, merge, down, win, gru, chars, tokens, first, second, rows,
    o_conv, o_qkv, o_out, o_merge, o_down, o_win, o_gru, o_chars, o_tokens, o_first, o_second,
    o_gain, o_bias, o_gate,
):
    for source, target in ((conv, o_conv), (qkv, o_qkv), (out, o_out)):
        half = source.shape[2]
        for k in range(2):
            target[:, k * half : (k + 1) * half] = source[k].astype(F32)
    for k in range(2):
        o_merge[:, k, :] = merge[k].astype(F32)
        o_gate[k : k + 1, :] = rows[8:9, k * LANE : k * LANE + units]
    for target, at in ((o_gain, 0), (o_bias, 2)):
        target[0:2] = rows[4 + at : 6 + at]
        target[2:4] = rows[at : at + 2]
    for source, target in ((down, o_down), (win, o_win), (gru, o_gru)):
        target[...] = source[...].astype(F32)
    for j in range(8):
        o_chars[0, j] = chars[0, :, j, :]
    for source, target in ((tokens, o_tokens), (first, o_first), (second, o_second)):
        target[...] = source[...]


def finish_call(grads, grad_chars, grad_tokens, token_out, char_out, rows, units):
    seqs, block_chars, char_width = grad_chars.shape
    steps = block_chars // 8
    turns = 2 * seqs
    chars = grad_chars.reshape(seqs, steps, 8, char_width)
    pairs = [
        grads[n].reshape(2, -1, grads[n].shape[1]) for n in ("conv", "qkv", "out", "merge")
    ]
    plain = [grads["down"], grads["win"], grads["gru"]]
    copied = [grad_tokens, token_out, char_out]
    flat = [(a.shape[1], 2 * a.shape[2]) for a in pairs[:3]]
    channels, width = pairs[3].shape[1:]
    merged = (channels, 2, width)
    plain_shapes = [a.shape for a in plain]
    ends = [(4, width), (4, width), (2, units)]

    def rows_spec(shape):
        return pl.BlockSpec((shape[0] // turns, shape[1]), lambda i: (i, 0))

    def pair_spec(shape):
        return pl.BlockSpec((2, shape[1] // turns, shape[2]), lambda i: (0, i, 0))

    def halves(shape):
        return pl.BlockSpec((1, shape[1] // 2, shape[2]), lambda i: (i // 2, i % 2, 0))

    return pl.pallas_call(
        functools.partial(finish_kernel, units),
        grid=(turns,),
        out_shape=[jax.ShapeDtypeStruct(shape, F32) for shape in flat + [merged] + plain_shapes]
        + [jax.ShapeDtypeStruct((seqs, 8, steps, char_width), F32)]
        + [jax.ShapeDtypeStruct(a.shape, a.dtype) for a in copied]
        + [jax.ShapeDtypeStruct(shape, F32) for shape in ends],
        in_specs=[pair_spec(a.shape) for a in pairs]
        + [rows_spec(a.shape) for a in plain]
        + [pl.BlockSpec((1, steps // 2, 8, char_width), lambda i: (i // 2, i % 2, 0, 0))]
        + [halves(a.shape) for a in copied]
        + [pl.BlockSpec(rows.shape, lambda i: (0, 0))],
        out_specs=[rows_spec(shape) for shape in flat]
        + [pl.BlockSpec((channels // turns, 2, width), lambda i: (i, 0, 0))]
        + [rows_spec(shape) for shape in plain_shapes]
        + [pl.BlockSpec((1, 8, steps // 2, char_width), lambda i: (i // 2, 0, i % 2, 0))]
        + [halves(a.shape) for a in copied]
        + [pl.BlockSpec(shape, lambda i: (0, 0)) for shape in ends],
        compiler_params=pltpu.CompilerParams(vmem_limit_bytes=62 * MIB),
    )(*pairs, *plain, chars, *copied, rows)


def local(
    tokens,
    characters,
    doc_lengths,
    token_chars,
    w_qkv,
    w_out,
    w_in,
    w_down,
    w_gru,
    gate_bias,
    w_conv,
    w_merge,
    norm_gain,
    norm_bias,
    token_cot,
    char_cot,
):
    micro_count = tokens.shape[0]
    shard_len = tokens.shape[1]
    model_width = tokens.shape[2]
    char_width = characters.shape[2]
    group_size = lax.axis_size("tensor")
    group_rank = lax.axis_index("tensor")
    length = shard_len * group_size
    char_total = characters.shape[1] * group_size
    head_cols = w_qkv.shape[2]
    heads_here = head_cols // HD
    units_here = w_gru.shape[3]
    merge_here = w_conv.shape[2]
    wq = jnp.transpose(w_qkv, (1, 2, 0)).reshape(3 * head_cols, model_width)
    wc = jnp.transpose(w_conv, (0, 2, 1)).reshape(3 * merge_here, 2 * model_width)
    wg = jnp.transpose(w_gru, (1, 2, 3, 0))
    more = -merge_here % LANE
    wm = jnp.pad(w_merge.reshape(merge_here, 2 * model_width), ((0, more), (0, 0)))
    small = dict(
        gain=norm_gain, bias=norm_bias, cot_t=token_cot, cot_c=char_cot, docs=doc_lengths,
        counts=token_chars, heads=heads_here, units=units_here, channels=merge_here,
    )
    weights = (wq, w_out, w_in, w_down, wg, gate_bias, wc, wm)
    fw = forward_call(tokens, characters, weights, small)
    weights = (fw["wq"], fw["wout"], w_in, w_down, fw["wg"], fw["wc"], wm, gate_bias)
    dp_size = lax.axis_size("dp")
    bw = backward_call(fw, weights, small, dp_size)
    rows = bw["small"]
    grads = {name: bw[name] for name in GRADS}
    if dp_size != 8:
        grads, gate_rows = lax.psum((grads, rows[8:]), "dp")
        rows = jnp.concatenate([lax.psum(rows[:8], ("dp", "tensor")), gate_rows], axis=0)
    (conv, qkv, out, merge, down, win, gru, chars, tokens_grad, first, second, gain_grad, bias_grad,
     gate_grad) = finish_call(
        grads, bw["grad_chars"], bw["grad_tokens"], fw["token_out"], fw["char_out"], rows,
        units_here,
    )
    conv = conv.reshape(3, merge_here, 2 * model_width)
    qkv = qkv.reshape(3, head_cols, model_width)
    gru = gru.reshape(2, 2, units_here, char_width)
    return (
        first,
        second,
        tokens_grad,
        chars.reshape(bw["grad_chars"].shape),
        jnp.transpose(qkv, (2, 0, 1)),
        out,
        win,
        down,
        jnp.transpose(gru, (3, 0, 1, 2)),
        gate_grad,
        jnp.transpose(conv, (0, 2, 1)),
        merge,
        gain_grad,
        bias_grad,
    )


def solution(mesh):
    return jax.shard_map(
        local,
        mesh=mesh,
        in_specs=(
            P("dp", "tensor", None),
            P("dp", "tensor", None),
            P("dp", None),
            P("dp", None),
            P(None, None, "tensor"),
            P("tensor", None),
            P(None, "tensor"),
            P("tensor", None),
            P(None, None, None, "tensor"),
            P(None, "tensor"),
            P(None, None, "tensor"),
            P("tensor", None, None),
            P(),
            P(),
            P("dp", "tensor", None),
            P("dp", "tensor", None),
        ),
        out_specs=(
            P("dp", "tensor", None),
            P("dp", "tensor", None),
            P("dp", "tensor", None),
            P("dp", "tensor", None),
            P(None, None, "tensor"),
            P("tensor", None),
            P(None, "tensor"),
            P("tensor", None),
            P(None, None, None, "tensor"),
            P(None, "tensor"),
            P(None, None, "tensor"),
            P("tensor", None, None),
            P(),
            P(),
        ),
        check_vma=False,
    )
```

```python
import functools
from types import SimpleNamespace

import jax
import jax.numpy as jnp
from jax import lax
from jax.experimental import pallas as pl
from jax.experimental.pallas import tpu as pltpu
from jax.sharding import PartitionSpec as P

HD = 64


NORM_EPSILON = 1e-06
MASK_VALUE = -1e30
HIGH_PRECISION = lax.Precision.HIGHEST


F32 = jnp.float32
BF16 = jnp.bfloat16
LANE = 128
MIB = 1024 * 1024


def nn(left, right):
    return jnp.dot(left, right, preferred_element_type=F32)


def nt(left, right):
    return lax.dot_general(left, right, (((1,), (1,)), ((), ())), preferred_element_type=F32)


def tn(left, right):
    return lax.dot_general(left, right, (((0,), (0,)), ((), ())), preferred_element_type=F32)


def gelu_pair(values):
    cdf = 0.5 * (1.0 + lax.erf(values * 0.7071067811865476))
    density = 0.3989422804014327 * jnp.exp(-0.5 * values * values)
    return values * cdf, cdf + values * density


def normalize(rows):
    centered = rows - jnp.mean(rows, axis=-1, keepdims=True)
    scale = lax.rsqrt(jnp.mean(centered * centered, axis=-1, keepdims=True) + NORM_EPSILON)
    return centered * scale, scale


def normalize_back(unit, scale, grad_unit):
    return scale * (
        grad_unit
        - jnp.mean(grad_unit, axis=-1, keepdims=True)
        - unit * jnp.mean(grad_unit * unit, axis=-1, keepdims=True)
    )


def roll_lanes(value, shift):
    return pltpu.roll(value, shift % value.shape[1], axis=1)


def unpack3(packed, size):
    room = -(-size // LANE) * LANE
    lane = lax.broadcasted_iota(jnp.int32, (packed.shape[0], room), 1)
    parts = []
    for k in range(3):
        first = k * size // LANE * LANE
        inner = k * size - first
        part = packed[:, first : min(first + room + LANE, packed.shape[1])]
        if inner:
            part = roll_lanes(part, -inner)
        parts.append(jnp.where(lane < size, part[:, :room], 0.0))
    return parts


def pack3(parts, size):
    room = parts[0].shape[1]
    columns = -(-3 * size // LANE) * LANE
    tiles = [None] * (columns // LANE)
    for k in range(3):
        first, inner = divmod(k * size, LANE)
        part = parts[k]
        if inner:
            part = jnp.concatenate([part, jnp.zeros_like(part[:, :LANE])], axis=1)
            part = roll_lanes(part, inner)
        for j in range(part.shape[1] // LANE):
            if first + j < len(tiles) and (first + j) * LANE < (k + 1) * size:
                tile = part[:, j * LANE : (j + 1) * LANE]
                old = tiles[first + j]
                tiles[first + j] = tile if old is None else old + tile
    return jnp.concatenate(tiles, axis=1)


class Group:
    def __init__(self, send, recv, seqs):
        self.me = lax.axis_index("tensor")
        self.low = self.me % 2
        self.high = self.me // 2
        self.pair = self.high * 2 + (1 - self.low)
        self.far = (1 - self.high) * 2 + self.low
        self.send, self.recv, self.seqs, self.used = send, recv, seqs, 0

    def block(self, turn):
        left = 3 - turn
        return ((self.high + left // 2) % 2) * 2 + (self.low + left % 2) % 2

    def slots(self, count):
        first = self.used
        self.used += count
        return [first + i for i in range(count)]

    def copy(self, slot, seq, source, target, peer):
        index = slot * self.seqs + seq
        return pltpu.make_async_remote_copy(
            src_ref=source,
            dst_ref=target,
            send_sem=self.send.at[index],
            recv_sem=self.recv.at[index],
            device_id={"tensor": peer},
            device_id_type=pl.DeviceIdType.MESH,
        )

    def greet(self):
        barrier = pltpu.get_barrier_semaphore()
        for peer in (self.pair, self.far):
            pl.semaphore_signal(
                barrier, inc=1, device_id={"tensor": peer}, device_id_type=pl.DeviceIdType.MESH
            )
        pl.semaphore_wait(barrier, 2)


class Gather:
    def __init__(self, group, buf, source=None, place=None):
        self.group, self.source = group, source
        self.at = place or (lambda seq, t: buf.at[seq, t])
        self.near, self.over, self.fwd = group.slots(3)

    def own(self, seq):
        return self.at(seq, self.group.me) if self.source is None else self.source.at[seq]

    def near_copy(self, seq):
        g = self.group
        return g.copy(self.near, seq, self.own(seq), self.at(seq, g.me), g.pair)

    def over_copy(self, seq):
        g = self.group
        return g.copy(self.over, seq, self.own(seq), self.at(seq, g.me), g.far)

    def fwd_copy(self, seq):
        g = self.group
        other = self.at(seq, g.far)
        return g.copy(self.fwd, seq, other, other, g.pair)

    def start(self, seq):
        self.over_copy(seq).start()
        self.near_copy(seq).start()

    def forward(self, seq):
        self.over_copy(seq).wait_recv()
        self.fwd_copy(seq).start()

    def finish(self, seq):
        near = self.near_copy(seq)
        fwd = self.fwd_copy(seq)
        near.wait_recv()
        fwd.wait_recv()
        near.wait_send()
        self.over_copy(seq).wait_send()
        fwd.wait_send()


class Scatter:
    def __init__(self, group, stage, got, own, temp):
        self.group, self.stage, self.got, self.held, self.temp = group, stage, got, own, temp
        self.names = group.slots(3)

    def copies(self, seq):
        g = self.group
        peers = (g.pair, g.pair, g.far)
        return [
            g.copy(self.names[i], seq, self.stage(seq, i), self.got(seq, i), peers[i])
            for i in range(3)
        ]

    def start(self, seq, part):
        mine, other, over = self.copies(seq)

        def turn(step, carry):
            part(self.group.block(step), self.temp)

            @pl.when(step == 0)
            def _():
                self.stage(seq, 1)[...] = self.temp[...].astype(BF16)
                other.start()

            @pl.when(step == 1)
            def _():
                other.wait_recv()
                self.stage(seq, 2)[...] = (self.temp[...] + self.got(seq, 1)[...]).astype(BF16)
                over.start()

            @pl.when(step == 2)
            def _():
                self.stage(seq, 0)[...] = self.temp[...].astype(BF16)
                mine.start()

            @pl.when(step == 3)
            def _():
                self.held(seq)[...] = self.temp[...]

            return carry

        lax.fori_loop(0, 4, turn, 0)

    def finish(self, seq):
        mine, other, over = self.copies(seq)
        mine.wait_recv()
        over.wait_recv()
        total = self.held(seq)[...] + self.got(seq, 0)[...] + self.got(seq, 2)[...]
        mine.wait_send()
        other.wait_send()
        over.wait_send()
        return total


def shift_rows(value, count, up, fill):
    edge = jnp.full((count, value.shape[1]), fill, value.dtype)
    if up:
        return jnp.concatenate([edge, value[:-count]], axis=0)
    return jnp.concatenate([value[count:], edge], axis=0)


def recur(ups, decays, drives, outs, block, back=False):
    steps = block // 8
    pairs = [(tile, t) for tile in range(2) for t in range(4)]

    def rows(tile, t, step):
        row = step if ups[tile] else steps - 1 - step
        return pl.ds(pl.multiple_of(t * block + row * 8, 8), 8)

    def summary(step, carry):
        new = []
        for i, (tile, t) in enumerate(pairs):
            state, mult = carry[2 * i], carry[2 * i + 1]
            here = rows(tile, t, step)
            decay, drive = decays[tile, here, :], drives[tile, here, :]
            state = decay * (state + drive) if back else decay * state + drive
            new += [state, decay * mult]
        return tuple(new)

    zero, one = jnp.zeros((8, LANE), F32), jnp.ones((8, LANE), F32)
    ends = lax.fori_loop(0, steps, summary, (zero, one) * 8, unroll=8)
    starts = []
    for tile in range(2):
        state = jnp.concatenate([ends[2 * (4 * tile + t)] for t in range(4)], axis=0)
        mult = jnp.concatenate([ends[2 * (4 * tile + t) + 1] for t in range(4)], axis=0)
        for count in (1, 2, 4, 8, 16):
            state = mult * shift_rows(state, count, ups[tile], 0.0) + state
            mult = mult * shift_rows(mult, count, ups[tile], 1.0)
        state = shift_rows(state, 1, ups[tile], 0.0)
        starts += [state[8 * t : 8 * t + 8] for t in range(4)]

    def write(step, carry):
        new = []
        for i, (tile, t) in enumerate(pairs):
            here = rows(tile, t, step)
            decay, drive = decays[tile, here, :], drives[tile, here, :]
            if back:
                value = drive + carry[i]
                new.append(decay * value)
            else:
                value = decay * carry[i] + drive
                new.append(value)
            outs[tile, here, :] = value
        return tuple(new)

    lax.fori_loop(0, steps, write, tuple(starts), unroll=8)


def forward_kernel(
    units, channels, docs, counts, tokens, chars, wq_in, wout_in, win_in, wdown_in, wg_in, gate_in,
    wc_in, wm_in, gain, bias, cot_t_in, cot_c_in,
    token_out, char_out, o_x, o_c, o_qkv, o_p, o_ctx, o_h, o_act, o_dact, o_mid, o_st, o_mg,
    o_dmg, o_states, o_decay, o_unit0, o_unit1, o_scale, o_res3, o_res4, o_branch,
    o_wq, o_wout, o_wg, o_wc, o_wm, norm_grads, pickr, edges,
    x, c, qkv, p, ctx, h, act, dact, mid, st, mg, dmg, low_states, decays, unit0, unit1, scale, res3, res4, branch,
    wq, wout, wg, wc, hidden, middle, outs_t, outs_c, states, drive, taps, perm, gate_bias,
    win, wdown, wm, cot_t, cot_c, segc, segr, pickc, keep,
    stage, got, held, temp, send, recv, local,
):
    seqs, length = counts.shape
    shard, width = tokens.shape[1], tokens.shape[2]
    block_chars = chars.shape[1]
    heads = p.shape[1] // 4
    g = Group(send, recv, seqs)
    me = g.me
    saves = []

    def keep_out(seq, source, target):
        saves.append((source, target, len(saves)))

    def local_copy(number, seq, source, target):
        return pltpu.make_async_copy(source, target, local.at[number * seqs + seq])

    gx, gc = Gather(g, x, tokens), Gather(g, c)
    gh, gm, gs = Gather(g, h), Gather(g, mid), Gather(g, st)
    narrow = lambda ref: (lambda s, i: ref.at[s, i, :, pl.ds(0, width)])
    wide = lambda ref: (lambda s, i: ref.at[s, i])
    own_n = lambda s: held.at[s, :, pl.ds(0, width)]
    own_w = lambda s: held.at[s]
    thin = temp.at[:, pl.ds(0, width)]
    s_attn = Scatter(g, narrow(stage), narrow(got), own_n, thin)
    s_ffn = Scatter(g, narrow(stage), narrow(got), own_n, thin)
    s_branch = Scatter(g, wide(stage), wide(got), own_w, temp)

    def own_x(seq):
        return local_copy(0, seq, tokens.at[seq], x.at[seq, me])

    def own_c(seq):
        return local_copy(1, seq, chars.at[seq], c.at[seq, me])

    plan = [
        (x, o_x), (c, o_c), (qkv, o_qkv), (p, o_p), (ctx, o_ctx), (h, o_h), (act, o_act),
        (dact, o_dact), (mid, o_mid), (st, o_st), (mg, o_mg), (dmg, o_dmg), (low_states, o_states),
        (decays, o_decay), (res4, o_res4), (unit0, o_unit0), (unit1, o_unit1), (scale, o_scale), (res3, o_res3), (branch, o_branch),
        (outs_t, token_out), (outs_c, char_out),
    ]

    def save(seq, *names):
        for name in names:
            for number, (source, target) in enumerate(plan):
                if source is name:
                    local_copy(2 + number, seq, source.at[seq], target.at[seq]).start()

    def each(body):
        def run(seq, carry):
            body(seq)
            return carry

        lax.fori_loop(0, seqs, run, 0)

    each(lambda s: (own_x(s).start(), own_c(s).start()))
    base = (2 + len(plan)) * seqs
    late = [(win_in, win), (wdown_in, wdown), (cot_t_in, cot_t), (cot_c_in, cot_c)]
    rows_in = wq_in.shape[0]
    fills = [
        (wq_in, wq.at[pl.ds(0, rows_in), :]),
        (wout_in, wout.at[pl.ds(0, wout_in.shape[0]), :]),
        (wc_in.at[:, pl.ds(0, width)], wc.at[pl.ds(0, rows_in), pl.ds(0, width)]),
    ]
    for d in range(2):
        for k in range(2):
            fills.append((wg_in.at[d, k], wg.at[pl.ds((2 * k + d) * LANE, units), :]))
    pieces = -(-rows_in // shard)
    for j in range(pieces):
        size = min(shard, rows_in - j * shard)
        fills.append(
            (
                wc_in.at[pl.ds(j * shard, size), pl.ds(width, width)],
                mid.at[j // 4, j % 4, pl.ds(0, size), :],
            )
        )

    fills += late

    def fill(number):
        return pltpu.make_async_copy(*fills[number], local.at[base + number])

    keeps = [(wq, o_wq), (wout, o_wout), (wg, o_wg), (wc, o_wc), (wm, o_wm)]

    def keep_weights(number):
        return pltpu.make_async_copy(*keeps[number], local.at[base + len(fills) + number])

    for number in range(len(fills)):
        fill(number).start()
    g.greet()
    each(gx.start)
    steps = block_chars // 8
    assert steps & (steps - 1) == 0

    def reorder(s):
        own_c(s).wait()
        row = lax.broadcasted_iota(jnp.int32, (block_chars, block_chars), 0)
        col = lax.broadcasted_iota(jnp.int32, (block_chars, block_chars), 1)
        hit = (col == (row & 7) * steps + (row >> 3)).astype(F32).astype(BF16)
        c[s, me] = nn(hit, c[s, me]).astype(BF16)
        gc.start(s)

    each(reorder)

    taps[...] = jnp.zeros_like(taps)
    norm_grads[...] = jnp.zeros_like(norm_grads)
    gate_bias[...] = jnp.zeros_like(gate_bias)
    gate_bias[:, pl.ds(0, units)] = gate_in[...]
    rest = wq.shape[0] - rows_in
    wq[pl.ds(rows_in, rest), :] = jnp.zeros((rest, width), BF16)
    wc[pl.ds(rows_in, rest), :] = jnp.zeros((rest, wc.shape[1]), BF16)
    more = wout.shape[0] - wout_in.shape[0]
    wout[pl.ds(wout_in.shape[0], more), :] = jnp.zeros((more, width), BF16)
    for j in range(4):
        wg[pl.ds(j * LANE + units, LANE - units), :] = jnp.zeros(
            (LANE - units, wg.shape[1]), BF16
        )
    fill(0).wait()
    fill(1).wait()
    lane = lax.broadcasted_iota(jnp.int32, (shard, LANE), 1)
    left = lane < HD

    def place(char):
        inner = char & (block_chars - 1)
        return char - inner + ((inner & (steps - 1)) << 3) + (inner >> (steps.bit_length() - 1))

    def hits(positions, marks):
        total = jnp.zeros(positions.shape, F32)
        for mark in marks:
            total = total + (positions == mark).astype(F32)
        return total

    def structure(s):
        ends, running = [], 0
        for d in range(docs.shape[1]):
            running = running + docs[s, d]
            ends.append(running)
        along = lax.broadcasted_iota(jnp.int32, (1, length), 1)
        down = lax.broadcasted_iota(jnp.int32, (length, 1), 0)
        seg_row, seg_col = jnp.zeros_like(along), jnp.zeros_like(down)
        for end in ends:
            seg_row = seg_row + (along >= end).astype(jnp.int32)
            seg_col = seg_col + (down >= end).astype(jnp.int32)
        segr[s] = seg_row
        segc[s] = seg_col
        edges[s, :, 0:1] = 1.0 - hits(down, [0] + ends[:-1])
        edges[s, :, 1:2] = 1.0 - hits(down + 1, ends)
        count = counts[pl.ds(s, 1), :].astype(F32)
        many = jnp.broadcast_to(count, (LANE, length)).astype(BF16)
        rows = lax.broadcasted_iota(jnp.int32, (length, length), 0)
        cols = lax.broadcasted_iota(jnp.int32, (length, length), 1)
        ends_row = nn(many[:16], (rows <= cols).astype(F32).astype(BF16))[0:1]
        ends_col = nt((cols <= rows).astype(F32).astype(BF16), many)[:, 0:1]
        starts_col = nt((cols < rows).astype(F32).astype(BF16), many)[:, 0:1]
        pickr[s, 0:1, :] = place(ends_row.astype(jnp.int32) - 1)
        pickr[s, 1:2, :] = place((ends_row - count).astype(jnp.int32))
        pickc[s, :, 0:1] = place(ends_col.astype(jnp.int32) - 1)
        pickc[s, :, 1:2] = place(starts_col.astype(jnp.int32))
        cuts = [
            jnp.sum(jnp.where(along < end, count, 0.0), axis=1, keepdims=True) for end in ends
        ]
        row = lax.broadcasted_iota(jnp.int32, (4 * block_chars, 1), 0)
        inner = row & (block_chars - 1)
        char = (row - inner + (inner & 7) * steps + (inner >> 3)).astype(F32)
        keep[s, :, 0:1] = 1.0 - hits(char, [0.0] + cuts[:-1])
        keep[s, :, 1:2] = 1.0 - hits(char + 1.0, cuts)

    each(structure)
    for number in (3, 4, 5, 6):
        fill(number).wait()

    def attention(s):
        gx.forward(s)
        gx.finish(s)
        own_x(s).wait()
        save(s, x)

        def project(t, carry):
            rows = pl.ds(pl.multiple_of(t * shard, shard), shard)
            first, second, third = unpack3(nt(x[s, t], wq[...]), HD * heads)
            qkv[s, 0, rows, :] = (first * 0.125).astype(BF16)
            qkv[s, 1, rows, :] = second.astype(BF16)
            qkv[s, 2, rows, :] = third.astype(BF16)
            return carry

        lax.fori_loop(0, 4, project, 0)
        save(s, qkv)

        def part(b, out):
            rows = pl.ds(pl.multiple_of(b * shard, shard), shard)
            same = segc[s, rows, :] == segr[s]
            for tile in range(qkv.shape[3] // LANE):
                cols = pl.ds(tile * LANE, LANE)
                result = None
                for half in range(2):
                    head = 2 * tile + half
                    if head >= heads:
                        continue
                    query = qkv[s, 0, rows, cols]
                    if 2 * tile + 1 < heads:
                        query = jnp.where(left if half == 0 else ~left, query, jnp.zeros_like(query))
                    scores = jnp.where(same, nt(query, qkv[s, 1, :, cols]), MASK_VALUE)
                    power = jnp.exp(scores - jnp.max(scores, axis=-1, keepdims=True))
                    probs = (power * (1.0 / jnp.sum(power, axis=-1, keepdims=True))).astype(BF16)
                    p[s, head * 4 + b] = probs
                    mixed = nn(probs, qkv[s, 2, :, cols])
                    result = mixed if result is None else jnp.where(left, result, mixed)
                ctx[s, rows, cols] = result.astype(BF16)
            out[...] = nn(ctx[s, rows, :], wout[...])

        s_attn.start(s, part)
        save(s, p, ctx)

    each(attention)

    def first_norm(s):
        total = x[s, me].astype(F32) + s_attn.finish(s)
        unit, spread = normalize(total)
        unit0[s] = unit
        scale[s, 0] = jnp.broadcast_to(spread, (shard, LANE))
        hidden[s] = unit * gain[0:1] + bias[0:1]
        h[s, me] = hidden[s].astype(BF16)
        gh.start(s)
        save(s, unit0)

    def gru(s):
        gc.forward(s)
        gc.finish(s)
        save(s, c)

        def gates(t, carry):
            rows = pl.ds(pl.multiple_of(t * LANE, LANE), LANE)
            per = block_chars // LANE
            inner = pl.ds(pl.multiple_of((t % per) * LANE, LANE), LANE)
            proj = nt(c[s, t // per, inner, :], wg[...])
            for tile in range(2):
                cols = slice(tile * LANE, (tile + 1) * LANE)
                gate = jax.nn.sigmoid(proj[:, cols] + gate_bias[tile : tile + 1])
                cand = proj[:, (2 + tile) * LANE : (3 + tile) * LANE]
                decays[s, tile, rows, :] = (1.0 - gate) * keep[s, rows, tile : tile + 1]
                drive[tile, rows, :] = gate * cand
            return carry

        total = 4 * block_chars
        lax.fori_loop(0, total // LANE, gates, 0)
        recur((True, False), decays.at[s], drive, states, block_chars)
        save(s, decays)

        for tile in range(2):
            low_states[s, tile] = states[tile].astype(BF16)

        def pick(t, carry):
            rows = pl.ds(pl.multiple_of(t * shard, shard), shard)
            for tile in range(2):
                ids = lax.broadcasted_iota(jnp.int32, (shard, total), 1)
                hot = (ids == pickc[s, rows, tile : tile + 1]).astype(F32).astype(BF16)
                out = nn(hot, low_states[s, tile])
                st[s, me, rows, pl.ds(tile * LANE, LANE)] = out.astype(BF16)
            return carry

        lax.fori_loop(0, 4, pick, 0)
        gs.start(s)
        save(s, low_states)

    def norm_and_gru(s):
        first_norm(s)
        gru(s)

    each(norm_and_gru)

    def ffn(s):
        gh.forward(s)
        gh.finish(s)
        save(s, h)

        def part(b, out):
            value, slope = gelu_pair(nn(h[s, b], win[...]))
            act[s, b] = value.astype(BF16)
            dact[s, b] = slope.astype(BF16)
            out[...] = nn(act[s, b], wdown[...])

        s_ffn.start(s, part)
        save(s, act, dact)

    for t in range(4):
        for d in range(2):
            row = lax.broadcasted_iota(jnp.int32, (LANE, width), 0)
            col = lax.broadcasted_iota(jnp.int32, (LANE, width), 1)
            first = d * 4 * units + t * units
            hit = (col - first == row) & (row < units)
            perm[pl.ds((2 * t + d) * LANE, LANE), :] = hit.astype(F32).astype(BF16)
    for number in range(2, len(fills)):
        if number not in (3, 4, 5, 6):
            fill(number).wait()
    for j in range(pieces):
        size = min(shard, rows_in - j * shard)
        wc[pl.ds(j * shard, size), pl.ds(width, 8 * LANE)] = nt(
            mid[j // 4, j % 4, pl.ds(0, size), :], perm[...]
        ).astype(BF16)
    for k in range(2):
        wm[pl.ds(0, channels), pl.ds(k * width, width)] = wm_in[:, k, :]
    wm[pl.ds(channels, wm.shape[0] - channels), :] = jnp.zeros(
        (wm.shape[0] - channels, 2 * width), BF16
    )
    for number in range(len(keeps)):
        keep_weights(number).start()

    each(ffn)

    def second_norm(s):
        unit, spread = normalize(hidden[s] + s_ffn.finish(s))
        unit1[s] = unit
        scale[s, 1] = jnp.broadcast_to(spread, (shard, LANE))
        middle[s] = unit * gain[1:2] + bias[1:2]
        mid[s, me] = middle[s].astype(BF16)
        gm.start(s)
        save(s, unit1, scale)

    each(second_norm)

    def merge(s):
        gs.forward(s)
        gm.forward(s)
        gs.finish(s)
        gm.finish(s)
        save(s, mid, st)
        def mix(t, carry):
            rows = pl.ds(pl.multiple_of(t * shard, shard), shard)
            total = nt(mid[s, t], wc[:, pl.ds(0, width)])
            for u in range(4):
                weights = wc[:, pl.ds(width + u * 2 * LANE, 2 * LANE)]
                total = total + nt(st[s, u, rows, :], weights)
            taps[pl.ds(pl.multiple_of(8 + t * shard, 8), shard), :] = total
            return carry

        lax.fori_loop(0, 4, mix, 0)

        def shifted(t, carry):
            rows = pl.ds(pl.multiple_of(t * shard, shard), shard)
            window = taps[pl.ds(pl.multiple_of(t * shard, 8), shard + 16), :]
            before = unpack3(window[7 : 7 + shard], channels)[0]
            center = unpack3(window[8 : 8 + shard], channels)[1]
            after = unpack3(window[9 : 9 + shard], channels)[2]
            value, slope = gelu_pair(
                before * edges[s, rows, 0:1] + center + after * edges[s, rows, 1:2]
            )
            mg[s, rows, :] = value.astype(BF16)
            dmg[s, rows, :] = slope.astype(BF16)
            return carry

        lax.fori_loop(0, 4, shifted, 0)

        def part(b, out):
            rows = pl.ds(pl.multiple_of(b * shard, shard), shard)
            out[...] = nn(mg[s, rows, :], wm[...])

        s_branch.start(s, part)
        save(s, mg, dmg)

    each(merge)

    def put_branch(s, first, value):
        span = branch.shape[3]
        at = 0
        while at < width:
            part, inner = divmod(first + at, span)
            size = min(span - inner, width - at)
            branch[s, part, :, pl.ds(inner, size)] = value[:, at : at + size]
            at += size

    def last_norms(s):
        total = s_branch.finish(s)
        rows = pl.ds(pl.multiple_of(me * shard, shard), shard)
        unit, spread = normalize(middle[s] + total[:, :width])
        outs_t[s] = (unit * gain[2:3] + bias[2:3]).astype(BF16)
        cot = cot_t[s]
        norm_grads[0:1] += jnp.sum(cot * unit, axis=0, keepdims=True)
        norm_grads[2:3] += jnp.sum(cot, axis=0, keepdims=True)
        back = normalize_back(unit, spread, cot * gain[2:3])
        res3[s] = back
        put_branch(s, 0, back.astype(BF16))
        mine = total[:, width:]
        for u in range(4):
            mine = mine + nn(st[s, u, rows, :], perm[pl.ds(u * 2 * LANE, 2 * LANE), :])
        unit, spread = normalize(mine)
        outs_c[s] = (unit * gain[3:4] + bias[3:4]).astype(BF16)
        cot = cot_c[s]
        norm_grads[1:2] += jnp.sum(cot * unit, axis=0, keepdims=True)
        norm_grads[3:4] += jnp.sum(cot, axis=0, keepdims=True)
        back = normalize_back(unit, spread, cot * gain[3:4]).astype(BF16)
        put_branch(s, width, back)
        for u in range(4):
            res4[s, u] = nt(back, perm[pl.ds(u * 2 * LANE, 2 * LANE), :]).astype(BF16)
        save(s, outs_t, outs_c, res3, res4, branch)

    each(last_norms)

    def drain(s):
        for number, (source, target) in enumerate(plan):
            local_copy(2 + number, s, source.at[s], target.at[s]).wait()

    each(drain)
    for number in range(len(keeps)):
        keep_weights(number).wait()


def forward_call(tokens, chars, weights, small, group_slots=27):
    seqs, shard, width = tokens.shape
    length, block_chars = shard * 4, chars.shape[1]
    total = block_chars * 4
    wq, wout, win, wdown, wg, gate_bias, wc, wm = weights
    cols = -(-wout.shape[0] // LANE) * LANE
    packed = -(-wq.shape[0] // LANE) * LANE
    heads = small["heads"]
    merge_shape = (-(-wm.shape[0] // LANE) * LANE, 2 * width)
    kept = [
        ((packed, width), BF16), ((cols, width), BF16), ((4 * LANE, chars.shape[2]), BF16),
        ((packed, width + 8 * LANE), BF16),
    ]
    sds = jax.ShapeDtypeStruct
    big = {
        "x": ((seqs, 4, shard, width), BF16),
        "c": ((seqs, 4, block_chars, chars.shape[2]), BF16),
        "qkv": ((seqs, 3, length, cols), BF16),
        "p": ((seqs, heads * 4, shard, length), BF16),
        "ctx": ((seqs, length, cols), BF16),
        "h": ((seqs, 4, shard, width), BF16),
        "act": ((seqs, 4, shard, win.shape[1]), BF16),
        "dact": ((seqs, 4, shard, win.shape[1]), BF16),
        "mid": ((seqs, 4, shard, width), BF16),
        "st": ((seqs, 4, length, 2 * LANE), BF16),
        "mg": ((seqs, length, merge_shape[0]), BF16),
        "dmg": ((seqs, length, merge_shape[0]), BF16),
        "states": ((seqs, 2, total, LANE), BF16),
        "decay": ((seqs, 2, total, LANE), F32),
        "unit0": ((seqs, shard, width), F32),
        "unit1": ((seqs, shard, width), F32),
        "scale": ((seqs, 2, shard, LANE), F32),
        "res3": ((seqs, shard, width), F32),
        "res4": ((seqs, 4, shard, 2 * LANE), BF16),
        "branch": ((seqs, 2 * width // length, shard, length), BF16),
    }
    rows = ((seqs, shard, width), F32)
    low_rows = ((seqs, shard, width), BF16)
    total = block_chars * 4
    scratch = list(big.values()) + kept + [
        rows, rows, low_rows, low_rows,
        ((2, total, LANE), F32),
        ((2, total, LANE), F32),
        ((length + 16, packed), F32),
        ((8 * LANE, width), BF16),
        ((2, LANE), F32),
        (win.shape, BF16), (wdown.shape, BF16), (merge_shape, BF16), rows, rows,
        ((seqs, length, 1), jnp.int32), ((seqs, 1, length), jnp.int32),
        ((seqs, length, 2), jnp.int32), ((seqs, total, 2), F32),
        ((seqs, 3, shard, 2 * width), BF16), ((seqs, 3, shard, 2 * width), BF16),
        ((seqs, shard, 2 * width), F32), ((shard, 2 * width), F32),
    ]
    anyspace = pl.BlockSpec(memory_space=pl.ANY)
    vmem = pl.BlockSpec(memory_space=pltpu.VMEM)
    out_shapes = [sds(low_rows[0], BF16)] * 2
    out_shapes += [sds(*v) for v in list(big.values()) + kept + [(merge_shape, BF16)]]
    ins = (
        small["docs"], small["counts"], tokens, chars, wq, wout, win, wdown, wg, gate_bias, wc, wm,
        small["gain"], small["bias"], small["cot_t"], small["cot_c"],
    )
    smem = pl.BlockSpec(memory_space=pltpu.SMEM)
    places = [smem, vmem] + [anyspace] * 7 + [vmem, anyspace] + [vmem] * 3 + [anyspace] * 2
    outs = pl.pallas_call(
        functools.partial(forward_kernel, small["units"], small["channels"]),
        out_shape=out_shapes
        + [
            sds((4, width), F32),
            sds((seqs, 2, length), jnp.int32),
            sds((seqs, length, 2), F32),
        ],
        in_specs=places,
        out_specs=[anyspace] * len(out_shapes) + [vmem] * 3,
        scratch_shapes=[pltpu.VMEM(*v) for v in scratch]
        + [
            pltpu.SemaphoreType.DMA((group_slots * seqs,)),
            pltpu.SemaphoreType.DMA((group_slots * seqs,)),
            pltpu.SemaphoreType.DMA((26 * seqs + 24,)),
        ],
        compiler_params=pltpu.CompilerParams(
            collective_id=0, has_side_effects=True, vmem_limit_bytes=62 * MIB
        ),
    )(*ins)
    names = ["token_out", "char_out"] + list(big) + ["wq", "wout", "wg", "wc", "wm", "norm_grads"]
    names += ["pickr", "edges"]
    return dict(zip(names, outs))


class Plane:
    def __init__(self, send, recv, marks):
        self.index = lax.axis_index("dp")
        self.x, self.z = self.index % 2, self.index // 2
        self.send, self.recv, self.marks, self.used, self.marked = send, recv, marks, 0, 0

    def mark(self):
        self.marked += 1
        return self.marks.at[self.marked - 1]

    def take(self, count):
        first = self.used
        self.used += count
        return [first + i for i in range(count)]

    def peer(self, way):
        if way == "x":
            return self.index + 1 - 2 * self.x
        return (self.index + (2 if way == "up" else 6)) % 8

    def pair(self, bit):
        digit = self.index // (1 << bit) % 2
        return self.index + (1 - 2 * digit) * (1 << bit)

    def copy(self, slot, source, target, peer):
        return pltpu.make_async_remote_copy(
            src_ref=source,
            dst_ref=target,
            send_sem=self.send.at[slot],
            recv_sem=self.recv.at[slot],
            device_id={"dp": peer},
            device_id_type=pl.DeviceIdType.MESH,
        )


class Reduce:
    steps = 9

    def __init__(self, plane, buf, out, land, first, land_first, rows, x_first):
        self.plane, self.buf, self.out, self.land = plane, buf, out, land
        self.first, self.land_first, self.rows, self.x_first = first, land_first, rows, x_first
        self.slots = plane.take(14)
        self.mark = plane.mark()
        x, z = plane.x, plane.z
        if x_first:
            self.quarter, self.half = rows // 8, rows // 2
            self.z_base, self.x_base = first + x * self.half, first
        else:
            self.quarter, self.half = rows // 4, rows // 8
            self.z_base, self.x_base = first, first + z * self.quarter
        self.x_land = land_first + 5 * self.quarter

    @staticmethod
    def landing_rows(rows, x_first):
        return 5 * rows // 8 + rows // 2 if x_first else 5 * rows // 4 + rows // 8

    def rows_of(self, ref, start, size):
        return ref.at[pl.ds(pl.multiple_of(start, 16), size), :]

    def add(self, start, land_start, size):
        def one(i, carry):
            rows = pl.ds(pl.multiple_of(start + i * 16, 16), 16)
            more = pl.ds(pl.multiple_of(land_start + i * 16, 16), 16)
            total = self.buf[rows, :].astype(F32) + self.land[more, :].astype(F32)
            self.buf[rows, :] = total.astype(BF16)
            return carry

        lax.fori_loop(0, size // 16, one, 0)

    def gather_copy(self, way, step, z):
        piece = 3 - step + z if way == "up" else step - 3 + z
        slot = piece if way == "up" else piece + (4 - piece) * (step // 2)
        return self.plane.copy(
            self.slots[step if way == "up" else 3 + step],
            self.rows_of(self.buf, self.z_base + piece * self.quarter, self.quarter),
            self.rows_of(self.land, self.land_first + slot * self.quarter, self.quarter),
            self.plane.peer(way),
        )

    def gather_send(self, step):
        z = self.plane.z
        pl.when(step >= z)(lambda: self.gather_copy("up", step, z).start())
        pl.when(step >= 3 - z)(lambda: self.gather_copy("down", step, z).start())

    def gather_wait(self, step):
        z = self.plane.z

        @pl.when((z >= 1) & (step >= z - 1))
        def _():
            self.gather_copy("up", step, z - 1).wait_recv()
            piece = 3 - step + z - 1
            self.add(
                self.z_base + piece * self.quarter,
                self.land_first + piece * self.quarter,
                self.quarter,
            )

        @pl.when((z <= 2) & (step >= 2 - z))
        def _():
            self.gather_copy("down", step, z + 1).wait_recv()
            piece = step - 3 + z + 1
            slot = piece if step < 2 else 4
            self.add(
                self.z_base + piece * self.quarter,
                self.land_first + slot * self.quarter,
                self.quarter,
            )

        pl.when(step >= z)(lambda: self.gather_copy("up", step, z).wait_send())
        pl.when(step >= 3 - z)(lambda: self.gather_copy("down", step, z).wait_send())

    def spread_copy(self, way, step, z):
        piece = z - step if way == "up" else z + step
        start = self.z_base + piece * self.quarter
        target = self.rows_of(self.out, start, self.quarter)
        source = target
        if self.x_first and step == 0:
            source = self.rows_of(self.buf, start, self.quarter)
        slot = self.slots[6 + step if way == "up" else 9 + step]
        return self.plane.copy(slot, source, target, self.plane.peer(way))

    def spread_send(self, step):
        z = self.plane.z
        pl.when((z <= 2) & (step <= z))(lambda: self.spread_copy("up", step, z).start())
        pl.when((z >= 1) & (step <= 3 - z))(lambda: self.spread_copy("down", step, z).start())

    def spread_wait(self, step):
        z = self.plane.z
        pl.when((z >= 1) & (step <= z - 1))(lambda: self.spread_copy("up", step, z - 1).wait_recv())
        pl.when((z <= 2) & (step <= 2 - z))(lambda: self.spread_copy("down", step, z + 1).wait_recv())
        pl.when((z <= 2) & (step <= z))(lambda: self.spread_copy("up", step, z).wait_send())
        pl.when((z >= 1) & (step <= 3 - z))(lambda: self.spread_copy("down", step, z).wait_send())

    def halve(self):
        other = self.x_base + (1 - self.plane.x) * self.half
        return self.plane.copy(
            self.slots[12],
            self.rows_of(self.buf, other, self.half),
            self.rows_of(self.land, self.x_land, self.half),
            self.plane.peer("x"),
        )

    def halve_wait(self):
        self.halve().wait()
        self.add(self.x_base + self.plane.x * self.half, self.x_land, self.half)

    def double(self):
        start = self.x_base + self.plane.x * self.half
        target = self.rows_of(self.out, start, self.half)
        source = target if self.x_first else self.rows_of(self.buf, start, self.half)
        return self.plane.copy(self.slots[13], source, target, self.plane.peer("x"))

    def keep(self):
        if self.x_first:
            start, size = self.z_base + self.plane.z * self.quarter, self.quarter
        else:
            start, size = self.x_base + self.plane.x * self.half, self.half
        return pltpu.make_async_copy(
            self.rows_of(self.buf, start, size), self.rows_of(self.out, start, size), self.mark
        )

    def step(self, number):
        if self.x_first:
            if number == 0:
                self.halve().start()
            elif number == 1:
                self.halve_wait()
                self.gather_send(0)
            elif number <= 3:
                self.gather_wait(number - 2)
                self.gather_send(number - 1)
            elif number == 4:
                self.gather_wait(2)
                self.keep().start()
                self.spread_send(0)
            elif number <= 6:
                self.spread_wait(number - 5)
                self.spread_send(number - 4)
            elif number == 7:
                self.spread_wait(2)
                self.keep().wait()
                self.double().start()
            else:
                self.double().wait()
        else:
            if number == 0:
                self.gather_send(0)
            elif number <= 2:
                self.gather_wait(number - 1)
                self.gather_send(number)
            elif number == 3:
                self.gather_wait(2)
                self.halve().start()
            elif number == 4:
                self.halve_wait()
                self.keep().start()
                self.double().start()
            elif number == 5:
                self.double().wait()
                self.keep().wait()
                self.spread_send(0)
            elif number <= 7:
                self.spread_wait(number - 6)
                self.spread_send(number - 5)
            else:
                self.spread_wait(2)


SAVED = (
    "branch", "mg", "dmg", "mid", "st", "res3", "res4", "unit0", "unit1", "scale", "act", "dact",
    "h", "p", "qkv", "ctx", "x", "c", "states", "decay",
)
GRADS = ("merge", "conv", "down", "win", "gru", "out", "qkv")
PIECES = (
    (0, 384, True),
    (1, 640, True),
    (1, 384, False),
    (1, 128, True),
    (2, 256, True),
    (2, 512, True),
    (3, 384, True),
    (3, 384, True),
    (4, 384, True),
    (5, 384, True),
    (6, 256, True),
    (6, 896, False),
)
SCHEDULE = (
    (),
    (10, 20, 30,),
    (),
    (21,),
    (1,),
    (),
    (40, 50, 22,),
    (60, 70, 2,),
    (11,),
    (23, 31,),
    (3,),
    (12, 41, 32, 4,),
    (),
    (13, 42, 51, 33,),
    (5,),
    (14, 43, 61,),
    (6, 52, 34,),
    (15, 44, 71, 7, 62, 24,),
    (53, 35,),
    (90, 100, 110, 16, 72, 45, 63,),
    (54, 8, 36, 25,),
    (17, 111, 46, 91, 73,),
    (64, 101, 37, 55, 26, 47,),
    (112,),
    (92, 18, 74, 56,),
    (80, 38, 65, 102, 27, 48, 113, 93,),
    (75, 57, 81,),
    (66, 103, 114, 82, 28, 94,),
    (76, 83, 67, 104, 95, 77,),
    (58, 84, 105, 96, 115, 85, 106, 97, 68, 116, 86, 107, 78, 117, 87, 98, 108, 118, 88,),
    (0,),
)


def backward_kernel(units, channels, dp_size, *refs):
    refs = list(refs)
    take = lambda count: [refs.pop(0) for _ in range(count)]
    hbm = SimpleNamespace(**dict(zip(SAVED, take(len(SAVED)))))
    weights_in = take(7)
    gate_in, gain, pickr, edges, norm_in = take(5)
    grad_tokens, grad_chars = take(2)
    grads_out = dict(zip(GRADS, take(len(GRADS))))
    (small_out,) = take(1)
    names = [n for n in SAVED if n not in ("branch", "states", "decay", "p", "x")]
    v = SimpleNamespace(**dict(zip(names, take(len(names)))))
    weights = take(7)
    wq, wout, win, wdown, wg, wc, wm = weights
    (pb, states, decay, drive, dpre, dyk, fg, gtok, dproj, gru_acc, res2, res1, ds, parts,
     stage, got, held, temp, cstage, cgot, cheld, ctemp) = take(22)
    land = dict(zip(GRADS, take(len(GRADS))))
    big = SimpleNamespace(**dict(zip(GRADS, take(len(GRADS)))))
    small, small_land, gate_bias, send, recv, dsend, drecv, local, marks, credit = take(10)

    seqs, shard, width = grad_tokens.shape
    length = 4 * shard
    block_chars = grad_chars.shape[1]
    total = 4 * block_chars
    heads = pb.shape[1] // 4
    cols = v.ctx.shape[2]
    g = Group(send, recv, seqs)
    me = g.me
    inside = dp_size == 8
    plane = Plane(dsend, drecv, marks)

    def each(body):
        def run(seq, carry):
            body(seq)
            return carry

        lax.fori_loop(0, seqs, run, 0)

    def load(name):
        index = names.index(name)
        return pltpu.make_async_copy(getattr(hbm, name), getattr(v, name), local.at[index])

    spare = len(names)
    p_copy = lambda: pltpu.make_async_copy(hbm.p, pb, local.at[spare])
    x_copy = lambda: pltpu.make_async_copy(hbm.x, v.h, local.at[39])

    def states_copy(s):
        return pltpu.make_async_copy(hbm.states.at[s], states, local.at[spare + 1])

    def decay_copy(s, tile):
        return pltpu.make_async_copy(
            hbm.decay.at[s, tile], decay.at[tile], local.at[spare + 2 + tile]
        )

    def out_copy(kind, s):
        source, target = ((res1, grad_tokens), (cheld, grad_chars))[kind]
        return pltpu.make_async_copy(
            source.at[s], target.at[s], local.at[spare + 4 + kind * seqs + s]
        )

    pieces = 2 * width // length
    gb = Gather(
        g, pb, hbm.branch, place=lambda s, t: pb.at[s, pl.ds(t * pieces, pieces)]
    )
    gf, ga = Gather(g, fg), Gather(g, v.mid)
    pick = lambda ref: (lambda s, i: ref.at[s, i])
    own = lambda ref: (lambda s: ref.at[s])
    s_mid = Scatter(g, pick(stage), pick(got), own(held), temp)
    s_hid = Scatter(g, pick(stage), pick(got), own(held), temp)
    s_tok = Scatter(g, pick(stage), pick(got), own(held), temp)
    s_chr = Scatter(g, pick(cstage), pick(cgot), own(cheld), ctemp)
    s_cout = Scatter(g, pick(cstage), pick(cgot), own(cheld), ctemp)

    def own_branch(s):
        return pltpu.make_async_copy(
            hbm.branch.at[s], gb.at(s, me), local.at[spare + 4 + 2 * seqs + s]
        )

    def weight(number):
        return pltpu.make_async_copy(weights_in[number], weights[number], local.at[40 + number])

    each(lambda s: own_branch(s).start())
    weight(6).start()
    for name in ("dmg", "res4", "mg", "mid", "st"):
        load(name).start()
    for number in (5, 3, 2, 1, 0, 4):
        weight(number).start()
    states_copy(0).start()
    for tile in range(2):
        decay_copy(0, tile).start()
    for name in names:
        if name not in ("dmg", "res4", "mg", "mid", "st"):
            load(name).start()

    barrier = pltpu.get_barrier_semaphore()
    places = [{"tensor": g.pair}, {"tensor": g.far}]
    if inside:
        places += [{"dp": plane.peer(way)} for way in ("x", "up", "down")]
        places += [{"dp": plane.pair(2)}]
    for place in places:
        pl.semaphore_signal(barrier, inc=1, device_id=place, device_id_type=pl.DeviceIdType.MESH)
    pl.semaphore_wait(barrier, len(places))
    each(gb.start)
    dpre[...] = jnp.zeros_like(dpre)
    gate_bias[...] = jnp.zeros_like(gate_bias)
    gate_bias[:, pl.ds(0, units)] = gate_in[...]
    side = 2 * LANE
    for t in range(4):
        for j in range(width // side):
            row = lax.broadcasted_iota(jnp.int32, (side, side), 0)
            col = lax.broadcasted_iota(jnp.int32, (side, side), 1) + j * side
            unit = row % LANE
            hit = (col == row // LANE * 4 * units + t * units + unit) & (unit < units)
            cstage[t // 2, j, pl.ds(t % 2 * side, side), :] = hit.astype(F32).astype(BF16)
    small[...] = jnp.zeros_like(small)
    small[0, pl.ds(0, 4), :] = norm_in[...]
    lane = lax.broadcasted_iota(jnp.int32, (shard, LANE), 1)
    left = lane < HD
    for name in ("dmg", "res4"):
        load(name).wait()
    weight(6).wait()
    weight(5).wait()

    def block_rows(t, size):
        return pl.ds(pl.multiple_of(t * size, size), size)

    def merge_back(s):
        gb.forward(s)
        gb.finish(s)
        own_branch(s).wait()

        def inner(t, carry):
            rows = block_rows(t, shard)
            back = None
            for j in range(pieces):
                piece = nt(pb[s, t * pieces + j], wm[:, j * length : (j + 1) * length])
                back = piece if back is None else back + piece
            dpre[pl.ds(pl.multiple_of(8 + t * shard, 8), shard), :] = (
                (back * v.dmg[s, rows, :].astype(F32)).astype(BF16).astype(F32)
            )
            return carry

        lax.fori_loop(0, 4, inner, 0)

        def taps(t, carry):
            rows = block_rows(t, shard)
            window = dpre[pl.ds(pl.multiple_of(t * shard, 8), shard + 16), :]
            marks = edges[s, rows, :]
            before = window[9 : 9 + shard] * marks[:, 1:2]
            after = window[7 : 7 + shard] * marks[:, 0:1]
            dyk[s, rows, :] = pack3(
                [before, window[8 : 8 + shard], after], channels
            ).astype(BF16)
            return carry

        lax.fori_loop(0, 4, taps, 0)

        def mid_part(b, out):
            out[...] = nn(dyk[s, block_rows(b, shard), :], wc[:, pl.ds(0, width)])

        s_mid.start(s, mid_part)

    each(merge_back)
    sums, marks_at = [], {}
    for which, height, x_first in PIECES if inside else ():
        name = GRADS[which]
        first, at = marks_at.get(name, (0, 0))
        sums.append(
            Reduce(
                plane, getattr(big, name), grads_out[name], land[name], first, at, height, x_first
            )
        )
        marks_at[name] = (first + height, at + Reduce.landing_rows(height, x_first))
    fired = [0] * len(sums)

    def fire(hook):
        for entry in SCHEDULE[hook] if inside else ():
            which, number = divmod(entry, 10)
            fired[which] += 1
            sums[which].step(number)

    def fire_in(seq, hook, stride):
        for k in range(2):
            pl.when(seq == k)(functools.partial(fire, hook + k * stride))

    tokens = seqs * length
    step_w = 2 * LANE

    def merge_weights():
        for name in ("mg", "mid", "st"):
            load(name).wait()

        half_w = width
        for j in range(pieces):
            right = jnp.concatenate(
                [pb[s, t * pieces + j] for s in range(seqs) for t in range(4)], axis=0
            )
            out = tn(v.mg[...].reshape(tokens, -1), right)[:channels].astype(BF16)
            at = 0
            while at < length:
                part, inside_at = divmod(j * length + at, half_w)
                size = min(length - at, half_w - inside_at)
                big.merge[pl.ds(part * channels, channels), pl.ds(inside_at, size)] = out[
                    :, at : at + size
                ]
                at += size
        fire(30)
        taps = 3 * channels

        def conv_rows(j, carry):
            lanes = pl.ds(pl.multiple_of(j * LANE, LANE), LANE)
            left_rows = dyk[:, :, lanes].reshape(tokens, LANE)
            size = min(LANE, taps - LANE * j) if isinstance(j, int) else LANE
            first = j * LANE if isinstance(j, int) else pl.multiple_of(j * LANE, LANE)
            out = tn(left_rows, v.mid[...].reshape(tokens, width))
            big.conv[pl.ds(first, size), :] = out[:size].astype(BF16)
            padded = [
                tn(left_rows, v.st[:, t].reshape(tokens, side)).astype(BF16) for t in range(4)
            ]
            first = taps + j * LANE if isinstance(j, int) else pl.multiple_of(taps + j * LANE, 64)
            for k in range(width // side):
                out = None
                for t in range(4):
                    piece = nn(padded[t], cstage[t // 2, k, pl.ds(t % 2 * side, side), :])
                    out = piece if out is None else out + piece
                big.conv[pl.ds(first, size), pl.ds(k * side, side)] = out[:size].astype(BF16)
            return carry

        lax.fori_loop(0, taps // LANE, conv_rows, 0)
        if taps % LANE:
            conv_rows(taps // LANE, 0)
        p_copy().start()
        fire(1)

    def second_back(s):
        incoming = v.res3[s] + s_mid.finish(s)
        unit = v.unit1[s]
        small[0, 5:6] += jnp.sum(incoming * unit, axis=0, keepdims=True)
        small[0, 7:8] += jnp.sum(incoming, axis=0, keepdims=True)
        spread = v.scale[s, 1][:, 0:1]
        res2[s] = normalize_back(unit, spread, incoming * gain[1:2])
        fg[s, me] = res2[s].astype(BF16)
        gf.start(s)
        fire_in(s, 0, 2)
        pl.when(s == 0)(merge_weights)

    for name in ("res3", "unit1", "scale"):
        load(name).wait()
    each(second_back)
    for name in ("dact", "act", "h"):
        load(name).wait()
    weight(3).wait()
    weight(2).wait()

    def ffn_back(s):
        gf.forward(s)
        gf.finish(s)

        def part(b, out):
            back = nt(fg[s, b], wdown[...]) * v.dact[s, b].astype(F32)
            v.dact[s, b] = back.astype(BF16)
            out[...] = nt(v.dact[s, b], win[...])

        s_hid.start(s, part)
        fire_in(s, 3, 1)

    each(ffn_back)

    def all_ffn_weights():
        def ffn_weights(j, carry):
            colsj = pl.ds(pl.multiple_of(j * step_w, step_w), step_w)
            out = tn(v.act[:, :, :, colsj].reshape(tokens, step_w), fg[...].reshape(tokens, width))
            big.down[block_rows(j, step_w), :] = out.astype(BF16)
            return carry

        lax.fori_loop(0, big.down.shape[0] // step_w, ffn_weights, 0)
        fire(6)

        def in_weights(j, carry):
            colsj = pl.ds(pl.multiple_of(j * step_w, step_w), step_w)
            out = tn(
                v.h[:, :, :, colsj].reshape(tokens, step_w), v.dact[...].reshape(tokens, -1)
            )
            big.win[block_rows(j, step_w), :] = out.astype(BF16)
            return carry

        lax.fori_loop(0, width // step_w, in_weights, 0)
        x_copy().start()
        fire(7)

    load("unit0").wait()

    def first_back(s):
        incoming = res2[s] + s_hid.finish(s)
        unit = v.unit0[s]
        small[0, 4:5] += jnp.sum(incoming * unit, axis=0, keepdims=True)
        small[0, 6:7] += jnp.sum(incoming, axis=0, keepdims=True)
        spread = v.scale[s, 0][:, 0:1]
        res1[s] = normalize_back(unit, spread, incoming * gain[0:1])
        v.mid[s, me] = res1[s].astype(BF16)
        ga.start(s)
        fire_in(s, 5, 3)
        pl.when(s == 0)(all_ffn_weights)

    each(first_back)

    def chars_back(s):
        def char_part(b, out):
            first = pl.multiple_of(width + b * 2 * LANE, 2 * LANE)
            out[...] = nn(dyk[s], wc[:, pl.ds(first, 2 * LANE)])
            out[block_rows(me, shard), :] += v.res4[s, b].astype(F32)

        s_chr.start(s, char_part)
        fire_in(s, 9, 1)

    each(chars_back)
    hops = [("t", g.pair), ("t", g.far)] + ([("d", k) for k in range(3)] if inside else [])
    slots_t, slots_d = g.slots(2), plane.take(3)

    def small_copy(number):
        kind, where = hops[number]
        source, target = small.at[number], small_land.at[number]
        if kind == "t":
            return g.copy(slots_t[number], 0, source, target, where)
        return plane.copy(slots_d[where], source, target, plane.pair(where))

    def small_step(number):
        if number > 0:
            small_copy(number - 1).wait()
            value, more = small[number - 1], small_land[number - 1]
            small[number, pl.ds(0, 8), :] = value[:8] + more[:8]
            rest = small[6, pl.ds(0, 8), :] if number <= 2 else value[8:] + more[8:]
            small[number, pl.ds(8, 8), :] = rest
        if number < len(hops):
            small_copy(number).start()

    if not inside:
        hops = []
    small_step(0) if hops else None
    for name in ("qkv", "ctx"):
        load(name).wait()
    weight(1).wait()
    weight(0).wait()
    p_copy().wait()

    def attention_back(s):
        ga.forward(s)
        ga.finish(s)
        dctx = v.dmg

        def context(t, carry):
            dctx[s, block_rows(t, shard), :] = nt(v.mid[s, t], wout[...]).astype(BF16)
            return carry

        lax.fori_loop(0, 4, context, 0)
        for tile in range(cols // LANE):
            lanes = pl.ds(tile * LANE, LANE)
            for half in range(2):
                head = 2 * tile + half
                if head >= heads:
                    continue
                paired = 2 * tile + 1 < heads

                def rows_of(b, carry):
                    rows = block_rows(b, shard)
                    grad = dctx[s, rows, lanes]
                    if paired:
                        grad = jnp.where(left if half == 0 else ~left, grad, jnp.zeros_like(grad))
                    back = nt(grad, v.qkv[s, 2, :, lanes])
                    probs = pb[s, head * 4 + b].astype(F32)
                    row_dot = jnp.sum(probs * back, axis=-1, keepdims=True)
                    ds[b] = (probs * (back - row_dot)).astype(BF16)
                    out = nn(ds[b], v.qkv[s, 1, :, lanes])
                    if half == 1:
                        out = jnp.where(left, ctemp[rows, lanes], out)
                    ctemp[rows, lanes] = out
                    return carry

                lax.fori_loop(0, 4, rows_of, 0)
                keys = tn(ds[...].reshape(length, length), v.qkv[s, 0, :, lanes])
                values = tn(
                    pb[s, pl.ds(head * 4, 4)].reshape(length, length), dctx[s, :, lanes]
                )
                if half == 1:
                    wide_left = lax.broadcasted_iota(jnp.int32, (length, LANE), 1) < HD
                    keys = jnp.where(wide_left, parts[0, :, lanes], keys)
                    values = jnp.where(wide_left, parts[1, :, lanes], values)
                parts[0, :, lanes] = keys
                parts[1, :, lanes] = values
                fire_in(s, 11 + head, 4)

        def pack(t, carry):
            rows = block_rows(t, shard)
            query = ctemp[rows, :].astype(BF16).astype(F32) * 0.125
            dyk[s, rows, :] = pack3(
                [query, parts[0, rows, :], parts[1, rows, :]], HD * heads
            ).astype(BF16)
            return carry

        lax.fori_loop(0, 4, pack, 0)

        def part(b, out):
            out[...] = nn(dyk[s, block_rows(b, shard), :], wq[...])

        s_tok.start(s, part)

        fire_in(s, 14, 4)

    each(attention_back)
    small_step(1) if hops else None

    x_copy().wait()

    tall = 3 * HD * heads
    half_w = width // 2

    def qkv_weights(j, carry):
        lanes = pl.ds(pl.multiple_of(j * LANE, LANE), LANE)
        size = min(LANE, tall - LANE * j) if isinstance(j, int) else LANE
        out = tn(dyk[:, :, lanes].reshape(tokens, LANE), v.h[...].reshape(tokens, width))
        for k in range(2):
            first = k * tall + j * LANE
            first = first if isinstance(j, int) else pl.multiple_of(first, 64)
            big.qkv[pl.ds(first, size), :] = out[:size, k * half_w : (k + 1) * half_w].astype(BF16)
        return carry

    lax.fori_loop(0, tall // LANE, qkv_weights, 0)
    if tall % LANE:
        qkv_weights(tall // LANE, 0)
    out = tn(v.ctx[...].reshape(tokens, -1), v.mid[...].reshape(tokens, width))
    for k in range(2):
        big.out[pl.ds(k * HD * heads, HD * heads), :] = out[
            : HD * heads, k * half_w : (k + 1) * half_w
        ].astype(BF16)
    fire(19)

    load("c").wait()
    weight(4).wait()

    def gru_back(s):
        gtok[...] = s_chr.finish(s).astype(BF16)
        for peer in (g.pair, g.far):
            pl.semaphore_signal(
                credit.at[s], inc=1, device_id={"tensor": peer},
                device_id_type=pl.DeviceIdType.MESH,
            )
        def spread_out(t, carry):
            rows = block_rows(t, LANE)
            for tile in range(2):
                ids = lax.broadcasted_iota(jnp.int32, (LANE, length), 0) + t * LANE
                hot = (ids == pickr[s, tile : tile + 1, :]).astype(F32).astype(BF16)
                drive[tile, rows, :] = nn(hot, gtok[:, pl.ds(tile * LANE, LANE)])
            return carry

        lax.fori_loop(0, total // LANE, spread_out, 0)
        fire_in(s, 20, 3)
        for tile in range(2):
            decay_copy(s, tile).wait()
        recur((False, True), decay, drive, drive, block_chars, back=True)
        fire_in(s, 21, 3)
        states_copy(s).wait()

        @pl.when(s == 0)
        def _():
            gru_acc[...] = jnp.zeros_like(gru_acc)

        def part(b, out):
            def finish(t, sums):
                inner = block_rows(t, LANE)
                rows = pl.ds(pl.multiple_of(b * block_chars + t * LANE, LANE), LANE)
                proj = nt(v.c[s, b, inner, :], wg[...])
                new = []
                for tile in range(2):
                    colst = slice(tile * LANE, (tile + 1) * LANE)
                    gate = jax.nn.sigmoid(proj[:, colst] + gate_bias[tile : tile + 1])
                    cand = proj[:, (2 + tile) * LANE : (3 + tile) * LANE]
                    flow = drive[tile, rows, :] * gate
                    logit = flow * (cand - states[tile, rows, :].astype(F32))
                    dproj[inner, pl.ds(tile * LANE, LANE)] = logit.astype(BF16)
                    dproj[inner, pl.ds((2 + tile) * LANE, LANE)] = flow.astype(BF16)
                    new.append(sums[tile] + jnp.sum(logit, axis=0, keepdims=True))
                return tuple(new)

            zero = jnp.zeros((1, LANE), F32)
            sums = lax.fori_loop(0, block_chars // LANE, finish, (zero, zero))
            for tile in range(2):
                small[6, 0:1, pl.ds(tile * LANE, LANE)] += sums[tile]
            out[...] = nn(dproj[...], wg[...])
            gru_acc[...] += tn(dproj[...], v.c[s, b])

        pl.semaphore_wait(credit.at[s], 2)
        s_cout.start(s, part)

        @pl.when(s + 1 < seqs)
        def _():
            states_copy(s + 1).start()
            for tile in range(2):
                decay_copy(s + 1, tile).start()

        if seqs > 1:
            pl.when(s == 0)(functools.partial(fire, 22))

    each(gru_back)
    for d in range(2):
        for k in range(2):
            big.gru[pl.ds((2 * d + k) * units, units), :] = gru_acc[
                pl.ds((2 * k + d) * LANE, units), :
            ].astype(BF16)
    small_step(2) if hops else None
    fire(25)

    def last(s):
        res1[s] = res1[s] + s_tok.finish(s)
        out_copy(0, s).start()
        cheld[s] = s_cout.finish(s)
        out_copy(1, s).start()

    each(last)

    def emit(name):
        return pltpu.make_async_copy(
            getattr(big, name), grads_out[name], local.at[spare + 4 + 3 * seqs + GRADS.index(name)]
        )

    if inside:
        fire(26)
        small_step(3)
        fire(27)
        small_step(4)
        fire(28)
        small_step(5)
        fire(29)
        assert all(count == Reduce.steps for count in fired)
    else:
        for name in GRADS:
            emit(name).start()
        for name in GRADS:
            emit(name).wait()
    small_out[...] = small[len(hops)]
    if not inside:
        small_out[pl.ds(8, 8), :] = small[6, pl.ds(0, 8), :]
    each(lambda s: (out_copy(0, s).wait(), out_copy(1, s).wait()))


def backward_call(saved, weights, small, dp_size):
    wq, wout, win, wdown, wg, wc, wm, gate_bias = weights
    sds = jax.ShapeDtypeStruct
    seqs, shard, width = saved["res3"].shape
    length = shard * 4
    block_chars, char_width = saved["c"].shape[2:]
    total = 4 * block_chars
    cols, packed = wout.shape[0], wc.shape[0]
    tall = 3 * HD * small["heads"]
    channels = small["channels"]
    saved_in = [saved[n] for n in SAVED]
    names = [n for n in SAVED if n not in ("branch", "states", "decay", "p", "x")]
    shapes = [(saved[n].shape, saved[n].dtype) for n in names]
    grads = {
        "merge": (2 * channels, width), "conv": (2 * 3 * channels, width),
        "down": (win.shape[1], width), "win": (width, win.shape[1]),
        "gru": (4 * small["units"], char_width), "out": (2 * tall // 3, width // 2),
        "qkv": (2 * tall, width // 2),
    }
    pad = (seqs, 3, shard, width)
    cpad = (seqs, 3, length, 2 * LANE)
    scratch = shapes + [(w.shape, BF16) for w in weights[:7]] + [
        (saved["p"].shape, BF16),
        ((2, total, LANE), BF16),
        ((2, total, LANE), F32),
        ((2, total, LANE), F32),
        ((length + 16, wm.shape[0]), F32),
        ((seqs, length, packed), BF16),
        ((seqs, 4, shard, width), BF16),
        ((length, 2 * LANE), BF16),
        ((block_chars, 4 * LANE), BF16),
        ((4 * LANE, char_width), F32),
        ((seqs, shard, width), F32),
        ((seqs, shard, width), F32),
        ((4, shard, length), BF16),
        ((2, length, cols), F32),
        (pad, BF16), (pad, BF16), ((seqs, shard, width), F32), ((shard, width), F32),
        (cpad, BF16), (cpad, BF16), ((seqs, length, 2 * LANE), F32), ((length, 2 * LANE), F32),
    ]
    for which, name in enumerate(GRADS):
        landing = sum(Reduce.landing_rows(n, way) for k, n, way in PIECES if k == which)
        scratch.append(((landing if dp_size == 8 else 16, grads[name][1]), BF16))
    scratch += [(shape, BF16) for shape in grads.values()]
    scratch += [((7, 16, width), F32), ((5, 16, width), F32), ((2, LANE), F32)]
    anyspace = pl.BlockSpec(memory_space=pl.ANY)
    vmem = pl.BlockSpec(memory_space=pltpu.VMEM)
    ins = saved_in + list(weights) + [small["gain"]]
    ins += [saved["pickr"], saved["edges"], saved["norm_grads"]]
    outs = pl.pallas_call(
        functools.partial(backward_kernel, small["units"], channels, dp_size),
        out_shape=[sds((seqs, shard, width), F32), sds((seqs, block_chars, char_width), F32)]
        + [sds(shape, BF16) for shape in grads.values()]
        + [sds((16, width), F32)],
        in_specs=[anyspace] * (len(saved_in) + 7) + [vmem] * 5,
        out_specs=[anyspace] * (2 + len(grads)) + [vmem],
        scratch_shapes=[pltpu.VMEM(*one) for one in scratch]
        + [
            pltpu.SemaphoreType.DMA((32 * seqs,)),
            pltpu.SemaphoreType.DMA((32 * seqs,)),
            pltpu.SemaphoreType.DMA((14 * len(PIECES) + 4,)),
            pltpu.SemaphoreType.DMA((14 * len(PIECES) + 4,)),
            pltpu.SemaphoreType.DMA((48,)),
            pltpu.SemaphoreType.DMA((len(PIECES),)),
            pltpu.SemaphoreType.REGULAR((seqs,)),
        ],
        compiler_params=pltpu.CompilerParams(
            collective_id=1, has_side_effects=True, vmem_limit_bytes=63 * MIB
        ),
    )(*ins)
    names = ["grad_tokens", "grad_chars"] + list(grads) + ["small"]
    return dict(zip(names, outs))


def finish_kernel(
    units, conv, qkv, out, merge, down, win, gru, chars, tokens, first, second, rows,
    o_conv, o_qkv, o_out, o_merge, o_down, o_win, o_gru, o_chars, o_tokens, o_first, o_second,
    o_gain, o_bias, o_gate,
):
    for source, target in ((conv, o_conv), (qkv, o_qkv), (out, o_out)):
        half = source.shape[2]
        for k in range(2):
            target[:, k * half : (k + 1) * half] = source[k].astype(F32)
    for k in range(2):
        o_merge[:, k, :] = merge[k].astype(F32)
        o_gate[k : k + 1, :] = rows[8:9, k * LANE : k * LANE + units]
    for target, at in ((o_gain, 0), (o_bias, 2)):
        target[0:2] = rows[4 + at : 6 + at]
        target[2:4] = rows[at : at + 2]
    for source, target in ((down, o_down), (win, o_win), (gru, o_gru)):
        target[...] = source[...].astype(F32)
    for j in range(8):
        o_chars[0, j] = chars[0, :, j, :]
    for source, target in ((tokens, o_tokens), (first, o_first), (second, o_second)):
        target[...] = source[...]


def finish_call(grads, grad_chars, grad_tokens, token_out, char_out, rows, units):
    seqs, block_chars, char_width = grad_chars.shape
    steps = block_chars // 8
    turns = 2 * seqs
    chars = grad_chars.reshape(seqs, steps, 8, char_width)
    pairs = [
        grads[n].reshape(2, -1, grads[n].shape[1]) for n in ("conv", "qkv", "out", "merge")
    ]
    plain = [grads["down"], grads["win"], grads["gru"]]
    copied = [grad_tokens, token_out, char_out]
    flat = [(a.shape[1], 2 * a.shape[2]) for a in pairs[:3]]
    channels, width = pairs[3].shape[1:]
    merged = (channels, 2, width)
    plain_shapes = [a.shape for a in plain]
    ends = [(4, width), (4, width), (2, units)]

    def rows_spec(shape):
        return pl.BlockSpec((shape[0] // turns, shape[1]), lambda i: (i, 0))

    def pair_spec(shape):
        return pl.BlockSpec((2, shape[1] // turns, shape[2]), lambda i: (0, i, 0))

    def halves(shape):
        return pl.BlockSpec((1, shape[1] // 2, shape[2]), lambda i: (i // 2, i % 2, 0))

    return pl.pallas_call(
        functools.partial(finish_kernel, units),
        grid=(turns,),
        out_shape=[jax.ShapeDtypeStruct(shape, F32) for shape in flat + [merged] + plain_shapes]
        + [jax.ShapeDtypeStruct((seqs, 8, steps, char_width), F32)]
        + [jax.ShapeDtypeStruct(a.shape, a.dtype) for a in copied]
        + [jax.ShapeDtypeStruct(shape, F32) for shape in ends],
        in_specs=[pair_spec(a.shape) for a in pairs]
        + [rows_spec(a.shape) for a in plain]
        + [pl.BlockSpec((1, steps // 2, 8, char_width), lambda i: (i // 2, i % 2, 0, 0))]
        + [halves(a.shape) for a in copied]
        + [pl.BlockSpec(rows.shape, lambda i: (0, 0))],
        out_specs=[rows_spec(shape) for shape in flat]
        + [pl.BlockSpec((channels // turns, 2, width), lambda i: (i, 0, 0))]
        + [rows_spec(shape) for shape in plain_shapes]
        + [pl.BlockSpec((1, 8, steps // 2, char_width), lambda i: (i // 2, 0, i % 2, 0))]
        + [halves(a.shape) for a in copied]
        + [pl.BlockSpec(shape, lambda i: (0, 0)) for shape in ends],
        compiler_params=pltpu.CompilerParams(vmem_limit_bytes=62 * MIB),
    )(*pairs, *plain, chars, *copied, rows)


def local(
    tokens,
    characters,
    doc_lengths,
    token_chars,
    w_qkv,
    w_out,
    w_in,
    w_down,
    w_gru,
    gate_bias,
    w_conv,
    w_merge,
    norm_gain,
    norm_bias,
    token_cot,
    char_cot,
):
    micro_count = tokens.shape[0]
    shard_len = tokens.shape[1]
    model_width = tokens.shape[2]
    char_width = characters.shape[2]
    group_size = lax.axis_size("tensor")
    group_rank = lax.axis_index("tensor")
    length = shard_len * group_size
    char_total = characters.shape[1] * group_size
    head_cols = w_qkv.shape[2]
    heads_here = head_cols // HD
    units_here = w_gru.shape[3]
    merge_here = w_conv.shape[2]
    wq = jnp.transpose(w_qkv, (1, 2, 0)).reshape(3 * head_cols, model_width)
    wc = jnp.transpose(w_conv, (0, 2, 1)).reshape(3 * merge_here, 2 * model_width)
    wg = jnp.transpose(w_gru, (1, 2, 3, 0))
    small = dict(
        gain=norm_gain, bias=norm_bias, cot_t=token_cot, cot_c=char_cot, docs=doc_lengths,
        counts=token_chars, heads=heads_here, units=units_here, channels=merge_here,
    )
    weights = (wq, w_out, w_in, w_down, wg, gate_bias, wc, w_merge)
    fw = forward_call(tokens, characters, weights, small)
    weights = (fw["wq"], fw["wout"], w_in, w_down, fw["wg"], fw["wc"], fw["wm"], gate_bias)
    dp_size = lax.axis_size("dp")
    bw = backward_call(fw, weights, small, dp_size)
    rows = bw["small"]
    grads = {name: bw[name] for name in GRADS}
    if dp_size != 8:
        grads, gate_rows = lax.psum((grads, rows[8:]), "dp")
        rows = jnp.concatenate([lax.psum(rows[:8], ("dp", "tensor")), gate_rows], axis=0)
    (conv, qkv, out, merge, down, win, gru, chars, tokens_grad, first, second, gain_grad, bias_grad,
     gate_grad) = finish_call(
        grads, bw["grad_chars"], bw["grad_tokens"], fw["token_out"], fw["char_out"], rows,
        units_here,
    )
    conv = conv.reshape(3, merge_here, 2 * model_width)
    qkv = qkv.reshape(3, head_cols, model_width)
    gru = gru.reshape(2, 2, units_here, char_width)
    return (
        first,
        second,
        tokens_grad,
        chars.reshape(bw["grad_chars"].shape),
        jnp.transpose(qkv, (2, 0, 1)),
        out,
        win,
        down,
        jnp.transpose(gru, (3, 0, 1, 2)),
        gate_grad,
        jnp.transpose(conv, (0, 2, 1)),
        merge,
        gain_grad,
        bias_grad,
    )


def solution(mesh):
    return jax.shard_map(
        local,
        mesh=mesh,
        in_specs=(
            P("dp", "tensor", None),
            P("dp", "tensor", None),
            P("dp", None),
            P("dp", None),
            P(None, None, "tensor"),
            P("tensor", None),
            P(None, "tensor"),
            P("tensor", None),
            P(None, None, None, "tensor"),
            P(None, "tensor"),
            P(None, None, "tensor"),
            P("tensor", None, None),
            P(),
            P(),
            P("dp", "tensor", None),
            P("dp", "tensor", None),
        ),
        out_specs=(
            P("dp", "tensor", None),
            P("dp", "tensor", None),
            P("dp", "tensor", None),
            P("dp", "tensor", None),
            P(None, None, "tensor"),
            P("tensor", None),
            P(None, "tensor"),
            P("tensor", None),
            P(None, None, None, "tensor"),
            P(None, "tensor"),
            P(None, None, "tensor"),
            P("tensor", None, None),
            P(),
            P(),
        ),
        check_vma=False,
    )
```
